32 devices in a mesh: tab: 4 (over y, x), blk: 8 (over z, core).
Axes of the slice: x: 2, y: 2, z: 4, core: 2. Of those that a mesh axis runs over, the one named last changes fastest.
Arguments:
- tokens: bfloat16 [8, 2048, 768], P('tab', 'blk'), may hold values from -6 to 6
- lengths: int32 [8], P('tab'), may hold values from 128 to 2048, as said below
- qkv_weight: bfloat16 [768, 2304], replicated, may hold values from -0.21875 to 0.21875
- qkv_bias: bfloat16 [1536], replicated, may hold values from -1 to 1
- out_weight: bfloat16 [768, 768], replicated, may hold values from -0.75 to 0.75
- out_bias: bfloat16 [768], replicated, may hold values from -3 to 3
- attn_gain: bfloat16 [768], replicated, may hold values from 0.5 to 1.5
- attn_shift: bfloat16 [768], replicated, may hold values from -3 to 3
- up_weight: bfloat16 [768, 3072], replicated, may hold values from -0.21875 to 0.21875
- up_bias: bfloat16 [3072], replicated, may hold values from -3 to 3
- down_weight: bfloat16 [3072, 768], replicated, may hold values from -0.109375 to 0.109375
- down_bias: bfloat16 [768], replicated, may hold values from -3 to 3
- ffn_gain: bfloat16 [768], replicated, may hold values from 0.5 to 1.5
- ffn_shift: bfloat16 [768], replicated, may hold values from -3 to 3
- cotangent: bfloat16 [8, 2048, 768], P('tab', 'blk'), may hold values from -6 to 6
Outputs:
- layer_out: bfloat16 [8, 2048, 768], P('tab', 'blk')
- token_grad: bfloat16 [8, 2048, 768], P('tab', 'blk')
- wgrad_qkv: float32 [768, 2304], P(('tab', 'blk'))
- bgrad_qkv: float32 [1536], P(('tab', 'blk'))
- wgrad_out: float32 [768, 768], P(('tab', 'blk'))
- bgrad_out: float32 [768], P(('tab', 'blk'))
- ggrad_attn: float32 [768], P(('tab', 'blk'))
- sgrad_attn: float32 [768], P(('tab', 'blk'))
- wgrad_up: float32 [768, 3072], P(('tab', 'blk'))
- bgrad_up: float32 [3072], P(('tab', 'blk'))
- wgrad_down: float32 [3072, 768], P(('tab', 'blk'))
- bgrad_down: float32 [768], P(('tab', 'blk'))
- ggrad_ffn: float32 [768], P(('tab', 'blk'))
- sgrad_ffn: float32 [768], P(('tab', 'blk'))
The draws below stay inside these ranges and needn't reach their ends.
Inputs may be any that keep to these rules, and one draw needn't show every extreme that they name: `lengths`: among each 2 consecutive tables one, drawn from the seed, has exactly 2048 tokens.
All inputs are finite; a program needn't handle non-finite values.
Results may differ from the reference program's by a relative error of at most 0.023.
Values may be sent and summed in bfloat16 or wider, within the bound.
A program may use at most 192 MiB of HBM per device.

```python
import jax
import jax.numpy as jnp
from jax import lax

D = 768
HD = 64
FF = 3072
LPAD = 2048
TAB_DEV = 2
ROWS_DEV = 256
TABLES = 8
N_BLK = 8


def draw_lengths(key, part):
    groups = TABLES // TAB_DEV
    spread = jax.random.randint(key, (TABLES,), max(1, LPAD // 16), LPAD + 1, dtype=jnp.int32)
    chosen = jax.random.randint(jax.random.fold_in(key, 7), (groups,), 0, TAB_DEV, dtype=jnp.int32)
    slot_index = jnp.arange(TABLES, dtype=jnp.int32) % TAB_DEV
    is_full = slot_index == jnp.repeat(chosen, TAB_DEV)
    return jnp.where(is_full, jnp.int32(LPAD), spread)


def level_of(stream_key, extent, shards, low, top_value):
    level, own = 1.0, jax.random.fold_in(stream_key, 6)
    for axis_at, blocks in shards:
        steps = jnp.exp(jax.random.uniform(jax.random.fold_in(own, axis_at), (blocks,), jnp.float32, low / len(shards), top_value / len(shards)))
        level = level * jnp.repeat(steps, extent[axis_at] // blocks).reshape([-1 if axis == axis_at else 1 for axis in range(len(extent))])
    return level


def scatter_about(key, shape, deviation, limit, pieces=(), held_as=jnp.bfloat16):
    loudness = level_of(key, shape, pieces, -0.22, 0.18) if pieces else 1.0
    values = jax.random.normal(key, shape, jnp.float32) * deviation * loudness
    return jnp.minimum(jnp.maximum(values, -limit), limit).astype(held_as)


def setup_inputs(seed: int = 0) -> dict:
    arg_keys = jax.random.split(jax.random.key(seed), 16)
    return {
        "tokens": scatter_about(arg_keys[0], (TABLES, LPAD, D), 1.0, 6.0, ((0, 4), (1, 8))),
        "lengths": draw_lengths(jax.random.fold_in(arg_keys[15], 71), 0),
        "qkv_weight": scatter_about(arg_keys[2], (D, 3 * D), D ** -0.5, 0.21875),
        "qkv_bias": scatter_about(arg_keys[3], (2 * D,), 0.2, 1.0),
        "out_weight": scatter_about(arg_keys[4], (D, D), 64 ** -0.5, 0.75),
        "out_bias": scatter_about(arg_keys[5], (D,), 0.5, 3.0),
        "attn_gain": jnp.clip(1.0 + 0.1 * jax.random.normal(arg_keys[6], (D,), jnp.float32), 0.5, 1.5).astype(jnp.bfloat16),
        "attn_shift": scatter_about(arg_keys[7], (D,), 0.5, 3.0),
        "up_weight": scatter_about(arg_keys[8], (D, FF), D ** -0.5, 0.21875),
        "up_bias": scatter_about(arg_keys[9], (FF,), 0.5, 3.0),
        "down_weight": scatter_about(arg_keys[10], (FF, D), FF ** -0.5, 0.109375),
        "down_bias": scatter_about(arg_keys[11], (D,), 0.5, 3.0),
        "ffn_gain": jnp.clip(1.0 + 0.1 * jax.random.normal(arg_keys[12], (D,), jnp.float32), 0.5, 1.5).astype(jnp.bfloat16),
        "ffn_shift": scatter_about(arg_keys[13], (D,), 0.5, 3.0),
        "cotangent": scatter_about(arg_keys[14], (TABLES, LPAD, D), 1.0, 6.0, ((0, 4), (1, 8))),
    }


@jax.custom_vjp
def low(v):
    return lax.optimization_barrier(v.astype(jnp.bfloat16)).astype(jnp.float32)

@jax.custom_vjp
def low_back(v):
    return v

def low_keep(v):
    return (low(v), None)

def low_pass(kept, grad):
    return (grad,)

def back_keep(v):
    return (v, None)

def back_low(kept, grad):
    return (low(grad),)
low.defvjp(low_keep, low_pass)
low_back.defvjp(back_keep, back_low)
EPSILON = 1e-05
NEGATIVE = -1e+30
PRECISE = lax.Precision.HIGHEST

def norm_rows(inputs, gains, shifts):
    row_mean = lax.optimization_barrier(jnp.mean(inputs, axis=-1, keepdims=True))
    centred = inputs - row_mean
    row_var = lax.optimization_barrier(jnp.mean(centred * centred, axis=-1, keepdims=True))
    return centred * lax.rsqrt(row_var + EPSILON) * gains + shifts

def block_size():
    per_block = 1
    while per_block * 2 * ROWS_DEV <= 512 and N_BLK % (per_block * 2) == 0:
        per_block = per_block * 2
    return per_block * ROWS_DEV

def table_layer(table_rows, table_length, params):
    qkv_weight, qkv_bias, out_weight, out_bias, attn_gain, attn_shift, up_weight, up_bias, down_weight, down_bias, ffn_gain, ffn_shift = params
    row_total = table_rows.shape[0]
    model_width = table_rows.shape[1]
    head_count = model_width // HD
    bias_full = jnp.concatenate([qkv_bias[:model_width], jnp.zeros((model_width,), jnp.float32), qkv_bias[model_width:]])
    qkv_full = low_back(low(jnp.dot(table_rows, qkv_weight, precision=PRECISE) + bias_full))
    queries = qkv_full[:, :model_width].reshape(row_total, head_count, HD)
    keys_all = qkv_full[:, model_width:2 * model_width].reshape(row_total, head_count, HD)
    values_all = qkv_full[:, 2 * model_width:].reshape(row_total, head_count, HD)
    is_valid = (jnp.arange(row_total, dtype=jnp.int32) < table_length)[None, None, :]
    block_rows = block_size()

    def attend(query_block):
        raw_scores = low_back(jnp.einsum('qhd,khd->hqk', query_block, keys_all, precision=PRECISE))
        scores = jnp.where(is_valid, raw_scores * HD ** (-0.5), NEGATIVE)
        weights = low(jax.nn.softmax(scores, axis=-1))
        return jnp.einsum('hqk,khd->qhd', weights, values_all, precision=PRECISE).reshape(block_rows, model_width)
    context = lax.map(jax.checkpoint(attend), queries.reshape(row_total // block_rows, block_rows, head_count, HD))
    context = low_back(low(context.reshape(row_total, model_width)))
    attended = low_back(jnp.dot(context, out_weight, precision=PRECISE) + out_bias)
    hidden = norm_rows(table_rows + attended, attn_gain, attn_shift)
    upper = low_back(jnp.dot(low(hidden), up_weight, precision=PRECISE) + up_bias)
    active = low(jax.nn.gelu(upper, approximate=False))
    branch_out = low_back(jnp.dot(active, down_weight, precision=PRECISE) + down_bias)
    return norm_rows(hidden + branch_out, ffn_gain, ffn_shift)

def reference(tokens, lengths, qkv_weight, qkv_bias, out_weight, out_bias, attn_gain, attn_shift, up_weight, up_bias, down_weight, down_bias, ffn_gain, ffn_shift, cotangent):
    params = (qkv_weight.astype(jnp.float32), qkv_bias.astype(jnp.float32), out_weight.astype(jnp.float32), out_bias.astype(jnp.float32), attn_gain.astype(jnp.float32), attn_shift.astype(jnp.float32), up_weight.astype(jnp.float32), up_bias.astype(jnp.float32), down_weight.astype(jnp.float32), down_bias.astype(jnp.float32), ffn_gain.astype(jnp.float32), ffn_shift.astype(jnp.float32))

    def forward(token_rows, weight_set):
        layer = jax.checkpoint(table_layer)

        def visit(carry_zero, item_pair):
            return (carry_zero, layer(item_pair[0], item_pair[1], weight_set))
        _, outputs = lax.scan(visit, jnp.zeros((), jnp.float32), (token_rows, lengths))
        return outputs
    result, pullback = jax.vjp(forward, tokens.astype(jnp.float32), params)
    token_part, param_part = pullback(cotangent.astype(jnp.float32))
    return (result.astype(jnp.bfloat16), token_part.astype(jnp.bfloat16), param_part[0], param_part[1], param_part[2], param_part[3], param_part[4], param_part[5], param_part[6], param_part[7], param_part[8], param_part[9], param_part[10], param_part[11])
```

```python
import functools
import math

import jax
import jax.numpy as jnp
from jax import lax
from jax.experimental import pallas as pl
from jax.experimental.pallas import tpu as pltpu
from jax.sharding import PartitionSpec as P

HD = 64


EPSILON = 1e-05
NEGATIVE = -1e30


def from_behind(block, axis, distance):
    devices = range(lax.axis_size(axis))
    route = [((i - distance) % len(devices), i) for i in devices]
    return lax.ppermute(block, axis, route)


def norm_rows(inputs, gains, shifts):
    row_mean = jnp.mean(inputs, axis=-1, keepdims=True)
    centred = inputs - row_mean
    row_var = jnp.mean(centred * centred, axis=-1, keepdims=True)
    return centred * lax.rsqrt(row_var + EPSILON) * gains + shifts


def gelu_exact(inputs):
    return jax.nn.gelu(inputs, approximate=False)


def times_back(left, right):
    return lax.dot_general(
        left, right, (((1,), (1,)), ((), ())), preferred_element_type=jnp.float32
    )


def over_rows(left, right):
    return lax.dot_general(
        left, right, (((0,), (0,)), ((), ())), preferred_element_type=jnp.float32
    )


def shards_ring(
    tokens,
    lengths,
    qkv_weight,
    qkv_bias,
    out_weight,
    out_bias,
    attn_gain,
    attn_shift,
    up_weight,
    up_bias,
    down_weight,
    down_bias,
    ffn_gain,
    ffn_shift,
    cotangent,
):
    table_count, row_count, model_width = tokens.shape
    head_count = model_width // HD
    cycle_size = lax.axis_size("blk")
    cycle_place = lax.axis_index("blk")
    score_scale = HD ** (-0.5)
    flat_tokens = tokens.reshape(table_count * row_count, model_width)
    bias_full = jnp.concatenate(
        [
            qkv_bias[:model_width].astype(jnp.float32),
            jnp.zeros((model_width,), jnp.float32),
            qkv_bias[model_width:].astype(jnp.float32),
        ]
    )
    qkv_low = (
        jnp.dot(flat_tokens, qkv_weight, preferred_element_type=jnp.float32) + bias_full
    ).astype(jnp.bfloat16)
    queries = qkv_low[:, :model_width].reshape(table_count, row_count, head_count, HD)
    key_values = qkv_low[:, model_width:].reshape(table_count, row_count, 2 * model_width)

    def key_mask(first_row, key_count):
        positions = first_row + jnp.arange(key_count, dtype=jnp.int32)
        return (positions[None, :] < lengths[:, None])[:, None, None, :]

    def split_pair(pair_block):
        key_count = pair_block.shape[1]
        keys_part = pair_block[:, :, :model_width].reshape(table_count, key_count, head_count, HD)
        values_part = pair_block[:, :, model_width:].reshape(table_count, key_count, head_count, HD)
        return (keys_part, values_part)

    pair_block = lax.all_gather(key_values, "blk", axis=1, tiled=True)
    running_max = jnp.full((table_count, row_count, head_count), NEGATIVE, jnp.float32)
    keys_part, values_part = split_pair(pair_block)
    is_valid = key_mask(jnp.int32(0), pair_block.shape[1])
    raw_scores = jnp.einsum(
        "trhd,tkhd->trhk", queries, keys_part, preferred_element_type=jnp.float32
    )
    scores = jnp.where(is_valid, raw_scores * score_scale, NEGATIVE)
    peak_new = jnp.maximum(running_max, jnp.max(scores, axis=-1))
    exponent = jnp.where(is_valid, jnp.exp(scores - peak_new[..., None]), 0.0)
    running_sum = jnp.sum(exponent, axis=-1)
    weighted = jnp.einsum(
        "trhk,tkhd->trhd",
        exponent.astype(jnp.bfloat16),
        values_part,
        preferred_element_type=jnp.float32,
    )
    running_max, running_sum, weighted = (peak_new, running_sum, weighted)
    context = weighted / running_sum[..., None]
    log_total = running_max + jnp.log(running_sum)
    context_low = context.reshape(table_count * row_count, model_width).astype(jnp.bfloat16)
    attended = jnp.dot(
        context_low, out_weight, preferred_element_type=jnp.float32
    ) + out_bias.astype(jnp.float32)
    pre_one = flat_tokens.astype(jnp.float32) + attended
    gain_one = attn_gain.astype(jnp.float32)
    shift_one = attn_shift.astype(jnp.float32)
    hidden = norm_rows(pre_one, gain_one, shift_one)
    hidden_low = hidden.astype(jnp.bfloat16)
    upper = jnp.dot(hidden_low, up_weight, preferred_element_type=jnp.float32) + up_bias.astype(
        jnp.float32
    )
    active = gelu_exact(upper).astype(jnp.bfloat16)
    pre_two = (
        hidden
        + jnp.dot(active, down_weight, preferred_element_type=jnp.float32)
        + down_bias.astype(jnp.float32)
    )
    gain_two = ffn_gain.astype(jnp.float32)
    shift_two = ffn_shift.astype(jnp.float32)
    layer_out = norm_rows(pre_two, gain_two, shift_two).astype(jnp.bfloat16).reshape(tokens.shape)
    grad_out = cotangent.reshape(table_count * row_count, model_width).astype(jnp.float32)
    _, norm_two_back = jax.vjp(norm_rows, pre_two, gain_two, shift_two)
    grad_pre_two, ggrad_ffn, sgrad_ffn = norm_two_back(grad_out)
    grad_branch = grad_pre_two.astype(jnp.bfloat16)
    wgrad_down = over_rows(active, grad_branch)
    bgrad_down = jnp.sum(grad_branch, axis=0, dtype=jnp.float32)
    grad_active = times_back(grad_branch, down_weight)
    _, gelu_back = jax.vjp(gelu_exact, upper)
    grad_upper = gelu_back(grad_active)[0].astype(jnp.bfloat16)
    wgrad_up = over_rows(hidden_low, grad_upper)
    bgrad_up = jnp.sum(grad_upper, axis=0, dtype=jnp.float32)
    grad_hidden = grad_pre_two + times_back(grad_upper, up_weight)
    _, norm_one_back = jax.vjp(norm_rows, pre_one, gain_one, shift_one)
    grad_pre_one, ggrad_attn, sgrad_attn = norm_one_back(grad_hidden)
    grad_attended = grad_pre_one.astype(jnp.bfloat16)
    wgrad_out = over_rows(context_low, grad_attended)
    bgrad_out = jnp.sum(grad_attended, axis=0, dtype=jnp.float32)
    grad_context = times_back(grad_attended, out_weight).astype(jnp.bfloat16)
    grad_heads = grad_context.reshape(table_count, row_count, head_count, HD)
    row_delta = jnp.sum(grad_heads.astype(jnp.float32) * context, axis=-1)

    def cycle_turn_step(cycle_turn, cycle_state):
        pair_now, pair_grads, grad_queries = cycle_state
        owner_index = (cycle_place - cycle_turn) % cycle_size
        keys_part, values_part = split_pair(pair_now)
        is_valid = key_mask(owner_index * row_count, row_count)
        raw_scores = jnp.einsum(
            "trhd,tkhd->trhk", queries, keys_part, preferred_element_type=jnp.float32
        )
        scores = jnp.where(is_valid, raw_scores * score_scale, NEGATIVE)
        probs = jnp.where(is_valid, jnp.exp(scores - log_total[..., None]), 0.0)
        grad_probs = jnp.einsum(
            "trhd,tkhd->trhk", grad_heads, values_part, preferred_element_type=jnp.float32
        )
        grad_raw = (probs * (grad_probs - row_delta[..., None]) * score_scale).astype(jnp.bfloat16)
        grad_queries = grad_queries + jnp.einsum(
            "trhk,tkhd->trhd", grad_raw, keys_part, preferred_element_type=jnp.float32
        )
        grad_keys = jnp.einsum(
            "trhk,trhd->tkhd", grad_raw, queries, preferred_element_type=jnp.float32
        )
        grad_values = jnp.einsum(
            "trhk,trhd->tkhd",
            probs.astype(jnp.bfloat16),
            grad_heads,
            preferred_element_type=jnp.float32,
        )
        pair_grads = pair_grads + jnp.concatenate(
            [
                grad_keys.reshape(table_count, row_count, model_width),
                grad_values.reshape(table_count, row_count, model_width),
            ],
            axis=-1,
        )
        pair_next = from_behind(pair_now, "blk", 1)
        grads_next = from_behind(pair_grads.astype(jnp.bfloat16), "blk", 1).astype(pair_grads.dtype)
        return (pair_next, grads_next, grad_queries)

    cycle_start = (
        key_values,
        jnp.zeros((table_count, row_count, 2 * model_width), jnp.float32),
        jnp.zeros((table_count, row_count, head_count, HD), jnp.float32),
    )
    _, pair_home, grad_queries = lax.fori_loop(0, cycle_size, cycle_turn_step, cycle_start)
    grad_qkv = jnp.concatenate(
        [
            grad_queries.reshape(table_count * row_count, model_width),
            pair_home.reshape(table_count * row_count, 2 * model_width),
        ],
        axis=-1,
    ).astype(jnp.bfloat16)
    wgrad_qkv = over_rows(flat_tokens, grad_qkv)
    column_sums = jnp.sum(grad_qkv, axis=0, dtype=jnp.float32)
    bgrad_qkv = jnp.concatenate([column_sums[:model_width], column_sums[2 * model_width :]])
    token_grad = (
        (grad_pre_one + times_back(grad_qkv, qkv_weight)).astype(jnp.bfloat16).reshape(tokens.shape)
    )
    (
        wgrad_qkv,
        bgrad_qkv,
        wgrad_out,
        bgrad_out,
        ggrad_attn,
        sgrad_attn,
        wgrad_up,
        bgrad_up,
        wgrad_down,
        bgrad_down,
        ggrad_ffn,
        sgrad_ffn,
    ) = (
        lax.psum_scatter(
            wgrad_qkv.astype(jnp.bfloat16), "tab", scatter_dimension=0, tiled=True
        ).astype(jnp.float32),
        lax.psum_scatter(
            bgrad_qkv.astype(jnp.bfloat16), "tab", scatter_dimension=0, tiled=True
        ).astype(jnp.float32),
        lax.psum_scatter(
            wgrad_out.astype(jnp.bfloat16), "tab", scatter_dimension=0, tiled=True
        ).astype(jnp.float32),
        lax.psum_scatter(
            bgrad_out.astype(jnp.bfloat16), "tab", scatter_dimension=0, tiled=True
        ).astype(jnp.float32),
        lax.psum_scatter(
            ggrad_attn.astype(jnp.bfloat16), "tab", scatter_dimension=0, tiled=True
        ).astype(jnp.float32),
        lax.psum_scatter(
            sgrad_attn.astype(jnp.bfloat16), "tab", scatter_dimension=0, tiled=True
        ).astype(jnp.float32),
        lax.psum_scatter(
            wgrad_up.astype(jnp.bfloat16), "tab", scatter_dimension=0, tiled=True
        ).astype(jnp.float32),
        lax.psum_scatter(
            bgrad_up.astype(jnp.bfloat16), "tab", scatter_dimension=0, tiled=True
        ).astype(jnp.float32),
        lax.psum_scatter(
            wgrad_down.astype(jnp.bfloat16), "tab", scatter_dimension=0, tiled=True
        ).astype(jnp.float32),
        lax.psum_scatter(
            bgrad_down.astype(jnp.bfloat16), "tab", scatter_dimension=0, tiled=True
        ).astype(jnp.float32),
        lax.psum_scatter(
            ggrad_ffn.astype(jnp.bfloat16), "tab", scatter_dimension=0, tiled=True
        ).astype(jnp.float32),
        lax.psum_scatter(
            sgrad_ffn.astype(jnp.bfloat16), "tab", scatter_dimension=0, tiled=True
        ).astype(jnp.float32),
    )
    (
        wgrad_qkv,
        bgrad_qkv,
        wgrad_out,
        bgrad_out,
        ggrad_attn,
        sgrad_attn,
        wgrad_up,
        bgrad_up,
        wgrad_down,
        bgrad_down,
        ggrad_ffn,
        sgrad_ffn,
    ) = (
        lax.psum_scatter(
            wgrad_qkv.astype(jnp.bfloat16), "blk", scatter_dimension=0, tiled=True
        ).astype(jnp.float32),
        lax.psum_scatter(
            bgrad_qkv.astype(jnp.bfloat16), "blk", scatter_dimension=0, tiled=True
        ).astype(jnp.float32),
        lax.psum_scatter(
            wgrad_out.astype(jnp.bfloat16), "blk", scatter_dimension=0, tiled=True
        ).astype(jnp.float32),
        lax.psum_scatter(
            bgrad_out.astype(jnp.bfloat16), "blk", scatter_dimension=0, tiled=True
        ).astype(jnp.float32),
        lax.psum_scatter(
            ggrad_attn.astype(jnp.bfloat16), "blk", scatter_dimension=0, tiled=True
        ).astype(jnp.float32),
        lax.psum_scatter(
            sgrad_attn.astype(jnp.bfloat16), "blk", scatter_dimension=0, tiled=True
        ).astype(jnp.float32),
        lax.psum_scatter(
            wgrad_up.astype(jnp.bfloat16), "blk", scatter_dimension=0, tiled=True
        ).astype(jnp.float32),
        lax.psum_scatter(
            bgrad_up.astype(jnp.bfloat16), "blk", scatter_dimension=0, tiled=True
        ).astype(jnp.float32),
        lax.psum_scatter(
            wgrad_down.astype(jnp.bfloat16), "blk", scatter_dimension=0, tiled=True
        ).astype(jnp.float32),
        lax.psum_scatter(
            bgrad_down.astype(jnp.bfloat16), "blk", scatter_dimension=0, tiled=True
        ).astype(jnp.float32),
        lax.psum_scatter(
            ggrad_ffn.astype(jnp.bfloat16), "blk", scatter_dimension=0, tiled=True
        ).astype(jnp.float32),
        lax.psum_scatter(
            sgrad_ffn.astype(jnp.bfloat16), "blk", scatter_dimension=0, tiled=True
        ).astype(jnp.float32),
    )
    return (
        layer_out,
        token_grad,
        wgrad_qkv,
        bgrad_qkv,
        wgrad_out,
        bgrad_out,
        ggrad_attn,
        sgrad_attn,
        wgrad_up,
        bgrad_up,
        wgrad_down,
        bgrad_down,
        ggrad_ffn,
        sgrad_ffn,
    )


GROUPS = 4
LANES = 128
LOG2E = math.log2(math.e)
MESH = pl.DeviceIdType.MESH
CHUNKS = 2


def times_t(left, right):
    return lax.dot_general(
        left, right, (((1,), (1,)), ((), ())), preferred_element_type=jnp.float32
    )


def place():
    tab, blk = lax.axis_index("tab"), lax.axis_index("blk")
    return tab, blk, blk // 2, blk % 2


def meet(tab, blk):
    barrier = pltpu.get_barrier_semaphore()

    @pl.loop(1, 8)
    def _(step):
        pl.semaphore_signal(
            barrier, inc=1, device_id=(tab, lax.rem(blk + step, 8)), device_id_type=MESH
        )

    pl.semaphore_wait(barrier, 7)


def attend_kernel(
    heads,
    tok_ref,
    len_ref,
    w_ref,
    bias_ref,
    ctx_ref,
    full_ref,
    qkv_ref,
    ot_ref,
    lse_ref,
    tokv,
    qkvv,
    vtv,
    otv,
    lsev,
    csend,
    send_a,
    send_b,
    send_c,
    send_d,
    send_e,
    recv,
    csend_sem,
    crecv_sem,
    local_sem,
):
    tab, blk, chip, core = place()
    half = chip // 2
    rows = tok_ref.shape[1]
    piece = rows // CHUNKS
    is_near = jnp.logical_or(chip == 1, chip == 2)
    mate = chip + 1 - 2 * lax.rem(chip, 2)
    other_near = 2 - half
    other_far = 3 - 3 * half
    own_far = 3 * half
    scale = LOG2E / math.sqrt(HD)

    def remote(src, dst, send_sem, recv_sem, to_chip, to_core):
        return pltpu.make_async_remote_copy(
            src_ref=src,
            dst_ref=dst,
            send_sem=send_sem,
            recv_sem=recv_sem,
            device_id=(tab, 2 * to_chip + to_core),
            device_id_type=MESH,
        )

    def own_copies(part):
        cut = pl.ds(part * piece, piece)
        here, there = tok_ref.at[half, cut], tok_ref.at[1 - half, cut]
        dst, done = tokv.at[blk, cut], recv.at[blk, part]
        return (
            remote(here, dst, send_a.at[part], done, mate, core),
            remote(there, dst, send_c.at[part], done, other_near, core),
            remote(here, dst, send_b.at[part], done, chip, 1 - core),
        )

    def onward(slot, part, src_chip):
        cut = pl.ds(part * piece, piece)
        which = 2 * src_chip + core
        ref, done = tokv.at[which, cut], recv.at[which, part]
        return (
            remote(ref, ref, send_d.at[slot, part], done, own_far, core),
            remote(ref, ref, send_e.at[slot, part], done, chip, 1 - core),
        )

    def arrived(which, part):
        ref = tokv.at[which, pl.ds(part * piece, piece)]
        pltpu.make_async_copy(ref, ref, recv.at[which, part]).wait()

    meet(tab, blk)
    for part in range(CHUNKS):
        for copy in own_copies(part):
            copy.start()
    tokv[blk] = tok_ref[half]

    length = len_ref[half]
    lane = lax.broadcasted_iota(jnp.int32, (rows, LANES), 1)
    row = lax.broadcasted_iota(jnp.int32, (rows, LANES), 0)

    def project(which):
        first = pl.multiple_of(which * rows, rows)
        y = (
            jnp.dot(tokv[which], w_ref[...], preferred_element_type=jnp.float32)
            + bias_ref[...]
        )
        pad = jnp.where((lane == HD) & (row + first >= length), NEGATIVE, 0.0)
        for head in range(heads):
            q, k, v = (
                y[:, (part * heads + head) * LANES :][:, :LANES] for part in range(3)
            )
            qkvv[head, pl.ds(first, rows)] = q.astype(jnp.bfloat16)
            qkvv[heads + head, pl.ds(first, rows)] = (k + pad).astype(jnp.bfloat16)
            qkvv[2 * heads + head, pl.ds(first, rows)] = v.astype(jnp.bfloat16)
            vtv[head, :, pl.ds(first, rows)] = v.T.astype(jnp.bfloat16)

    project(blk)
    for part in range(CHUNKS):
        arrived(2 * mate + core, part)
        onward(0, part, mate)[1].start()
    project(2 * mate + core)
    for part in range(CHUNKS):
        arrived(2 * chip + 1 - core, part)
    project(2 * chip + 1 - core)
    for part in range(CHUNKS):
        arrived(2 * mate + 1 - core, part)
    project(2 * mate + 1 - core)
    for part in range(CHUNKS):
        for slot, src_chip in ((1, other_near), (2, other_far)):
            arrived(2 * src_chip + core, part)
            to_far, to_core = onward(slot, part, src_chip)
            pl.when(is_near)(to_far.start)
            to_core.start()
    for src_chip in (other_near, other_far):
        project(2 * src_chip + core)
        for part in range(CHUNKS):
            arrived(2 * src_chip + 1 - core, part)
        project(2 * src_chip + 1 - core)

    keep = (
        pltpu.make_async_copy(tokv, full_ref, local_sem.at[0]),
        pltpu.make_async_copy(qkvv, qkv_ref, local_sem.at[1]),
    )
    for copy in keep:
        copy.start()

    group = 2 * lax.rem(chip, 2) + core

    def context_copy(which):
        return remote(
            csend.at[which],
            ctx_ref.at[half, group],
            csend_sem.at[which],
            crecv_sem.at[blk],
            which // 2,
            lax.rem(which, 2),
        )

    own_context = pltpu.make_async_copy(
        csend.at[blk], ctx_ref.at[half, group], local_sem.at[2]
    )

    @pl.loop(0, 8)
    def _(step):
        which = lax.rem(blk + 1 + step, 8)
        first = pl.multiple_of(which * rows, rows)
        for head in range(heads):
            q = qkvv[head, pl.ds(first, rows)]
            st = times_t(qkvv[heads + head], q)
            peak = jnp.max(st, axis=0, keepdims=True)
            pt = jnp.exp2((st - peak) * scale).astype(jnp.bfloat16)
            ot = jnp.dot(vtv[head], pt, preferred_element_type=jnp.float32)
            total = ot[HD : HD + 1]
            otv[which, head * HD : (head + 1) * HD] = ot[:HD] / total
            lsev[which, head : head + 1] = peak * scale + jnp.log(total) * LOG2E
        csend[which] = otv[which].T.astype(jnp.bfloat16)

        @pl.when(step < 7)
        def _():
            context_copy(which).start()

        @pl.when(step == 7)
        def _():
            own_context.start()

    more = (
        pltpu.make_async_copy(otv, ot_ref, local_sem.at[3]),
        pltpu.make_async_copy(lsev, lse_ref, local_sem.at[4]),
    )
    for copy in more:
        copy.start()
    for part in range(CHUNKS):
        for copy in own_copies(part):
            copy.wait_send()
        onward(0, part, mate)[1].wait_send()
        for slot, src_chip in ((1, other_near), (2, other_far)):
            to_far, to_core = onward(slot, part, src_chip)
            pl.when(is_near)(to_far.wait_send)
            to_core.wait_send()

    @pl.loop(0, 7)
    def _(step):
        which = lax.rem(blk + 1 + step, 8)
        context_copy(which).wait_send()
        pltpu.make_async_copy(
            ctx_ref.at[which // 4, lax.rem(which, 4)],
            ctx_ref.at[which // 4, lax.rem(which, 4)],
            crecv_sem.at[which],
        ).wait()

    own_context.wait()
    for copy in keep + more:
        copy.wait()


def attend(tokens, lengths, own_weight, own_bias, heads):
    tables, rows, width = tokens.shape
    blocks = 8
    total = blocks * rows
    any_space = pl.BlockSpec(memory_space=pl.ANY)
    vmem = pl.BlockSpec(memory_space=pltpu.VMEM)
    bf16, f32 = jnp.bfloat16, jnp.float32
    dma = pltpu.SemaphoreType.DMA
    return pl.pallas_call(
        functools.partial(attend_kernel, heads),
        name="attend",
        out_shape=(
            jax.ShapeDtypeStruct((tables, GROUPS, rows, heads * HD), bf16),
            jax.ShapeDtypeStruct((blocks, rows, width), bf16),
            jax.ShapeDtypeStruct((3 * heads, total, LANES), bf16),
            jax.ShapeDtypeStruct((blocks, heads * HD, rows), f32),
            jax.ShapeDtypeStruct((blocks, 8, rows), f32),
        ),
        in_specs=[vmem, pl.BlockSpec(memory_space=pltpu.SMEM), vmem, vmem],
        out_specs=(any_space,) * 5,
        scratch_shapes=[
            pltpu.VMEM((blocks, rows, width), bf16),
            pltpu.VMEM((3 * heads, total, LANES), bf16),
            pltpu.VMEM((heads, LANES, total), bf16),
            pltpu.VMEM((blocks, heads * HD, rows), f32),
            pltpu.VMEM((blocks, 8, rows), f32),
            pltpu.VMEM((blocks, rows, heads * HD), bf16),
            dma((CHUNKS,)),
            dma((CHUNKS,)),
            dma((CHUNKS,)),
            dma((3, CHUNKS)),
            dma((3, CHUNKS)),
            dma((blocks, CHUNKS)),
            dma((blocks,)),
            dma((blocks,)),
            dma((5,)),
        ],
        compiler_params=pltpu.CompilerParams(
            collective_id=1, has_side_effects=True, vmem_limit_bytes=56 << 20
        ),
    )(tokens, lengths, own_weight, own_bias)


def attend_back_kernel(
    heads,
    dctx_ref,
    qkv_ref,
    ot_ref,
    lse_ref,
    full_ref,
    w_ref,
    pre_ref,
    tgrad_ref,
    wgrad_ref,
    sums_ref,
    dov,
    qkvv,
    otv,
    lsev,
    tokv,
    wv,
    prev,
    ktv,
    dqv,
    dkv,
    dvv,
    dqkv,
    arrive,
    dsend_sem,
    drecv_sem,
    gsend_sem,
    grecv_sem,
    local_sem,
    own_sem,
):
    tab, blk, chip, core = place()
    half = chip // 2
    group = 2 * lax.rem(chip, 2) + core
    blocks, rows = dov.shape[0], dov.shape[1]
    scale = LOG2E / math.sqrt(HD)

    loads = [
        pltpu.make_async_copy(src, dst, local_sem.at[at])
        for at, (src, dst) in enumerate(
            (
                (qkv_ref, qkvv),
                (ot_ref, otv),
                (lse_ref, lsev),
                (dctx_ref.at[half, group], dov.at[blk]),
                (full_ref, tokv),
                (w_ref, wv),
                (pre_ref, prev),
            )
        )
    ]
    for copy in loads:
        copy.start()
    meet(tab, blk)

    def context_copy(which):
        return pltpu.make_async_remote_copy(
            src_ref=dctx_ref.at[which // 4, lax.rem(which, 4)],
            dst_ref=dov.at[blk],
            send_sem=dsend_sem.at[which],
            recv_sem=drecv_sem.at[blk],
            device_id=(tab, which),
            device_id_type=MESH,
        )

    @pl.loop(1, 8)
    def _(step):
        context_copy(lax.rem(blk + 8 - step, 8)).start()

    for copy in loads[:4]:
        copy.wait()
    for head in range(heads):
        ktv[head] = qkvv[heads + head].T

    def gradient_copy(head, which):
        return pltpu.make_async_remote_copy(
            src_ref=dqkv.at[head, which],
            dst_ref=arrive.at[half, group * heads + head],
            send_sem=gsend_sem.at[head, which],
            recv_sem=grecv_sem.at[half, group * heads + head],
            device_id=(tab, which),
            device_id_type=MESH,
        )

    def own_gradient(head):
        return pltpu.make_async_copy(
            dqkv.at[head, blk], arrive.at[half, group * heads + head], own_sem.at[head]
        )

    for head in range(heads):

        @pl.loop(0, 8)
        def _(step, head=head):
            which = lax.rem(blk + step, 8)
            first = pl.multiple_of(which * rows, rows)
            if head == 0:

                @pl.when(step > 0)
                def _():
                    pltpu.make_async_copy(
                        dov.at[which], dov.at[which], drecv_sem.at[which]
                    ).wait()

            q = qkvv[head, pl.ds(first, rows)][:, :HD]
            q_full = qkvv[head, pl.ds(first, rows)]
            do = dov[which][:, head * HD : (head + 1) * HD]
            ot = otv[which, head * HD : (head + 1) * HD]
            delta = jnp.sum(ot * do.astype(jnp.float32).T, axis=0, keepdims=True)
            st = times_t(qkvv[heads + head], q_full)
            pt = jnp.exp2(st * scale - lsev[which, head : head + 1])
            dpt = times_t(qkvv[2 * heads + head][:, :HD], do)
            dst = (pt * (dpt - delta)).astype(jnp.bfloat16)
            dv = jnp.dot(pt.astype(jnp.bfloat16), do, preferred_element_type=jnp.float32)
            dk = jnp.dot(dst, q, preferred_element_type=jnp.float32)

            @pl.when(step == 0)
            def _():
                dvv[...] = dv
                dkv[...] = dk

            @pl.when(step > 0)
            def _():
                dvv[...] += dv
                dkv[...] += dk

            dqt = jnp.dot(ktv[head], dst, preferred_element_type=jnp.float32)
            dqv[which] = dqt[:HD].T * (HD**-0.5)

        @pl.loop(0, 8)
        def _(step, head=head):
            which = lax.rem(blk + 1 + step, 8)
            first = pl.multiple_of(which * rows, rows)
            dqkv[head, which] = jnp.concatenate(
                [
                    dqv[which],
                    dkv[pl.ds(first, rows)] * (HD**-0.5),
                    dvv[pl.ds(first, rows)],
                ],
                axis=1,
            ).astype(jnp.bfloat16)

            @pl.when(step < 7)
            def _():
                gradient_copy(head, which).start()

            @pl.when(step == 7)
            def _():
                own_gradient(head).start()

    for copy in loads[4:]:
        copy.wait()
    for head in range(heads):
        flat = dqkv[head].reshape(blocks * rows, 3 * HD)
        tok = tokv[...].reshape(blocks * rows, tokv.shape[2])
        wgrad_ref[head] = lax.dot_general(
            tok, flat, (((0,), (0,)), ((), ())), preferred_element_type=jnp.float32
        ).astype(jnp.bfloat16)
        sums_ref[head : head + 1] = jnp.sum(
            flat.astype(jnp.float32), axis=0, keepdims=True
        )

    for head in range(heads):
        own_gradient(head).wait()

        @pl.loop(1, 8)
        def _(step, head=head):
            which = lax.rem(blk + step, 8)
            slot = lax.rem(which, 4) * heads + head
            gradient_copy(head, which).wait_send()
            pltpu.make_async_copy(
                arrive.at[which // 4, slot],
                arrive.at[which // 4, slot],
                grecv_sem.at[which // 4, slot],
            ).wait()

    for table in range(2):

        def add(at, total, table=table):
            return total + times_t(arrive[table, at], wv[at])

        total = lax.fori_loop(0, GROUPS * heads, add, prev[table])
        tgrad_ref[table] = total.astype(jnp.bfloat16)

    @pl.loop(1, 8)
    def _(step):
        context_copy(lax.rem(blk + 8 - step, 8)).wait_send()


def attend_back(dctx, qkv, ot, lse, full, by_head, pre, heads):
    blocks, rows, width = full.shape
    total = blocks * rows
    any_space = pl.BlockSpec(memory_space=pl.ANY)
    vmem = pl.BlockSpec(memory_space=pltpu.VMEM)
    bf16, f32 = jnp.bfloat16, jnp.float32
    dma = pltpu.SemaphoreType.DMA
    return pl.pallas_call(
        functools.partial(attend_back_kernel, heads),
        name="attend_back",
        out_shape=(
            jax.ShapeDtypeStruct((2, rows, width), bf16),
            jax.ShapeDtypeStruct((heads, width, 3 * HD), bf16),
            jax.ShapeDtypeStruct((8, 3 * HD), f32),
        ),
        in_specs=[any_space] * 7,
        out_specs=(vmem,) * 3,
        scratch_shapes=[
            pltpu.VMEM((blocks, rows, heads * HD), bf16),
            pltpu.VMEM((3 * heads, total, LANES), bf16),
            pltpu.VMEM((blocks, heads * HD, rows), f32),
            pltpu.VMEM((blocks, 8, rows), f32),
            pltpu.VMEM((blocks, rows, width), bf16),
            pltpu.VMEM(by_head.shape, bf16),
            pltpu.VMEM((2, rows, width), f32),
            pltpu.VMEM((heads, LANES, total), bf16),
            pltpu.VMEM((blocks, rows, HD), f32),
            pltpu.VMEM((total, HD), f32),
            pltpu.VMEM((total, HD), f32),
            pltpu.VMEM((heads, blocks, rows, 3 * HD), bf16),
            pltpu.VMEM((2, GROUPS * heads, rows, 3 * HD), bf16),
            dma((blocks,)),
            dma((blocks,)),
            dma((heads, blocks)),
            dma((2, GROUPS * heads)),
            dma((7,)),
            dma((heads,)),
        ],
        compiler_params=pltpu.CompilerParams(
            collective_id=2, has_side_effects=True, vmem_limit_bytes=60 << 20
        ),
    )(dctx, qkv, ot, lse, full, by_head, pre)


def scatter_sum(grad):
    return lax.psum_scatter(
        lax.psum_scatter(
            grad.astype(jnp.bfloat16), "tab", scatter_dimension=0, tiled=True
        ),
        "blk",
        scatter_dimension=0,
        tiled=True,
    ).astype(jnp.float32)


def shards_direct(
    tokens,
    lengths,
    qkv_weight,
    qkv_bias,
    out_weight,
    out_bias,
    attn_gain,
    attn_shift,
    up_weight,
    up_bias,
    down_weight,
    down_bias,
    ffn_gain,
    ffn_shift,
    cotangent,
):
    tables, rows, width = tokens.shape
    f32, bf16 = jnp.float32, jnp.bfloat16
    all_heads = width // HD
    heads = all_heads // GROUPS
    blk = lax.axis_index("blk")
    group = blk % GROUPS
    flat_tokens = tokens.reshape(tables * rows, width)

    by_group = qkv_weight.reshape(width, 3, GROUPS, heads, HD)
    own = lax.dynamic_index_in_dim(by_group, group, 2, keepdims=False)
    own_weight = jnp.pad(own, ((0, 0), (0, 0), (0, 0), (0, LANES - HD))).reshape(width, -1)
    bias_full = jnp.concatenate(
        [
            qkv_bias[:width].astype(f32),
            jnp.zeros((width,), f32),
            qkv_bias[width:].astype(f32),
        ]
    ).reshape(3, GROUPS, heads, HD)
    own_bias = jnp.pad(
        lax.dynamic_index_in_dim(bias_full, group, 1, keepdims=False),
        ((0, 0), (0, 0), (0, LANES - HD)),
    )
    ones = jnp.zeros((3, 1, LANES), f32).at[0::2, :, HD].set(1.0)
    own_bias = (own_bias + ones).reshape(1, -1)
    by_head = (
        qkv_weight.reshape(width, 3, all_heads, HD)
        .transpose(2, 0, 1, 3)
        .reshape(all_heads, width, 3 * HD)
    )

    ctx, full, qkv, ot, lse = attend(tokens, lengths, own_weight, own_bias, heads)

    context_low = ctx.transpose(0, 2, 1, 3).reshape(tables * rows, width)
    attended = jnp.dot(context_low, out_weight, preferred_element_type=f32) + out_bias.astype(
        f32
    )
    pre_one = flat_tokens.astype(f32) + attended
    gain_one = attn_gain.astype(f32)
    shift_one = attn_shift.astype(f32)
    hidden = norm_rows(pre_one, gain_one, shift_one)
    hidden_low = hidden.astype(bf16)
    upper = jnp.dot(hidden_low, up_weight, preferred_element_type=f32) + up_bias.astype(f32)
    active = gelu_exact(upper).astype(bf16)
    pre_two = (
        hidden
        + jnp.dot(active, down_weight, preferred_element_type=f32)
        + down_bias.astype(f32)
    )
    gain_two = ffn_gain.astype(f32)
    shift_two = ffn_shift.astype(f32)
    layer_out = norm_rows(pre_two, gain_two, shift_two).astype(bf16).reshape(tokens.shape)
    grad_out = cotangent.reshape(tables * rows, width).astype(f32)
    _, norm_two_back = jax.vjp(norm_rows, pre_two, gain_two, shift_two)
    grad_pre_two, ggrad_ffn, sgrad_ffn = norm_two_back(grad_out)
    grad_branch = grad_pre_two.astype(bf16)
    wgrad_down = over_rows(active, grad_branch)
    bgrad_down = jnp.sum(grad_branch, axis=0, dtype=f32)
    grad_active = times_back(grad_branch, down_weight)
    _, gelu_back = jax.vjp(gelu_exact, upper)
    grad_upper = gelu_back(grad_active)[0].astype(bf16)
    wgrad_up = over_rows(hidden_low, grad_upper)
    bgrad_up = jnp.sum(grad_upper, axis=0, dtype=f32)
    grad_hidden = grad_pre_two + times_back(grad_upper, up_weight)
    _, norm_one_back = jax.vjp(norm_rows, pre_one, gain_one, shift_one)
    grad_pre_one, ggrad_attn, sgrad_attn = norm_one_back(grad_hidden)
    grad_attended = grad_pre_one.astype(bf16)
    wgrad_out = over_rows(context_low, grad_attended)
    bgrad_out = jnp.sum(grad_attended, axis=0, dtype=f32)
    grad_context = times_back(grad_attended, out_weight).astype(bf16)
    dctx = grad_context.reshape(tables, rows, GROUPS, heads * HD).transpose(0, 2, 1, 3)

    token_grad, wgrad_part, sums = attend_back(
        dctx, qkv, ot, lse, full, by_head, grad_pre_one.reshape(tokens.shape), heads
    )

    part = lax.psum_scatter(
        wgrad_part.transpose(1, 0, 2), "tab", scatter_dimension=0, tiled=True
    )
    part = lax.all_to_all(
        part.reshape(8, -1, heads, 3 * HD), "blk", split_axis=0, concat_axis=0, tiled=True
    )
    part = part.reshape(2, GROUPS, -1, heads, 3, HD).astype(f32).sum(axis=0)
    wgrad_qkv = part.transpose(1, 3, 0, 2, 4).reshape(-1, 3 * width)

    sums = sums[:heads].reshape(heads, 3, HD)[:, 0::2].transpose(1, 0, 2)
    placed = jnp.zeros((2, GROUPS, heads, HD), f32)
    placed = lax.dynamic_update_slice(placed, sums[:, None], (0, group, 0, 0)).reshape(-1)
    small = (placed, bgrad_out, ggrad_attn, sgrad_attn, bgrad_up, bgrad_down, ggrad_ffn, sgrad_ffn)
    small = jnp.concatenate([s.reshape(32, -1) for s in small], axis=1).astype(f32)
    small = lax.psum_scatter(
        small.reshape(4, -1), "tab", scatter_dimension=0, tiled=True
    ).reshape(8, -1)
    small = lax.psum_scatter(small, "blk", scatter_dimension=0, tiled=True).reshape(-1)
    each = width // 32
    cuts = [2 * each, 3 * each, 4 * each, 5 * each]
    cuts += [cuts[-1] + up_bias.shape[0] // 32]
    cuts += [cuts[-1] + each, cuts[-1] + 2 * each]
    (
        bgrad_qkv,
        bgrad_out,
        ggrad_attn,
        sgrad_attn,
        bgrad_up,
        bgrad_down,
        ggrad_ffn,
        sgrad_ffn,
    ) = jnp.split(small, cuts)
    return (
        layer_out,
        token_grad,
        wgrad_qkv,
        bgrad_qkv,
        scatter_sum(wgrad_out),
        bgrad_out,
        ggrad_attn,
        sgrad_attn,
        scatter_sum(wgrad_up),
        bgrad_up,
        scatter_sum(wgrad_down),
        bgrad_down,
        ggrad_ffn,
        sgrad_ffn,
    )


def solution(mesh):
    in_specs = (
        P("tab", "blk", None),
        P("tab"),
        P(),
        P(),
        P(),
        P(),
        P(),
        P(),
        P(),
        P(),
        P(),
        P(),
        P(),
        P(),
        P("tab", "blk", None),
    )
    out_specs = (
        P("tab", "blk", None),
        P("tab", "blk", None),
        P(("tab", "blk"), None),
        P(("tab", "blk")),
        P(("tab", "blk"), None),
        P(("tab", "blk")),
        P(("tab", "blk")),
        P(("tab", "blk")),
        P(("tab", "blk"), None),
        P(("tab", "blk")),
        P(("tab", "blk"), None),
        P(("tab", "blk")),
        P(("tab", "blk")),
        P(("tab", "blk")),
    )
    tab_count, blk_count = mesh.shape["tab"], mesh.shape["blk"]

    def pick(*operands):
        table_count = operands[0].shape[0] // tab_count
        head_count = operands[0].shape[2] // HD
        direct = table_count == 2 and blk_count == 8 and tab_count == 4 and head_count % 4 == 0
        body = shards_direct if direct else shards_ring
        return jax.shard_map(
            body, mesh=mesh, in_specs=in_specs, out_specs=out_specs, check_vma=False
        )(*operands)

    return pick
```

```python
import functools
import math

import jax
import jax.numpy as jnp
from jax import lax
from jax.experimental import pallas as pl
from jax.experimental.pallas import tpu as pltpu
from jax.sharding import PartitionSpec as P

HD = 64


EPSILON = 1e-05
NEGATIVE = -1e30


def from_behind(block, axis, distance):
    devices = range(lax.axis_size(axis))
    route = [((i - distance) % len(devices), i) for i in devices]
    return lax.ppermute(block, axis, route)


def norm_rows(inputs, gains, shifts):
    row_mean = jnp.mean(inputs, axis=-1, keepdims=True)
    centred = inputs - row_mean
    row_var = jnp.mean(centred * centred, axis=-1, keepdims=True)
    return centred * lax.rsqrt(row_var + EPSILON) * gains + shifts


def gelu_exact(inputs):
    return jax.nn.gelu(inputs, approximate=False)


def times_back(left, right):
    return lax.dot_general(
        left, right, (((1,), (1,)), ((), ())), preferred_element_type=jnp.float32
    )


def over_rows(left, right):
    return lax.dot_general(
        left, right, (((0,), (0,)), ((), ())), preferred_element_type=jnp.float32
    )


def shards_ring(
    tokens,
    lengths,
    qkv_weight,
    qkv_bias,
    out_weight,
    out_bias,
    attn_gain,
    attn_shift,
    up_weight,
    up_bias,
    down_weight,
    down_bias,
    ffn_gain,
    ffn_shift,
    cotangent,
):
    table_count, row_count, model_width = tokens.shape
    head_count = model_width // HD
    cycle_size = lax.axis_size("blk")
    cycle_place = lax.axis_index("blk")
    score_scale = HD ** (-0.5)
    flat_tokens = tokens.reshape(table_count * row_count, model_width)
    bias_full = jnp.concatenate(
        [
            qkv_bias[:model_width].astype(jnp.float32),
            jnp.zeros((model_width,), jnp.float32),
            qkv_bias[model_width:].astype(jnp.float32),
        ]
    )
    qkv_low = (
        jnp.dot(flat_tokens, qkv_weight, preferred_element_type=jnp.float32) + bias_full
    ).astype(jnp.bfloat16)
    queries = qkv_low[:, :model_width].reshape(table_count, row_count, head_count, HD)
    key_values = qkv_low[:, model_width:].reshape(table_count, row_count, 2 * model_width)

    def key_mask(first_row, key_count):
        positions = first_row + jnp.arange(key_count, dtype=jnp.int32)
        return (positions[None, :] < lengths[:, None])[:, None, None, :]

    def split_pair(pair_block):
        key_count = pair_block.shape[1]
        keys_part = pair_block[:, :, :model_width].reshape(table_count, key_count, head_count, HD)
        values_part = pair_block[:, :, model_width:].reshape(table_count, key_count, head_count, HD)
        return (keys_part, values_part)

    pair_block = lax.all_gather(key_values, "blk", axis=1, tiled=True)
    running_max = jnp.full((table_count, row_count, head_count), NEGATIVE, jnp.float32)
    keys_part, values_part = split_pair(pair_block)
    is_valid = key_mask(jnp.int32(0), pair_block.shape[1])
    raw_scores = jnp.einsum(
        "trhd,tkhd->trhk", queries, keys_part, preferred_element_type=jnp.float32
    )
    scores = jnp.where(is_valid, raw_scores * score_scale, NEGATIVE)
    peak_new = jnp.maximum(running_max, jnp.max(scores, axis=-1))
    exponent = jnp.where(is_valid, jnp.exp(scores - peak_new[..., None]), 0.0)
    running_sum = jnp.sum(exponent, axis=-1)
    weighted = jnp.einsum(
        "trhk,tkhd->trhd",
        exponent.astype(jnp.bfloat16),
        values_part,
        preferred_element_type=jnp.float32,
    )
    running_max, running_sum, weighted = (peak_new, running_sum, weighted)
    context = weighted / running_sum[..., None]
    log_total = running_max + jnp.log(running_sum)
    context_low = context.reshape(table_count * row_count, model_width).astype(jnp.bfloat16)
    attended = jnp.dot(
        context_low, out_weight, preferred_element_type=jnp.float32
    ) + out_bias.astype(jnp.float32)
    pre_one = flat_tokens.astype(jnp.float32) + attended
    gain_one = attn_gain.astype(jnp.float32)
    shift_one = attn_shift.astype(jnp.float32)
    hidden = norm_rows(pre_one, gain_one, shift_one)
    hidden_low = hidden.astype(jnp.bfloat16)
    upper = jnp.dot(hidden_low, up_weight, preferred_element_type=jnp.float32) + up_bias.astype(
        jnp.float32
    )
    active = gelu_exact(upper).astype(jnp.bfloat16)
    pre_two = (
        hidden
        + jnp.dot(active, down_weight, preferred_element_type=jnp.float32)
        + down_bias.astype(jnp.float32)
    )
    gain_two = ffn_gain.astype(jnp.float32)
    shift_two = ffn_shift.astype(jnp.float32)
    layer_out = norm_rows(pre_two, gain_two, shift_two).astype(jnp.bfloat16).reshape(tokens.shape)
    grad_out = cotangent.reshape(table_count * row_count, model_width).astype(jnp.float32)
    _, norm_two_back = jax.vjp(norm_rows, pre_two, gain_two, shift_two)
    grad_pre_two, ggrad_ffn, sgrad_ffn = norm_two_back(grad_out)
    grad_branch = grad_pre_two.astype(jnp.bfloat16)
    wgrad_down = over_rows(active, grad_branch)
    bgrad_down = jnp.sum(grad_branch, axis=0, dtype=jnp.float32)
    grad_active = times_back(grad_branch, down_weight)
    _, gelu_back = jax.vjp(gelu_exact, upper)
    grad_upper = gelu_back(grad_active)[0].astype(jnp.bfloat16)
    wgrad_up = over_rows(hidden_low, grad_upper)
    bgrad_up = jnp.sum(grad_upper, axis=0, dtype=jnp.float32)
    grad_hidden = grad_pre_two + times_back(grad_upper, up_weight)
    _, norm_one_back = jax.vjp(norm_rows, pre_one, gain_one, shift_one)
    grad_pre_one, ggrad_attn, sgrad_attn = norm_one_back(grad_hidden)
    grad_attended = grad_pre_one.astype(jnp.bfloat16)
    wgrad_out = over_rows(context_low, grad_attended)
    bgrad_out = jnp.sum(grad_attended, axis=0, dtype=jnp.float32)
    grad_context = times_back(grad_attended, out_weight).astype(jnp.bfloat16)
    grad_heads = grad_context.reshape(table_count, row_count, head_count, HD)
    row_delta = jnp.sum(grad_heads.astype(jnp.float32) * context, axis=-1)

    def cycle_turn_step(cycle_turn, cycle_state):
        pair_now, pair_grads, grad_queries = cycle_state
        owner_index = (cycle_place - cycle_turn) % cycle_size
        keys_part, values_part = split_pair(pair_now)
        is_valid = key_mask(owner_index * row_count, row_count)
        raw_scores = jnp.einsum(
            "trhd,tkhd->trhk", queries, keys_part, preferred_element_type=jnp.float32
        )
        scores = jnp.where(is_valid, raw_scores * score_scale, NEGATIVE)
        probs = jnp.where(is_valid, jnp.exp(scores - log_total[..., None]), 0.0)
        grad_probs = jnp.einsum(
            "trhd,tkhd->trhk", grad_heads, values_part, preferred_element_type=jnp.float32
        )
        grad_raw = (probs * (grad_probs - row_delta[..., None]) * score_scale).astype(jnp.bfloat16)
        grad_queries = grad_queries + jnp.einsum(
            "trhk,tkhd->trhd", grad_raw, keys_part, preferred_element_type=jnp.float32
        )
        grad_keys = jnp.einsum(
            "trhk,trhd->tkhd", grad_raw, queries, preferred_element_type=jnp.float32
        )
        grad_values = jnp.einsum(
            "trhk,trhd->tkhd",
            probs.astype(jnp.bfloat16),
            grad_heads,
            preferred_element_type=jnp.float32,
        )
        pair_grads = pair_grads + jnp.concatenate(
            [
                grad_keys.reshape(table_count, row_count, model_width),
                grad_values.reshape(table_count, row_count, model_width),
            ],
            axis=-1,
        )
        pair_next = from_behind(pair_now, "blk", 1)
        grads_next = from_behind(pair_grads.astype(jnp.bfloat16), "blk", 1).astype(pair_grads.dtype)
        return (pair_next, grads_next, grad_queries)

    cycle_start = (
        key_values,
        jnp.zeros((table_count, row_count, 2 * model_width), jnp.float32),
        jnp.zeros((table_count, row_count, head_count, HD), jnp.float32),
    )
    _, pair_home, grad_queries = lax.fori_loop(0, cycle_size, cycle_turn_step, cycle_start)
    grad_qkv = jnp.concatenate(
        [
            grad_queries.reshape(table_count * row_count, model_width),
            pair_home.reshape(table_count * row_count, 2 * model_width),
        ],
        axis=-1,
    ).astype(jnp.bfloat16)
    wgrad_qkv = over_rows(flat_tokens, grad_qkv)
    column_sums = jnp.sum(grad_qkv, axis=0, dtype=jnp.float32)
    bgrad_qkv = jnp.concatenate([column_sums[:model_width], column_sums[2 * model_width :]])
    token_grad = (
        (grad_pre_one + times_back(grad_qkv, qkv_weight)).astype(jnp.bfloat16).reshape(tokens.shape)
    )
    (
        wgrad_qkv,
        bgrad_qkv,
        wgrad_out,
        bgrad_out,
        ggrad_attn,
        sgrad_attn,
        wgrad_up,
        bgrad_up,
        wgrad_down,
        bgrad_down,
        ggrad_ffn,
        sgrad_ffn,
    ) = (
        lax.psum_scatter(
            wgrad_qkv.astype(jnp.bfloat16), "tab", scatter_dimension=0, tiled=True
        ).astype(jnp.float32),
        lax.psum_scatter(
            bgrad_qkv.astype(jnp.bfloat16), "tab", scatter_dimension=0, tiled=True
        ).astype(jnp.float32),
        lax.psum_scatter(
            wgrad_out.astype(jnp.bfloat16), "tab", scatter_dimension=0, tiled=True
        ).astype(jnp.float32),
        lax.psum_scatter(
            bgrad_out.astype(jnp.bfloat16), "tab", scatter_dimension=0, tiled=True
        ).astype(jnp.float32),
        lax.psum_scatter(
            ggrad_attn.astype(jnp.bfloat16), "tab", scatter_dimension=0, tiled=True
        ).astype(jnp.float32),
        lax.psum_scatter(
            sgrad_attn.astype(jnp.bfloat16), "tab", scatter_dimension=0, tiled=True
        ).astype(jnp.float32),
        lax.psum_scatter(
            wgrad_up.astype(jnp.bfloat16), "tab", scatter_dimension=0, tiled=True
        ).astype(jnp.float32),
        lax.psum_scatter(
            bgrad_up.astype(jnp.bfloat16), "tab", scatter_dimension=0, tiled=True
        ).astype(jnp.float32),
        lax.psum_scatter(
            wgrad_down.astype(jnp.bfloat16), "tab", scatter_dimension=0, tiled=True
        ).astype(jnp.float32),
        lax.psum_scatter(
            bgrad_down.astype(jnp.bfloat16), "tab", scatter_dimension=0, tiled=True
        ).astype(jnp.float32),
        lax.psum_scatter(
            ggrad_ffn.astype(jnp.bfloat16), "tab", scatter_dimension=0, tiled=True
        ).astype(jnp.float32),
        lax.psum_scatter(
            sgrad_ffn.astype(jnp.bfloat16), "tab", scatter_dimension=0, tiled=True
        ).astype(jnp.float32),
    )
    (
        wgrad_qkv,
        bgrad_qkv,
        wgrad_out,
        bgrad_out,
        ggrad_attn,
        sgrad_attn,
        wgrad_up,
        bgrad_up,
        wgrad_down,
        bgrad_down,
        ggrad_ffn,
        sgrad_ffn,
    ) = (
        lax.psum_scatter(
            wgrad_qkv.astype(jnp.bfloat16), "blk", scatter_dimension=0, tiled=True
        ).astype(jnp.float32),
        lax.psum_scatter(
            bgrad_qkv.astype(jnp.bfloat16), "blk", scatter_dimension=0, tiled=True
        ).astype(jnp.float32),
        lax.psum_scatter(
            wgrad_out.astype(jnp.bfloat16), "blk", scatter_dimension=0, tiled=True
        ).astype(jnp.float32),
        lax.psum_scatter(
            bgrad_out.astype(jnp.bfloat16), "blk", scatter_dimension=0, tiled=True
        ).astype(jnp.float32),
        lax.psum_scatter(
            ggrad_attn.astype(jnp.bfloat16), "blk", scatter_dimension=0, tiled=True
        ).astype(jnp.float32),
        lax.psum_scatter(
            sgrad_attn.astype(jnp.bfloat16), "blk", scatter_dimension=0, tiled=True
        ).astype(jnp.float32),
        lax.psum_scatter(
            wgrad_up.astype(jnp.bfloat16), "blk", scatter_dimension=0, tiled=True
        ).astype(jnp.float32),
        lax.psum_scatter(
            bgrad_up.astype(jnp.bfloat16), "blk", scatter_dimension=0, tiled=True
        ).astype(jnp.float32),
        lax.psum_scatter(
            wgrad_down.astype(jnp.bfloat16), "blk", scatter_dimension=0, tiled=True
        ).astype(jnp.float32),
        lax.psum_scatter(
            bgrad_down.astype(jnp.bfloat16), "blk", scatter_dimension=0, tiled=True
        ).astype(jnp.float32),
        lax.psum_scatter(
            ggrad_ffn.astype(jnp.bfloat16), "blk", scatter_dimension=0, tiled=True
        ).astype(jnp.float32),
        lax.psum_scatter(
            sgrad_ffn.astype(jnp.bfloat16), "blk", scatter_dimension=0, tiled=True
        ).astype(jnp.float32),
    )
    return (
        layer_out,
        token_grad,
        wgrad_qkv,
        bgrad_qkv,
        wgrad_out,
        bgrad_out,
        ggrad_attn,
        sgrad_attn,
        wgrad_up,
        bgrad_up,
        wgrad_down,
        bgrad_down,
        ggrad_ffn,
        sgrad_ffn,
    )


GROUPS = 4
LANES = 128
LOG2E = math.log2(math.e)
MESH = pl.DeviceIdType.MESH
CHUNKS = 2


def times_t(left, right):
    return lax.dot_general(
        left, right, (((1,), (1,)), ((), ())), preferred_element_type=jnp.float32
    )


def place():
    tab, blk = lax.axis_index("tab"), lax.axis_index("blk")
    return tab, blk, blk // 2, blk % 2


def meet(tab, blk):
    barrier = pltpu.get_barrier_semaphore()

    @pl.loop(1, 8)
    def _(step):
        pl.semaphore_signal(
            barrier, inc=1, device_id=(tab, lax.rem(blk + step, 8)), device_id_type=MESH
        )

    pl.semaphore_wait(barrier, 7)


def own_window(group, first, rows_ref, out):
    start = pl.multiple_of(first + LANES * ((3 * group) // 2), LANES)
    window = rows_ref[:, pl.ds(start, 2 * LANES)].astype(jnp.float32)
    window = pltpu.roll(window, lax.rem(2 * LANES - HD * lax.rem(group, 2), 2 * LANES), 1)
    left = window[:, :LANES]
    low = lax.broadcasted_iota(jnp.int32, left.shape, 1) < HD
    for head, lanes in enumerate((left, pltpu.roll(left, HD, 1), window[:, LANES:])):
        out(head, jnp.where(low, lanes, 0.0))


def attend_kernel(
    heads,
    tok_ref,
    len_ref,
    par_ref,
    w_hbm,
    ctx_ref,
    fullt_ref,
    qkv_ref,
    ot_ref,
    lse_ref,
    tokv,
    toktv,
    wfull,
    wown,
    bown,
    qkvv,
    vtv,
    otv,
    lsev,
    csend,
    send_a,
    send_b,
    send_c,
    send_d,
    send_e,
    recv,
    csend_sem,
    crecv_sem,
    local_sem,
):
    tab, blk, chip, core = place()
    half = chip // 2
    group = 2 * lax.rem(chip, 2) + core
    rows = tok_ref.shape[1]
    width = tok_ref.shape[2]
    piece = rows // CHUNKS
    is_near = jnp.logical_or(chip == 1, chip == 2)
    mate = chip + 1 - 2 * lax.rem(chip, 2)
    other_near = 2 - half
    other_far = 3 - 3 * half
    own_far = 3 * half
    scale = LOG2E / math.sqrt(HD)

    def remote(src, dst, send_sem, recv_sem, to_chip, to_core):
        return pltpu.make_async_remote_copy(
            src_ref=src,
            dst_ref=dst,
            send_sem=send_sem,
            recv_sem=recv_sem,
            device_id=(tab, 2 * to_chip + to_core),
            device_id_type=MESH,
        )

    def own_copies(part):
        cut = pl.ds(part * piece, piece)
        here, there = tok_ref.at[half, cut], tok_ref.at[1 - half, cut]
        dst, done = tokv.at[blk, cut], recv.at[blk, part]
        return (
            remote(here, dst, send_a.at[part], done, mate, core),
            remote(there, dst, send_c.at[part], done, other_near, core),
            remote(here, dst, send_b.at[part], done, chip, 1 - core),
        )

    def to_far(slot, part, src_chip):
        which = 2 * src_chip + core
        ref = tokv.at[which, pl.ds(part * piece, piece)]
        return remote(ref, ref, send_d.at[slot, part], recv.at[which, part], own_far, core)

    def to_core(slot, part, src_chip):
        which = 2 * src_chip + core
        ref = tokv.at[which, pl.ds(part * piece, piece)]
        return remote(ref, ref, send_e.at[slot, part], recv.at[which, part], chip, 1 - core)

    def arrived(which, part):
        ref = tokv.at[which, pl.ds(part * piece, piece)]
        pltpu.make_async_copy(ref, ref, recv.at[which, part]).wait()

    load = pltpu.make_async_copy(w_hbm, wfull, local_sem.at[5])
    load.start()
    meet(tab, blk)
    for part in range(CHUNKS):
        for copy in own_copies(part):
            copy.start()
    tokv[blk] = tok_ref[half]

    lane1 = lax.broadcasted_iota(jnp.int32, (8, LANES), 1)
    for at in (0, 2):

        def keep_bias(head, lanes, at=at):
            row = jnp.where(lane1 == HD, 1.0, lanes)
            bown[:, pl.ds((at * heads + head) * LANES, LANES)] = row

        own_window(group, 0, par_ref.at[pl.ds(8 * (1 + at // 2), 8)], keep_bias)
    for head in range(heads):
        bown[:, pl.ds((heads + head) * LANES, LANES)] = jnp.zeros((8, LANES), jnp.float32)
    load.wait()
    for at in range(3):

        def keep_weight(head, lanes, at=at):
            wown[:, pl.ds((at * heads + head) * LANES, LANES)] = lanes.astype(jnp.bfloat16)

        own_window(group, at * width, wfull, keep_weight)

    length = len_ref[half]
    lane = lax.broadcasted_iota(jnp.int32, (rows, LANES), 1)
    row = lax.broadcasted_iota(jnp.int32, (rows, LANES), 0)

    def project(which):
        first = pl.multiple_of(which * rows, rows)
        tok = tokv[which]
        y = jnp.dot(tok, wown[...], preferred_element_type=jnp.float32) + bown[:1]
        pad = jnp.where((lane == HD) & (row + first >= length), NEGATIVE, 0.0)
        for head in range(heads):
            q, k, v = (
                y[:, (part * heads + head) * LANES :][:, :LANES] for part in range(3)
            )
            qkvv[head, pl.ds(first, rows)] = q.astype(jnp.bfloat16)
            qkvv[heads + head, pl.ds(first, rows)] = (k + pad).astype(jnp.bfloat16)
            qkvv[2 * heads + head, pl.ds(first, rows)] = v.astype(jnp.bfloat16)
            vtv[head, :, pl.ds(first, rows)] = v.T.astype(jnp.bfloat16)
        toktv[:, pl.ds(first, rows)] = tok.T

    project(blk)
    for part in range(CHUNKS):
        arrived(2 * mate + core, part)
        to_core(0, part, mate).start()
    project(2 * mate + core)
    for part in range(CHUNKS):
        arrived(2 * chip + 1 - core, part)
    project(2 * chip + 1 - core)
    for part in range(CHUNKS):
        arrived(2 * mate + 1 - core, part)
    project(2 * mate + 1 - core)
    for part in range(CHUNKS):
        for slot, src_chip in ((1, other_near), (2, other_far)):
            arrived(2 * src_chip + core, part)
            pl.when(is_near)(to_far(slot, part, src_chip).start)
            to_core(slot, part, src_chip).start()
    for src_chip in (other_near, other_far):
        project(2 * src_chip + core)
        for part in range(CHUNKS):
            arrived(2 * src_chip + 1 - core, part)
        project(2 * src_chip + 1 - core)

    keep = (
        pltpu.make_async_copy(toktv, fullt_ref, local_sem.at[0]),
        pltpu.make_async_copy(qkvv, qkv_ref, local_sem.at[1]),
    )
    for copy in keep:
        copy.start()

    def context_copy(which):
        return remote(
            csend.at[which],
            ctx_ref.at[half, group],
            csend_sem.at[which],
            crecv_sem.at[blk],
            which // 2,
            lax.rem(which, 2),
        )

    own_context = pltpu.make_async_copy(
        csend.at[blk], ctx_ref.at[half, group], local_sem.at[2]
    )

    @pl.loop(0, 4)
    def _(step):
        which = lax.rem(chip + 1 + step, 4)
        first = pl.multiple_of(which * 2 * rows, 2 * rows)
        for head in range(heads):
            q = qkvv[head, pl.ds(first, 2 * rows)]
            st = times_t(qkvv[heads + head], q)
            peak = jnp.max(st, axis=0, keepdims=True)
            pt = jnp.exp2((st - peak) * scale).astype(jnp.bfloat16)
            ot = jnp.dot(vtv[head], pt, preferred_element_type=jnp.float32)
            total = ot[HD : HD + 1]
            otv[which, head * HD : (head + 1) * HD] = ot[:HD] / total
            lsev[which, head : head + 1] = peak * scale + jnp.log(total) * LOG2E
        out = otv[which].T.astype(jnp.bfloat16)
        csend[2 * which] = out[:rows]
        csend[2 * which + 1] = out[rows:]

        @pl.when(step < 3)
        def _():
            context_copy(2 * which).start()
            context_copy(2 * which + 1).start()

        @pl.when(step == 3)
        def _():
            context_copy(2 * which + 1 - core).start()
            own_context.start()

    more = (
        pltpu.make_async_copy(otv, ot_ref, local_sem.at[3]),
        pltpu.make_async_copy(lsev, lse_ref, local_sem.at[4]),
    )
    for copy in more:
        copy.start()
    for part in range(CHUNKS):
        for copy in own_copies(part):
            copy.wait_send()
        to_core(0, part, mate).wait_send()
        for slot, src_chip in ((1, other_near), (2, other_far)):
            pl.when(is_near)(to_far(slot, part, src_chip).wait_send)
            to_core(slot, part, src_chip).wait_send()

    @pl.loop(1, 8)
    def _(step):
        which = lax.rem(blk + step, 8)
        context_copy(which).wait_send()
        pltpu.make_async_copy(
            ctx_ref.at[which // 4, lax.rem(which, 4)],
            ctx_ref.at[which // 4, lax.rem(which, 4)],
            crecv_sem.at[which],
        ).wait()

    own_context.wait()
    for copy in keep + more:
        copy.wait()


def attend(tokens, lengths, params, qkv_weight, heads):
    tables, rows, width = tokens.shape
    blocks = 8
    total = blocks * rows
    any_space = pl.BlockSpec(memory_space=pl.ANY)
    vmem = pl.BlockSpec(memory_space=pltpu.VMEM)
    bf16, f32 = jnp.bfloat16, jnp.float32
    dma = pltpu.SemaphoreType.DMA
    return pl.pallas_call(
        functools.partial(attend_kernel, heads),
        name="attend",
        out_shape=(
            jax.ShapeDtypeStruct((tables, GROUPS, rows, heads * HD), bf16),
            jax.ShapeDtypeStruct((width, total), bf16),
            jax.ShapeDtypeStruct((3 * heads, total, LANES), bf16),
            jax.ShapeDtypeStruct((4, heads * HD, 2 * rows), f32),
            jax.ShapeDtypeStruct((4, 8, 2 * rows), f32),
        ),
        in_specs=[vmem, pl.BlockSpec(memory_space=pltpu.SMEM), vmem, any_space],
        out_specs=(any_space,) * 5,
        scratch_shapes=[
            pltpu.VMEM((blocks, rows, width), bf16),
            pltpu.VMEM((width, total), bf16),
            pltpu.VMEM(qkv_weight.shape, bf16),
            pltpu.VMEM((width, 3 * heads * LANES), bf16),
            pltpu.VMEM((8, 3 * heads * LANES), f32),
            pltpu.VMEM((3 * heads, total, LANES), bf16),
            pltpu.VMEM((heads, LANES, total), bf16),
            pltpu.VMEM((4, heads * HD, 2 * rows), f32),
            pltpu.VMEM((4, 8, 2 * rows), f32),
            pltpu.VMEM((blocks, rows, heads * HD), bf16),
            dma((CHUNKS,)),
            dma((CHUNKS,)),
            dma((CHUNKS,)),
            dma((3, CHUNKS)),
            dma((3, CHUNKS)),
            dma((blocks, CHUNKS)),
            dma((blocks,)),
            dma((blocks,)),
            dma((6,)),
        ],
        compiler_params=pltpu.CompilerParams(
            collective_id=1, has_side_effects=True, vmem_limit_bytes=60 << 20
        ),
    )(tokens, lengths, params, qkv_weight)


UNITS = 9
TURNS = 4
STAGES = 5
PHASE = (1, 3, 5, 7, 9)


def attend_back_kernel(
    heads,
    dctx_ref,
    qkv_ref,
    ot_ref,
    lse_ref,
    fullt_ref,
    w_ref,
    pre_ref,
    parts_ref,
    small_ref,
    tgrad_ref,
    wqkv_ref,
    wout_ref,
    wup_ref,
    wdown_ref,
    little_ref,
    dov,
    doh,
    deltas,
    qkvv,
    otv,
    lsev,
    toktv,
    wv,
    prev,
    ktv,
    dqv,
    dkv,
    dvv,
    dqkv,
    arrive,
    joined,
    mine,
    sum0,
    sum1,
    sum2,
    sum3,
    sum4,
    slab,
    slab_in,
    line,
    line_in,
    small_in,
    small_line,
    small_line_in,
    dsend_sem,
    drecv_sem,
    gsend_sem,
    grecv_sem,
    ssend_sem,
    srecv_sem,
    tsend_sem,
    trecv_sem,
    lsend_sem,
    lrecv_sem,
    local_sem,
    own_sem,
    mine_sem,
):
    f32, bf16 = jnp.float32, jnp.bfloat16
    tab, blk, chip, core = place()
    y, x, zh, zl = tab // 2, lax.rem(tab, 2), chip // 2, lax.rem(chip, 2)
    half = zh
    group = 2 * zl + core
    blocks, rows = dov.shape[0], dov.shape[1]
    width = toktv.shape[0]
    tile = 2 * rows
    piece = 256
    scale = LOG2E / math.sqrt(HD)
    shrink = HD**-0.5

    def remote(src, dst, send_sem, recv_sem, device):
        return pltpu.make_async_remote_copy(
            src_ref=src,
            dst_ref=dst,
            send_sem=send_sem,
            recv_sem=recv_sem,
            device_id=device,
            device_id_type=MESH,
        )

    def landed(ref, sem):
        pltpu.make_async_copy(ref, ref, sem).wait()

    loads = [
        pltpu.make_async_copy(src, dst, local_sem.at[at])
        for at, (src, dst) in enumerate(
            (
                (qkv_ref, qkvv),
                (ot_ref, otv),
                (lse_ref, lsev),
                (dctx_ref.at[half, group], dov.at[blk]),
                (fullt_ref, toktv),
                (w_ref, wv),
                (pre_ref, prev),
            )
        )
    ]
    for copy in loads:
        copy.start()

    barrier = pltpu.get_barrier_semaphore()
    for step in range(1, 8):
        pl.semaphore_signal(
            barrier, inc=1, device_id=(tab, lax.rem(blk + step, 8)), device_id_type=MESH
        )
    for step in range(1, 4):
        pl.semaphore_signal(
            barrier, inc=1, device_id=(lax.rem(tab + step, 4), blk), device_id_type=MESH
        )
    pl.semaphore_wait(barrier, 10)

    def context_copy(which):
        return remote(
            dctx_ref.at[which // 4, lax.rem(which, 4)],
            dov.at[blk],
            dsend_sem.at[which],
            drecv_sem.at[blk],
            (tab, which),
        )

    for step in range(1, 8):
        which = 2 * lax.rem(chip + 4 - step // 2, 4) + (
            (1 - core) if step == 1 else (core if step % 2 == 0 else 1 - core)
        )
        context_copy(which).start()

    def stage_copy(stage, unit, order=None):
        send, done = ssend_sem.at[stage, unit], srecv_sem.at[stage, unit]
        if stage == 0:
            src = parts_ref.at[unit, :, :, :, :, 1 - core]
            return remote(src, sum0.at[unit], send, done, (tab, 2 * chip + 1 - core))
        if stage == 1 and order == 0:
            return remote(
                sum0.at[unit, :, 1 - x], sum1.at[unit], send, done, (2 * y + 1 - x, blk)
            )
        if stage == 1:
            return remote(
                sum0.at[unit, 1 - y], sum1.at[unit], send, done, (2 * (1 - y) + x, blk)
            )
        if stage == 2 and order == 0:
            return remote(
                sum1.at[unit, 1 - y], sum2.at[unit], send, done, (2 * (1 - y) + x, blk)
            )
        if stage == 2:
            return remote(
                sum1.at[unit, 1 - x], sum2.at[unit], send, done, (2 * y + 1 - x, blk)
            )
        if stage == 3:
            src, there = sum2.at[unit, :, 1 - zl], 2 * zh + 1 - zl
            return remote(src, sum3.at[unit], send, done, (tab, 2 * there + core))
        src, there = sum3.at[unit, 1 - zh], 2 * (1 - zh) + zl
        return remote(src, sum4.at[unit], send, done, (tab, 2 * there + core))

    def both(act):
        pl.when(core == 0)(functools.partial(act, 0))
        pl.when(core == 1)(functools.partial(act, 1))

    def mine_copy(unit):
        slot = lax.rem(unit, 2)
        return pltpu.make_async_copy(
            parts_ref.at[unit, :, :, :, :, core], mine.at[slot], mine_sem.at[slot]
        )

    def finish(unit):
        done = sum4[unit].astype(f32) + sum3[unit, zh].astype(f32)
        top, low = done[: done.shape[0] // 2], done[done.shape[0] // 2 :]
        each, cut = top.shape

        @pl.when(unit < 4)
        def _():
            at = pl.ds(pl.multiple_of(unit * each, each), each)
            wdown_ref[at, :cut] = top
            wdown_ref[at, cut:] = low

        @pl.when(jnp.logical_and(unit >= 4, unit < 8))
        def _():
            at = pl.multiple_of((unit - 4) * 2 * cut, 2 * cut)
            wup_ref[:, pl.ds(at, cut)] = top
            wup_ref[:, pl.ds(pl.multiple_of(at + cut, cut), cut)] = low

        @pl.when(unit == 8)
        def _():
            wout_ref[:, :cut] = top
            wout_ref[:, cut:] = low

    def advance(stage, unit):
        if stage == 0:
            landed(sum0.at[unit], srecv_sem.at[0, unit])
            mine_copy(unit).wait()
            slot = lax.rem(unit, 2)
            for a in range(2):
                for b in range(2):
                    sum0[unit, a, b] = sum0[unit, a, b] + mine[slot, a, b]

            @pl.when(unit + 2 < UNITS)
            def _():
                mine_copy(unit + 2).start()

            both(lambda order: stage_copy(1, unit, order).start())
        elif stage == 1:
            landed(sum1.at[unit], srecv_sem.at[1, unit])

            def act(order):
                own = sum0[unit, :, x] if order == 0 else sum0[unit, y]
                sum1[unit] = sum1[unit] + own
                stage_copy(2, unit, order).start()

            both(act)
        elif stage == 2:
            landed(sum2.at[unit], srecv_sem.at[2, unit])

            def act(order):
                sum2[unit] = sum2[unit] + sum1[unit, y if order == 0 else x]

            both(act)
            stage_copy(3, unit).start()
        elif stage == 3:
            landed(sum3.at[unit], srecv_sem.at[3, unit])
            sum3[unit] = sum3[unit] + sum2[unit, :, zl]
            stage_copy(4, unit).start()
        else:
            landed(sum4.at[unit], srecv_sem.at[4, unit])
            finish(unit)

    def tick(now):
        for stage in range(STAGES):
            at = now - PHASE[stage]
            unit = (5 * at + 6) // 7
            due = (at >= 0) & (unit < UNITS) & ((7 * unit) // 5 == at)
            pl.when(due)(functools.partial(advance, stage, unit))

    for unit in range(UNITS):
        stage_copy(0, unit).start()
    for unit in range(2):
        mine_copy(unit).start()

    def tab_copy(src, dst, sem_at, step):
        there = lax.rem(tab + step, 4)
        return remote(
            src(there), dst(tab), tsend_sem.at[sem_at, there], trecv_sem.at[sem_at, tab], (there, blk)
        )

    def line_copy(src, dst, sem_at, step):
        there = lax.rem(blk + step, 8)
        return remote(
            src(there), dst(blk), lsend_sem.at[sem_at, there], lrecv_sem.at[sem_at, blk], (tab, there)
        )

    def small_tab(step):
        return tab_copy(lambda t: small_ref, lambda t: small_in.at[t], heads, step)

    def small_blk(step):
        return line_copy(lambda b: small_line, lambda b: small_line_in.at[b], heads, step)

    def slab_tab(head, step):
        return tab_copy(
            lambda t: slab.at[head, t], lambda t: slab_in.at[head, t], head, step
        )

    def slab_blk(head, step):
        return line_copy(
            lambda b: line.at[head, b], lambda b: line_in.at[head, b], head, step
        )

    for step in range(1, 4):
        small_tab(step).start()

    def pass_small():
        total = small_ref[...]
        for step in range(1, 4):
            there = lax.rem(tab + step, 4)
            landed(small_in.at[there], trecv_sem.at[heads, there])
            total += small_in[there]
        small_line[...] = total
        for step in range(1, 8):
            small_blk(step).start()

    def make_slab(head):
        flat = dqkv[head].reshape(blocks * rows, 3 * HD)
        grad = jnp.dot(toktv[...], flat, preferred_element_type=f32)
        sums = jnp.sum(flat.astype(f32), axis=0, keepdims=True)
        sums = jnp.broadcast_to(sums, (8, 3 * HD))
        grad = grad.reshape(4, 8, width // 32, 3 * HD)
        for t in range(4):
            for b in range(8):
                slab[head, t, b] = jnp.concatenate([grad[t, b], sums], axis=0).astype(bf16)
        for step in range(1, 4):
            slab_tab(head, step).start()

    def pass_slab(head):
        total = slab[head, tab].astype(f32)
        for step in range(1, 4):
            there = lax.rem(tab + step, 4)
            landed(slab_in.at[head, there], trecv_sem.at[head, there])
            total += slab_in[head, there].astype(f32)
        line[head] = total.astype(bf16)
        line_in[head, blk] = line[head, blk]
        for step in range(1, 8):
            slab_blk(head, step).start()

    for copy in loads[:4]:
        copy.wait()
    for head in range(heads):
        ktv[head] = qkvv[heads + head].T

    def gradient_copy(head, which):
        return remote(
            dqkv.at[head, which],
            arrive.at[half, group * heads + head],
            gsend_sem.at[head, which],
            grecv_sem.at[half, group * heads + head],
            (tab, which),
        )

    def own_gradient(head):
        return pltpu.make_async_copy(
            dqkv.at[head, blk], arrive.at[half, group * heads + head], own_sem.at[head]
        )

    @pl.loop(0, heads * TURNS)
    def _(turn):
        head, step = turn // TURNS, lax.rem(turn, TURNS)
        which = lax.rem(chip + step, 4)
        first = pl.multiple_of(which * tile, tile)

        @pl.when(head == 0)
        def _():
            for side in range(2):
                block = 2 * which + side

                @pl.when(block != blk)
                def _():
                    landed(dov.at[block], drecv_sem.at[block])

                for at in range(heads):
                    do = dov[block][:, at * HD : (at + 1) * HD]
                    doh[at, pl.ds(first + side * rows, rows)] = do
                    ot = otv[which, at * HD : (at + 1) * HD, side * rows : (side + 1) * rows]
                    deltas[at, which, :1, side * rows : (side + 1) * rows] = jnp.sum(
                        ot * do.astype(f32).T, axis=0, keepdims=True
                    )

        @pl.when(step == 0)
        def _():
            dkv[...] = jnp.zeros_like(dkv)
            dvv[...] = jnp.zeros_like(dvv)

        tick(turn)

        q_full = qkvv[head, pl.ds(first, tile)]
        q = q_full[:, :HD]
        do = doh[head, pl.ds(first, tile)]
        delta = deltas[head, which, :1]
        lse = lsev[which, pl.ds(head, 1)]
        dqt = jnp.zeros((LANES, tile), f32)
        for at in range(blocks * rows // piece):
            cut = pl.ds(at * piece, piece)
            st = times_t(qkvv[heads + head, cut], q_full)
            pt = jnp.exp2(st * scale - lse)
            dpt = times_t(qkvv[2 * heads + head, cut][:, :HD], do)
            dst = (pt * (dpt - delta)).astype(bf16)
            dvv[cut] += jnp.dot(pt.astype(bf16), do, preferred_element_type=f32)
            dkv[cut] += jnp.dot(dst, q, preferred_element_type=f32)
            dqt += jnp.dot(ktv[head, :, cut], dst, preferred_element_type=f32)
        dqv[pl.ds(first, tile)] = dqt[:HD].T * shrink

        @pl.when(step == TURNS - 1)
        def _():
            @pl.loop(0, 8)
            def _(at):
                block = lax.rem(blk + 1 + at, 8)
                cut = pl.ds(pl.multiple_of(block * rows, rows), rows)
                dqkv[head, block] = jnp.concatenate(
                    [dqv[cut], dkv[cut] * shrink, dvv[cut]], axis=1
                ).astype(bf16)

                @pl.when(at < 7)
                def _():
                    gradient_copy(head, block).start()

                @pl.when(at == 7)
                def _():
                    own_gradient(head).start()

        @pl.when(jnp.logical_and(head > 0, step == 0))
        def _():
            @pl.when(head == 1)
            def _():
                loads[4].wait()
                pass_small()

            make_slab(head - 1)

        @pl.when(jnp.logical_and(head > 0, step == 2))
        def _():
            pass_slab(head - 1)

    make_slab(heads - 1)
    for now in range(heads * TURNS, PHASE[1] + 12):
        tick(now)
    loads[5].wait()
    loads[6].wait()

    @pl.loop(0, heads)
    def _(head):
        own_gradient(head).wait()

        @pl.loop(1, 8)
        def _(step):
            which = lax.rem(blk + step, 8)
            slot = lax.rem(which, 4) * heads + head
            gradient_copy(head, which).wait_send()
            landed(arrive.at[which // 4, slot], grecv_sem.at[which // 4, slot])

    pass_slab(heads - 1)

    for table in range(2):
        for pair in range(GROUPS * heads // 2):
            left, right = arrive[table, 2 * pair], arrive[table, 2 * pair + 1]
            for part in range(3):
                cut = slice(part * HD, (part + 1) * HD)
                joined[:, pl.ds(part * width + pair * LANES, LANES)] = jnp.concatenate(
                    [left[:, cut], right[:, cut]], axis=1
                )
        at = pl.ds(table * rows, rows)
        tgrad_ref[table] = (prev[at] + times_t(joined[...], wv[...])).astype(bf16)

    for now in range(PHASE[1] + 12, PHASE[-1] + 12):
        tick(now)

    def slabs_in(head, at):
        return [line_in[head, half_at * GROUPS + at].astype(f32) for half_at in range(2)]

    for head in range(heads):
        for step in range(1, 8):
            there = lax.rem(blk + step, 8)
            landed(line_in.at[head, there], lrecv_sem.at[head, there])
    total = small_line[...]
    for step in range(1, 8):
        there = lax.rem(blk + step, 8)
        landed(small_line_in.at[there], lrecv_sem.at[heads, there])
        total += small_line_in[there]
    own = [
        functools.reduce(jnp.add, slabs_in(at % heads, at // heads))
        for at in range(GROUPS * heads)
    ]
    each = width // 32
    bias = []
    for part in range(3):
        cut = slice(part * HD, (part + 1) * HD)
        for pair in range(GROUPS * heads // 2):
            both_heads = jnp.concatenate([own[2 * pair][:, cut], own[2 * pair + 1][:, cut]], axis=1)
            lanes = slice(part * width + pair * LANES, part * width + (pair + 1) * LANES)
            wqkv_ref[:, lanes] = both_heads[:each]
            bias.append(both_heads[each:])
    pairs = GROUPS * heads // 2
    bias_q = jnp.concatenate(bias[:pairs], axis=1)
    bias_v = jnp.concatenate(bias[2 * pairs :], axis=1)
    bias = jnp.where(tab < 2, bias_q, bias_v)

    row = lax.broadcasted_iota(jnp.int32, (width, LANES), 0)
    lane = lax.broadcasted_iota(jnp.int32, (width, LANES), 1)

    def take(block, first, count):
        chosen = jnp.where((row == first + lane) & (lane < count), 1.0, 0.0)
        return jnp.dot(
            block, chosen, preferred_element_type=f32, precision=lax.Precision.HIGHEST
        )

    index = 8 * tab + blk
    little_ref[0:8] = take(total[:8], each * index, each)
    at_row = lax.broadcasted_iota(jnp.int32, total.shape, 0) == 6 + tab
    wide = jnp.sum(jnp.where(at_row, total, 0.0), axis=0, keepdims=True)
    little_ref[6:7] = take(jnp.broadcast_to(wide, (8, width)), 4 * each * blk, 4 * each)[:1]
    little_ref[7:8] = take(bias, 2 * each * lax.rem(index, 16), 2 * each)[:1]

    for step in range(1, 8):
        context_copy(lax.rem(blk + step, 8)).wait_send()
        small_blk(step).wait_send()
        for head in range(heads):
            slab_blk(head, step).wait_send()
    for step in range(1, 4):
        small_tab(step).wait_send()
        for head in range(heads):
            slab_tab(head, step).wait_send()

    @pl.loop(0, UNITS)
    def _(unit):
        for stage in range(STAGES):
            if stage in (1, 2):
                both(lambda order, stage=stage: stage_copy(stage, unit, order).wait_send())
            else:
                stage_copy(stage, unit).wait_send()


def attend_back(dctx, qkv, ot, lse, full_t, qkv_weight, pre, small, parts, heads):
    width, total = full_t.shape
    blocks = 8
    rows = total // blocks
    each, ff = width // 32, 4 * width
    any_space = pl.BlockSpec(memory_space=pl.ANY)
    vmem = pl.BlockSpec(memory_space=pltpu.VMEM)
    bf16, f32 = jnp.bfloat16, jnp.float32
    dma = pltpu.SemaphoreType.DMA
    unit = parts.shape[2:]
    parts = parts.reshape(UNITS, 2, 2, 2, 2, 2, *unit)
    shape = jax.ShapeDtypeStruct
    return pl.pallas_call(
        functools.partial(attend_back_kernel, heads),
        name="attend_back",
        out_shape=(
            shape((2, rows, width), bf16),
            shape((each, 3 * width), f32),
            shape((each, width), f32),
            shape((each, ff), f32),
            shape((4 * each, width), f32),
            shape((8, LANES), f32),
        ),
        in_specs=[any_space] * 8 + [vmem],
        out_specs=(vmem,) * 6,
        scratch_shapes=[
            pltpu.VMEM((blocks, rows, heads * HD), bf16),
            pltpu.VMEM((heads, total, HD), bf16),
            pltpu.VMEM((heads, 4, 8, 2 * rows), f32),
            pltpu.VMEM((3 * heads, total, LANES), bf16),
            pltpu.VMEM(ot.shape, f32),
            pltpu.VMEM(lse.shape, f32),
            pltpu.VMEM((width, total), bf16),
            pltpu.VMEM(qkv_weight.shape, bf16),
            pltpu.VMEM((2 * rows, width), f32),
            pltpu.VMEM((heads, LANES, total), bf16),
            pltpu.VMEM((total, HD), f32),
            pltpu.VMEM((total, HD), f32),
            pltpu.VMEM((total, HD), f32),
            pltpu.VMEM((heads, blocks, rows, 3 * HD), bf16),
            pltpu.VMEM((2, GROUPS * heads, rows, 3 * HD), bf16),
            pltpu.VMEM((rows, 3 * width), bf16),
            pltpu.VMEM((2, 2, 2, 2, 2, *unit), bf16),
            pltpu.VMEM((UNITS, 2, 2, 2, 2, *unit), bf16),
            pltpu.VMEM((UNITS, 2, 2, 2, *unit), bf16),
            pltpu.VMEM((UNITS, 2, 2, *unit), bf16),
            pltpu.VMEM((UNITS, 2, *unit), bf16),
            pltpu.VMEM((UNITS, *unit), bf16),
            pltpu.VMEM((heads, 4, 8, each + 8, 3 * HD), bf16),
            pltpu.VMEM((heads, 4, 8, each + 8, 3 * HD), bf16),
            pltpu.VMEM((heads, 8, each + 8, 3 * HD), bf16),
            pltpu.VMEM((heads, 8, each + 8, 3 * HD), bf16),
            pltpu.VMEM((4, 16, width), f32),
            pltpu.VMEM((16, width), f32),
            pltpu.VMEM((8, 16, width), f32),
            dma((blocks,)),
            dma((blocks,)),
            dma((heads, blocks)),
            dma((2, GROUPS * heads)),
            dma((STAGES, UNITS)),
            dma((STAGES, UNITS)),
            dma((heads + 1, 4)),
            dma((heads + 1, 4)),
            dma((heads + 1, 8)),
            dma((heads + 1, 8)),
            dma((7,)),
            dma((heads,)),
            dma((2,)),
        ],
        compiler_params=pltpu.CompilerParams(
            collective_id=2, has_side_effects=True, vmem_limit_bytes=62 << 20
        ),
    )(dctx, qkv, ot, lse, full_t, qkv_weight, pre, parts, small)


def halves(grad):
    cut = grad.shape[2] // 2
    return jnp.concatenate([grad[:, :, :cut], grad[:, :, cut:]], axis=1)


def norm_parts(inputs):
    centred = inputs - jnp.mean(inputs, axis=-1, keepdims=True)
    inverse = lax.rsqrt(jnp.mean(centred * centred, axis=-1, keepdims=True) + EPSILON)
    return centred * inverse, inverse


def norm_back(grad, normed, inverse, gain):
    e = grad * gain
    return inverse * (
        e
        - jnp.mean(e, axis=-1, keepdims=True)
        - normed * jnp.mean(e * normed, axis=-1, keepdims=True)
    )


def column_sum(block):
    return jnp.sum(block.astype(jnp.float32), axis=0, keepdims=True)


def ffn_kernel(
    tok_ref,
    ctx_ref,
    cot_ref,
    par_ref,
    outw_ref,
    upw_hbm,
    downw_hbm,
    out_ref,
    dctx_ref,
    pre_ref,
    small_ref,
    parts_ref,
    upw,
    downw,
    hid,
    hlow,
    hlow_t,
    norm1,
    slopes,
    active_t,
    pre2,
    gbranch,
    ghid,
    stage_d,
    stage_u,
    load_sem,
    stage_sem,
):
    f32, bf16 = jnp.float32, jnp.bfloat16
    tables, groups, rows, cols = ctx_ref.shape
    width = tok_ref.shape[1]
    chunks = active_t.shape[0]
    loads = (
        pltpu.make_async_copy(upw_hbm, upw, load_sem.at[0]),
        pltpu.make_async_copy(downw_hbm, downw, load_sem.at[1]),
    )
    for copy in loads:
        copy.start()

    def par(at):
        return par_ref[at : at + 1]

    inverse1 = []
    for table in range(tables):
        cut = pl.ds(table * rows, rows)
        pre1 = tok_ref[cut].astype(f32) + par(0)
        for group in range(groups):
            pre1 += jnp.dot(
                ctx_ref[table, group],
                outw_ref[group * cols : (group + 1) * cols],
                preferred_element_type=f32,
            )
        normed, inverse = norm_parts(pre1)
        inverse1.append(inverse)
        hidden = normed * par(1) + par(2)
        low = hidden.astype(bf16)
        norm1[cut] = normed
        hid[cut] = hidden
        hlow[cut] = low
        hlow_t[:, cut] = low.T

    pre2[...] = hid[...] + par(3)
    for copy in loads:
        copy.wait()

    @pl.loop(0, chunks)
    def _(at):
        cut = pl.ds(pl.multiple_of(at * width, width), width)
        upper = jnp.dot(
            hlow[...], upw[:, cut], preferred_element_type=f32
        ) + par_ref[pl.ds(24 + at, 1)]
        cdf = 0.5 + 0.5 * lax.erf(upper * math.sqrt(0.5))
        act = (upper * cdf).astype(bf16)
        slopes[at] = cdf + upper * jnp.exp(-0.5 * upper * upper) * (1 / math.sqrt(2 * math.pi))
        active_t[at] = act.T
        pre2[...] += jnp.dot(act, downw[cut], preferred_element_type=f32)

    normed, inverse = norm_parts(pre2[...])
    out_ref[...] = (normed * par(4) + par(5)).astype(bf16)
    grad = cot_ref[...].astype(f32)
    small_ref[4:5] = column_sum(grad * normed)
    small_ref[5:6] = column_sum(grad)
    gpre2 = norm_back(grad, normed, inverse, par(4))
    ghid[...] = gpre2
    low = gpre2.astype(bf16)
    gbranch[...] = low
    small_ref[3:4] = column_sum(low)

    each = width // 32

    def down_copies(at):
        return [
            pltpu.make_async_copy(
                stage_d.at[part],
                parts_ref.at[part, pl.ds(8 * at, 8)],
                stage_sem.at[part],
            )
            for part in range(4)
        ]

    def up_copy(at):
        return pltpu.make_async_copy(stage_u, parts_ref.at[4 + at], stage_sem.at[4])

    @pl.loop(0, chunks)
    def _(at):
        cut = pl.ds(pl.multiple_of(at * width, width), width)
        wdown = jnp.dot(active_t[at], gbranch[...], preferred_element_type=f32)
        wdown = wdown.reshape(8, 4, each, width)

        @pl.when(at > 0)
        def _():
            for copy in down_copies(at - 1):
                copy.wait()
            up_copy(at - 1).wait()

        for part in range(4):
            stage_d[part] = halves(wdown[:, part]).astype(bf16)
        for copy in down_copies(at):
            copy.start()
        gact = times_t(gbranch[...], downw[cut])
        gup = (gact * slopes[at]).astype(bf16)
        small_ref[pl.ds(6 + at, 1)] = column_sum(gup)
        ghid[...] += times_t(gup, upw[:, cut])
        wup = jnp.dot(hlow_t[...], gup, preferred_element_type=f32)
        stage_u[...] = halves(wup.reshape(32, each, width)).astype(bf16)
        up_copy(at).start()

    for copy in down_copies(chunks - 1):
        copy.wait()
    up_copy(chunks - 1).wait()
    small = [0.0, 0.0, 0.0]
    lows = []
    for table in range(tables):
        cut = pl.ds(table * rows, rows)
        grad, normed = ghid[cut], norm1[cut]
        small[1] += column_sum(grad * normed)
        small[2] += column_sum(grad)
        gpre1 = norm_back(grad, normed, inverse1[table], par(1))
        pre_ref[cut] = gpre1
        low = gpre1.astype(bf16)
        small[0] += column_sum(low)
        lows.append(low)
        for group in range(groups):
            dctx_ref[table, group] = times_t(
                low, outw_ref[group * cols : (group + 1) * cols]
            ).astype(bf16)
    for at in range(3):
        small_ref[at : at + 1] = small[at]
    small_ref[10:] = jnp.zeros((6, width), f32)
    for group in range(groups):
        wout = 0.0
        for table in range(tables):
            wout += jnp.dot(ctx_ref[table, group].T, lows[table], preferred_element_type=f32)
        stage_u[group * 8 : (group + 1) * 8] = halves(wout.reshape(8, each, width)).astype(bf16)
    last = pltpu.make_async_copy(stage_u, parts_ref.at[8], stage_sem.at[4])
    last.start()
    last.wait()


def ffn(tokens, ctx, cotangent, params, out_weight, up_weight, down_weight):
    total, width = tokens.shape
    chunks = up_weight.shape[1] // width
    each = width // 32
    any_space = pl.BlockSpec(memory_space=pl.ANY)
    vmem = pl.BlockSpec(memory_space=pltpu.VMEM)
    bf16, f32 = jnp.bfloat16, jnp.float32
    flops = 18 * total * width * chunks * width + 6 * total * width * width
    return pl.pallas_call(
        ffn_kernel,
        name="ffn",
        out_shape=(
            jax.ShapeDtypeStruct((total, width), bf16),
            jax.ShapeDtypeStruct(ctx.shape, bf16),
            jax.ShapeDtypeStruct((total, width), f32),
            jax.ShapeDtypeStruct((16, width), f32),
            jax.ShapeDtypeStruct((9, 32, 2 * each, width // 2), bf16),
        ),
        in_specs=[vmem, vmem, vmem, vmem, vmem, any_space, any_space],
        out_specs=(vmem, vmem, vmem, vmem, any_space),
        scratch_shapes=[
            pltpu.VMEM(up_weight.shape, bf16),
            pltpu.VMEM(down_weight.shape, bf16),
            pltpu.VMEM((total, width), f32),
            pltpu.VMEM((total, width), bf16),
            pltpu.VMEM((width, total), bf16),
            pltpu.VMEM((total, width), f32),
            pltpu.VMEM((chunks, total, width), f32),
            pltpu.VMEM((chunks, width, total), bf16),
            pltpu.VMEM((total, width), f32),
            pltpu.VMEM((total, width), bf16),
            pltpu.VMEM((total, width), f32),
            pltpu.VMEM((4, 8, 2 * each, width // 2), bf16),
            pltpu.VMEM((32, 2 * each, width // 2), bf16),
            pltpu.SemaphoreType.DMA((2,)),
            pltpu.SemaphoreType.DMA((5,)),
        ],
        compiler_params=pltpu.CompilerParams(vmem_limit_bytes=60 << 20),
        cost_estimate=pl.CostEstimate(
            flops=flops, bytes_accessed=40 << 20, transcendentals=total * width * chunks
        ),
    )(tokens, ctx, cotangent, params, out_weight, up_weight, down_weight)


def scatter_sum(grad):
    return lax.psum_scatter(
        lax.psum_scatter(
            grad.astype(jnp.bfloat16), "tab", scatter_dimension=0, tiled=True
        ),
        "blk",
        scatter_dimension=0,
        tiled=True,
    ).astype(jnp.float32)


def shards_direct(
    tokens,
    lengths,
    qkv_weight,
    qkv_bias,
    out_weight,
    out_bias,
    attn_gain,
    attn_shift,
    up_weight,
    up_bias,
    down_weight,
    down_bias,
    ffn_gain,
    ffn_shift,
    cotangent,
):
    tables, rows, width = tokens.shape
    f32 = jnp.float32
    heads = width // HD // GROUPS
    flat_tokens = tokens.reshape(tables * rows, width)
    six = jnp.stack([out_bias, attn_gain, attn_shift, down_bias, ffn_gain, ffn_shift])
    params = jnp.concatenate(
        [
            six,
            jnp.zeros((2, width), six.dtype),
            jnp.broadcast_to(qkv_bias[None, :width], (8, width)),
            jnp.broadcast_to(qkv_bias[None, width:], (8, width)),
            up_bias.reshape(-1, width),
            jnp.zeros((4, width), six.dtype),
        ]
    ).astype(f32)

    ctx, full_t, qkv, ot, lse = attend(tokens, lengths, params, qkv_weight, heads)
    layer_out, dctx, pre, small, parts = ffn(
        flat_tokens,
        ctx,
        cotangent.reshape(tables * rows, width),
        params,
        out_weight,
        up_weight,
        down_weight,
    )
    token_grad, wgrad_qkv, wgrad_out, wgrad_up, wgrad_down, little = attend_back(
        dctx, qkv, ot, lse, full_t, qkv_weight, pre, small, parts, heads
    )
    each = width // 32
    return (
        layer_out.reshape(tokens.shape),
        token_grad,
        wgrad_qkv,
        little[7, : 2 * each],
        wgrad_out,
        little[0, :each],
        little[1, :each],
        little[2, :each],
        wgrad_up,
        little[6, : 4 * each],
        wgrad_down,
        little[3, :each],
        little[4, :each],
        little[5, :each],
    )


def solution(mesh):
    in_specs = (
        P("tab", "blk", None),
        P("tab"),
        P(),
        P(),
        P(),
        P(),
        P(),
        P(),
        P(),
        P(),
        P(),
        P(),
        P(),
        P(),
        P("tab", "blk", None),
    )
    out_specs = (
        P("tab", "blk", None),
        P("tab", "blk", None),
        P(("tab", "blk"), None),
        P(("tab", "blk")),
        P(("tab", "blk"), None),
        P(("tab", "blk")),
        P(("tab", "blk")),
        P(("tab", "blk")),
        P(("tab", "blk"), None),
        P(("tab", "blk")),
        P(("tab", "blk"), None),
        P(("tab", "blk")),
        P(("tab", "blk")),
        P(("tab", "blk")),
    )
    tab_count, blk_count = mesh.shape["tab"], mesh.shape["blk"]

    def pick(*operands):
        table_count = operands[0].shape[0] // tab_count
        head_count = operands[0].shape[2] // HD
        direct = table_count == 2 and blk_count == 8 and tab_count == 4 and head_count % 4 == 0
        body = shards_direct if direct else shards_ring
        return jax.shard_map(
            body, mesh=mesh, in_specs=in_specs, out_specs=out_specs, check_vma=False
        )(*operands)

    return pick
```

```python
import functools
import math

import jax
import jax.numpy as jnp
from jax import lax
from jax.experimental import pallas as pl
from jax.experimental.pallas import tpu as pltpu
from jax.sharding import PartitionSpec as P

HD = 64


EPSILON = 1e-05
NEGATIVE = -1e30


def from_behind(block, axis, distance):
    devices = range(lax.axis_size(axis))
    route = [((i - distance) % len(devices), i) for i in devices]
    return lax.ppermute(block, axis, route)


def norm_rows(inputs, gains, shifts):
    row_mean = jnp.mean(inputs, axis=-1, keepdims=True)
    centred = inputs - row_mean
    row_var = jnp.mean(centred * centred, axis=-1, keepdims=True)
    return centred * lax.rsqrt(row_var + EPSILON) * gains + shifts


def gelu_exact(inputs):
    return jax.nn.gelu(inputs, approximate=False)


def times_back(left, right):
    return lax.dot_general(
        left, right, (((1,), (1,)), ((), ())), preferred_element_type=jnp.float32
    )


def over_rows(left, right):
    return lax.dot_general(
        left, right, (((0,), (0,)), ((), ())), preferred_element_type=jnp.float32
    )


def shards_ring(
    tokens,
    lengths,
    qkv_weight,
    qkv_bias,
    out_weight,
    out_bias,
    attn_gain,
    attn_shift,
    up_weight,
    up_bias,
    down_weight,
    down_bias,
    ffn_gain,
    ffn_shift,
    cotangent,
):
    table_count, row_count, model_width = tokens.shape
    head_count = model_width // HD
    cycle_size = lax.axis_size("blk")
    cycle_place = lax.axis_index("blk")
    score_scale = HD ** (-0.5)
    flat_tokens = tokens.reshape(table_count * row_count, model_width)
    bias_full = jnp.concatenate(
        [
            qkv_bias[:model_width].astype(jnp.float32),
            jnp.zeros((model_width,), jnp.float32),
            qkv_bias[model_width:].astype(jnp.float32),
        ]
    )
    qkv_low = (
        jnp.dot(flat_tokens, qkv_weight, preferred_element_type=jnp.float32) + bias_full
    ).astype(jnp.bfloat16)
    queries = qkv_low[:, :model_width].reshape(table_count, row_count, head_count, HD)
    key_values = qkv_low[:, model_width:].reshape(table_count, row_count, 2 * model_width)

    def key_mask(first_row, key_count):
        positions = first_row + jnp.arange(key_count, dtype=jnp.int32)
        return (positions[None, :] < lengths[:, None])[:, None, None, :]

    def split_pair(pair_block):
        key_count = pair_block.shape[1]
        keys_part = pair_block[:, :, :model_width].reshape(table_count, key_count, head_count, HD)
        values_part = pair_block[:, :, model_width:].reshape(table_count, key_count, head_count, HD)
        return (keys_part, values_part)

    pair_block = lax.all_gather(key_values, "blk", axis=1, tiled=True)
    running_max = jnp.full((table_count, row_count, head_count), NEGATIVE, jnp.float32)
    keys_part, values_part = split_pair(pair_block)
    is_valid = key_mask(jnp.int32(0), pair_block.shape[1])
    raw_scores = jnp.einsum(
        "trhd,tkhd->trhk", queries, keys_part, preferred_element_type=jnp.float32
    )
    scores = jnp.where(is_valid, raw_scores * score_scale, NEGATIVE)
    peak_new = jnp.maximum(running_max, jnp.max(scores, axis=-1))
    exponent = jnp.where(is_valid, jnp.exp(scores - peak_new[..., None]), 0.0)
    running_sum = jnp.sum(exponent, axis=-1)
    weighted = jnp.einsum(
        "trhk,tkhd->trhd",
        exponent.astype(jnp.bfloat16),
        values_part,
        preferred_element_type=jnp.float32,
    )
    running_max, running_sum, weighted = (peak_new, running_sum, weighted)
    context = weighted / running_sum[..., None]
    log_total = running_max + jnp.log(running_sum)
    context_low = context.reshape(table_count * row_count, model_width).astype(jnp.bfloat16)
    attended = jnp.dot(
        context_low, out_weight, preferred_element_type=jnp.float32
    ) + out_bias.astype(jnp.float32)
    pre_one = flat_tokens.astype(jnp.float32) + attended
    gain_one = attn_gain.astype(jnp.float32)
    shift_one = attn_shift.astype(jnp.float32)
    hidden = norm_rows(pre_one, gain_one, shift_one)
    hidden_low = hidden.astype(jnp.bfloat16)
    upper = jnp.dot(hidden_low, up_weight, preferred_element_type=jnp.float32) + up_bias.astype(
        jnp.float32
    )
    active = gelu_exact(upper).astype(jnp.bfloat16)
    pre_two = (
        hidden
        + jnp.dot(active, down_weight, preferred_element_type=jnp.float32)
        + down_bias.astype(jnp.float32)
    )
    gain_two = ffn_gain.astype(jnp.float32)
    shift_two = ffn_shift.astype(jnp.float32)
    layer_out = norm_rows(pre_two, gain_two, shift_two).astype(jnp.bfloat16).reshape(tokens.shape)
    grad_out = cotangent.reshape(table_count * row_count, model_width).astype(jnp.float32)
    _, norm_two_back = jax.vjp(norm_rows, pre_two, gain_two, shift_two)
    grad_pre_two, ggrad_ffn, sgrad_ffn = norm_two_back(grad_out)
    grad_branch = grad_pre_two.astype(jnp.bfloat16)
    wgrad_down = over_rows(active, grad_branch)
    bgrad_down = jnp.sum(grad_branch, axis=0, dtype=jnp.float32)
    grad_active = times_back(grad_branch, down_weight)
    _, gelu_back = jax.vjp(gelu_exact, upper)
    grad_upper = gelu_back(grad_active)[0].astype(jnp.bfloat16)
    wgrad_up = over_rows(hidden_low, grad_upper)
    bgrad_up = jnp.sum(grad_upper, axis=0, dtype=jnp.float32)
    grad_hidden = grad_pre_two + times_back(grad_upper, up_weight)
    _, norm_one_back = jax.vjp(norm_rows, pre_one, gain_one, shift_one)
    grad_pre_one, ggrad_attn, sgrad_attn = norm_one_back(grad_hidden)
    grad_attended = grad_pre_one.astype(jnp.bfloat16)
    wgrad_out = over_rows(context_low, grad_attended)
    bgrad_out = jnp.sum(grad_attended, axis=0, dtype=jnp.float32)
    grad_context = times_back(grad_attended, out_weight).astype(jnp.bfloat16)
    grad_heads = grad_context.reshape(table_count, row_count, head_count, HD)
    row_delta = jnp.sum(grad_heads.astype(jnp.float32) * context, axis=-1)

    def cycle_turn_step(cycle_turn, cycle_state):
        pair_now, pair_grads, grad_queries = cycle_state
        owner_index = (cycle_place - cycle_turn) % cycle_size
        keys_part, values_part = split_pair(pair_now)
        is_valid = key_mask(owner_index * row_count, row_count)
        raw_scores = jnp.einsum(
            "trhd,tkhd->trhk", queries, keys_part, preferred_element_type=jnp.float32
        )
        scores = jnp.where(is_valid, raw_scores * score_scale, NEGATIVE)
        probs = jnp.where(is_valid, jnp.exp(scores - log_total[..., None]), 0.0)
        grad_probs = jnp.einsum(
            "trhd,tkhd->trhk", grad_heads, values_part, preferred_element_type=jnp.float32
        )
        grad_raw = (probs * (grad_probs - row_delta[..., None]) * score_scale).astype(jnp.bfloat16)
        grad_queries = grad_queries + jnp.einsum(
            "trhk,tkhd->trhd", grad_raw, keys_part, preferred_element_type=jnp.float32
        )
        grad_keys = jnp.einsum(
            "trhk,trhd->tkhd", grad_raw, queries, preferred_element_type=jnp.float32
        )
        grad_values = jnp.einsum(
            "trhk,trhd->tkhd",
            probs.astype(jnp.bfloat16),
            grad_heads,
            preferred_element_type=jnp.float32,
        )
        pair_grads = pair_grads + jnp.concatenate(
            [
                grad_keys.reshape(table_count, row_count, model_width),
                grad_values.reshape(table_count, row_count, model_width),
            ],
            axis=-1,
        )
        pair_next = from_behind(pair_now, "blk", 1)
        grads_next = from_behind(pair_grads.astype(jnp.bfloat16), "blk", 1).astype(pair_grads.dtype)
        return (pair_next, grads_next, grad_queries)

    cycle_start = (
        key_values,
        jnp.zeros((table_count, row_count, 2 * model_width), jnp.float32),
        jnp.zeros((table_count, row_count, head_count, HD), jnp.float32),
    )
    _, pair_home, grad_queries = lax.fori_loop(0, cycle_size, cycle_turn_step, cycle_start)
    grad_qkv = jnp.concatenate(
        [
            grad_queries.reshape(table_count * row_count, model_width),
            pair_home.reshape(table_count * row_count, 2 * model_width),
        ],
        axis=-1,
    ).astype(jnp.bfloat16)
    wgrad_qkv = over_rows(flat_tokens, grad_qkv)
    column_sums = jnp.sum(grad_qkv, axis=0, dtype=jnp.float32)
    bgrad_qkv = jnp.concatenate([column_sums[:model_width], column_sums[2 * model_width :]])
    token_grad = (
        (grad_pre_one + times_back(grad_qkv, qkv_weight)).astype(jnp.bfloat16).reshape(tokens.shape)
    )
    (
        wgrad_qkv,
        bgrad_qkv,
        wgrad_out,
        bgrad_out,
        ggrad_attn,
        sgrad_attn,
        wgrad_up,
        bgrad_up,
        wgrad_down,
        bgrad_down,
        ggrad_ffn,
        sgrad_ffn,
    ) = (
        lax.psum_scatter(
            wgrad_qkv.astype(jnp.bfloat16), "tab", scatter_dimension=0, tiled=True
        ).astype(jnp.float32),
        lax.psum_scatter(
            bgrad_qkv.astype(jnp.bfloat16), "tab", scatter_dimension=0, tiled=True
        ).astype(jnp.float32),
        lax.psum_scatter(
            wgrad_out.astype(jnp.bfloat16), "tab", scatter_dimension=0, tiled=True
        ).astype(jnp.float32),
        lax.psum_scatter(
            bgrad_out.astype(jnp.bfloat16), "tab", scatter_dimension=0, tiled=True
        ).astype(jnp.float32),
        lax.psum_scatter(
            ggrad_attn.astype(jnp.bfloat16), "tab", scatter_dimension=0, tiled=True
        ).astype(jnp.float32),
        lax.psum_scatter(
            sgrad_attn.astype(jnp.bfloat16), "tab", scatter_dimension=0, tiled=True
        ).astype(jnp.float32),
        lax.psum_scatter(
            wgrad_up.astype(jnp.bfloat16), "tab", scatter_dimension=0, tiled=True
        ).astype(jnp.float32),
        lax.psum_scatter(
            bgrad_up.astype(jnp.bfloat16), "tab", scatter_dimension=0, tiled=True
        ).astype(jnp.float32),
        lax.psum_scatter(
            wgrad_down.astype(jnp.bfloat16), "tab", scatter_dimension=0, tiled=True
        ).astype(jnp.float32),
        lax.psum_scatter(
            bgrad_down.astype(jnp.bfloat16), "tab", scatter_dimension=0, tiled=True
        ).astype(jnp.float32),
        lax.psum_scatter(
            ggrad_ffn.astype(jnp.bfloat16), "tab", scatter_dimension=0, tiled=True
        ).astype(jnp.float32),
        lax.psum_scatter(
            sgrad_ffn.astype(jnp.bfloat16), "tab", scatter_dimension=0, tiled=True
        ).astype(jnp.float32),
    )
    (
        wgrad_qkv,
        bgrad_qkv,
        wgrad_out,
        bgrad_out,
        ggrad_attn,
        sgrad_attn,
        wgrad_up,
        bgrad_up,
        wgrad_down,
        bgrad_down,
        ggrad_ffn,
        sgrad_ffn,
    ) = (
        lax.psum_scatter(
            wgrad_qkv.astype(jnp.bfloat16), "blk", scatter_dimension=0, tiled=True
        ).astype(jnp.float32),
        lax.psum_scatter(
            bgrad_qkv.astype(jnp.bfloat16), "blk", scatter_dimension=0, tiled=True
        ).astype(jnp.float32),
        lax.psum_scatter(
            wgrad_out.astype(jnp.bfloat16), "blk", scatter_dimension=0, tiled=True
        ).astype(jnp.float32),
        lax.psum_scatter(
            bgrad_out.astype(jnp.bfloat16), "blk", scatter_dimension=0, tiled=True
        ).astype(jnp.float32),
        lax.psum_scatter(
            ggrad_attn.astype(jnp.bfloat16), "blk", scatter_dimension=0, tiled=True
        ).astype(jnp.float32),
        lax.psum_scatter(
            sgrad_attn.astype(jnp.bfloat16), "blk", scatter_dimension=0, tiled=True
        ).astype(jnp.float32),
        lax.psum_scatter(
            wgrad_up.astype(jnp.bfloat16), "blk", scatter_dimension=0, tiled=True
        ).astype(jnp.float32),
        lax.psum_scatter(
            bgrad_up.astype(jnp.bfloat16), "blk", scatter_dimension=0, tiled=True
        ).astype(jnp.float32),
        lax.psum_scatter(
            wgrad_down.astype(jnp.bfloat16), "blk", scatter_dimension=0, tiled=True
        ).astype(jnp.float32),
        lax.psum_scatter(
            bgrad_down.astype(jnp.bfloat16), "blk", scatter_dimension=0, tiled=True
        ).astype(jnp.float32),
        lax.psum_scatter(
            ggrad_ffn.astype(jnp.bfloat16), "blk", scatter_dimension=0, tiled=True
        ).astype(jnp.float32),
        lax.psum_scatter(
            sgrad_ffn.astype(jnp.bfloat16), "blk", scatter_dimension=0, tiled=True
        ).astype(jnp.float32),
    )
    return (
        layer_out,
        token_grad,
        wgrad_qkv,
        bgrad_qkv,
        wgrad_out,
        bgrad_out,
        ggrad_attn,
        sgrad_attn,
        wgrad_up,
        bgrad_up,
        wgrad_down,
        bgrad_down,
        ggrad_ffn,
        sgrad_ffn,
    )


GROUPS = 4
LANES = 128
LOG2E = math.log2(math.e)
MESH = pl.DeviceIdType.MESH


def times_t(left, right):
    return lax.dot_general(
        left, right, (((1,), (1,)), ((), ())), preferred_element_type=jnp.float32
    )


def place():
    tab, blk = lax.axis_index("tab"), lax.axis_index("blk")
    return tab, blk, blk // 2, blk % 2


def meet(tab, blk):
    barrier = pltpu.get_barrier_semaphore()

    @pl.loop(1, 8)
    def _(step):
        pl.semaphore_signal(
            barrier, inc=1, device_id=(tab, lax.rem(blk + step, 8)), device_id_type=MESH
        )

    pl.semaphore_wait(barrier, 7)


def fold(block):
    cut = block.shape[0] // 2
    return jnp.concatenate([block[:cut], block[cut:]], axis=1)


def unfold(block):
    cut = block.shape[1] // 2
    return jnp.concatenate([block[:, :cut], block[:, cut:]], axis=0)


def own_window(group, first, rows_ref, out):
    start = pl.multiple_of(first + LANES * ((3 * group) // 2), LANES)
    window = rows_ref[:, pl.ds(start, 2 * LANES)].astype(jnp.float32)
    window = pltpu.roll(window, lax.rem(2 * LANES - HD * lax.rem(group, 2), 2 * LANES), 1)
    left = window[:, :LANES]
    low = lax.broadcasted_iota(jnp.int32, left.shape, 1) < HD
    for head, lanes in enumerate((left, pltpu.roll(left, HD, 1), window[:, LANES:])):
        out(head, jnp.where(low, lanes, 0.0))


def attend_kernel(
    heads,
    tok_ref,
    len_ref,
    par_ref,
    w_hbm,
    ctx_ref,
    fullt_ref,
    qkv_ref,
    ot_ref,
    lse_ref,
    wr_ref,
    tokv,
    toktv,
    wfull,
    wrv,
    wown,
    bown,
    qkvv,
    vtv,
    otv,
    lsev,
    csend,
    send_sem,
    recv,
    csend_sem,
    crecv_sem,
    local_sem,
):
    tab, blk, chip, core = place()
    half = chip // 2
    group = 2 * lax.rem(chip, 2) + core
    rows = tok_ref.shape[1]
    width = tok_ref.shape[2]
    is_near = jnp.logical_or(chip == 1, chip == 2)
    mate = chip + 1 - 2 * lax.rem(chip, 2)
    other_near = 2 - half
    other_far = 3 - 3 * half
    own_far = 3 * half
    scale = LOG2E / math.sqrt(HD)

    def remote(src, dst, send_sem, recv_sem, to_chip, to_core):
        return pltpu.make_async_remote_copy(
            src_ref=src,
            dst_ref=dst,
            send_sem=send_sem,
            recv_sem=recv_sem,
            device_id=(tab, 2 * to_chip + to_core),
            device_id_type=MESH,
        )

    here, there = tok_ref.at[half], tok_ref.at[1 - half]
    to_mate = remote(here, tokv.at[blk], send_sem.at[0], recv.at[blk], mate, core)
    to_other = remote(there, tokv.at[blk], send_sem.at[1], recv.at[blk], other_near, core)
    to_side = remote(here, tokv.at[blk], send_sem.at[2], recv.at[blk], chip, 1 - core)

    def to_far(slot, src_chip):
        which = 2 * src_chip + core
        ref = tokv.at[which]
        return remote(ref, ref, send_sem.at[2 + slot], recv.at[which], own_far, core)

    def to_core(slot, src_chip):
        which = 2 * src_chip + core
        ref = tokv.at[which]
        return remote(ref, ref, send_sem.at[5 + slot], recv.at[which], chip, 1 - core)

    def arrived(which):
        pltpu.make_async_copy(tokv.at[which], tokv.at[which], recv.at[which]).wait()

    load = pltpu.make_async_copy(w_hbm, wfull, local_sem.at[5])
    load.start()
    meet(tab, blk)
    pl.when(is_near)(to_other.start)
    to_mate.start()
    to_side.start()
    tokv[blk] = tok_ref[half]

    lane1 = lax.broadcasted_iota(jnp.int32, (8, LANES), 1)
    for at in (0, 2):

        def keep_bias(head, lanes, at=at):
            row = jnp.where(lane1 == HD, 1.0, lanes)
            bown[:, pl.ds((at * heads + head) * LANES, LANES)] = row

        own_window(group, 0, par_ref.at[pl.ds(8 * (1 + at // 2), 8)], keep_bias)
    for head in range(heads):
        bown[:, pl.ds((heads + head) * LANES, LANES)] = jnp.zeros((8, LANES), jnp.float32)
    load.wait()
    for at in range(3):

        def keep_weight(head, lanes, at=at):
            wown[:, pl.ds((at * heads + head) * LANES, LANES)] = lanes.astype(jnp.bfloat16)

        own_window(group, at * width, wfull, keep_weight)

    length = len_ref[half]
    lane = lax.broadcasted_iota(jnp.int32, (rows, LANES), 1)
    row = lax.broadcasted_iota(jnp.int32, (rows, LANES), 0)

    def project(which):
        first = pl.multiple_of(which * rows, rows)
        tok = tokv[which]
        y = jnp.dot(tok, wown[...], preferred_element_type=jnp.float32) + bown[:1]
        pad = jnp.where((lane == HD) & (row + first >= length), NEGATIVE, 0.0)
        for head in range(heads):
            q, k, v = (
                y[:, (part * heads + head) * LANES :][:, :LANES] for part in range(3)
            )
            qkvv[head, pl.ds(first, rows)] = q.astype(jnp.bfloat16)
            qkvv[heads + head, pl.ds(first, rows)] = (k + pad).astype(jnp.bfloat16)
            qkvv[2 * heads + head, pl.ds(first, rows)] = v.astype(jnp.bfloat16)
            vtv[head, :, pl.ds(first, rows)] = v.T.astype(jnp.bfloat16)
        toktv[:, pl.ds(first, rows)] = tok.T

    project(blk)

    def half_lanes(part, at):
        first = part * width + LANES * (at // 2)
        return wfull[:, first : first + LANES][:, HD * (at % 2) :][:, :HD]

    for head in range(heads):
        for part in range(3):
            for pair in range(GROUPS // 2):
                at = 2 * pair * heads + head
                wrv[head, :, pl.ds((2 * part + pair) * LANES, LANES)] = jnp.concatenate(
                    [half_lanes(part, at), half_lanes(part, at + heads)], axis=1
                )
    arrived(2 * mate + core)
    to_core(0, mate).start()

    @pl.when(jnp.logical_not(is_near))
    def _():
        to_mate.wait_send()
        to_other.start()

    project(2 * mate + core)
    arrived(2 * chip + 1 - core)
    project(2 * chip + 1 - core)
    arrived(2 * mate + 1 - core)
    project(2 * mate + 1 - core)
    for slot, src_chip in ((1, other_near), (2, other_far)):
        arrived(2 * src_chip + core)
        pl.when(is_near)(to_far(slot, src_chip).start)
        to_core(slot, src_chip).start()
        project(2 * src_chip + core)
        arrived(2 * src_chip + 1 - core)
        project(2 * src_chip + 1 - core)

    keep = (
        pltpu.make_async_copy(toktv, fullt_ref, local_sem.at[0]),
        pltpu.make_async_copy(qkvv, qkv_ref, local_sem.at[1]),
        pltpu.make_async_copy(wrv, wr_ref, local_sem.at[6]),
    )
    for copy in keep:
        copy.start()

    def context_copy(which):
        return remote(
            csend.at[which],
            ctx_ref.at[half, group],
            csend_sem.at[which],
            crecv_sem.at[blk],
            which // 2,
            lax.rem(which, 2),
        )

    own_context = pltpu.make_async_copy(
        csend.at[blk], ctx_ref.at[half, group], local_sem.at[2]
    )

    @pl.loop(0, 4)
    def _(step):
        which = lax.rem(chip + 1 + step, 4)
        first = pl.multiple_of(which * 2 * rows, 2 * rows)
        for head in range(heads):
            q = qkvv[head, pl.ds(first, 2 * rows)]
            st = times_t(qkvv[heads + head], q)
            peak = jnp.max(st, axis=0, keepdims=True)
            pt = jnp.exp2((st - peak) * scale).astype(jnp.bfloat16)
            ot = jnp.dot(vtv[head], pt, preferred_element_type=jnp.float32)
            total = ot[HD : HD + 1]
            otv[which, head * HD : (head + 1) * HD] = ot[:HD] / total
            lsev[which, head : head + 1] = peak * scale + jnp.log(total) * LOG2E
        out = otv[which].T.astype(jnp.bfloat16)
        for side in range(2):
            csend[2 * which + side] = fold(out[side * rows : (side + 1) * rows])

        @pl.when(step < 3)
        def _():
            context_copy(2 * which).start()
            context_copy(2 * which + 1).start()

        @pl.when(step == 3)
        def _():
            context_copy(2 * which + 1 - core).start()
            own_context.start()

    more = (
        pltpu.make_async_copy(otv, ot_ref, local_sem.at[3]),
        pltpu.make_async_copy(lsev, lse_ref, local_sem.at[4]),
    )
    for copy in more:
        copy.start()
    pl.when(is_near)(to_mate.wait_send)
    to_other.wait_send()
    to_side.wait_send()
    to_core(0, mate).wait_send()
    for slot, src_chip in ((1, other_near), (2, other_far)):
        pl.when(is_near)(to_far(slot, src_chip).wait_send)
        to_core(slot, src_chip).wait_send()

    @pl.loop(1, 8)
    def _(step):
        which = lax.rem(blk + step, 8)
        context_copy(which).wait_send()
        pltpu.make_async_copy(
            ctx_ref.at[which // 4, lax.rem(which, 4)],
            ctx_ref.at[which // 4, lax.rem(which, 4)],
            crecv_sem.at[which],
        ).wait()

    own_context.wait()
    for copy in keep + more:
        copy.wait()


def attend(tokens, lengths, params, qkv_weight, heads):
    tables, rows, width = tokens.shape
    blocks = 8
    total = blocks * rows
    any_space = pl.BlockSpec(memory_space=pl.ANY)
    vmem = pl.BlockSpec(memory_space=pltpu.VMEM)
    bf16, f32 = jnp.bfloat16, jnp.float32
    dma = pltpu.SemaphoreType.DMA
    return pl.pallas_call(
        functools.partial(attend_kernel, heads),
        name="attend",
        out_shape=(
            jax.ShapeDtypeStruct((tables, GROUPS, rows // 2, 2 * heads * HD), bf16),
            jax.ShapeDtypeStruct((width, total), bf16),
            jax.ShapeDtypeStruct((3 * heads, total, LANES), bf16),
            jax.ShapeDtypeStruct((4, heads * HD, 2 * rows), f32),
            jax.ShapeDtypeStruct((4, 8, 2 * rows), f32),
            jax.ShapeDtypeStruct((heads, width, width), bf16),
        ),
        in_specs=[vmem, pl.BlockSpec(memory_space=pltpu.SMEM), vmem, any_space],
        out_specs=(any_space,) * 6,
        scratch_shapes=[
            pltpu.VMEM((blocks, rows, width), bf16),
            pltpu.VMEM((width, total), bf16),
            pltpu.VMEM(qkv_weight.shape, bf16),
            pltpu.VMEM((heads, width, width), bf16),
            pltpu.VMEM((width, 3 * heads * LANES), bf16),
            pltpu.VMEM((8, 3 * heads * LANES), f32),
            pltpu.VMEM((3 * heads, total, LANES), bf16),
            pltpu.VMEM((heads, LANES, total), bf16),
            pltpu.VMEM((4, heads * HD, 2 * rows), f32),
            pltpu.VMEM((4, 8, 2 * rows), f32),
            pltpu.VMEM((blocks, rows // 2, 2 * heads * HD), bf16),
            dma((8,)),
            dma((blocks,)),
            dma((blocks,)),
            dma((blocks,)),
            dma((7,)),
        ],
        compiler_params=pltpu.CompilerParams(
            collective_id=1, has_side_effects=True, vmem_limit_bytes=60 << 20
        ),
    )(tokens, lengths, params, qkv_weight)


UNITS = 9
TURNS = 4
STAGES = 5
PHASE = (2, 5, 7, 9, 11)


def attend_back_kernel(
    heads,
    dctx_ref,
    qkv_ref,
    ot_ref,
    lse_ref,
    fullt_ref,
    w_ref,
    pre_ref,
    parts_ref,
    small_ref,
    tgrad_ref,
    wqkv_ref,
    wout_ref,
    wup_ref,
    wdown_ref,
    little_ref,
    dov,
    doh,
    deltas,
    qkvv,
    otv,
    lsev,
    toktv,
    wv,
    prev,
    ktv,
    dqv,
    dkv,
    dvv,
    dqkv,
    qsend,
    kvsend,
    arrive_q,
    arrive_kv,
    joined,
    xacc,
    xsend,
    back,
    mine,
    sum0,
    sum1,
    sum2,
    sum3,
    sum4,
    slab,
    slab_in,
    line,
    line_in,
    small_in,
    small_line,
    small_line_in,
    dsend_sem,
    drecv_sem,
    gsend_sem,
    grecv_sem,
    xsend_sem,
    xrecv_sem,
    ssend_sem,
    srecv_sem,
    tsend_sem,
    trecv_sem,
    lsend_sem,
    lrecv_sem,
    local_sem,
    mine_sem,
):
    f32, bf16 = jnp.float32, jnp.bfloat16
    tab, blk, chip, core = place()
    y, x, zh, zl = tab // 2, lax.rem(tab, 2), chip // 2, lax.rem(chip, 2)
    half = zh
    group = 2 * zl + core
    blocks, rows = dov.shape[0], 2 * dov.shape[1]
    width = toktv.shape[0]
    tile = 2 * rows
    piece = 256
    scale = LOG2E / math.sqrt(HD)
    shrink = HD**-0.5

    def remote(src, dst, send_sem, recv_sem, device):
        return pltpu.make_async_remote_copy(
            src_ref=src,
            dst_ref=dst,
            send_sem=send_sem,
            recv_sem=recv_sem,
            device_id=device,
            device_id_type=MESH,
        )

    def landed(ref, sem):
        pltpu.make_async_copy(ref, ref, sem).wait()

    loads = [
        pltpu.make_async_copy(src, dst, local_sem.at[at])
        for at, (src, dst) in enumerate(
            (
                (qkv_ref, qkvv),
                (ot_ref, otv),
                (lse_ref, lsev),
                (dctx_ref.at[half, group], dov.at[blk]),
                (fullt_ref, toktv),
                (w_ref, wv),
                (pre_ref, prev),
            )
        )
    ]
    for copy in loads:
        copy.start()

    barrier = pltpu.get_barrier_semaphore()
    for step in range(1, 8):
        pl.semaphore_signal(
            barrier, inc=1, device_id=(tab, lax.rem(blk + step, 8)), device_id_type=MESH
        )
    for step in range(1, 4):
        pl.semaphore_signal(
            barrier, inc=1, device_id=(lax.rem(tab + step, 4), blk), device_id_type=MESH
        )
    pl.semaphore_wait(barrier, 10)

    def context_copy(which):
        return remote(
            dctx_ref.at[which // 4, lax.rem(which, 4)],
            dov.at[blk],
            dsend_sem.at[which],
            drecv_sem.at[blk],
            (tab, which),
        )

    def chip_at(step):
        mate = 2 * half + 1 - zl
        return jnp.where(
            step < 2,
            jnp.where(step == 0, chip, mate),
            jnp.where(step == 2, 2 - half, 3 - 3 * half),
        )

    context_copy(2 * chip + 1 - core).start()
    for step in range(1, 4):
        for side in (core, 1 - core):
            context_copy(2 * chip_at(step) + side).start()

    def stage_copy(stage, unit, order=None):
        send, done = ssend_sem.at[stage, unit], srecv_sem.at[stage, unit]
        if stage == 0:
            src = parts_ref.at[unit, :, :, :, :, 1 - core]
            return remote(src, sum0.at[unit], send, done, (tab, 2 * chip + 1 - core))
        if stage == 1 and order == 0:
            return remote(
                sum0.at[unit, :, 1 - x], sum1.at[unit], send, done, (2 * y + 1 - x, blk)
            )
        if stage == 1:
            return remote(
                sum0.at[unit, 1 - y], sum1.at[unit], send, done, (2 * (1 - y) + x, blk)
            )
        if stage == 2 and order == 0:
            return remote(
                sum1.at[unit, 1 - y], sum2.at[unit], send, done, (2 * (1 - y) + x, blk)
            )
        if stage == 2:
            return remote(
                sum1.at[unit, 1 - x], sum2.at[unit], send, done, (2 * y + 1 - x, blk)
            )
        if stage == 3:
            src, there = sum2.at[unit, :, 1 - zl], 2 * zh + 1 - zl
            return remote(src, sum3.at[unit], send, done, (tab, 2 * there + core))
        src, there = sum3.at[unit, 1 - zh], 2 * (1 - zh) + zl
        return remote(src, sum4.at[unit], send, done, (tab, 2 * there + core))

    def both(act):
        pl.when(core == 0)(functools.partial(act, 0))
        pl.when(core == 1)(functools.partial(act, 1))

    def mine_copy(unit):
        slot = lax.rem(unit, 2)
        return pltpu.make_async_copy(
            parts_ref.at[unit, :, :, :, :, core], mine.at[slot], mine_sem.at[slot]
        )

    def finish(unit):
        done = sum4[unit].astype(f32) + sum3[unit, zh].astype(f32)
        top, low = done[: done.shape[0] // 2], done[done.shape[0] // 2 :]
        each, cut = top.shape

        @pl.when(unit < 4)
        def _():
            at = pl.ds(pl.multiple_of(unit * each, each), each)
            wdown_ref[at, :cut] = top
            wdown_ref[at, cut:] = low

        @pl.when(jnp.logical_and(unit >= 4, unit < 8))
        def _():
            at = pl.multiple_of((unit - 4) * 2 * cut, 2 * cut)
            wup_ref[:, pl.ds(at, cut)] = top
            wup_ref[:, pl.ds(pl.multiple_of(at + cut, cut), cut)] = low

        @pl.when(unit == 8)
        def _():
            wout_ref[:, :cut] = top
            wout_ref[:, cut:] = low

    def advance(stage, unit):
        if stage == 0:
            landed(sum0.at[unit], srecv_sem.at[0, unit])
            mine_copy(unit).wait()
            slot = lax.rem(unit, 2)
            for a in range(2):
                for b in range(2):
                    sum0[unit, a, b] = sum0[unit, a, b] + mine[slot, a, b]

            @pl.when(unit + 2 < UNITS)
            def _():
                mine_copy(unit + 2).start()

            both(lambda order: stage_copy(1, unit, order).start())
        elif stage == 1:
            landed(sum1.at[unit], srecv_sem.at[1, unit])

            def act(order):
                own = sum0[unit, :, x] if order == 0 else sum0[unit, y]
                sum1[unit] = sum1[unit] + own
                stage_copy(2, unit, order).start()

            both(act)
        elif stage == 2:
            landed(sum2.at[unit], srecv_sem.at[2, unit])

            def act(order):
                sum2[unit] = sum2[unit] + sum1[unit, y if order == 0 else x]

            both(act)
            stage_copy(3, unit).start()
        elif stage == 3:
            landed(sum3.at[unit], srecv_sem.at[3, unit])
            sum3[unit] = sum3[unit] + sum2[unit, :, zl]
            stage_copy(4, unit).start()
        else:
            landed(sum4.at[unit], srecv_sem.at[4, unit])
            finish(unit)

    def tick(now):
        for stage in range(STAGES):
            unit = now - PHASE[stage]
            due = (unit >= 0) & (unit < UNITS)
            pl.when(due)(functools.partial(advance, stage, unit))

    for unit in range(UNITS):
        stage_copy(0, unit).start()
    for unit in range(2):
        mine_copy(unit).start()

    def tab_copy(src, dst, sem_at, step):
        there = lax.rem(tab + step, 4)
        return remote(
            src(there), dst(tab), tsend_sem.at[sem_at, there], trecv_sem.at[sem_at, tab], (there, blk)
        )

    def line_copy(src, dst, sem_at, step):
        there = lax.rem(blk + step, 8)
        return remote(
            src(there), dst(blk), lsend_sem.at[sem_at, there], lrecv_sem.at[sem_at, blk], (tab, there)
        )

    def small_tab(step):
        return tab_copy(lambda t: small_ref, lambda t: small_in.at[t], heads, step)

    def small_blk(step):
        return line_copy(lambda b: small_line, lambda b: small_line_in.at[b], heads, step)

    def slab_tab(head, step):
        return tab_copy(
            lambda t: slab.at[head, t], lambda t: slab_in.at[head, t], head, step
        )

    def slab_blk(head, step):
        return line_copy(
            lambda b: line.at[head, b], lambda b: line_in.at[head, b], head, step
        )

    for step in range(1, 4):
        small_tab(step).start()

    def pass_small():
        total = small_ref[...]
        for step in range(1, 4):
            there = lax.rem(tab + step, 4)
            landed(small_in.at[there], trecv_sem.at[heads, there])
            total += small_in[there]
        small_line[...] = total
        for step in range(1, 8):
            small_blk(step).start()

    def make_slab(head):
        flat = dqkv[head]
        grad = jnp.dot(toktv[...], flat, preferred_element_type=f32)
        sums = jnp.sum(flat.astype(f32), axis=0, keepdims=True)
        sums = jnp.broadcast_to(sums, (8, 3 * HD))
        grad = grad.reshape(4, 8, width // 32, 3 * HD)
        for t in range(4):
            for b in range(8):
                slab[head, t, b] = jnp.concatenate([grad[t, b], sums], axis=0).astype(bf16)
        for step in range(1, 4):
            slab_tab(head, step).start()

    def pass_slab(head):
        total = slab[head, tab].astype(f32)
        for step in range(1, 4):
            there = lax.rem(tab + step, 4)
            landed(slab_in.at[head, there], trecv_sem.at[head, there])
            total += slab_in[head, there].astype(f32)
        line[head] = total.astype(bf16)
        line_in[head, blk] = line[head, blk]
        for step in range(1, 8):
            slab_blk(head, step).start()

    for copy in loads[:4]:
        copy.wait()
    for head in range(heads):
        ktv[head] = qkvv[heads + head].T

    def gradient_copies(head, which, own):
        slot = group * heads + head
        pairs = (
            (qsend.at[head, which], arrive_q.at[slot]),
            (kvsend.at[head, which], arrive_kv.at[slot]),
        )
        for kind, (src, dst) in enumerate(pairs):
            if own:
                yield pltpu.make_async_copy(src, dst, grecv_sem.at[kind, slot])
            else:
                yield remote(
                    src,
                    dst,
                    gsend_sem.at[kind, head, which],
                    grecv_sem.at[kind, slot],
                    (tab, 4 * half + which),
                )

    def send_gradient(kind, head, which):
        @pl.when(which == group)
        def _():
            list(gradient_copies(head, which, True))[kind].start()

        @pl.when(which != group)
        def _():
            list(gradient_copies(head, which, False))[kind].start()

    def absorb(head):
        for at in range(GROUPS):
            slot = at * heads + head
            landed(arrive_q.at[slot], grecv_sem.at[0, slot])
            landed(arrive_kv.at[slot], grecv_sem.at[1, slot])
        for pair in range(GROUPS // 2):
            left, right = 2 * pair * heads + head, (2 * pair + 1) * heads + head
            lanes = slice(pair * LANES, (pair + 1) * LANES)
            for side in range(2):
                cut = slice(side * HD, (side + 1) * HD)
                joined[side * rows : (side + 1) * rows, lanes] = jnp.concatenate(
                    [arrive_q[left][:, cut], arrive_q[right][:, cut]], axis=1
                )
                lanes_kv = slice((2 * side + 2 + pair) * LANES, (2 * side + 3 + pair) * LANES)
                joined[:, lanes_kv] = jnp.concatenate(
                    [arrive_kv[left][:, cut], arrive_kv[right][:, cut]], axis=1
                )

    def give_back(side, own):
        src, dst = xsend.at[side], back.at[half]
        if own:
            return pltpu.make_async_copy(src, dst, xrecv_sem.at[half])
        return remote(src, dst, xsend_sem.at[side], xrecv_sem.at[half], (tab, 2 * group + side))

    def is_own(side):
        return jnp.logical_and(chip == group, core == side)

    @pl.loop(0, heads * TURNS)
    def _(turn):
        head, step = turn // TURNS, lax.rem(turn, TURNS)
        which = chip_at(step)
        first = pl.multiple_of(which * tile, tile)

        @pl.when(head == 0)
        def _():
            for side in range(2):
                block = 2 * which + side

                @pl.when(block != blk)
                def _():
                    landed(dov.at[block], drecv_sem.at[block])

                dos = unfold(dov[block])
                for at in range(heads):
                    do = dos[:, at * HD : (at + 1) * HD]
                    doh[at, pl.ds(first + side * rows, rows)] = do
                    ot = otv[which, at * HD : (at + 1) * HD, side * rows : (side + 1) * rows]
                    deltas[at, which, :1, side * rows : (side + 1) * rows] = jnp.sum(
                        ot * do.astype(f32).T, axis=0, keepdims=True
                    )

        @pl.when(step == 0)
        def _():
            dkv[...] = jnp.zeros_like(dkv)
            dvv[...] = jnp.zeros_like(dvv)

        tick(turn)

        q_full = qkvv[head, pl.ds(first, tile)]
        q = q_full[:, :HD]
        do = doh[head, pl.ds(first, tile)]
        delta = deltas[head, which, :1]
        lse = lsev[which, pl.ds(head, 1)]
        dqt = jnp.zeros((LANES, tile), f32)
        for at in range(blocks * rows // piece):
            cut = pl.ds(at * piece, piece)
            st = times_t(qkvv[heads + head, cut], q_full)
            pt = jnp.exp2(st * scale - lse)
            dpt = times_t(qkvv[2 * heads + head, cut][:, :HD], do)
            dst = (pt * (dpt - delta)).astype(bf16)
            dvv[cut] += jnp.dot(pt.astype(bf16), do, preferred_element_type=f32)
            dkv[cut] += jnp.dot(dst, q, preferred_element_type=f32)
            dqt += jnp.dot(ktv[head, :, cut], dst, preferred_element_type=f32)
        dq = (dqt[:HD].T * shrink).astype(bf16)
        dqv[pl.ds(first, tile)] = dq
        qsend[head, which] = jnp.concatenate([dq[:rows], dq[rows:]], axis=1)
        send_gradient(0, head, which)

        @pl.when(step == TURNS - 1)
        def _():
            @pl.loop(0, 4)
            def _(at):
                there = lax.rem(group + 1 + at, 4)
                cut = pl.ds(pl.multiple_of(there * tile, tile), tile)
                pair = jnp.concatenate([dkv[cut] * shrink, dvv[cut]], axis=1).astype(bf16)
                kvsend[head, there] = pair
                send_gradient(1, head, there)
                dqkv[head, cut] = jnp.concatenate([pair, dqv[cut]], axis=1)

        @pl.when(turn == TURNS)
        def _():
            pass_small()

    loads[5].wait()
    for head in range(heads - 1):
        absorb(head)
        product = times_t(joined[...], wv[head])
        xacc[...] = product if head == 0 else xacc[...] + product
    tick(heads * TURNS)
    absorb(heads - 1)
    for side in range(2):
        at = pl.ds(side * rows, rows)
        xsend[side] = (xacc[at] + times_t(joined[at], wv[heads - 1])).astype(bf16)
        pl.when(is_own(side))(give_back(side, True).start)
        pl.when(jnp.logical_not(is_own(side)))(give_back(side, False).start)

    loads[4].wait()
    for head in range(heads):
        make_slab(head)
        tick(heads * TURNS + 1 + head)
    for head in range(heads):
        pass_slab(head)
    for now in range(heads * TURNS + 1 + heads, PHASE[-1] + UNITS):
        tick(now)
    loads[6].wait()

    def slabs_in(head, at):
        return [line_in[head, half_at * GROUPS + at].astype(f32) for half_at in range(2)]

    for head in range(heads):
        for step in range(1, 8):
            there = lax.rem(blk + step, 8)
            landed(line_in.at[head, there], lrecv_sem.at[head, there])
    total = small_line[...]
    for step in range(1, 8):
        there = lax.rem(blk + step, 8)
        landed(small_line_in.at[there], lrecv_sem.at[heads, there])
        total += small_line_in[there]
    own = [
        functools.reduce(jnp.add, slabs_in(at % heads, at // heads))
        for at in range(GROUPS * heads)
    ]
    each = width // 32
    bias = []
    for part in range(3):
        cut = slice((part + 2) % 3 * HD, (part + 2) % 3 * HD + HD)
        for pair in range(GROUPS * heads // 2):
            both_heads = jnp.concatenate([own[2 * pair][:, cut], own[2 * pair + 1][:, cut]], axis=1)
            lanes = slice(part * width + pair * LANES, part * width + (pair + 1) * LANES)
            wqkv_ref[:, lanes] = both_heads[:each]
            bias.append(both_heads[each:])
    pairs = GROUPS * heads // 2
    bias_q = jnp.concatenate(bias[:pairs], axis=1)
    bias_v = jnp.concatenate(bias[2 * pairs :], axis=1)
    bias = jnp.where(tab < 2, bias_q, bias_v)

    row = lax.broadcasted_iota(jnp.int32, (width, LANES), 0)
    lane = lax.broadcasted_iota(jnp.int32, (width, LANES), 1)

    def take(block, first, count):
        chosen = jnp.where((row == first + lane) & (lane < count), 1.0, 0.0)
        return jnp.dot(
            block, chosen, preferred_element_type=f32, precision=lax.Precision.HIGHEST
        )

    index = 8 * tab + blk
    little_ref[0:8] = take(total[:8], each * index, each)
    at_row = lax.broadcasted_iota(jnp.int32, total.shape, 0) == 6 + tab
    wide = jnp.sum(jnp.where(at_row, total, 0.0), axis=0, keepdims=True)
    little_ref[6:7] = take(jnp.broadcast_to(wide, (8, width)), 4 * each * blk, 4 * each)[:1]
    little_ref[7:8] = take(bias, 2 * each * lax.rem(index, 16), 2 * each)[:1]

    for table in range(2):
        landed(back.at[table], xrecv_sem.at[table])
        tgrad_ref[table] = (
            prev[pl.ds(table * rows, rows)] + back[table].astype(f32)
        ).astype(bf16)

    for side in range(2):
        pl.when(jnp.logical_not(is_own(side)))(give_back(side, False).wait_send)

    @pl.loop(0, heads)
    def _(head):
        @pl.loop(1, 4)
        def _(step):
            for copy in gradient_copies(head, lax.rem(group + step, 4), False):
                copy.wait_send()

    for step in range(1, 8):
        context_copy(lax.rem(blk + step, 8)).wait_send()
        small_blk(step).wait_send()
        for head in range(heads):
            slab_blk(head, step).wait_send()
    for step in range(1, 4):
        small_tab(step).wait_send()
        for head in range(heads):
            slab_tab(head, step).wait_send()

    @pl.loop(0, UNITS)
    def _(unit):
        for stage in range(STAGES):
            if stage in (1, 2):
                both(lambda order, stage=stage: stage_copy(stage, unit, order).wait_send())
            else:
                stage_copy(stage, unit).wait_send()


def attend_back(dctx, qkv, ot, lse, full_t, by_head, pre, small, parts, heads):
    width, total = full_t.shape
    blocks = 8
    rows = total // blocks
    each, ff = width // 32, 4 * width
    any_space = pl.BlockSpec(memory_space=pl.ANY)
    vmem = pl.BlockSpec(memory_space=pltpu.VMEM)
    bf16, f32 = jnp.bfloat16, jnp.float32
    dma = pltpu.SemaphoreType.DMA
    unit = parts.shape[2:]
    parts = parts.reshape(UNITS, 2, 2, 2, 2, 2, *unit)
    shape = jax.ShapeDtypeStruct
    return pl.pallas_call(
        functools.partial(attend_back_kernel, heads),
        name="attend_back",
        out_shape=(
            shape((2, rows, width), bf16),
            shape((each, 3 * width), f32),
            shape((each, width), f32),
            shape((each, ff), f32),
            shape((4 * each, width), f32),
            shape((8, LANES), f32),
        ),
        in_specs=[any_space] * 8 + [vmem],
        out_specs=(vmem,) * 6,
        scratch_shapes=[
            pltpu.VMEM((blocks, rows // 2, 2 * heads * HD), bf16),
            pltpu.VMEM((heads, total, HD), bf16),
            pltpu.VMEM((heads, 4, 8, 2 * rows), f32),
            pltpu.VMEM((3 * heads, total, LANES), bf16),
            pltpu.VMEM(ot.shape, f32),
            pltpu.VMEM(lse.shape, f32),
            pltpu.VMEM((width, total), bf16),
            pltpu.VMEM(by_head.shape, bf16),
            pltpu.VMEM((2 * rows, width), f32),
            pltpu.VMEM((heads, LANES, total), bf16),
            pltpu.VMEM((total, HD), bf16),
            pltpu.VMEM((total, HD), f32),
            pltpu.VMEM((total, HD), f32),
            pltpu.VMEM((heads, total, 3 * HD), bf16),
            pltpu.VMEM((heads, 4, rows, 2 * HD), bf16),
            pltpu.VMEM((heads, 4, 2 * rows, 2 * HD), bf16),
            pltpu.VMEM((GROUPS * heads, rows, 2 * HD), bf16),
            pltpu.VMEM((GROUPS * heads, 2 * rows, 2 * HD), bf16),
            pltpu.VMEM((2 * rows, width), bf16),
            pltpu.VMEM((2 * rows, width), f32),
            pltpu.VMEM((2, rows, width), bf16),
            pltpu.VMEM((2, rows, width), bf16),
            pltpu.VMEM((2, 2, 2, 2, 2, *unit), bf16),
            pltpu.VMEM((UNITS, 2, 2, 2, 2, *unit), bf16),
            pltpu.VMEM((UNITS, 2, 2, 2, *unit), bf16),
            pltpu.VMEM((UNITS, 2, 2, *unit), bf16),
            pltpu.VMEM((UNITS, 2, *unit), bf16),
            pltpu.VMEM((UNITS, *unit), bf16),
            pltpu.VMEM((heads, 4, 8, each + 8, 3 * HD), bf16),
            pltpu.VMEM((heads, 4, 8, each + 8, 3 * HD), bf16),
            pltpu.VMEM((heads, 8, each + 8, 3 * HD), bf16),
            pltpu.VMEM((heads, 8, each + 8, 3 * HD), bf16),
            pltpu.VMEM((4, 16, width), f32),
            pltpu.VMEM((16, width), f32),
            pltpu.VMEM((8, 16, width), f32),
            dma((blocks,)),
            dma((blocks,)),
            dma((2, heads, 4)),
            dma((2, GROUPS * heads)),
            dma((2,)),
            dma((2,)),
            dma((STAGES, UNITS)),
            dma((STAGES, UNITS)),
            dma((heads + 1, 4)),
            dma((heads + 1, 4)),
            dma((heads + 1, 8)),
            dma((heads + 1, 8)),
            dma((7,)),
            dma((2,)),
        ],
        compiler_params=pltpu.CompilerParams(
            collective_id=2, has_side_effects=True, vmem_limit_bytes=62 << 20
        ),
    )(dctx, qkv, ot, lse, full_t, by_head, pre, parts, small)


def finish_kernel(whole, *refs):
    little_ref, outs = refs[whole], refs[whole + 1 :]
    for src, dst in zip(refs[:whole], outs[:whole]):
        dst[...] = src[...]
    for at, dst in enumerate(outs[whole:]):
        dst[...] = little_ref[at, : dst.shape[0]]


def finish(arrays, little, counts):
    vmem = pl.BlockSpec(memory_space=pltpu.VMEM)
    shapes = [jax.ShapeDtypeStruct(a.shape, a.dtype) for a in arrays]
    shapes += [jax.ShapeDtypeStruct((count,), jnp.float32) for count in counts]
    return pl.pallas_call(
        functools.partial(finish_kernel, len(arrays)),
        name="finish",
        out_shape=tuple(shapes),
        in_specs=[vmem] * (len(arrays) + 1),
        out_specs=(vmem,) * len(shapes),
    )(*arrays, little)


def halves(grad):
    cut = grad.shape[2] // 2
    return jnp.concatenate([grad[:, :, :cut], grad[:, :, cut:]], axis=1)


def norm_parts(inputs):
    centred = inputs - jnp.mean(inputs, axis=-1, keepdims=True)
    inverse = lax.rsqrt(jnp.mean(centred * centred, axis=-1, keepdims=True) + EPSILON)
    return centred * inverse, inverse


def norm_back(grad, normed, inverse, gain):
    e = grad * gain
    return inverse * (
        e
        - jnp.mean(e, axis=-1, keepdims=True)
        - normed * jnp.mean(e * normed, axis=-1, keepdims=True)
    )


def column_sum(block):
    return jnp.sum(block.astype(jnp.float32), axis=0, keepdims=True)


def ffn_kernel(
    tok_ref,
    ctx_ref,
    cot_ref,
    par_ref,
    outw_ref,
    upw_hbm,
    downw_hbm,
    out_ref,
    dctx_ref,
    pre_ref,
    small_ref,
    parts_ref,
    upw,
    downw,
    hid,
    hlow,
    hlow_t,
    norm1,
    slopes,
    active_t,
    pre2,
    gbranch,
    ghid,
    stage_d,
    stage_u,
    load_sem,
    stage_sem,
):
    f32, bf16 = jnp.float32, jnp.bfloat16
    tables, groups, rows, cols = ctx_ref.shape
    rows, cols = 2 * rows, cols // 2
    width = tok_ref.shape[1]
    chunks = active_t.shape[0]
    loads = (
        pltpu.make_async_copy(upw_hbm, upw, load_sem.at[0]),
        pltpu.make_async_copy(downw_hbm, downw, load_sem.at[1]),
    )
    for copy in loads:
        copy.start()

    def par(at):
        return par_ref[at : at + 1]

    inverse1 = []
    for table in range(tables):
        cut = pl.ds(table * rows, rows)
        pre1 = tok_ref[cut].astype(f32) + par(0)
        for group in range(groups):
            pre1 += jnp.dot(
                unfold(ctx_ref[table, group]),
                outw_ref[group * cols : (group + 1) * cols],
                preferred_element_type=f32,
            )
        normed, inverse = norm_parts(pre1)
        inverse1.append(inverse)
        hidden = normed * par(1) + par(2)
        low = hidden.astype(bf16)
        norm1[cut] = normed
        hid[cut] = hidden
        hlow[cut] = low
        hlow_t[:, cut] = low.T

    pre2[...] = hid[...] + par(3)
    for copy in loads:
        copy.wait()

    @pl.loop(0, chunks)
    def _(at):
        cut = pl.ds(pl.multiple_of(at * width, width), width)
        upper = jnp.dot(
            hlow[...], upw[:, cut], preferred_element_type=f32
        ) + par_ref[pl.ds(24 + at, 1)]
        cdf = 0.5 + 0.5 * lax.erf(upper * math.sqrt(0.5))
        act = (upper * cdf).astype(bf16)
        slopes[at] = cdf + upper * jnp.exp(-0.5 * upper * upper) * (1 / math.sqrt(2 * math.pi))
        active_t[at] = act.T
        pre2[...] += jnp.dot(act, downw[cut], preferred_element_type=f32)

    normed, inverse = norm_parts(pre2[...])
    out_ref[...] = (normed * par(4) + par(5)).astype(bf16)
    grad = cot_ref[...].astype(f32)
    small_ref[4:5] = column_sum(grad * normed)
    small_ref[5:6] = column_sum(grad)
    gpre2 = norm_back(grad, normed, inverse, par(4))
    ghid[...] = gpre2
    low = gpre2.astype(bf16)
    gbranch[...] = low
    small_ref[3:4] = column_sum(low)

    each = width // 32

    def down_copies(at):
        return [
            pltpu.make_async_copy(
                stage_d.at[part],
                parts_ref.at[part, pl.ds(8 * at, 8)],
                stage_sem.at[part],
            )
            for part in range(4)
        ]

    def up_copy(at):
        return pltpu.make_async_copy(stage_u, parts_ref.at[4 + at], stage_sem.at[4])

    @pl.loop(0, chunks)
    def _(at):
        cut = pl.ds(pl.multiple_of(at * width, width), width)
        wdown = jnp.dot(active_t[at], gbranch[...], preferred_element_type=f32)
        wdown = wdown.reshape(8, 4, each, width)

        @pl.when(at > 0)
        def _():
            for copy in down_copies(at - 1):
                copy.wait()
            up_copy(at - 1).wait()

        for part in range(4):
            stage_d[part] = halves(wdown[:, part]).astype(bf16)
        for copy in down_copies(at):
            copy.start()
        gact = times_t(gbranch[...], downw[cut])
        gup = (gact * slopes[at]).astype(bf16)
        small_ref[pl.ds(6 + at, 1)] = column_sum(gup)
        ghid[...] += times_t(gup, upw[:, cut])
        wup = jnp.dot(hlow_t[...], gup, preferred_element_type=f32)
        stage_u[...] = halves(wup.reshape(32, each, width)).astype(bf16)
        up_copy(at).start()

    for copy in down_copies(chunks - 1):
        copy.wait()
    up_copy(chunks - 1).wait()
    small = [0.0, 0.0, 0.0]
    lows = []
    for table in range(tables):
        cut = pl.ds(table * rows, rows)
        grad, normed = ghid[cut], norm1[cut]
        small[1] += column_sum(grad * normed)
        small[2] += column_sum(grad)
        gpre1 = norm_back(grad, normed, inverse1[table], par(1))
        pre_ref[cut] = gpre1
        low = gpre1.astype(bf16)
        small[0] += column_sum(low)
        lows.append(low)
        for group in range(groups):
            dctx_ref[table, group] = fold(
                times_t(low, outw_ref[group * cols : (group + 1) * cols]).astype(bf16)
            )
    for at in range(3):
        small_ref[at : at + 1] = small[at]
    small_ref[10:] = jnp.zeros((6, width), f32)
    for group in range(groups):
        wout = 0.0
        for table in range(tables):
            wout += jnp.dot(
                unfold(ctx_ref[table, group]).T, lows[table], preferred_element_type=f32
            )
        stage_u[group * 8 : (group + 1) * 8] = halves(wout.reshape(8, each, width)).astype(bf16)
    last = pltpu.make_async_copy(stage_u, parts_ref.at[8], stage_sem.at[4])
    last.start()
    last.wait()


def ffn(tokens, ctx, cotangent, params, out_weight, up_weight, down_weight):
    total, width = tokens.shape
    chunks = up_weight.shape[1] // width
    each = width // 32
    any_space = pl.BlockSpec(memory_space=pl.ANY)
    vmem = pl.BlockSpec(memory_space=pltpu.VMEM)
    bf16, f32 = jnp.bfloat16, jnp.float32
    flops = 18 * total * width * chunks * width + 6 * total * width * width
    return pl.pallas_call(
        ffn_kernel,
        name="ffn",
        out_shape=(
            jax.ShapeDtypeStruct((total, width), bf16),
            jax.ShapeDtypeStruct(ctx.shape, bf16),
            jax.ShapeDtypeStruct((total, width), f32),
            jax.ShapeDtypeStruct((16, width), f32),
            jax.ShapeDtypeStruct((9, 32, 2 * each, width // 2), bf16),
        ),
        in_specs=[vmem, vmem, vmem, vmem, vmem, any_space, any_space],
        out_specs=(vmem, vmem, vmem, vmem, any_space),
        scratch_shapes=[
            pltpu.VMEM(up_weight.shape, bf16),
            pltpu.VMEM(down_weight.shape, bf16),
            pltpu.VMEM((total, width), f32),
            pltpu.VMEM((total, width), bf16),
            pltpu.VMEM((width, total), bf16),
            pltpu.VMEM((total, width), f32),
            pltpu.VMEM((chunks, total, width), f32),
            pltpu.VMEM((chunks, width, total), bf16),
            pltpu.VMEM((total, width), f32),
            pltpu.VMEM((total, width), bf16),
            pltpu.VMEM((total, width), f32),
            pltpu.VMEM((4, 8, 2 * each, width // 2), bf16),
            pltpu.VMEM((32, 2 * each, width // 2), bf16),
            pltpu.SemaphoreType.DMA((2,)),
            pltpu.SemaphoreType.DMA((5,)),
        ],
        compiler_params=pltpu.CompilerParams(vmem_limit_bytes=60 << 20),
        cost_estimate=pl.CostEstimate(
            flops=flops, bytes_accessed=40 << 20, transcendentals=total * width * chunks
        ),
    )(tokens, ctx, cotangent, params, out_weight, up_weight, down_weight)


def scatter_sum(grad):
    return lax.psum_scatter(
        lax.psum_scatter(
            grad.astype(jnp.bfloat16), "tab", scatter_dimension=0, tiled=True
        ),
        "blk",
        scatter_dimension=0,
        tiled=True,
    ).astype(jnp.float32)


def shards_direct(
    tokens,
    lengths,
    qkv_weight,
    qkv_bias,
    out_weight,
    out_bias,
    attn_gain,
    attn_shift,
    up_weight,
    up_bias,
    down_weight,
    down_bias,
    ffn_gain,
    ffn_shift,
    cotangent,
):
    tables, rows, width = tokens.shape
    f32 = jnp.float32
    heads = width // HD // GROUPS
    flat_tokens = tokens.reshape(tables * rows, width)
    row = lax.broadcasted_iota(jnp.int32, (32, width), 0)
    params = jnp.zeros((32, width), jnp.bfloat16)
    spans = [
        (at, at + 1, vector)
        for at, vector in enumerate(
            (out_bias, attn_gain, attn_shift, down_bias, ffn_gain, ffn_shift)
        )
    ]
    spans += [(8, 16, qkv_bias[:width]), (16, 24, qkv_bias[width:])]
    spans += [
        (24 + at, 25 + at, up_bias[at * width : (at + 1) * width])
        for at in range(up_bias.shape[0] // width)
    ]
    for first, last, vector in spans:
        params = jnp.where((row >= first) & (row < last), vector[None], params)

    params = params.astype(f32)
    ctx, full_t, qkv, ot, lse, by_head = attend(tokens, lengths, params, qkv_weight, heads)
    layer_out, dctx, pre, small, parts = ffn(
        flat_tokens,
        ctx,
        cotangent.reshape(tables * rows, width),
        params,
        out_weight,
        up_weight,
        down_weight,
    )
    *whole, little = attend_back(
        dctx, qkv, ot, lse, full_t, by_head, pre, small, parts, heads
    )
    each = width // 32
    (
        token_grad,
        wgrad_qkv,
        wgrad_out,
        wgrad_up,
        wgrad_down,
        bgrad_out,
        ggrad_attn,
        sgrad_attn,
        bgrad_down,
        ggrad_ffn,
        sgrad_ffn,
        bgrad_up,
        bgrad_qkv,
    ) = finish(whole, little, [each] * 6 + [4 * each, 2 * each])
    return (
        layer_out.reshape(tokens.shape),
        token_grad,
        wgrad_qkv,
        bgrad_qkv,
        wgrad_out,
        bgrad_out,
        ggrad_attn,
        sgrad_attn,
        wgrad_up,
        bgrad_up,
        wgrad_down,
        bgrad_down,
        ggrad_ffn,
        sgrad_ffn,
    )


def solution(mesh):
    in_specs = (
        P("tab", "blk", None),
        P("tab"),
        P(),
        P(),
        P(),
        P(),
        P(),
        P(),
        P(),
        P(),
        P(),
        P(),
        P(),
        P(),
        P("tab", "blk", None),
    )
    out_specs = (
        P("tab", "blk", None),
        P("tab", "blk", None),
        P(("tab", "blk"), None),
        P(("tab", "blk")),
        P(("tab", "blk"), None),
        P(("tab", "blk")),
        P(("tab", "blk")),
        P(("tab", "blk")),
        P(("tab", "blk"), None),
        P(("tab", "blk")),
        P(("tab", "blk"), None),
        P(("tab", "blk")),
        P(("tab", "blk")),
        P(("tab", "blk")),
    )
    tab_count, blk_count = mesh.shape["tab"], mesh.shape["blk"]

    def pick(*operands):
        table_count = operands[0].shape[0] // tab_count
        head_count = operands[0].shape[2] // HD
        direct = table_count == 2 and blk_count == 8 and tab_count == 4 and head_count % 4 == 0
        body = shards_direct if direct else shards_ring
        return jax.shard_map(
            body, mesh=mesh, in_specs=in_specs, out_specs=out_specs, check_vma=False
        )(*operands)

    return pick
```

```python
import functools
import math

import jax
import jax.numpy as jnp
from jax import lax
from jax.experimental import pallas as pl
from jax.experimental.pallas import tpu as pltpu
from jax.sharding import PartitionSpec as P

HD = 64


EPSILON = 1e-05
NEGATIVE = -1e30


def from_behind(block, axis, distance):
    devices = range(lax.axis_size(axis))
    route = [((i - distance) % len(devices), i) for i in devices]
    return lax.ppermute(block, axis, route)


def norm_rows(inputs, gains, shifts):
    row_mean = jnp.mean(inputs, axis=-1, keepdims=True)
    centred = inputs - row_mean
    row_var = jnp.mean(centred * centred, axis=-1, keepdims=True)
    return centred * lax.rsqrt(row_var + EPSILON) * gains + shifts


def gelu_exact(inputs):
    return jax.nn.gelu(inputs, approximate=False)


def times_back(left, right):
    return lax.dot_general(
        left, right, (((1,), (1,)), ((), ())), preferred_element_type=jnp.float32
    )


def over_rows(left, right):
    return lax.dot_general(
        left, right, (((0,), (0,)), ((), ())), preferred_element_type=jnp.float32
    )


def shards_ring(
    tokens,
    lengths,
    qkv_weight,
    qkv_bias,
    out_weight,
    out_bias,
    attn_gain,
    attn_shift,
    up_weight,
    up_bias,
    down_weight,
    down_bias,
    ffn_gain,
    ffn_shift,
    cotangent,
):
    table_count, row_count, model_width = tokens.shape
    head_count = model_width // HD
    cycle_size = lax.axis_size("blk")
    cycle_place = lax.axis_index("blk")
    score_scale = HD ** (-0.5)
    flat_tokens = tokens.reshape(table_count * row_count, model_width)
    bias_full = jnp.concatenate(
        [
            qkv_bias[:model_width].astype(jnp.float32),
            jnp.zeros((model_width,), jnp.float32),
            qkv_bias[model_width:].astype(jnp.float32),
        ]
    )
    qkv_low = (
        jnp.dot(flat_tokens, qkv_weight, preferred_element_type=jnp.float32) + bias_full
    ).astype(jnp.bfloat16)
    queries = qkv_low[:, :model_width].reshape(table_count, row_count, head_count, HD)
    key_values = qkv_low[:, model_width:].reshape(table_count, row_count, 2 * model_width)

    def key_mask(first_row, key_count):
        positions = first_row + jnp.arange(key_count, dtype=jnp.int32)
        return (positions[None, :] < lengths[:, None])[:, None, None, :]

    def split_pair(pair_block):
        key_count = pair_block.shape[1]
        keys_part = pair_block[:, :, :model_width].reshape(table_count, key_count, head_count, HD)
        values_part = pair_block[:, :, model_width:].reshape(table_count, key_count, head_count, HD)
        return (keys_part, values_part)

    pair_block = lax.all_gather(key_values, "blk", axis=1, tiled=True)
    running_max = jnp.full((table_count, row_count, head_count), NEGATIVE, jnp.float32)
    keys_part, values_part = split_pair(pair_block)
    is_valid = key_mask(jnp.int32(0), pair_block.shape[1])
    raw_scores = jnp.einsum(
        "trhd,tkhd->trhk", queries, keys_part, preferred_element_type=jnp.float32
    )
    scores = jnp.where(is_valid, raw_scores * score_scale, NEGATIVE)
    peak_new = jnp.maximum(running_max, jnp.max(scores, axis=-1))
    exponent = jnp.where(is_valid, jnp.exp(scores - peak_new[..., None]), 0.0)
    running_sum = jnp.sum(exponent, axis=-1)
    weighted = jnp.einsum(
        "trhk,tkhd->trhd",
        exponent.astype(jnp.bfloat16),
        values_part,
        preferred_element_type=jnp.float32,
    )
    running_max, running_sum, weighted = (peak_new, running_sum, weighted)
    context = weighted / running_sum[..., None]
    log_total = running_max + jnp.log(running_sum)
    context_low = context.reshape(table_count * row_count, model_width).astype(jnp.bfloat16)
    attended = jnp.dot(
        context_low, out_weight, preferred_element_type=jnp.float32
    ) + out_bias.astype(jnp.float32)
    pre_one = flat_tokens.astype(jnp.float32) + attended
    gain_one = attn_gain.astype(jnp.float32)
    shift_one = attn_shift.astype(jnp.float32)
    hidden = norm_rows(pre_one, gain_one, shift_one)
    hidden_low = hidden.astype(jnp.bfloat16)
    upper = jnp.dot(hidden_low, up_weight, preferred_element_type=jnp.float32) + up_bias.astype(
        jnp.float32
    )
    active = gelu_exact(upper).astype(jnp.bfloat16)
    pre_two = (
        hidden
        + jnp.dot(active, down_weight, preferred_element_type=jnp.float32)
        + down_bias.astype(jnp.float32)
    )
    gain_two = ffn_gain.astype(jnp.float32)
    shift_two = ffn_shift.astype(jnp.float32)
    layer_out = norm_rows(pre_two, gain_two, shift_two).astype(jnp.bfloat16).reshape(tokens.shape)
    grad_out = cotangent.reshape(table_count * row_count, model_width).astype(jnp.float32)
    _, norm_two_back = jax.vjp(norm_rows, pre_two, gain_two, shift_two)
    grad_pre_two, ggrad_ffn, sgrad_ffn = norm_two_back(grad_out)
    grad_branch = grad_pre_two.astype(jnp.bfloat16)
    wgrad_down = over_rows(active, grad_branch)
    bgrad_down = jnp.sum(grad_branch, axis=0, dtype=jnp.float32)
    grad_active = times_back(grad_branch, down_weight)
    _, gelu_back = jax.vjp(gelu_exact, upper)
    grad_upper = gelu_back(grad_active)[0].astype(jnp.bfloat16)
    wgrad_up = over_rows(hidden_low, grad_upper)
    bgrad_up = jnp.sum(grad_upper, axis=0, dtype=jnp.float32)
    grad_hidden = grad_pre_two + times_back(grad_upper, up_weight)
    _, norm_one_back = jax.vjp(norm_rows, pre_one, gain_one, shift_one)
    grad_pre_one, ggrad_attn, sgrad_attn = norm_one_back(grad_hidden)
    grad_attended = grad_pre_one.astype(jnp.bfloat16)
    wgrad_out = over_rows(context_low, grad_attended)
    bgrad_out = jnp.sum(grad_attended, axis=0, dtype=jnp.float32)
    grad_context = times_back(grad_attended, out_weight).astype(jnp.bfloat16)
    grad_heads = grad_context.reshape(table_count, row_count, head_count, HD)
    row_delta = jnp.sum(grad_heads.astype(jnp.float32) * context, axis=-1)

    def cycle_turn_step(cycle_turn, cycle_state):
        pair_now, pair_grads, grad_queries = cycle_state
        owner_index = (cycle_place - cycle_turn) % cycle_size
        keys_part, values_part = split_pair(pair_now)
        is_valid = key_mask(owner_index * row_count, row_count)
        raw_scores = jnp.einsum(
            "trhd,tkhd->trhk", queries, keys_part, preferred_element_type=jnp.float32
        )
        scores = jnp.where(is_valid, raw_scores * score_scale, NEGATIVE)
        probs = jnp.where(is_valid, jnp.exp(scores - log_total[..., None]), 0.0)
        grad_probs = jnp.einsum(
            "trhd,tkhd->trhk", grad_heads, values_part, preferred_element_type=jnp.float32
        )
        grad_raw = (probs * (grad_probs - row_delta[..., None]) * score_scale).astype(jnp.bfloat16)
        grad_queries = grad_queries + jnp.einsum(
            "trhk,tkhd->trhd", grad_raw, keys_part, preferred_element_type=jnp.float32
        )
        grad_keys = jnp.einsum(
            "trhk,trhd->tkhd", grad_raw, queries, preferred_element_type=jnp.float32
        )
        grad_values = jnp.einsum(
            "trhk,trhd->tkhd",
            probs.astype(jnp.bfloat16),
            grad_heads,
            preferred_element_type=jnp.float32,
        )
        pair_grads = pair_grads + jnp.concatenate(
            [
                grad_keys.reshape(table_count, row_count, model_width),
                grad_values.reshape(table_count, row_count, model_width),
            ],
            axis=-1,
        )
        pair_next = from_behind(pair_now, "blk", 1)
        grads_next = from_behind(pair_grads.astype(jnp.bfloat16), "blk", 1).astype(pair_grads.dtype)
        return (pair_next, grads_next, grad_queries)

    cycle_start = (
        key_values,
        jnp.zeros((table_count, row_count, 2 * model_width), jnp.float32),
        jnp.zeros((table_count, row_count, head_count, HD), jnp.float32),
    )
    _, pair_home, grad_queries = lax.fori_loop(0, cycle_size, cycle_turn_step, cycle_start)
    grad_qkv = jnp.concatenate(
        [
            grad_queries.reshape(table_count * row_count, model_width),
            pair_home.reshape(table_count * row_count, 2 * model_width),
        ],
        axis=-1,
    ).astype(jnp.bfloat16)
    wgrad_qkv = over_rows(flat_tokens, grad_qkv)
    column_sums = jnp.sum(grad_qkv, axis=0, dtype=jnp.float32)
    bgrad_qkv = jnp.concatenate([column_sums[:model_width], column_sums[2 * model_width :]])
    token_grad = (
        (grad_pre_one + times_back(grad_qkv, qkv_weight)).astype(jnp.bfloat16).reshape(tokens.shape)
    )
    (
        wgrad_qkv,
        bgrad_qkv,
        wgrad_out,
        bgrad_out,
        ggrad_attn,
        sgrad_attn,
        wgrad_up,
        bgrad_up,
        wgrad_down,
        bgrad_down,
        ggrad_ffn,
        sgrad_ffn,
    ) = (
        lax.psum_scatter(
            wgrad_qkv.astype(jnp.bfloat16), "tab", scatter_dimension=0, tiled=True
        ).astype(jnp.float32),
        lax.psum_scatter(
            bgrad_qkv.astype(jnp.bfloat16), "tab", scatter_dimension=0, tiled=True
        ).astype(jnp.float32),
        lax.psum_scatter(
            wgrad_out.astype(jnp.bfloat16), "tab", scatter_dimension=0, tiled=True
        ).astype(jnp.float32),
        lax.psum_scatter(
            bgrad_out.astype(jnp.bfloat16), "tab", scatter_dimension=0, tiled=True
        ).astype(jnp.float32),
        lax.psum_scatter(
            ggrad_attn.astype(jnp.bfloat16), "tab", scatter_dimension=0, tiled=True
        ).astype(jnp.float32),
        lax.psum_scatter(
            sgrad_attn.astype(jnp.bfloat16), "tab", scatter_dimension=0, tiled=True
        ).astype(jnp.float32),
        lax.psum_scatter(
            wgrad_up.astype(jnp.bfloat16), "tab", scatter_dimension=0, tiled=True
        ).astype(jnp.float32),
        lax.psum_scatter(
            bgrad_up.astype(jnp.bfloat16), "tab", scatter_dimension=0, tiled=True
        ).astype(jnp.float32),
        lax.psum_scatter(
            wgrad_down.astype(jnp.bfloat16), "tab", scatter_dimension=0, tiled=True
        ).astype(jnp.float32),
        lax.psum_scatter(
            bgrad_down.astype(jnp.bfloat16), "tab", scatter_dimension=0, tiled=True
        ).astype(jnp.float32),
        lax.psum_scatter(
            ggrad_ffn.astype(jnp.bfloat16), "tab", scatter_dimension=0, tiled=True
        ).astype(jnp.float32),
        lax.psum_scatter(
            sgrad_ffn.astype(jnp.bfloat16), "tab", scatter_dimension=0, tiled=True
        ).astype(jnp.float32),
    )
    (
        wgrad_qkv,
        bgrad_qkv,
        wgrad_out,
        bgrad_out,
        ggrad_attn,
        sgrad_attn,
        wgrad_up,
        bgrad_up,
        wgrad_down,
        bgrad_down,
        ggrad_ffn,
        sgrad_ffn,
    ) = (
        lax.psum_scatter(
            wgrad_qkv.astype(jnp.bfloat16), "blk", scatter_dimension=0, tiled=True
        ).astype(jnp.float32),
        lax.psum_scatter(
            bgrad_qkv.astype(jnp.bfloat16), "blk", scatter_dimension=0, tiled=True
        ).astype(jnp.float32),
        lax.psum_scatter(
            wgrad_out.astype(jnp.bfloat16), "blk", scatter_dimension=0, tiled=True
        ).astype(jnp.float32),
        lax.psum_scatter(
            bgrad_out.astype(jnp.bfloat16), "blk", scatter_dimension=0, tiled=True
        ).astype(jnp.float32),
        lax.psum_scatter(
            ggrad_attn.astype(jnp.bfloat16), "blk", scatter_dimension=0, tiled=True
        ).astype(jnp.float32),
        lax.psum_scatter(
            sgrad_attn.astype(jnp.bfloat16), "blk", scatter_dimension=0, tiled=True
        ).astype(jnp.float32),
        lax.psum_scatter(
            wgrad_up.astype(jnp.bfloat16), "blk", scatter_dimension=0, tiled=True
        ).astype(jnp.float32),
        lax.psum_scatter(
            bgrad_up.astype(jnp.bfloat16), "blk", scatter_dimension=0, tiled=True
        ).astype(jnp.float32),
        lax.psum_scatter(
            wgrad_down.astype(jnp.bfloat16), "blk", scatter_dimension=0, tiled=True
        ).astype(jnp.float32),
        lax.psum_scatter(
            bgrad_down.astype(jnp.bfloat16), "blk", scatter_dimension=0, tiled=True
        ).astype(jnp.float32),
        lax.psum_scatter(
            ggrad_ffn.astype(jnp.bfloat16), "blk", scatter_dimension=0, tiled=True
        ).astype(jnp.float32),
        lax.psum_scatter(
            sgrad_ffn.astype(jnp.bfloat16), "blk", scatter_dimension=0, tiled=True
        ).astype(jnp.float32),
    )
    return (
        layer_out,
        token_grad,
        wgrad_qkv,
        bgrad_qkv,
        wgrad_out,
        bgrad_out,
        ggrad_attn,
        sgrad_attn,
        wgrad_up,
        bgrad_up,
        wgrad_down,
        bgrad_down,
        ggrad_ffn,
        sgrad_ffn,
    )


GROUPS = 4
LANES = 128
LOG2E = math.log2(math.e)
MESH = pl.DeviceIdType.MESH


def times_t(left, right):
    return lax.dot_general(
        left, right, (((1,), (1,)), ((), ())), preferred_element_type=jnp.float32
    )


def place():
    tab, blk = lax.axis_index("tab"), lax.axis_index("blk")
    return tab, blk, blk // 2, blk % 2


def meet(tab, blk):
    barrier = pltpu.get_barrier_semaphore()

    @pl.loop(1, 8)
    def _(step):
        pl.semaphore_signal(
            barrier, inc=1, device_id=(tab, lax.rem(blk + step, 8)), device_id_type=MESH
        )

    pl.semaphore_wait(barrier, 7)


def greet_all(tab, blk):
    barrier = pltpu.get_barrier_semaphore()
    for step in range(1, 8):
        pl.semaphore_signal(
            barrier, inc=1, device_id=(tab, lax.rem(blk + step, 8)), device_id_type=MESH
        )
    for step in range(1, 4):
        pl.semaphore_signal(
            barrier, inc=1, device_id=(lax.rem(tab + step, 4), blk), device_id_type=MESH
        )
    pl.semaphore_wait(barrier, 10)


def send_to(src, dst, send_sem, recv_sem, device):
    return pltpu.make_async_remote_copy(
        src_ref=src,
        dst_ref=dst,
        send_sem=send_sem,
        recv_sem=recv_sem,
        device_id=device,
        device_id_type=MESH,
    )


def landed(ref, sem):
    pltpu.make_async_copy(ref, ref, sem).wait()


def return_rows(src, dst, send_sem, recv_sem, act):
    tab, _, chip, core = place()
    half, group = chip // 2, 2 * lax.rem(chip, 2) + core
    for side in range(2):
        is_own = jnp.logical_and(chip == group, core == side)
        own = pltpu.make_async_copy(src.at[side], dst.at[half], recv_sem.at[half])
        away = send_to(
            src.at[side],
            dst.at[half],
            send_sem.at[side],
            recv_sem.at[half],
            (tab, 2 * group + side),
        )
        if act == "start":
            pl.when(is_own)(own.start)
            pl.when(jnp.logical_not(is_own))(away.start)
        else:
            pl.when(jnp.logical_not(is_own))(away.wait_send)
            landed(dst.at[side], recv_sem.at[side])


def by_core(core, act):
    pl.when(core == 0)(functools.partial(act, 0))
    pl.when(core == 1)(functools.partial(act, 1))


def fold(block):
    cut = block.shape[0] // 2
    return jnp.concatenate([block[:cut], block[cut:]], axis=1)


def unfold(block):
    cut = block.shape[1] // 2
    return jnp.concatenate([block[:, :cut], block[:, cut:]], axis=0)


def own_window(group, first, rows_ref, out):
    start = pl.multiple_of(first + LANES * ((3 * group) // 2), LANES)
    window = rows_ref[:, pl.ds(start, 2 * LANES)].astype(jnp.float32)
    window = pltpu.roll(window, lax.rem(2 * LANES - HD * lax.rem(group, 2), 2 * LANES), 1)
    left = window[:, :LANES]
    low = lax.broadcasted_iota(jnp.int32, left.shape, 1) < HD
    for head, lanes in enumerate((left, pltpu.roll(left, HD, 1), window[:, LANES:])):
        out(head, jnp.where(low, lanes, 0.0))


def attend_kernel(
    heads,
    tok_ref,
    len_ref,
    par_ref,
    w_hbm,
    cot_hbm,
    ctx_ref,
    mytok_ref,
    mycot_ref,
    fullt_ref,
    qkv_ref,
    ot_ref,
    lse_ref,
    wr_ref,
    tokv,
    toktv,
    wfull,
    wrv,
    wown,
    bown,
    qkvv,
    vtv,
    otv,
    lsev,
    acc,
    peaks,
    csend,
    send_sem,
    recv,
    csend_sem,
    crecv_sem,
    osend_sem,
    orecv_sem,
    local_sem,
):
    tab, blk, chip, core = place()
    half = chip // 2
    group = 2 * lax.rem(chip, 2) + core
    rows = tok_ref.shape[1]
    width = tok_ref.shape[2]
    is_near = jnp.logical_or(chip == 1, chip == 2)
    mate = chip + 1 - 2 * lax.rem(chip, 2)
    other_near = 2 - half
    other_far = 3 - 3 * half
    own_far = 3 * half
    scale = LOG2E / math.sqrt(HD)

    def remote(src, dst, send_sem, recv_sem, to_chip, to_core):
        return pltpu.make_async_remote_copy(
            src_ref=src,
            dst_ref=dst,
            send_sem=send_sem,
            recv_sem=recv_sem,
            device_id=(tab, 2 * to_chip + to_core),
            device_id_type=MESH,
        )

    here, there = tok_ref.at[half], tok_ref.at[1 - half]
    to_mate = remote(here, tokv.at[blk], send_sem.at[0], recv.at[blk], mate, core)
    to_other = remote(there, tokv.at[blk], send_sem.at[1], recv.at[blk], other_near, core)
    to_side = remote(here, tokv.at[blk], send_sem.at[2], recv.at[blk], chip, 1 - core)

    def to_far(slot, src_chip):
        which = 2 * src_chip + core
        ref = tokv.at[which]
        return remote(ref, ref, send_sem.at[2 + slot], recv.at[which], own_far, core)

    def to_core(slot, src_chip):
        which = 2 * src_chip + core
        ref = tokv.at[which]
        return remote(ref, ref, send_sem.at[5 + slot], recv.at[which], chip, 1 - core)

    def arrived(which):
        pltpu.make_async_copy(tokv.at[which], tokv.at[which], recv.at[which]).wait()

    load = pltpu.make_async_copy(w_hbm, wfull, local_sem.at[5])
    load.start()
    meet(tab, blk)
    pl.when(is_near)(to_other.start)
    to_mate.start()
    to_side.start()
    tokv[blk] = tok_ref[half]

    lane1 = lax.broadcasted_iota(jnp.int32, (8, LANES), 1)
    for at in (0, 2):

        def keep_bias(head, lanes, at=at):
            row = jnp.where(lane1 == HD, 1.0, lanes)
            bown[:, pl.ds((at * heads + head) * LANES, LANES)] = row

        own_window(group, 0, par_ref.at[pl.ds(8 * (1 + at // 2), 8)], keep_bias)
    for head in range(heads):
        bown[:, pl.ds((heads + head) * LANES, LANES)] = jnp.zeros((8, LANES), jnp.float32)
    load.wait()
    for at in range(3):

        def keep_weight(head, lanes, at=at):
            wown[:, pl.ds((at * heads + head) * LANES, LANES)] = lanes.astype(jnp.bfloat16)

        own_window(group, at * width, wfull, keep_weight)

    length = len_ref[half]
    lane = lax.broadcasted_iota(jnp.int32, (rows, LANES), 1)
    row = lax.broadcasted_iota(jnp.int32, (rows, LANES), 0)

    def project(which):
        first = pl.multiple_of(which * rows, rows)
        tok = tokv[which]
        y = jnp.dot(tok, wown[...], preferred_element_type=jnp.float32) + bown[:1]
        pad = jnp.where((lane == HD) & (row + first >= length), NEGATIVE, 0.0)
        for head in range(heads):
            q, k, v = (
                y[:, (part * heads + head) * LANES :][:, :LANES] for part in range(3)
            )
            qkvv[head, pl.ds(first, rows)] = q.astype(jnp.bfloat16)
            qkvv[heads + head, pl.ds(first, rows)] = (k + pad).astype(jnp.bfloat16)
            qkvv[2 * heads + head, pl.ds(first, rows)] = v.astype(jnp.bfloat16)
            vtv[head, :, pl.ds(first, rows)] = v.T.astype(jnp.bfloat16)
        toktv[:, pl.ds(first, rows)] = tok.T

    def take_keys(tile, head, first_key, count, fresh):
        queries = pl.ds(pl.multiple_of(tile * 2 * rows, 2 * rows), 2 * rows)
        keys = pl.ds(pl.multiple_of(first_key, count), count)
        st = times_t(qkvv[heads + head, keys], qkvv[head, queries])
        peak = jnp.max(st, axis=0, keepdims=True)
        if not fresh:
            before = peaks[tile, pl.ds(head, 1)]
            peak = jnp.maximum(peak, before)
        pt = jnp.exp2((st - peak) * scale).astype(jnp.bfloat16)
        ot = jnp.dot(vtv[head, :, keys], pt, preferred_element_type=jnp.float32)
        if not fresh:
            ot += acc[tile, head] * jnp.exp2((before - peak) * scale)
        acc[tile, head] = ot
        peaks[tile, pl.ds(head, 1)] = peak

    def meet_keys_of_own_half():
        @pl.loop(0, 2 * heads)
        def _(at):
            tile = jnp.where(at < heads, chip, mate)
            take_keys(tile, lax.rem(at, heads), half * 4 * rows, 4 * rows, True)

    def meet_keys_of_near():
        @pl.loop(0, heads)
        def _(head):
            take_keys(other_near, head, half * 4 * rows, 4 * rows, True)

        @pl.loop(0, 3 * heads)
        def _(at):
            tile = jnp.where(at < heads, chip, jnp.where(at < 2 * heads, mate, other_near))
            take_keys(tile, lax.rem(at, heads), other_near * 2 * rows, 2 * rows, False)

    project(blk)

    def half_lanes(part, at):
        first = part * width + LANES * (at // 2)
        return wfull[:, first : first + LANES][:, HD * (at % 2) :][:, :HD]

    for head in range(heads):
        for part in range(3):
            for pair in range(GROUPS // 2):
                at = 2 * pair * heads + head
                wrv[head, :, pl.ds((2 * part + pair) * LANES, LANES)] = jnp.concatenate(
                    [half_lanes(part, at), half_lanes(part, at + heads)], axis=1
                )
    arrived(2 * mate + core)
    to_core(0, mate).start()

    @pl.when(jnp.logical_not(is_near))
    def _():
        to_mate.wait_send()
        to_other.start()

    project(2 * mate + core)
    arrived(2 * chip + 1 - core)
    project(2 * chip + 1 - core)
    arrived(2 * mate + 1 - core)
    project(2 * mate + 1 - core)

    def pass_on(slot, src_chip):
        arrived(2 * src_chip + core)
        pl.when(is_near)(to_far(slot, src_chip).start)
        to_core(slot, src_chip).start()

    def project_chip(src_chip):
        project(2 * src_chip + core)
        arrived(2 * src_chip + 1 - core)
        project(2 * src_chip + 1 - core)

    def owner_of(table):
        return 2 * table + chip // 2, lax.rem(chip, 2)

    def cotangent_copy(table, own):
        src, dst = cot_hbm.at[table], mycot_ref.at[core]
        if own:
            return pltpu.make_async_copy(src, dst, orecv_sem.at[core])
        return remote(src, dst, osend_sem.at[table], orecv_sem.at[core], *owner_of(table))

    def is_owner(table):
        to_chip, to_core = owner_of(table)
        return jnp.logical_and(to_chip == chip, to_core == core)

    pl.when(is_near)(functools.partial(pass_on, 1, other_near))
    meet_keys_of_own_half()
    pl.when(jnp.logical_not(is_near))(functools.partial(pass_on, 1, other_near))
    pl.when(is_near)(functools.partial(pass_on, 2, other_far))
    cotangent_copy(1 - half, False).start()
    project_chip(other_near)
    meet_keys_of_near()
    pl.when(jnp.logical_not(is_near))(functools.partial(pass_on, 2, other_far))
    project_chip(other_far)

    keep = (
        pltpu.make_async_copy(toktv, fullt_ref, local_sem.at[0]),
        pltpu.make_async_copy(qkvv, qkv_ref, local_sem.at[1]),
        pltpu.make_async_copy(wrv, wr_ref, local_sem.at[6]),
    )
    for copy in keep:
        copy.start()

    pl.when(is_owner(half))(cotangent_copy(half, True).start)
    pl.when(jnp.logical_not(is_owner(half)))(cotangent_copy(half, False).start)
    my_tokens = [
        pltpu.make_async_copy(
            tokv.at[2 * group + side], mytok_ref.at[side], local_sem.at[7 + side]
        )
        for side in range(2)
    ]
    for copy in my_tokens:
        copy.start()

    def context_copy(which):
        return remote(
            csend.at[which],
            ctx_ref.at[group],
            csend_sem.at[which],
            crecv_sem.at[group],
            2 * half + which // 2,
            lax.rem(which, 2),
        )

    own_context = pltpu.make_async_copy(
        csend.at[group], ctx_ref.at[group], local_sem.at[2]
    )

    @pl.loop(0, 4)
    def _(step):
        at = jnp.where(is_near, step, 3 - step)
        which = jnp.where(
            at < 2, jnp.where(at == 0, chip, mate), jnp.where(at == 2, other_near, other_far)
        )

        @pl.when(at == 3)
        def _():
            @pl.loop(0, heads)
            def _(head):
                take_keys(which, head, 0, 8 * rows, True)

        @pl.when(at < 3)
        def _():
            @pl.loop(0, heads)
            def _(head):
                take_keys(which, head, other_far * 2 * rows, 2 * rows, False)

        for head in range(heads):
            ot = acc[which, head]
            total = ot[HD : HD + 1]
            otv[which, head * HD : (head + 1) * HD] = ot[:HD] / total
            peak = peaks[which, head : head + 1]
            lsev[which, head : head + 1] = peak * scale + jnp.log(total) * LOG2E
        csend[which] = fold(otv[which].T.astype(jnp.bfloat16))

        pl.when(which == group)(own_context.start)
        pl.when(which != group)(context_copy(which).start)

    more = (
        pltpu.make_async_copy(otv, ot_ref, local_sem.at[3]),
        pltpu.make_async_copy(lsev, lse_ref, local_sem.at[4]),
    )
    for copy in more:
        copy.start()
    pl.when(is_near)(to_mate.wait_send)
    to_other.wait_send()
    to_side.wait_send()
    to_core(0, mate).wait_send()
    for slot, src_chip in ((1, other_near), (2, other_far)):
        pl.when(is_near)(to_far(slot, src_chip).wait_send)
        to_core(slot, src_chip).wait_send()

    for step in range(1, 4):
        which = lax.rem(group + step, 4)
        context_copy(which).wait_send()
        pltpu.make_async_copy(ctx_ref.at[which], ctx_ref.at[which], crecv_sem.at[which]).wait()
    own_context.wait()
    pl.when(jnp.logical_not(is_owner(half)))(cotangent_copy(half, False).wait_send)
    cotangent_copy(1 - half, False).wait_send()
    for side in range(2):
        pltpu.make_async_copy(mycot_ref.at[side], mycot_ref.at[side], orecv_sem.at[side]).wait()
    for copy in [*keep, *more, *my_tokens]:
        copy.wait()


def attend(tokens, lengths, params, qkv_weight, cotangent, heads):
    _, rows, width = tokens.shape
    blocks = 8
    total = blocks * rows
    any_space = pl.BlockSpec(memory_space=pl.ANY)
    vmem = pl.BlockSpec(memory_space=pltpu.VMEM)
    bf16, f32 = jnp.bfloat16, jnp.float32
    dma = pltpu.SemaphoreType.DMA
    return pl.pallas_call(
        functools.partial(attend_kernel, heads),
        name="attend",
        out_shape=(
            jax.ShapeDtypeStruct((GROUPS, rows, 2 * heads * HD), bf16),
            jax.ShapeDtypeStruct((2, rows, width), bf16),
            jax.ShapeDtypeStruct((2, rows, width), bf16),
            jax.ShapeDtypeStruct((width, total), bf16),
            jax.ShapeDtypeStruct((3 * heads, total, LANES), bf16),
            jax.ShapeDtypeStruct((4, heads * HD, 2 * rows), f32),
            jax.ShapeDtypeStruct((4, 8, 2 * rows), f32),
            jax.ShapeDtypeStruct((heads, width, width), bf16),
        ),
        in_specs=[vmem, pl.BlockSpec(memory_space=pltpu.SMEM), vmem, any_space, any_space],
        out_specs=(any_space,) * 8,
        scratch_shapes=[
            pltpu.VMEM((blocks, rows, width), bf16),
            pltpu.VMEM((width, total), bf16),
            pltpu.VMEM(qkv_weight.shape, bf16),
            pltpu.VMEM((heads, width, width), bf16),
            pltpu.VMEM((width, 3 * heads * LANES), bf16),
            pltpu.VMEM((8, 3 * heads * LANES), f32),
            pltpu.VMEM((3 * heads, total, LANES), bf16),
            pltpu.VMEM((heads, LANES, total), bf16),
            pltpu.VMEM((4, heads * HD, 2 * rows), f32),
            pltpu.VMEM((4, 8, 2 * rows), f32),
            pltpu.VMEM((4, heads, LANES, 2 * rows), f32),
            pltpu.VMEM((4, 8, 2 * rows), f32),
            pltpu.VMEM((GROUPS, rows, 2 * heads * HD), bf16),
            dma((8,)),
            dma((blocks,)),
            dma((GROUPS,)),
            dma((GROUPS,)),
            dma((2,)),
            dma((2,)),
            dma((9,)),
        ],
        compiler_params=pltpu.CompilerParams(
            collective_id=1, has_side_effects=True, vmem_limit_bytes=60 << 20
        ),
    )(tokens, lengths, params, qkv_weight, cotangent)


UNITS = 9
TURNS = 4
STAGES = 5
PHASE = ((1, 4, -1), (2, 0, 1), (3, 0, 4), (4, 0, 7))


def attend_back_kernel(
    heads,
    dctx_ref,
    qkv_ref,
    ot_ref,
    lse_ref,
    fullt_ref,
    w_ref,
    pre_ref,
    down_ref,
    up_ref,
    parts_ref,
    small_ref,
    tgrad_ref,
    wqkv_ref,
    wout_ref,
    wup_ref,
    wdown_ref,
    little_ref,
    dov,
    doh,
    deltas,
    qkvv,
    otv,
    lsev,
    toktv,
    wv,
    prev,
    ktv,
    dqv,
    dkv,
    dvv,
    dqkv,
    qsend,
    kvsend,
    arrive_q,
    arrive_kv,
    joined,
    xacc,
    xsend,
    mine,
    sum0,
    sum1,
    sum2,
    sum3,
    sum4,
    slab,
    slab_in,
    sums,
    sums_in,
    line,
    line_in,
    small_in,
    small_sum,
    small_pairs,
    dsend_sem,
    drecv_sem,
    gsend_sem,
    grecv_sem,
    xsend_sem,
    xrecv_sem,
    ssend_sem,
    srecv_sem,
    tsend_sem,
    trecv_sem,
    lsend_sem,
    lrecv_sem,
    local_sem,
    mine_sem,
):
    f32, bf16 = jnp.float32, jnp.bfloat16
    tab, blk, chip, core = place()
    y, x, zh, zl = tab // 2, lax.rem(tab, 2), chip // 2, lax.rem(chip, 2)
    half = zh
    group = 2 * zl + core
    blocks, rows = 8, dov.shape[1]
    width = toktv.shape[0]
    tile = 2 * rows
    piece = 256
    scale = LOG2E / math.sqrt(HD)
    shrink = HD**-0.5

    remote = send_to

    loads = [
        pltpu.make_async_copy(src, dst, local_sem.at[at])
        for at, (src, dst) in enumerate(
            (
                (qkv_ref, qkvv),
                (ot_ref, otv),
                (lse_ref, lsev),
                (dctx_ref.at[group], dov.at[group]),
                (fullt_ref, toktv),
                (w_ref, wv),
                (pre_ref, prev),
                (down_ref, sum1.at[:4]),
                (up_ref, sum0.at[:4]),
            )
        )
    ]
    for copy in loads:
        copy.start()

    greet_all(tab, blk)

    def group_at(step):
        to_chip = jnp.where(step < 2, zl, 1 - zl)
        return 2 * to_chip + jnp.where(lax.rem(step, 2) == 0, core, 1 - core)

    def context_copy(which):
        return remote(
            dctx_ref.at[which],
            dov.at[group],
            dsend_sem.at[which],
            drecv_sem.at[group],
            (tab, 4 * half + which),
        )

    for step in range(1, 4):
        context_copy(group_at(step)).start()

    def stage_copy(stage, unit, order=None):
        send, done = ssend_sem.at[stage, unit], srecv_sem.at[stage, unit]
        if stage == 0:
            src = parts_ref.at[:, :, :, :, 1 - core]
            return remote(src, sum0.at[unit - 4], send, done, (tab, 2 * chip + 1 - core))
        if stage == 1 and order == 0:
            return remote(
                sum0.at[unit - 4, :, 1 - x], sum1.at[unit], send, done, (2 * y + 1 - x, blk)
            )
        if stage == 1:
            return remote(
                sum0.at[unit - 4, 1 - y], sum1.at[unit], send, done, (2 * (1 - y) + x, blk)
            )
        if stage == 2 and order == 0:
            return remote(
                sum1.at[unit, 1 - y], sum2.at[unit], send, done, (2 * (1 - y) + x, blk)
            )
        if stage == 2:
            return remote(
                sum1.at[unit, 1 - x], sum2.at[unit], send, done, (2 * y + 1 - x, blk)
            )
        if stage == 3:
            src, there = sum2.at[unit, :, 1 - zl], 2 * zh + 1 - zl
            return remote(src, sum3.at[unit], send, done, (tab, 2 * there + core))
        src, there = sum3.at[unit, 1 - zh], 2 * (1 - zh) + zl
        return remote(src, sum4.at[unit], send, done, (tab, 2 * there + core))

    both = functools.partial(by_core, core)
    mine_copy = pltpu.make_async_copy(
        parts_ref.at[:, :, :, :, core], mine, mine_sem.at[0]
    )

    def finish(unit):
        done = sum4[unit].astype(f32) + sum3[unit, zh].astype(f32)
        top, low = done[: done.shape[0] // 2], done[done.shape[0] // 2 :]
        each, cut = top.shape

        @pl.when(unit < 4)
        def _():
            at = pl.ds(pl.multiple_of(unit * each, each), each)
            wdown_ref[at, :cut] = top
            wdown_ref[at, cut:] = low

        @pl.when(jnp.logical_and(unit >= 4, unit < 8))
        def _():
            at = pl.multiple_of((unit - 4) * 2 * cut, 2 * cut)
            wup_ref[:, pl.ds(at, cut)] = top
            wup_ref[:, pl.ds(pl.multiple_of(at + cut, cut), cut)] = low

        @pl.when(unit == 8)
        def _():
            wout_ref[:, :cut] = top
            wout_ref[:, cut:] = low

    def advance(stage, unit):
        if stage == 0:
            landed(sum0.at[unit - 4], srecv_sem.at[0, unit])
            mine_copy.wait()
            for a in range(2):
                for b in range(2):
                    sum0[unit - 4, a, b] = sum0[unit - 4, a, b] + mine[a, b]

            both(lambda order: stage_copy(1, unit, order).start())
        elif stage == 1:
            landed(sum1.at[unit], srecv_sem.at[1, unit])

            def act(order):
                own = sum0[unit - 4, :, x] if order == 0 else sum0[unit - 4, y]
                sum1[unit] = sum1[unit] + own
                stage_copy(2, unit, order).start()

            both(act)
        elif stage == 2:
            landed(sum2.at[unit], srecv_sem.at[2, unit])

            def act(order):
                sum2[unit] = sum2[unit] + sum1[unit, y if order == 0 else x]

            both(act)
            stage_copy(3, unit).start()
        elif stage == 3:
            landed(sum3.at[unit], srecv_sem.at[3, unit])
            sum3[unit] = sum3[unit] + sum2[unit, :, zl]
            stage_copy(4, unit).start()
        else:
            landed(sum4.at[unit], srecv_sem.at[4, unit])
            finish(unit)

    def tick(now):
        pl.when(now == 2)(functools.partial(advance, 0, UNITS - 1))

        @pl.when((now >= 0) & (now < 4))
        def _():
            both(lambda order: stage_copy(1, 4 + now, order).start())

        for stage, first, lag in PHASE:
            unit = now - lag
            due = (unit >= first) & (unit < UNITS)
            pl.when(due)(functools.partial(advance, stage, unit))

    stage_copy(0, UNITS - 1).start()
    mine_copy.start()
    for copy in loads[7:]:
        copy.wait()

    @pl.loop(0, 4)
    def _(at):
        both(lambda order: stage_copy(2, at, order).start())

    def tab_copy(src, dst, sem_at, step):
        there = lax.rem(tab + step, 4)
        return remote(
            src(there), dst(tab), tsend_sem.at[sem_at, there], trecv_sem.at[sem_at, tab], (there, blk)
        )

    def line_copy(src, dst, sem_at, step):
        there = lax.rem(blk + step, 8)
        return remote(
            src(there), dst(blk), lsend_sem.at[sem_at, there], lrecv_sem.at[sem_at, blk], (tab, there)
        )

    def small_tab(step):
        return tab_copy(lambda t: small_ref, lambda t: small_in.at[t], heads, step)

    def small_pair(at):
        there = (2 * chip + 1 - core, 2 * (2 * zh + 1 - zl) + core, 2 * (2 * (1 - zh) + zl) + core)
        return remote(
            small_sum.at[at],
            small_pairs.at[at],
            lsend_sem.at[heads, at],
            lrecv_sem.at[heads, at],
            (tab, there[at]),
        )

    def slab_tab(head, step):
        return tab_copy(
            lambda t: slab.at[head, t], lambda t: slab_in.at[head, t], head, step
        )

    def slab_blk(head, step):
        return line_copy(
            lambda b: line.at[head, b], lambda b: line_in.at[head, b], head, step
        )

    for step in range(1, 4):
        small_tab(step).start()

    def pass_small(at):
        if at == 0:
            total = small_ref[...]
            for step in range(1, 4):
                there = lax.rem(tab + step, 4)
                landed(small_in.at[there], trecv_sem.at[heads, there])
                total += small_in[there]
        else:
            landed(small_pairs.at[at - 1], lrecv_sem.at[heads, at - 1])
            total = small_sum[at - 1] + small_pairs[at - 1]
        small_sum[at] = total
        if at < 3:
            small_pair(at).start()

    def sums_tab(head, step):
        return tab_copy(
            lambda t: sums.at[head], lambda t: sums_in.at[head, t], heads + 1 + head, step
        )

    def make_slab(head):
        flat = dqkv[head]
        sums[head] = jnp.broadcast_to(
            jnp.sum(flat.astype(f32), axis=0, keepdims=True), (8, 3 * HD)
        )
        grad = jnp.dot(toktv[...], flat, preferred_element_type=f32)
        each = width // 32
        slab[head, :, :4] = grad[:, : 2 * HD].reshape(4, 4, 2 * each, 2 * HD).astype(bf16)
        q = grad[:, 2 * HD :].reshape(16, 2, each, HD)
        q = jnp.concatenate([q[:, 0], q[:, 1]], axis=2)
        slab[head, :, 4:] = q.reshape(4, 2, 2 * each, 2 * HD).astype(bf16)
        for step in range(1, 4):
            slab_tab(head, step).start()
            sums_tab(head, step).start()

    def pass_slab(head):
        total = slab[head, tab].astype(f32)
        sums_total = sums[head]
        for step in range(1, 4):
            there = lax.rem(tab + step, 4)
            landed(slab_in.at[head, there], trecv_sem.at[head, there])
            landed(sums_in.at[head, there], trecv_sem.at[heads + 1 + head, there])
            total += slab_in[head, there].astype(f32)
            sums_total += sums_in[head, there]
        each = width // 32
        for b in range(8):
            kv = total[b // 2, b % 2 * each :][:each]
            q = total[4 + b // 4, b // 2 % 2 * each :][:each, b % 2 * HD :][:, :HD]
            rows_b = jnp.concatenate([jnp.concatenate([kv, q], axis=1), sums_total], axis=0)
            line[head, b] = rows_b.astype(bf16)
        line_in[head, blk] = line[head, blk]
        for step in range(1, 8):
            slab_blk(head, step).start()

    for copy in loads[:4]:
        copy.wait()
    for head in range(heads):
        ktv[head] = qkvv[heads + head].T

    def gradient_copies(head, which, own):
        slot = group * heads + head
        pairs = (
            (qsend.at[head, which], arrive_q.at[slot]),
            (kvsend.at[head, which], arrive_kv.at[slot]),
        )
        for kind, (src, dst) in enumerate(pairs):
            if own:
                yield pltpu.make_async_copy(src, dst, grecv_sem.at[kind, slot])
            else:
                yield remote(
                    src,
                    dst,
                    gsend_sem.at[kind, head, which],
                    grecv_sem.at[kind, slot],
                    (tab, 4 * half + which),
                )

    def send_gradient(kind, head, which):
        @pl.when(which == group)
        def _():
            list(gradient_copies(head, which, True))[kind].start()

        @pl.when(which != group)
        def _():
            list(gradient_copies(head, which, False))[kind].start()

    def absorb(head):
        for at in range(GROUPS):
            slot = at * heads + head
            landed(arrive_q.at[slot], grecv_sem.at[0, slot])
            landed(arrive_kv.at[slot], grecv_sem.at[1, slot])
        for pair in range(GROUPS // 2):
            left, right = 2 * pair * heads + head, (2 * pair + 1) * heads + head
            lanes = slice(pair * LANES, (pair + 1) * LANES)
            for side in range(2):
                cut = slice(side * HD, (side + 1) * HD)
                joined[side * rows : (side + 1) * rows, lanes] = jnp.concatenate(
                    [arrive_q[left][:, cut], arrive_q[right][:, cut]], axis=1
                )
                lanes_kv = slice((2 * side + 2 + pair) * LANES, (2 * side + 3 + pair) * LANES)
                joined[:, lanes_kv] = jnp.concatenate(
                    [arrive_kv[left][:, cut], arrive_kv[right][:, cut]], axis=1
                )

    @pl.loop(0, heads * TURNS)
    def _(turn):
        head, step = turn // TURNS, lax.rem(turn, TURNS)
        which = group_at(step)
        first = pl.multiple_of(which * tile, tile)

        @pl.when(head == 0)
        def _():
            @pl.when(step > 0)
            def _():
                landed(dov.at[which], drecv_sem.at[which])

            dos = unfold(dov[which])
            for at in range(heads):
                do = dos[:, at * HD : (at + 1) * HD]
                doh[at, pl.ds(first, tile)] = do
                ot = otv[which, at * HD : (at + 1) * HD]
                deltas[at, which, :1] = jnp.sum(ot * do.astype(f32).T, axis=0, keepdims=True)

        @pl.when(step == 0)
        def _():
            dkv[...] = jnp.zeros_like(dkv)
            dvv[...] = jnp.zeros_like(dvv)

        tick(turn)

        q_full = qkvv[head, pl.ds(first, tile)]
        q = q_full[:, :HD]
        do = doh[head, pl.ds(first, tile)]
        delta = deltas[head, which, :1]
        lse = lsev[which, pl.ds(head, 1)]
        dqt = jnp.zeros((LANES, tile), f32)
        for at in range(blocks * rows // piece):
            cut = pl.ds(at * piece, piece)
            st = times_t(qkvv[heads + head, cut], q_full)
            pt = jnp.exp2(st * scale - lse)
            dpt = times_t(qkvv[2 * heads + head, cut][:, :HD], do)
            dst = (pt * (dpt - delta)).astype(bf16)
            dvv[cut] += jnp.dot(pt.astype(bf16), do, preferred_element_type=f32)
            dkv[cut] += jnp.dot(dst, q, preferred_element_type=f32)
            dqt += jnp.dot(ktv[head, :, cut], dst, preferred_element_type=f32)
        dq = (dqt[:HD].T * shrink).astype(bf16)
        dqv[pl.ds(first, tile)] = dq
        qsend[head, which] = jnp.concatenate([dq[:rows], dq[rows:]], axis=1)
        send_gradient(0, head, which)

        @pl.when(step == TURNS - 1)
        def _():
            @pl.loop(0, 4)
            def _(at):
                there = lax.rem(group + 1 + at, 4)
                cut = pl.ds(pl.multiple_of(there * tile, tile), tile)
                pair = jnp.concatenate([dkv[cut] * shrink, dvv[cut]], axis=1).astype(bf16)
                kvsend[head, there] = pair
                send_gradient(1, head, there)
                dqkv[head, cut] = jnp.concatenate([pair, dqv[cut]], axis=1)

        @pl.when(turn == TURNS)
        def _():
            loads[4].wait()
            pass_small(0)

        for at in range(1, 4):
            pl.when(turn == TURNS + at)(functools.partial(pass_small, at))

        @pl.when(jnp.logical_and(head > 0, step == 0))
        def _():
            make_slab(head - 1)

        @pl.when(jnp.logical_and(head > 0, step == 3))
        def _():
            pass_slab(head - 1)

    loads[5].wait()
    for head in range(heads - 1):
        absorb(head)
        product = times_t(joined[...], wv[head])
        xacc[...] = product if head == 0 else xacc[...] + product
    tick(heads * TURNS)
    absorb(heads - 1)
    loads[6].wait()
    for side in range(2):
        at = pl.ds(side * rows, rows)
        total = prev[at] + xacc[at] + times_t(joined[at], wv[heads - 1])
        xsend[side] = total.astype(bf16)
    return_rows(xsend, tgrad_ref, xsend_sem, xrecv_sem, "start")

    make_slab(heads - 1)
    for now in range(heads * TURNS + 1, PHASE[-1][2] + UNITS):
        tick(now)
    pass_slab(heads - 1)

    def slabs_in(head, at):
        return [line_in[head, half_at * GROUPS + at].astype(f32) for half_at in range(2)]

    for head in range(heads):
        for step in range(1, 8):
            there = lax.rem(blk + step, 8)
            landed(line_in.at[head, there], lrecv_sem.at[head, there])
    total = small_sum[3]
    own = [
        functools.reduce(jnp.add, slabs_in(at % heads, at // heads))
        for at in range(GROUPS * heads)
    ]
    each = width // 32
    bias = []
    for part in range(3):
        cut = slice((part + 2) % 3 * HD, (part + 2) % 3 * HD + HD)
        for pair in range(GROUPS * heads // 2):
            both_heads = jnp.concatenate([own[2 * pair][:, cut], own[2 * pair + 1][:, cut]], axis=1)
            lanes = slice(part * width + pair * LANES, part * width + (pair + 1) * LANES)
            wqkv_ref[:, lanes] = both_heads[:each]
            bias.append(both_heads[each:])
    pairs = GROUPS * heads // 2
    bias_q = jnp.concatenate(bias[:pairs], axis=1)
    bias_v = jnp.concatenate(bias[2 * pairs :], axis=1)
    bias = jnp.where(tab < 2, bias_q, bias_v)

    row = lax.broadcasted_iota(jnp.int32, (width, LANES), 0)
    lane = lax.broadcasted_iota(jnp.int32, (width, LANES), 1)

    def take(block, first, count):
        chosen = jnp.where((row == first + lane) & (lane < count), 1.0, 0.0)
        return jnp.dot(
            block, chosen, preferred_element_type=f32, precision=lax.Precision.HIGHEST
        )

    index = 8 * tab + blk
    little_ref[0:8] = take(total[:8], each * index, each)
    at_row = lax.broadcasted_iota(jnp.int32, total.shape, 0) == 6 + tab
    wide = jnp.sum(jnp.where(at_row, total, 0.0), axis=0, keepdims=True)
    little_ref[6:7] = take(jnp.broadcast_to(wide, (8, width)), 4 * each * blk, 4 * each)[:1]
    little_ref[7:8] = take(bias, 2 * each * lax.rem(index, 16), 2 * each)[:1]

    return_rows(xsend, tgrad_ref, xsend_sem, xrecv_sem, "wait")
    for step in range(1, 4):
        context_copy(group_at(step)).wait_send()

    @pl.loop(0, heads)
    def _(head):
        @pl.loop(1, 4)
        def _(step):
            for copy in gradient_copies(head, lax.rem(group + step, 4), False):
                copy.wait_send()

    for step in range(1, 8):
        for head in range(heads):
            slab_blk(head, step).wait_send()
    for at in range(3):
        small_pair(at).wait_send()
    for step in range(1, 4):
        small_tab(step).wait_send()
        for head in range(heads):
            slab_tab(head, step).wait_send()
            sums_tab(head, step).wait_send()

    stage_copy(0, UNITS - 1).wait_send()

    @pl.loop(0, UNITS)
    def _(unit):
        @pl.when(unit >= 4)
        def _():
            both(lambda order: stage_copy(1, unit, order).wait_send())

        both(lambda order: stage_copy(2, unit, order).wait_send())
        stage_copy(3, unit).wait_send()
        stage_copy(4, unit).wait_send()


def attend_back(dctx, qkv, ot, lse, full_t, by_head, pre, small, down, up, parts, heads):
    width, total = full_t.shape
    blocks = 8
    rows = total // blocks
    each, ff = width // 32, 4 * width
    any_space = pl.BlockSpec(memory_space=pl.ANY)
    vmem = pl.BlockSpec(memory_space=pltpu.VMEM)
    bf16, f32 = jnp.bfloat16, jnp.float32
    dma = pltpu.SemaphoreType.DMA
    unit = parts.shape[-2:]
    shape = jax.ShapeDtypeStruct
    return pl.pallas_call(
        functools.partial(attend_back_kernel, heads),
        name="attend_back",
        out_shape=(
            shape((2, rows, width), bf16),
            shape((each, 3 * width), f32),
            shape((each, width), f32),
            shape((each, ff), f32),
            shape((4 * each, width), f32),
            shape((8, LANES), f32),
        ),
        in_specs=[any_space] * 10 + [vmem],
        out_specs=(any_space,) + (vmem,) * 5,
        scratch_shapes=[
            pltpu.VMEM((GROUPS, rows, 2 * heads * HD), bf16),
            pltpu.VMEM((heads, total, HD), bf16),
            pltpu.VMEM((heads, 4, 8, 2 * rows), f32),
            pltpu.VMEM((3 * heads, total, LANES), bf16),
            pltpu.VMEM(ot.shape, f32),
            pltpu.VMEM(lse.shape, f32),
            pltpu.VMEM((width, total), bf16),
            pltpu.VMEM(by_head.shape, bf16),
            pltpu.VMEM((2 * rows, width), f32),
            pltpu.VMEM((heads, LANES, total), bf16),
            pltpu.VMEM((total, HD), bf16),
            pltpu.VMEM((total, HD), f32),
            pltpu.VMEM((total, HD), f32),
            pltpu.VMEM((heads, total, 3 * HD), bf16),
            pltpu.VMEM((heads, 4, rows, 2 * HD), bf16),
            pltpu.VMEM((heads, 4, 2 * rows, 2 * HD), bf16),
            pltpu.VMEM((GROUPS * heads, rows, 2 * HD), bf16),
            pltpu.VMEM((GROUPS * heads, 2 * rows, 2 * HD), bf16),
            pltpu.VMEM((2 * rows, width), bf16),
            pltpu.VMEM((2 * rows, width), f32),
            pltpu.VMEM((2, rows, width), bf16),
            pltpu.VMEM((2, 2, 2, 2, *unit), bf16),
            pltpu.VMEM((UNITS - 4, 2, 2, 2, 2, *unit), bf16),
            pltpu.VMEM((UNITS, 2, 2, 2, *unit), bf16),
            pltpu.VMEM((UNITS, 2, 2, *unit), bf16),
            pltpu.VMEM((UNITS, 2, *unit), bf16),
            pltpu.VMEM((UNITS, *unit), bf16),
            pltpu.VMEM((heads, 4, 6, 2 * each, 2 * HD), bf16),
            pltpu.VMEM((heads, 4, 6, 2 * each, 2 * HD), bf16),
            pltpu.VMEM((heads, 8, 3 * HD), f32),
            pltpu.VMEM((heads, 4, 8, 3 * HD), f32),
            pltpu.VMEM((heads, 8, each + 8, 3 * HD), bf16),
            pltpu.VMEM((heads, 8, each + 8, 3 * HD), bf16),
            pltpu.VMEM((4, 16, width), f32),
            pltpu.VMEM((4, 16, width), f32),
            pltpu.VMEM((3, 16, width), f32),
            dma((GROUPS,)),
            dma((GROUPS,)),
            dma((2, heads, 4)),
            dma((2, GROUPS * heads)),
            dma((2,)),
            dma((2,)),
            dma((STAGES, UNITS)),
            dma((STAGES, UNITS)),
            dma((2 * heads + 1, 4)),
            dma((2 * heads + 1, 4)),
            dma((heads + 1, 8)),
            dma((heads + 1, 8)),
            dma((9,)),
            dma((1,)),
        ],
        compiler_params=pltpu.CompilerParams(
            collective_id=2, has_side_effects=True, vmem_limit_bytes=62 << 20
        ),
    )(dctx, qkv, ot, lse, full_t, by_head, pre, down, up, parts, small)


def finish_kernel(whole, *refs):
    little_ref, outs = refs[whole], refs[whole + 1 :]
    for src, dst in zip(refs[:whole], outs[:whole]):
        dst[...] = src[...]
    for at, dst in enumerate(outs[whole:]):
        dst[...] = little_ref[at, : dst.shape[0]]


def finish(arrays, little, counts):
    vmem = pl.BlockSpec(memory_space=pltpu.VMEM)
    shapes = [jax.ShapeDtypeStruct(a.shape, a.dtype) for a in arrays]
    shapes += [jax.ShapeDtypeStruct((count,), jnp.float32) for count in counts]
    return pl.pallas_call(
        functools.partial(finish_kernel, len(arrays)),
        name="finish",
        out_shape=tuple(shapes),
        in_specs=[vmem] * (len(arrays) + 1),
        out_specs=(vmem,) * len(shapes),
    )(*arrays, little)


def halves(grad):
    cut = grad.shape[2] // 2
    return jnp.concatenate([grad[:, :, :cut], grad[:, :, cut:]], axis=1)


def norm_parts(inputs):
    centred = inputs - jnp.mean(inputs, axis=-1, keepdims=True)
    inverse = lax.rsqrt(jnp.mean(centred * centred, axis=-1, keepdims=True) + EPSILON)
    return centred * inverse, inverse


def norm_back(grad, normed, inverse, gain):
    e = grad * gain
    return inverse * (
        e
        - jnp.mean(e, axis=-1, keepdims=True)
        - normed * jnp.mean(e * normed, axis=-1, keepdims=True)
    )


def column_sum(block):
    return jnp.sum(block.astype(jnp.float32), axis=0, keepdims=True)


def ffn_kernel(
    tok_ref,
    ctx_ref,
    cot_ref,
    par_ref,
    outw_ref,
    upw_hbm,
    downw_hbm,
    layer_ref,
    dctx_ref,
    pre_ref,
    small_ref,
    down_ref,
    up_ref,
    parts_ref,
    upw,
    downw,
    hid,
    hlow,
    hlow_t,
    norm1,
    slopes,
    active_t,
    pre2,
    gbranch,
    ghid,
    out,
    dparts,
    uparts,
    sum0,
    sum1,
    load_sem,
    keep_sem,
    osend_sem,
    orecv_sem,
    ssend_sem,
    srecv_sem,
):
    f32, bf16 = jnp.float32, jnp.bfloat16
    groups, rows, cols = ctx_ref.shape
    cols = cols // 2
    sides = 2
    width = tok_ref.shape[1]
    chunks = active_t.shape[0]
    each = width // 32
    tab, blk, chip, core = place()
    y, x = tab // 2, lax.rem(tab, 2)
    loads = (
        pltpu.make_async_copy(upw_hbm, upw, load_sem.at[0]),
        pltpu.make_async_copy(downw_hbm, downw, load_sem.at[1]),
    )
    for copy in loads:
        copy.start()

    greet_all(tab, blk)

    def par(at):
        return par_ref[at : at + 1]

    inverse1 = []
    contexts = [unfold(ctx_ref[group]) for group in range(groups)]
    for table in range(sides):
        cut = pl.ds(table * rows, rows)
        pre1 = tok_ref[cut].astype(f32) + par(0)
        for group in range(groups):
            pre1 += jnp.dot(
                contexts[group][table * rows : (table + 1) * rows],
                outw_ref[group * cols : (group + 1) * cols],
                preferred_element_type=f32,
            )
        normed, inverse = norm_parts(pre1)
        inverse1.append(inverse)
        hidden = normed * par(1) + par(2)
        low = hidden.astype(bf16)
        norm1[cut] = normed
        hid[cut] = hidden
        hlow[cut] = low
        hlow_t[:, cut] = low.T

    pre2[...] = hid[...] + par(3)
    for copy in loads:
        copy.wait()

    @pl.loop(0, chunks)
    def _(at):
        cut = pl.ds(pl.multiple_of(at * width, width), width)
        upper = jnp.dot(
            hlow[...], upw[:, cut], preferred_element_type=f32
        ) + par_ref[pl.ds(24 + at, 1)]
        cdf = 0.5 + 0.5 * lax.erf(upper * math.sqrt(0.5))
        act = (upper * cdf).astype(bf16)
        slopes[at] = cdf + upper * jnp.exp(-0.5 * upper * upper) * (1 / math.sqrt(2 * math.pi))
        active_t[at] = act.T
        pre2[...] += jnp.dot(act, downw[cut], preferred_element_type=f32)

    normed, inverse = norm_parts(pre2[...])
    out[...] = (normed * par(4) + par(5)).astype(bf16).reshape(out.shape)
    return_rows(out, layer_ref, osend_sem, orecv_sem, "start")
    grad = cot_ref[...].astype(f32)
    small_ref[4:5] = column_sum(grad * normed)
    small_ref[5:6] = column_sum(grad)
    gpre2 = norm_back(grad, normed, inverse, par(4))
    ghid[...] = gpre2
    low = gpre2.astype(bf16)
    gbranch[...] = low
    small_ref[3:4] = column_sum(low)

    def core_copy(unit, src):
        return send_to(
            src.at[:, :, :, :, 1 - core],
            sum0.at[unit],
            ssend_sem.at[0, unit],
            srecv_sem.at[0, unit],
            (tab, 2 * chip + 1 - core),
        )

    def axis_copy(unit, order):
        if order == 0:
            src, there = sum0.at[unit, :, 1 - x], 2 * y + 1 - x
        else:
            src, there = sum0.at[unit, 1 - y], 2 * (1 - y) + x
        return send_to(
            src, sum1.at[unit], ssend_sem.at[1, unit], srecv_sem.at[1, unit], (there, blk)
        )

    def add_core(unit, parts):
        landed(sum0.at[unit], srecv_sem.at[0, unit])
        for a in range(2):
            for b in range(2):
                sum0[unit, a, b] = sum0[unit, a, b] + parts[a, b, :, :, core]

    @pl.loop(0, chunks)
    def _(at):
        wdown = jnp.dot(active_t[at], gbranch[...], preferred_element_type=f32)
        wdown = wdown.reshape(8, 4, each, width)
        for part in range(4):
            dparts[part, at // 2, lax.rem(at, 2)] = (
                halves(wdown[:, part]).astype(bf16).reshape(dparts.shape[3:])
            )

    for unit in range(4):
        core_copy(unit, dparts.at[unit]).start()

    @pl.loop(0, chunks)
    def _(at):
        cut = pl.ds(pl.multiple_of(at * width, width), width)

        @pl.when(jnp.logical_or(at == 1, at == 2))
        def _():
            for unit in (2 * at - 2, 2 * at - 1):
                add_core(unit, dparts.at[unit])
                by_core(core, lambda order, unit=unit: axis_copy(unit, order).start())

        gact = times_t(gbranch[...], downw[cut])
        gup = (gact * slopes[at]).astype(bf16)
        small_ref[pl.ds(6 + at, 1)] = column_sum(gup)
        ghid[...] += times_t(gup, upw[:, cut])
        wup = jnp.dot(hlow_t[...], gup, preferred_element_type=f32)
        uparts[at] = halves(wup.reshape(32, each, width)).astype(bf16).reshape(uparts.shape[1:])
        core_copy(4 + at, uparts.at[at]).start()

    small = [0.0, 0.0, 0.0]
    lows = []
    for table in range(sides):
        cut = pl.ds(table * rows, rows)
        grad, normed = ghid[cut], norm1[cut]
        small[1] += column_sum(grad * normed)
        small[2] += column_sum(grad)
        gpre1 = norm_back(grad, normed, inverse1[table], par(1))
        pre_ref[cut] = gpre1
        low = gpre1.astype(bf16)
        small[0] += column_sum(low)
        lows.append(low)
    low = jnp.concatenate(lows, axis=0)
    for at in range(3):
        small_ref[at : at + 1] = small[at]
    small_ref[10:] = jnp.zeros((6, width), f32)
    wouts = []
    for group in range(groups):
        dctx_ref[group] = fold(
            times_t(low, outw_ref[group * cols : (group + 1) * cols]).astype(bf16)
        )
        wout = jnp.dot(unfold(ctx_ref[group]).T, low, preferred_element_type=f32)
        wouts.append(halves(wout.reshape(8, each, width)).astype(bf16))
    for unit in range(4):
        core_copy(unit, dparts.at[unit]).wait_send()
    dparts[0] = jnp.concatenate(wouts, axis=0).reshape(dparts.shape[1:])
    keep = [pltpu.make_async_copy(dparts.at[0], parts_ref, keep_sem.at[0])]

    @pl.loop(0, 4)
    def _(at):
        add_core(4 + at, uparts.at[at])
        landed(sum1.at[at], srecv_sem.at[1, at])

        def act(order):
            sum1[at] = sum1[at] + (sum0[at, :, x] if order == 0 else sum0[at, y])
            axis_copy(at, order).wait_send()

        by_core(core, act)
        core_copy(4 + at, uparts.at[at]).wait_send()

    keep.append(pltpu.make_async_copy(sum1, down_ref, keep_sem.at[1]))
    keep.append(pltpu.make_async_copy(sum0.at[4:], up_ref, keep_sem.at[2]))
    for copy in keep:
        copy.start()
    return_rows(out, layer_ref, osend_sem, orecv_sem, "wait")
    for copy in keep:
        copy.wait()


def ffn(tokens, ctx, cotangent, params, out_weight, up_weight, down_weight):
    total, width = tokens.shape
    chunks = up_weight.shape[1] // width
    unit = (2 * (width // 32), width // 2)
    any_space = pl.BlockSpec(memory_space=pl.ANY)
    vmem = pl.BlockSpec(memory_space=pltpu.VMEM)
    bf16, f32 = jnp.bfloat16, jnp.float32
    flops = 18 * total * width * chunks * width + 6 * total * width * width
    return pl.pallas_call(
        ffn_kernel,
        name="ffn",
        out_shape=(
            jax.ShapeDtypeStruct((2, total // 2, width), bf16),
            jax.ShapeDtypeStruct(ctx.shape, bf16),
            jax.ShapeDtypeStruct((total, width), f32),
            jax.ShapeDtypeStruct((16, width), f32),
            jax.ShapeDtypeStruct((4, 2, 2, 2, *unit), bf16),
            jax.ShapeDtypeStruct((4, 2, 2, 2, 2, *unit), bf16),
            jax.ShapeDtypeStruct((2, 2, 2, 2, 2, *unit), bf16),
        ),
        in_specs=[vmem, vmem, vmem, vmem, vmem, any_space, any_space],
        out_specs=(any_space, vmem, vmem, vmem, any_space, any_space, any_space),
        scratch_shapes=[
            pltpu.VMEM(up_weight.shape, bf16),
            pltpu.VMEM(down_weight.shape, bf16),
            pltpu.VMEM((total, width), f32),
            pltpu.VMEM((total, width), bf16),
            pltpu.VMEM((width, total), bf16),
            pltpu.VMEM((total, width), f32),
            pltpu.VMEM((chunks, total, width), f32),
            pltpu.VMEM((chunks, width, total), bf16),
            pltpu.VMEM((total, width), f32),
            pltpu.VMEM((total, width), bf16),
            pltpu.VMEM((total, width), f32),
            pltpu.VMEM((2, total // 2, width), bf16),
            pltpu.VMEM((4, 2, 2, 2, 2, 2, *unit), bf16),
            pltpu.VMEM((4, 2, 2, 2, 2, 2, *unit), bf16),
            pltpu.VMEM((8, 2, 2, 2, 2, *unit), bf16),
            pltpu.VMEM((4, 2, 2, 2, *unit), bf16),
            pltpu.SemaphoreType.DMA((2,)),
            pltpu.SemaphoreType.DMA((3,)),
            pltpu.SemaphoreType.DMA((2,)),
            pltpu.SemaphoreType.DMA((2,)),
            pltpu.SemaphoreType.DMA((2, 8)),
            pltpu.SemaphoreType.DMA((2, 8)),
        ],
        compiler_params=pltpu.CompilerParams(
            collective_id=3, has_side_effects=True, vmem_limit_bytes=63 << 20
        ),
        cost_estimate=pl.CostEstimate(
            flops=flops, bytes_accessed=40 << 20, transcendentals=total * width * chunks
        ),
    )(tokens, ctx, cotangent, params, out_weight, up_weight, down_weight)


def shards_direct(
    tokens,
    lengths,
    qkv_weight,
    qkv_bias,
    out_weight,
    out_bias,
    attn_gain,
    attn_shift,
    up_weight,
    up_bias,
    down_weight,
    down_bias,
    ffn_gain,
    ffn_shift,
    cotangent,
):
    tables, rows, width = tokens.shape
    f32 = jnp.float32
    heads = width // HD // GROUPS
    row = lax.broadcasted_iota(jnp.int32, (32, width), 0)
    params = jnp.zeros((32, width), jnp.bfloat16)
    spans = [
        (at, at + 1, vector)
        for at, vector in enumerate(
            (out_bias, attn_gain, attn_shift, down_bias, ffn_gain, ffn_shift)
        )
    ]
    spans += [(8, 16, qkv_bias[:width]), (16, 24, qkv_bias[width:])]
    spans += [
        (24 + at, 25 + at, up_bias[at * width : (at + 1) * width])
        for at in range(up_bias.shape[0] // width)
    ]
    for first, last, vector in spans:
        params = jnp.where((row >= first) & (row < last), vector[None], params)

    params = params.astype(f32)
    ctx, my_tokens, my_cotangent, full_t, qkv, ot, lse, by_head = attend(
        tokens, lengths, params, qkv_weight, cotangent, heads
    )
    layer_out, dctx, pre, small, down, up, parts = ffn(
        my_tokens.reshape(tables * rows, width),
        ctx,
        my_cotangent.reshape(tables * rows, width),
        params,
        out_weight,
        up_weight,
        down_weight,
    )
    *whole, little = attend_back(
        dctx, qkv, ot, lse, full_t, by_head, pre, small, down, up, parts, heads
    )
    each = width // 32
    whole.insert(1, layer_out)
    (
        token_grad,
        layer_out,
        wgrad_qkv,
        wgrad_out,
        wgrad_up,
        wgrad_down,
        bgrad_out,
        ggrad_attn,
        sgrad_attn,
        bgrad_down,
        ggrad_ffn,
        sgrad_ffn,
        bgrad_up,
        bgrad_qkv,
    ) = finish(whole, little, [each] * 6 + [4 * each, 2 * each])
    return (
        layer_out,
        token_grad,
        wgrad_qkv,
        bgrad_qkv,
        wgrad_out,
        bgrad_out,
        ggrad_attn,
        sgrad_attn,
        wgrad_up,
        bgrad_up,
        wgrad_down,
        bgrad_down,
        ggrad_ffn,
        sgrad_ffn,
    )


def solution(mesh):
    in_specs = (
        P("tab", "blk", None),
        P("tab"),
        P(),
        P(),
        P(),
        P(),
        P(),
        P(),
        P(),
        P(),
        P(),
        P(),
        P(),
        P(),
        P("tab", "blk", None),
    )
    out_specs = (
        P("tab", "blk", None),
        P("tab", "blk", None),
        P(("tab", "blk"), None),
        P(("tab", "blk")),
        P(("tab", "blk"), None),
        P(("tab", "blk")),
        P(("tab", "blk")),
        P(("tab", "blk")),
        P(("tab", "blk"), None),
        P(("tab", "blk")),
        P(("tab", "blk"), None),
        P(("tab", "blk")),
        P(("tab", "blk")),
        P(("tab", "blk")),
    )
    tab_count, blk_count = mesh.shape["tab"], mesh.shape["blk"]

    def pick(*operands):
        table_count = operands[0].shape[0] // tab_count
        head_count = operands[0].shape[2] // HD
        direct = table_count == 2 and blk_count == 8 and tab_count == 4 and head_count % 4 == 0
        body = shards_direct if direct else shards_ring
        return jax.shard_map(
            body, mesh=mesh, in_specs=in_specs, out_specs=out_specs, check_vma=False
        )(*operands)

    return pick
```

```python
import functools
import math

import jax
import jax.numpy as jnp
from jax import lax
from jax.experimental import pallas as pl
from jax.experimental.pallas import tpu as pltpu
from jax.sharding import PartitionSpec as P

HD = 64


EPSILON = 1e-05
NEGATIVE = -1e30


def from_behind(block, axis, distance):
    devices = range(lax.axis_size(axis))
    route = [((i - distance) % len(devices), i) for i in devices]
    return lax.ppermute(block, axis, route)


def norm_rows(inputs, gains, shifts):
    row_mean = jnp.mean(inputs, axis=-1, keepdims=True)
    centred = inputs - row_mean
    row_var = jnp.mean(centred * centred, axis=-1, keepdims=True)
    return centred * lax.rsqrt(row_var + EPSILON) * gains + shifts


def gelu_exact(inputs):
    return jax.nn.gelu(inputs, approximate=False)


def times_back(left, right):
    return lax.dot_general(
        left, right, (((1,), (1,)), ((), ())), preferred_element_type=jnp.float32
    )


def over_rows(left, right):
    return lax.dot_general(
        left, right, (((0,), (0,)), ((), ())), preferred_element_type=jnp.float32
    )


def shards_ring(
    tokens,
    lengths,
    qkv_weight,
    qkv_bias,
    out_weight,
    out_bias,
    attn_gain,
    attn_shift,
    up_weight,
    up_bias,
    down_weight,
    down_bias,
    ffn_gain,
    ffn_shift,
    cotangent,
):
    table_count, row_count, model_width = tokens.shape
    head_count = model_width // HD
    cycle_size = lax.axis_size("blk")
    cycle_place = lax.axis_index("blk")
    score_scale = HD ** (-0.5)
    flat_tokens = tokens.reshape(table_count * row_count, model_width)
    bias_full = jnp.concatenate(
        [
            qkv_bias[:model_width].astype(jnp.float32),
            jnp.zeros((model_width,), jnp.float32),
            qkv_bias[model_width:].astype(jnp.float32),
        ]
    )
    qkv_low = (
        jnp.dot(flat_tokens, qkv_weight, preferred_element_type=jnp.float32) + bias_full
    ).astype(jnp.bfloat16)
    queries = qkv_low[:, :model_width].reshape(table_count, row_count, head_count, HD)
    key_values = qkv_low[:, model_width:].reshape(table_count, row_count, 2 * model_width)

    def key_mask(first_row, key_count):
        positions = first_row + jnp.arange(key_count, dtype=jnp.int32)
        return (positions[None, :] < lengths[:, None])[:, None, None, :]

    def split_pair(pair_block):
        key_count = pair_block.shape[1]
        keys_part = pair_block[:, :, :model_width].reshape(table_count, key_count, head_count, HD)
        values_part = pair_block[:, :, model_width:].reshape(table_count, key_count, head_count, HD)
        return (keys_part, values_part)

    pair_block = lax.all_gather(key_values, "blk", axis=1, tiled=True)
    running_max = jnp.full((table_count, row_count, head_count), NEGATIVE, jnp.float32)
    keys_part, values_part = split_pair(pair_block)
    is_valid = key_mask(jnp.int32(0), pair_block.shape[1])
    raw_scores = jnp.einsum(
        "trhd,tkhd->trhk", queries, keys_part, preferred_element_type=jnp.float32
    )
    scores = jnp.where(is_valid, raw_scores * score_scale, NEGATIVE)
    peak_new = jnp.maximum(running_max, jnp.max(scores, axis=-1))
    exponent = jnp.where(is_valid, jnp.exp(scores - peak_new[..., None]), 0.0)
    running_sum = jnp.sum(exponent, axis=-1)
    weighted = jnp.einsum(
        "trhk,tkhd->trhd",
        exponent.astype(jnp.bfloat16),
        values_part,
        preferred_element_type=jnp.float32,
    )
    running_max, running_sum, weighted = (peak_new, running_sum, weighted)
    context = weighted / running_sum[..., None]
    log_total = running_max + jnp.log(running_sum)
    context_low = context.reshape(table_count * row_count, model_width).astype(jnp.bfloat16)
    attended = jnp.dot(
        context_low, out_weight, preferred_element_type=jnp.float32
    ) + out_bias.astype(jnp.float32)
    pre_one = flat_tokens.astype(jnp.float32) + attended
    gain_one = attn_gain.astype(jnp.float32)
    shift_one = attn_shift.astype(jnp.float32)
    hidden = norm_rows(pre_one, gain_one, shift_one)
    hidden_low = hidden.astype(jnp.bfloat16)
    upper = jnp.dot(hidden_low, up_weight, preferred_element_type=jnp.float32) + up_bias.astype(
        jnp.float32
    )
    active = gelu_exact(upper).astype(jnp.bfloat16)
    pre_two = (
        hidden
        + jnp.dot(active, down_weight, preferred_element_type=jnp.float32)
        + down_bias.astype(jnp.float32)
    )
    gain_two = ffn_gain.astype(jnp.float32)
    shift_two = ffn_shift.astype(jnp.float32)
    layer_out = norm_rows(pre_two, gain_two, shift_two).astype(jnp.bfloat16).reshape(tokens.shape)
    grad_out = cotangent.reshape(table_count * row_count, model_width).astype(jnp.float32)
    _, norm_two_back = jax.vjp(norm_rows, pre_two, gain_two, shift_two)
    grad_pre_two, ggrad_ffn, sgrad_ffn = norm_two_back(grad_out)
    grad_branch = grad_pre_two.astype(jnp.bfloat16)
    wgrad_down = over_rows(active, grad_branch)
    bgrad_down = jnp.sum(grad_branch, axis=0, dtype=jnp.float32)
    grad_active = times_back(grad_branch, down_weight)
    _, gelu_back = jax.vjp(gelu_exact, upper)
    grad_upper = gelu_back(grad_active)[0].astype(jnp.bfloat16)
    wgrad_up = over_rows(hidden_low, grad_upper)
    bgrad_up = jnp.sum(grad_upper, axis=0, dtype=jnp.float32)
    grad_hidden = grad_pre_two + times_back(grad_upper, up_weight)
    _, norm_one_back = jax.vjp(norm_rows, pre_one, gain_one, shift_one)
    grad_pre_one, ggrad_attn, sgrad_attn = norm_one_back(grad_hidden)
    grad_attended = grad_pre_one.astype(jnp.bfloat16)
    wgrad_out = over_rows(context_low, grad_attended)
    bgrad_out = jnp.sum(grad_attended, axis=0, dtype=jnp.float32)
    grad_context = times_back(grad_attended, out_weight).astype(jnp.bfloat16)
    grad_heads = grad_context.reshape(table_count, row_count, head_count, HD)
    row_delta = jnp.sum(grad_heads.astype(jnp.float32) * context, axis=-1)

    def cycle_turn_step(cycle_turn, cycle_state):
        pair_now, pair_grads, grad_queries = cycle_state
        owner_index = (cycle_place - cycle_turn) % cycle_size
        keys_part, values_part = split_pair(pair_now)
        is_valid = key_mask(owner_index * row_count, row_count)
        raw_scores = jnp.einsum(
            "trhd,tkhd->trhk", queries, keys_part, preferred_element_type=jnp.float32
        )
        scores = jnp.where(is_valid, raw_scores * score_scale, NEGATIVE)
        probs = jnp.where(is_valid, jnp.exp(scores - log_total[..., None]), 0.0)
        grad_probs = jnp.einsum(
            "trhd,tkhd->trhk", grad_heads, values_part, preferred_element_type=jnp.float32
        )
        grad_raw = (probs * (grad_probs - row_delta[..., None]) * score_scale).astype(jnp.bfloat16)
        grad_queries = grad_queries + jnp.einsum(
            "trhk,tkhd->trhd", grad_raw, keys_part, preferred_element_type=jnp.float32
        )
        grad_keys = jnp.einsum(
            "trhk,trhd->tkhd", grad_raw, queries, preferred_element_type=jnp.float32
        )
        grad_values = jnp.einsum(
            "trhk,trhd->tkhd",
            probs.astype(jnp.bfloat16),
            grad_heads,
            preferred_element_type=jnp.float32,
        )
        pair_grads = pair_grads + jnp.concatenate(
            [
                grad_keys.reshape(table_count, row_count, model_width),
                grad_values.reshape(table_count, row_count, model_width),
            ],
            axis=-1,
        )
        pair_next = from_behind(pair_now, "blk", 1)
        grads_next = from_behind(pair_grads.astype(jnp.bfloat16), "blk", 1).astype(pair_grads.dtype)
        return (pair_next, grads_next, grad_queries)

    cycle_start = (
        key_values,
        jnp.zeros((table_count, row_count, 2 * model_width), jnp.float32),
        jnp.zeros((table_count, row_count, head_count, HD), jnp.float32),
    )
    _, pair_home, grad_queries = lax.fori_loop(0, cycle_size, cycle_turn_step, cycle_start)
    grad_qkv = jnp.concatenate(
        [
            grad_queries.reshape(table_count * row_count, model_width),
            pair_home.reshape(table_count * row_count, 2 * model_width),
        ],
        axis=-1,
    ).astype(jnp.bfloat16)
    wgrad_qkv = over_rows(flat_tokens, grad_qkv)
    column_sums = jnp.sum(grad_qkv, axis=0, dtype=jnp.float32)
    bgrad_qkv = jnp.concatenate([column_sums[:model_width], column_sums[2 * model_width :]])
    token_grad = (
        (grad_pre_one + times_back(grad_qkv, qkv_weight)).astype(jnp.bfloat16).reshape(tokens.shape)
    )
    (
        wgrad_qkv,
        bgrad_qkv,
        wgrad_out,
        bgrad_out,
        ggrad_attn,
        sgrad_attn,
        wgrad_up,
        bgrad_up,
        wgrad_down,
        bgrad_down,
        ggrad_ffn,
        sgrad_ffn,
    ) = (
        lax.psum_scatter(
            wgrad_qkv.astype(jnp.bfloat16), "tab", scatter_dimension=0, tiled=True
        ).astype(jnp.float32),
        lax.psum_scatter(
            bgrad_qkv.astype(jnp.bfloat16), "tab", scatter_dimension=0, tiled=True
        ).astype(jnp.float32),
        lax.psum_scatter(
            wgrad_out.astype(jnp.bfloat16), "tab", scatter_dimension=0, tiled=True
        ).astype(jnp.float32),
        lax.psum_scatter(
            bgrad_out.astype(jnp.bfloat16), "tab", scatter_dimension=0, tiled=True
        ).astype(jnp.float32),
        lax.psum_scatter(
            ggrad_attn.astype(jnp.bfloat16), "tab", scatter_dimension=0, tiled=True
        ).astype(jnp.float32),
        lax.psum_scatter(
            sgrad_attn.astype(jnp.bfloat16), "tab", scatter_dimension=0, tiled=True
        ).astype(jnp.float32),
        lax.psum_scatter(
            wgrad_up.astype(jnp.bfloat16), "tab", scatter_dimension=0, tiled=True
        ).astype(jnp.float32),
        lax.psum_scatter(
            bgrad_up.astype(jnp.bfloat16), "tab", scatter_dimension=0, tiled=True
        ).astype(jnp.float32),
        lax.psum_scatter(
            wgrad_down.astype(jnp.bfloat16), "tab", scatter_dimension=0, tiled=True
        ).astype(jnp.float32),
        lax.psum_scatter(
            bgrad_down.astype(jnp.bfloat16), "tab", scatter_dimension=0, tiled=True
        ).astype(jnp.float32),
        lax.psum_scatter(
            ggrad_ffn.astype(jnp.bfloat16), "tab", scatter_dimension=0, tiled=True
        ).astype(jnp.float32),
        lax.psum_scatter(
            sgrad_ffn.astype(jnp.bfloat16), "tab", scatter_dimension=0, tiled=True
        ).astype(jnp.float32),
    )
    (
        wgrad_qkv,
        bgrad_qkv,
        wgrad_out,
        bgrad_out,
        ggrad_attn,
        sgrad_attn,
        wgrad_up,
        bgrad_up,
        wgrad_down,
        bgrad_down,
        ggrad_ffn,
        sgrad_ffn,
    ) = (
        lax.psum_scatter(
            wgrad_qkv.astype(jnp.bfloat16), "blk", scatter_dimension=0, tiled=True
        ).astype(jnp.float32),
        lax.psum_scatter(
            bgrad_qkv.astype(jnp.bfloat16), "blk", scatter_dimension=0, tiled=True
        ).astype(jnp.float32),
        lax.psum_scatter(
            wgrad_out.astype(jnp.bfloat16), "blk", scatter_dimension=0, tiled=True
        ).astype(jnp.float32),
        lax.psum_scatter(
            bgrad_out.astype(jnp.bfloat16), "blk", scatter_dimension=0, tiled=True
        ).astype(jnp.float32),
        lax.psum_scatter(
            ggrad_attn.astype(jnp.bfloat16), "blk", scatter_dimension=0, tiled=True
        ).astype(jnp.float32),
        lax.psum_scatter(
            sgrad_attn.astype(jnp.bfloat16), "blk", scatter_dimension=0, tiled=True
        ).astype(jnp.float32),
        lax.psum_scatter(
            wgrad_up.astype(jnp.bfloat16), "blk", scatter_dimension=0, tiled=True
        ).astype(jnp.float32),
        lax.psum_scatter(
            bgrad_up.astype(jnp.bfloat16), "blk", scatter_dimension=0, tiled=True
        ).astype(jnp.float32),
        lax.psum_scatter(
            wgrad_down.astype(jnp.bfloat16), "blk", scatter_dimension=0, tiled=True
        ).astype(jnp.float32),
        lax.psum_scatter(
            bgrad_down.astype(jnp.bfloat16), "blk", scatter_dimension=0, tiled=True
        ).astype(jnp.float32),
        lax.psum_scatter(
            ggrad_ffn.astype(jnp.bfloat16), "blk", scatter_dimension=0, tiled=True
        ).astype(jnp.float32),
        lax.psum_scatter(
            sgrad_ffn.astype(jnp.bfloat16), "blk", scatter_dimension=0, tiled=True
        ).astype(jnp.float32),
    )
    return (
        layer_out,
        token_grad,
        wgrad_qkv,
        bgrad_qkv,
        wgrad_out,
        bgrad_out,
        ggrad_attn,
        sgrad_attn,
        wgrad_up,
        bgrad_up,
        wgrad_down,
        bgrad_down,
        ggrad_ffn,
        sgrad_ffn,
    )


GROUPS = 4
LANES = 128
LOG2E = math.log2(math.e)
MESH = pl.DeviceIdType.MESH


def times_t(left, right):
    return lax.dot_general(
        left, right, (((1,), (1,)), ((), ())), preferred_element_type=jnp.float32
    )


def place():
    tab, blk = lax.axis_index("tab"), lax.axis_index("blk")
    return tab, blk, blk // 2, blk % 2


def meet(tab, blk):
    barrier = pltpu.get_barrier_semaphore()

    @pl.loop(1, 8)
    def _(step):
        pl.semaphore_signal(
            barrier, inc=1, device_id=(tab, lax.rem(blk + step, 8)), device_id_type=MESH
        )

    pl.semaphore_wait(barrier, 7)


def greet_all(tab, blk):
    barrier = pltpu.get_barrier_semaphore()
    for step in range(1, 8):
        pl.semaphore_signal(
            barrier, inc=1, device_id=(tab, lax.rem(blk + step, 8)), device_id_type=MESH
        )
    for step in range(1, 4):
        pl.semaphore_signal(
            barrier, inc=1, device_id=(lax.rem(tab + step, 4), blk), device_id_type=MESH
        )
    pl.semaphore_wait(barrier, 10)


def send_to(src, dst, send_sem, recv_sem, device):
    return pltpu.make_async_remote_copy(
        src_ref=src,
        dst_ref=dst,
        send_sem=send_sem,
        recv_sem=recv_sem,
        device_id=device,
        device_id_type=MESH,
    )


def landed(ref, sem):
    pltpu.make_async_copy(ref, ref, sem).wait()


def return_rows(src, dst, send_sem, recv_sem, act):
    tab, _, chip, core = place()
    half, group = chip // 2, 2 * lax.rem(chip, 2) + core
    for side in range(2):
        is_own = jnp.logical_and(chip == group, core == side)
        own = pltpu.make_async_copy(src.at[side], dst.at[half], recv_sem.at[half])
        away = send_to(
            src.at[side],
            dst.at[half],
            send_sem.at[side],
            recv_sem.at[half],
            (tab, 2 * group + side),
        )
        if act == "start":
            pl.when(is_own)(own.start)
            pl.when(jnp.logical_not(is_own))(away.start)
        else:
            pl.when(jnp.logical_not(is_own))(away.wait_send)
            landed(dst.at[side], recv_sem.at[side])


def by_core(core, act):
    pl.when(core == 0)(functools.partial(act, 0))
    pl.when(core == 1)(functools.partial(act, 1))


def fold(block):
    cut = block.shape[0] // 2
    return jnp.concatenate([block[:cut], block[cut:]], axis=1)


def unfold(block):
    cut = block.shape[1] // 2
    return jnp.concatenate([block[:, :cut], block[:, cut:]], axis=0)


def own_window(group, first, rows_ref, out):
    start = pl.multiple_of(first + LANES * ((3 * group) // 2), LANES)
    window = rows_ref[:, pl.ds(start, 2 * LANES)].astype(jnp.float32)
    window = pltpu.roll(window, lax.rem(2 * LANES - HD * lax.rem(group, 2), 2 * LANES), 1)
    left = window[:, :LANES]
    low = lax.broadcasted_iota(jnp.int32, left.shape, 1) < HD
    for head, lanes in enumerate((left, pltpu.roll(left, HD, 1), window[:, LANES:])):
        out(head, jnp.where(low, lanes, 0.0))


def attend_kernel(
    heads,
    tok_ref,
    len_ref,
    par_ref,
    w_hbm,
    cot_hbm,
    ctx_ref,
    mytok_ref,
    mycot_ref,
    fullt_ref,
    qkv_ref,
    ot_ref,
    lse_ref,
    wr_ref,
    tokv,
    toktv,
    wfull,
    wrv,
    wown,
    bown,
    qkvv,
    vtv,
    otv,
    lsev,
    acc,
    peaks,
    csend,
    send_sem,
    recv,
    csend_sem,
    crecv_sem,
    osend_sem,
    orecv_sem,
    local_sem,
):
    tab, blk, chip, core = place()
    half = chip // 2
    group = 2 * lax.rem(chip, 2) + core
    rows = tok_ref.shape[1]
    width = tok_ref.shape[2]
    is_near = jnp.logical_or(chip == 1, chip == 2)
    mate = chip + 1 - 2 * lax.rem(chip, 2)
    other_near = 2 - half
    other_far = 3 - 3 * half
    own_far = 3 * half
    scale = LOG2E / math.sqrt(HD)

    def remote(src, dst, send_sem, recv_sem, to_chip, to_core):
        return pltpu.make_async_remote_copy(
            src_ref=src,
            dst_ref=dst,
            send_sem=send_sem,
            recv_sem=recv_sem,
            device_id=(tab, 2 * to_chip + to_core),
            device_id_type=MESH,
        )

    here, there = tok_ref.at[half], tok_ref.at[1 - half]
    to_mate = remote(here, tokv.at[blk], send_sem.at[0], recv.at[blk], mate, core)
    to_other = remote(there, tokv.at[blk], send_sem.at[1], recv.at[blk], other_near, core)
    to_side = remote(here, tokv.at[blk], send_sem.at[2], recv.at[blk], chip, 1 - core)

    def to_far(slot, src_chip):
        which = 2 * src_chip + core
        ref = tokv.at[which]
        return remote(ref, ref, send_sem.at[2 + slot], recv.at[which], own_far, core)

    def to_core(slot, src_chip):
        which = 2 * src_chip + core
        ref = tokv.at[which]
        return remote(ref, ref, send_sem.at[5 + slot], recv.at[which], chip, 1 - core)

    def arrived(which):
        pltpu.make_async_copy(tokv.at[which], tokv.at[which], recv.at[which]).wait()

    load = pltpu.make_async_copy(w_hbm, wfull, local_sem.at[5])
    load.start()
    meet(tab, blk)
    pl.when(is_near)(to_other.start)
    to_mate.start()
    to_side.start()
    tokv[blk] = tok_ref[half]

    lane1 = lax.broadcasted_iota(jnp.int32, (8, LANES), 1)
    for at in (0, 2):

        def keep_bias(head, lanes, at=at):
            row = jnp.where(lane1 == HD, 1.0, lanes)
            bown[:, pl.ds((at * heads + head) * LANES, LANES)] = row

        own_window(group, 0, par_ref.at[pl.ds(8 * (1 + at // 2), 8)], keep_bias)
    for head in range(heads):
        bown[:, pl.ds((heads + head) * LANES, LANES)] = jnp.zeros((8, LANES), jnp.float32)
    load.wait()
    for at in range(3):

        def keep_weight(head, lanes, at=at):
            wown[:, pl.ds((at * heads + head) * LANES, LANES)] = lanes.astype(jnp.bfloat16)

        own_window(group, at * width, wfull, keep_weight)

    length = len_ref[half]
    lane = lax.broadcasted_iota(jnp.int32, (rows, LANES), 1)
    row = lax.broadcasted_iota(jnp.int32, (rows, LANES), 0)

    def project(which):
        first = pl.multiple_of(which * rows, rows)
        tok = tokv[which]
        y = jnp.dot(tok, wown[...], preferred_element_type=jnp.float32) + bown[:1]
        pad = jnp.where((lane == HD) & (row + first >= length), NEGATIVE, 0.0)
        for head in range(heads):
            q, k, v = (
                y[:, (part * heads + head) * LANES :][:, :LANES] for part in range(3)
            )
            qkvv[head, pl.ds(first, rows)] = q.astype(jnp.bfloat16)
            qkvv[heads + head, pl.ds(first, rows)] = (k + pad).astype(jnp.bfloat16)
            qkvv[2 * heads + head, pl.ds(first, rows)] = v.astype(jnp.bfloat16)
            vtv[head, :, pl.ds(first, rows)] = v.T.astype(jnp.bfloat16)
        toktv[:, pl.ds(first, rows)] = tok.T

    def take_keys(tile, head, first_key, count, fresh):
        queries = pl.ds(pl.multiple_of(tile * 2 * rows, 2 * rows), 2 * rows)
        keys = pl.ds(pl.multiple_of(first_key, count), count)
        st = times_t(qkvv[heads + head, keys], qkvv[head, queries])
        peak = jnp.max(st, axis=0, keepdims=True)
        if not fresh:
            before = peaks[tile, pl.ds(head, 1)]
            peak = jnp.maximum(peak, before)
        pt = jnp.exp2((st - peak) * scale).astype(jnp.bfloat16)
        ot = jnp.dot(vtv[head, :, keys], pt, preferred_element_type=jnp.float32)
        if not fresh:
            ot += acc[tile, head] * jnp.exp2((before - peak) * scale)
        acc[tile, head] = ot
        peaks[tile, pl.ds(head, 1)] = peak

    def meet_keys_of_own_half():
        @pl.loop(0, 2 * heads)
        def _(at):
            tile = jnp.where(at < heads, chip, mate)
            take_keys(tile, lax.rem(at, heads), half * 4 * rows, 4 * rows, True)

    def meet_keys_of_near():
        @pl.loop(0, heads)
        def _(head):
            take_keys(other_near, head, half * 4 * rows, 4 * rows, True)

        @pl.loop(0, 3 * heads)
        def _(at):
            tile = jnp.where(at < heads, chip, jnp.where(at < 2 * heads, mate, other_near))
            take_keys(tile, lax.rem(at, heads), other_near * 2 * rows, 2 * rows, False)

    project(blk)

    def half_lanes(part, at):
        first = part * width + LANES * (at // 2)
        return wfull[:, first : first + LANES][:, HD * (at % 2) :][:, :HD]

    for head in range(heads):
        for part in range(3):
            for pair in range(GROUPS // 2):
                at = 2 * pair * heads + head
                wrv[head, :, pl.ds((2 * part + pair) * LANES, LANES)] = jnp.concatenate(
                    [half_lanes(part, at), half_lanes(part, at + heads)], axis=1
                )
    arrived(2 * mate + core)
    to_core(0, mate).start()

    @pl.when(jnp.logical_not(is_near))
    def _():
        to_mate.wait_send()
        to_other.start()

    project(2 * mate + core)
    arrived(2 * chip + 1 - core)
    project(2 * chip + 1 - core)
    arrived(2 * mate + 1 - core)
    project(2 * mate + 1 - core)

    def pass_on(slot, src_chip):
        arrived(2 * src_chip + core)
        pl.when(is_near)(to_far(slot, src_chip).start)
        to_core(slot, src_chip).start()

    def project_chip(src_chip):
        project(2 * src_chip + core)
        arrived(2 * src_chip + 1 - core)
        project(2 * src_chip + 1 - core)

    def owner_of(table):
        return 2 * table + chip // 2, lax.rem(chip, 2)

    def cotangent_copy(table, own):
        src, dst = cot_hbm.at[table], mycot_ref.at[core]
        if own:
            return pltpu.make_async_copy(src, dst, orecv_sem.at[core])
        return remote(src, dst, osend_sem.at[table], orecv_sem.at[core], *owner_of(table))

    def is_owner(table):
        to_chip, to_core = owner_of(table)
        return jnp.logical_and(to_chip == chip, to_core == core)

    pl.when(is_near)(functools.partial(pass_on, 1, other_near))
    meet_keys_of_own_half()
    pl.when(jnp.logical_not(is_near))(functools.partial(pass_on, 1, other_near))
    pl.when(is_near)(functools.partial(pass_on, 2, other_far))
    cotangent_copy(1 - half, False).start()
    project_chip(other_near)
    meet_keys_of_near()
    pl.when(jnp.logical_not(is_near))(functools.partial(pass_on, 2, other_far))
    project_chip(other_far)

    keep = (
        pltpu.make_async_copy(toktv, fullt_ref, local_sem.at[0]),
        pltpu.make_async_copy(qkvv, qkv_ref, local_sem.at[1]),
        pltpu.make_async_copy(wrv, wr_ref, local_sem.at[6]),
    )
    for copy in keep:
        copy.start()

    pl.when(is_owner(half))(cotangent_copy(half, True).start)
    pl.when(jnp.logical_not(is_owner(half)))(cotangent_copy(half, False).start)
    my_tokens = [
        pltpu.make_async_copy(
            tokv.at[2 * group + side], mytok_ref.at[side], local_sem.at[7 + side]
        )
        for side in range(2)
    ]
    for copy in my_tokens:
        copy.start()

    def context_copy(which):
        return remote(
            csend.at[which],
            ctx_ref.at[group],
            csend_sem.at[which],
            crecv_sem.at[group],
            2 * half + which // 2,
            lax.rem(which, 2),
        )

    own_context = pltpu.make_async_copy(
        csend.at[group], ctx_ref.at[group], local_sem.at[2]
    )

    @pl.loop(0, 4)
    def _(step):
        at = jnp.where(is_near, step, 3 - step)
        which = jnp.where(
            at < 2, jnp.where(at == 0, chip, mate), jnp.where(at == 2, other_near, other_far)
        )

        @pl.when(at == 3)
        def _():
            @pl.loop(0, heads)
            def _(head):
                take_keys(which, head, 0, 8 * rows, True)

        @pl.when(at < 3)
        def _():
            @pl.loop(0, heads)
            def _(head):
                take_keys(which, head, other_far * 2 * rows, 2 * rows, False)

        for head in range(heads):
            ot = acc[which, head]
            total = ot[HD : HD + 1]
            otv[which, head * HD : (head + 1) * HD] = ot[:HD] / total
            peak = peaks[which, head : head + 1]
            lsev[which, head : head + 1] = peak * scale + jnp.log(total) * LOG2E
        csend[which] = fold(otv[which].T.astype(jnp.bfloat16))

        pl.when(which == group)(own_context.start)
        pl.when(which != group)(context_copy(which).start)

    more = (
        pltpu.make_async_copy(otv, ot_ref, local_sem.at[3]),
        pltpu.make_async_copy(lsev, lse_ref, local_sem.at[4]),
    )
    for copy in more:
        copy.start()
    pl.when(is_near)(to_mate.wait_send)
    to_other.wait_send()
    to_side.wait_send()
    to_core(0, mate).wait_send()
    for slot, src_chip in ((1, other_near), (2, other_far)):
        pl.when(is_near)(to_far(slot, src_chip).wait_send)
        to_core(slot, src_chip).wait_send()

    for step in range(1, 4):
        which = lax.rem(group + step, 4)
        context_copy(which).wait_send()
        pltpu.make_async_copy(ctx_ref.at[which], ctx_ref.at[which], crecv_sem.at[which]).wait()
    own_context.wait()
    pl.when(jnp.logical_not(is_owner(half)))(cotangent_copy(half, False).wait_send)
    cotangent_copy(1 - half, False).wait_send()
    for side in range(2):
        pltpu.make_async_copy(mycot_ref.at[side], mycot_ref.at[side], orecv_sem.at[side]).wait()
    for copy in [*keep, *more, *my_tokens]:
        copy.wait()


def attend(tokens, lengths, params, qkv_weight, cotangent, heads):
    _, rows, width = tokens.shape
    blocks = 8
    total = blocks * rows
    any_space = pl.BlockSpec(memory_space=pl.ANY)
    vmem = pl.BlockSpec(memory_space=pltpu.VMEM)
    bf16, f32 = jnp.bfloat16, jnp.float32
    dma = pltpu.SemaphoreType.DMA
    return pl.pallas_call(
        functools.partial(attend_kernel, heads),
        name="attend",
        out_shape=(
            jax.ShapeDtypeStruct((GROUPS, rows, 2 * heads * HD), bf16),
            jax.ShapeDtypeStruct((2, rows, width), bf16),
            jax.ShapeDtypeStruct((2, rows, width), bf16),
            jax.ShapeDtypeStruct((width, total), bf16),
            jax.ShapeDtypeStruct((3 * heads, total, LANES), bf16),
            jax.ShapeDtypeStruct((4, heads * HD, 2 * rows), f32),
            jax.ShapeDtypeStruct((4, 8, 2 * rows), f32),
            jax.ShapeDtypeStruct((heads, width, width), bf16),
        ),
        in_specs=[vmem, pl.BlockSpec(memory_space=pltpu.SMEM), vmem, any_space, any_space],
        out_specs=(any_space,) * 8,
        scratch_shapes=[
            pltpu.VMEM((blocks, rows, width), bf16),
            pltpu.VMEM((width, total), bf16),
            pltpu.VMEM(qkv_weight.shape, bf16),
            pltpu.VMEM((heads, width, width), bf16),
            pltpu.VMEM((width, 3 * heads * LANES), bf16),
            pltpu.VMEM((8, 3 * heads * LANES), f32),
            pltpu.VMEM((3 * heads, total, LANES), bf16),
            pltpu.VMEM((heads, LANES, total), bf16),
            pltpu.VMEM((4, heads * HD, 2 * rows), f32),
            pltpu.VMEM((4, 8, 2 * rows), f32),
            pltpu.VMEM((4, heads, LANES, 2 * rows), f32),
            pltpu.VMEM((4, 8, 2 * rows), f32),
            pltpu.VMEM((GROUPS, rows, 2 * heads * HD), bf16),
            dma((8,)),
            dma((blocks,)),
            dma((GROUPS,)),
            dma((GROUPS,)),
            dma((2,)),
            dma((2,)),
            dma((9,)),
        ],
        compiler_params=pltpu.CompilerParams(
            collective_id=1, has_side_effects=True, vmem_limit_bytes=60 << 20
        ),
    )(tokens, lengths, params, qkv_weight, cotangent)


UNITS = 9
TURNS = 4
STAGES = 5
PHASE = ((1, 2), (2, 4), (3, 6), (4, 8))


def attend_back_kernel(
    heads,
    dctx_ref,
    qkv_ref,
    ot_ref,
    lse_ref,
    fullt_ref,
    w_ref,
    pre_ref,
    sums_ref,
    parts_ref,
    small_ref,
    tgrad_ref,
    wqkv_ref,
    wout_ref,
    wup_ref,
    wdown_ref,
    little_ref,
    dov,
    doh,
    deltas,
    qkvv,
    otv,
    lsev,
    toktv,
    wv,
    prev,
    ktv,
    dqv,
    dkv,
    dvv,
    dqkv,
    qsend,
    kvsend,
    arrive_q,
    arrive_kv,
    joined,
    xacc,
    xsend,
    mine,
    sum0,
    sum1,
    sum2,
    sum3,
    sum4,
    slab,
    slab_in,
    sums,
    sums_in,
    line,
    line_in,
    small_in,
    small_sum,
    small_pairs,
    dsend_sem,
    drecv_sem,
    gsend_sem,
    grecv_sem,
    xsend_sem,
    xrecv_sem,
    ssend_sem,
    srecv_sem,
    tsend_sem,
    trecv_sem,
    lsend_sem,
    lrecv_sem,
    local_sem,
    mine_sem,
):
    f32, bf16 = jnp.float32, jnp.bfloat16
    tab, blk, chip, core = place()
    y, x, zh, zl = tab // 2, lax.rem(tab, 2), chip // 2, lax.rem(chip, 2)
    half = zh
    group = 2 * zl + core
    blocks, rows = 8, dov.shape[1]
    width = toktv.shape[0]
    tile = 2 * rows
    piece = 256
    scale = LOG2E / math.sqrt(HD)
    shrink = HD**-0.5

    remote = send_to

    loads = [
        pltpu.make_async_copy(src, dst, local_sem.at[at])
        for at, (src, dst) in enumerate(
            (
                (qkv_ref, qkvv),
                (ot_ref, otv),
                (lse_ref, lsev),
                (dctx_ref.at[group], dov.at[group]),
                (fullt_ref, toktv),
                (w_ref, wv),
                (pre_ref, prev),
                (sums_ref, sum0.at[: UNITS - 1]),
            )
        )
    ]
    for copy in loads:
        copy.start()

    greet_all(tab, blk)

    def group_at(step):
        to_chip = jnp.where(step < 2, zl, 1 - zl)
        return 2 * to_chip + jnp.where(lax.rem(step, 2) == 0, core, 1 - core)

    def context_copy(which):
        return remote(
            dctx_ref.at[which],
            dov.at[group],
            dsend_sem.at[which],
            drecv_sem.at[group],
            (tab, 4 * half + which),
        )

    for step in range(1, 4):
        context_copy(group_at(step)).start()

    def stage_copy(stage, unit, order=None):
        send, done = ssend_sem.at[stage, unit], srecv_sem.at[stage, unit]
        if stage == 0:
            src = parts_ref.at[:, :, :, :, 1 - core]
            return remote(src, sum0.at[unit], send, done, (tab, 2 * chip + 1 - core))
        if stage == 1 and order == 0:
            return remote(
                sum0.at[unit, :, 1 - x], sum1.at[unit], send, done, (2 * y + 1 - x, blk)
            )
        if stage == 1:
            return remote(
                sum0.at[unit, 1 - y], sum1.at[unit], send, done, (2 * (1 - y) + x, blk)
            )
        if stage == 2 and order == 0:
            return remote(
                sum1.at[unit, 1 - y], sum2.at[unit], send, done, (2 * (1 - y) + x, blk)
            )
        if stage == 2:
            return remote(
                sum1.at[unit, 1 - x], sum2.at[unit], send, done, (2 * y + 1 - x, blk)
            )
        if stage == 3:
            src, there = sum2.at[unit, :, 1 - zl], 2 * zh + 1 - zl
            return remote(src, sum3.at[unit], send, done, (tab, 2 * there + core))
        src, there = sum3.at[unit, 1 - zh], 2 * (1 - zh) + zl
        return remote(src, sum4.at[unit], send, done, (tab, 2 * there + core))

    both = functools.partial(by_core, core)
    mine_copy = pltpu.make_async_copy(
        parts_ref.at[:, :, :, :, core], mine, mine_sem.at[0]
    )

    def finish(unit):
        done = sum4[unit].astype(f32) + sum3[unit, zh].astype(f32)
        top, low = done[: done.shape[0] // 2], done[done.shape[0] // 2 :]
        each, cut = top.shape

        @pl.when(unit < 4)
        def _():
            at = pl.ds(pl.multiple_of(unit * each, each), each)
            wdown_ref[at, :cut] = top
            wdown_ref[at, cut:] = low

        @pl.when(jnp.logical_and(unit >= 4, unit < 8))
        def _():
            at = pl.multiple_of((unit - 4) * 2 * cut, 2 * cut)
            wup_ref[:, pl.ds(at, cut)] = top
            wup_ref[:, pl.ds(pl.multiple_of(at + cut, cut), cut)] = low

        @pl.when(unit == 8)
        def _():
            wout_ref[:, :cut] = top
            wout_ref[:, cut:] = low

    def advance(stage, unit):
        if stage == 0:
            landed(sum0.at[unit], srecv_sem.at[0, unit])
            mine_copy.wait()
            for a in range(2):
                for b in range(2):
                    sum0[unit, a, b] = sum0[unit, a, b] + mine[a, b]

            both(lambda order: stage_copy(1, unit, order).start())
        elif stage == 1:
            landed(sum1.at[unit], srecv_sem.at[1, unit])

            def act(order):
                own = sum0[unit, :, x] if order == 0 else sum0[unit, y]
                sum1[unit] = sum1[unit] + own
                stage_copy(2, unit, order).start()

            both(act)
        elif stage == 2:
            landed(sum2.at[unit], srecv_sem.at[2, unit])

            def act(order):
                sum2[unit] = sum2[unit] + sum1[unit, y if order == 0 else x]

            both(act)
            stage_copy(3, unit).start()
        elif stage == 3:
            landed(sum3.at[unit], srecv_sem.at[3, unit])
            sum3[unit] = sum3[unit] + sum2[unit, :, zl]
            stage_copy(4, unit).start()
        else:
            landed(sum4.at[unit], srecv_sem.at[4, unit])
            finish(unit)

    def tick(now):
        @pl.when(now < UNITS - 1)
        def _():
            both(lambda order: stage_copy(1, now, order).start())

        pl.when(now == UNITS - 1)(functools.partial(advance, 0, UNITS - 1))
        for stage, lag in PHASE:
            unit = now - lag
            due = (unit >= 0) & (unit < UNITS)
            pl.when(due)(functools.partial(advance, stage, unit))

    stage_copy(0, UNITS - 1).start()
    mine_copy.start()
    for copy in loads[7:]:
        copy.wait()

    def tab_copy(src, dst, sem_at, step):
        there = lax.rem(tab + step, 4)
        return remote(
            src(there), dst(tab), tsend_sem.at[sem_at, there], trecv_sem.at[sem_at, tab], (there, blk)
        )

    def line_copy(src, dst, sem_at, step):
        there = lax.rem(blk + step, 8)
        return remote(
            src(there), dst(blk), lsend_sem.at[sem_at, there], lrecv_sem.at[sem_at, blk], (tab, there)
        )

    def small_tab(step):
        return tab_copy(lambda t: small_ref, lambda t: small_in.at[t], heads, step)

    def small_pair(at):
        there = (2 * chip + 1 - core, 2 * (2 * zh + 1 - zl) + core, 2 * (2 * (1 - zh) + zl) + core)
        return remote(
            small_sum.at[at],
            small_pairs.at[at],
            lsend_sem.at[heads, at],
            lrecv_sem.at[heads, at],
            (tab, there[at]),
        )

    def slab_tab(head, step):
        return tab_copy(
            lambda t: slab.at[head, t], lambda t: slab_in.at[head, t], head, step
        )

    def slab_blk(head, step):
        return line_copy(
            lambda b: line.at[head, b], lambda b: line_in.at[head, b], head, step
        )

    for step in range(1, 4):
        small_tab(step).start()

    def pass_small(at):
        if at == 0:
            total = small_ref[...]
            for step in range(1, 4):
                there = lax.rem(tab + step, 4)
                landed(small_in.at[there], trecv_sem.at[heads, there])
                total += small_in[there]
        else:
            landed(small_pairs.at[at - 1], lrecv_sem.at[heads, at - 1])
            total = small_sum[at - 1] + small_pairs[at - 1]
        small_sum[at] = total
        if at < 3:
            small_pair(at).start()

    def sums_tab(head, step):
        return tab_copy(
            lambda t: sums.at[head], lambda t: sums_in.at[head, t], heads + 1 + head, step
        )

    def make_slab(head):
        flat = dqkv[head]
        sums[head] = jnp.broadcast_to(
            jnp.sum(flat.astype(f32), axis=0, keepdims=True), (8, 3 * HD)
        )
        grad = jnp.dot(toktv[...], flat, preferred_element_type=f32)
        each = width // 32
        slab[head, :, :4] = grad[:, : 2 * HD].reshape(4, 4, 2 * each, 2 * HD).astype(bf16)
        q = grad[:, 2 * HD :].reshape(16, 2, each, HD)
        q = jnp.concatenate([q[:, 0], q[:, 1]], axis=2)
        slab[head, :, 4:] = q.reshape(4, 2, 2 * each, 2 * HD).astype(bf16)
        for step in range(1, 4):
            slab_tab(head, step).start()
            sums_tab(head, step).start()

    def pass_slab(head):
        total = slab[head, tab].astype(f32)
        sums_total = sums[head]
        for step in range(1, 4):
            there = lax.rem(tab + step, 4)
            landed(slab_in.at[head, there], trecv_sem.at[head, there])
            landed(sums_in.at[head, there], trecv_sem.at[heads + 1 + head, there])
            total += slab_in[head, there].astype(f32)
            sums_total += sums_in[head, there]
        each = width // 32
        for b in range(8):
            kv = total[b // 2, b % 2 * each :][:each]
            q = total[4 + b // 4, b // 2 % 2 * each :][:each, b % 2 * HD :][:, :HD]
            rows_b = jnp.concatenate([jnp.concatenate([kv, q], axis=1), sums_total], axis=0)
            line[head, b] = rows_b.astype(bf16)
        line_in[head, blk] = line[head, blk]
        for step in range(1, 8):
            slab_blk(head, step).start()

    for copy in loads[:4]:
        copy.wait()
    for head in range(heads):
        ktv[head] = qkvv[heads + head].T

    def gradient_copies(head, which, own):
        slot = group * heads + head
        pairs = (
            (qsend.at[head, which], arrive_q.at[slot]),
            (kvsend.at[head, which], arrive_kv.at[slot]),
        )
        for kind, (src, dst) in enumerate(pairs):
            if own:
                yield pltpu.make_async_copy(src, dst, grecv_sem.at[kind, slot])
            else:
                yield remote(
                    src,
                    dst,
                    gsend_sem.at[kind, head, which],
                    grecv_sem.at[kind, slot],
                    (tab, 4 * half + which),
                )

    def send_gradient(kind, head, which):
        @pl.when(which == group)
        def _():
            list(gradient_copies(head, which, True))[kind].start()

        @pl.when(which != group)
        def _():
            list(gradient_copies(head, which, False))[kind].start()

    def absorb(head):
        for at in range(GROUPS):
            slot = at * heads + head
            landed(arrive_q.at[slot], grecv_sem.at[0, slot])
            landed(arrive_kv.at[slot], grecv_sem.at[1, slot])
        for pair in range(GROUPS // 2):
            left, right = 2 * pair * heads + head, (2 * pair + 1) * heads + head
            lanes = slice(pair * LANES, (pair + 1) * LANES)
            for side in range(2):
                cut = slice(side * HD, (side + 1) * HD)
                joined[side * rows : (side + 1) * rows, lanes] = jnp.concatenate(
                    [arrive_q[left][:, cut], arrive_q[right][:, cut]], axis=1
                )
                lanes_kv = slice((2 * side + 2 + pair) * LANES, (2 * side + 3 + pair) * LANES)
                joined[:, lanes_kv] = jnp.concatenate(
                    [arrive_kv[left][:, cut], arrive_kv[right][:, cut]], axis=1
                )

    @pl.loop(0, heads * TURNS)
    def _(turn):
        head, step = turn // TURNS, lax.rem(turn, TURNS)
        which = group_at(step)
        first = pl.multiple_of(which * tile, tile)

        @pl.when(head == 0)
        def _():
            @pl.when(step > 0)
            def _():
                landed(dov.at[which], drecv_sem.at[which])

            dos = unfold(dov[which])
            for at in range(heads):
                do = dos[:, at * HD : (at + 1) * HD]
                doh[at, pl.ds(first, tile)] = do
                ot = otv[which, at * HD : (at + 1) * HD]
                deltas[at, which, :1] = jnp.sum(ot * do.astype(f32).T, axis=0, keepdims=True)

        @pl.when(step == 0)
        def _():
            dkv[...] = jnp.zeros_like(dkv)
            dvv[...] = jnp.zeros_like(dvv)

        tick(turn)

        q_full = qkvv[head, pl.ds(first, tile)]
        q = q_full[:, :HD]
        do = doh[head, pl.ds(first, tile)]
        delta = deltas[head, which, :1]
        lse = lsev[which, pl.ds(head, 1)]
        dqt = jnp.zeros((LANES, tile), f32)
        for at in range(blocks * rows // piece):
            cut = pl.ds(at * piece, piece)
            st = times_t(qkvv[heads + head, cut], q_full)
            pt = jnp.exp2(st * scale - lse)
            dpt = times_t(qkvv[2 * heads + head, cut][:, :HD], do)
            dst = (pt * (dpt - delta)).astype(bf16)
            dvv[cut] += jnp.dot(pt.astype(bf16), do, preferred_element_type=f32)
            dkv[cut] += jnp.dot(dst, q, preferred_element_type=f32)
            dqt += jnp.dot(ktv[head, :, cut], dst, preferred_element_type=f32)
        dq = (dqt[:HD].T * shrink).astype(bf16)
        dqv[pl.ds(first, tile)] = dq
        qsend[head, which] = jnp.concatenate([dq[:rows], dq[rows:]], axis=1)
        send_gradient(0, head, which)

        @pl.when(step == TURNS - 1)
        def _():
            @pl.loop(0, 4)
            def _(at):
                there = lax.rem(group + 1 + at, 4)
                cut = pl.ds(pl.multiple_of(there * tile, tile), tile)
                pair = jnp.concatenate([dkv[cut] * shrink, dvv[cut]], axis=1).astype(bf16)
                kvsend[head, there] = pair
                send_gradient(1, head, there)
                dqkv[head, cut] = jnp.concatenate([pair, dqv[cut]], axis=1)

        @pl.when(turn == TURNS)
        def _():
            loads[4].wait()
            pass_small(0)

        for at in range(1, 4):
            pl.when(turn == TURNS + at)(functools.partial(pass_small, at))


    loads[5].wait()
    for head in range(heads - 1):
        absorb(head)
        product = times_t(joined[...], wv[head])
        xacc[...] = product if head == 0 else xacc[...] + product
    tick(heads * TURNS)
    absorb(heads - 1)
    loads[6].wait()
    for side in range(2):
        at = pl.ds(side * rows, rows)
        total = prev[at] + xacc[at] + times_t(joined[at], wv[heads - 1])
        xsend[side] = total.astype(bf16)
    return_rows(xsend, tgrad_ref, xsend_sem, xrecv_sem, "start")

    for head in range(heads):
        make_slab(head)
        tick(heads * TURNS + 1 + head)
    for head in range(heads):
        pass_slab(head)
    for now in range(heads * TURNS + 1 + heads, PHASE[-1][1] + UNITS):
        tick(now)

    def slabs_in(head, at):
        return [line_in[head, half_at * GROUPS + at].astype(f32) for half_at in range(2)]

    for head in range(heads):
        for step in range(1, 8):
            there = lax.rem(blk + step, 8)
            landed(line_in.at[head, there], lrecv_sem.at[head, there])
    total = small_sum[3]
    own = [
        functools.reduce(jnp.add, slabs_in(at % heads, at // heads))
        for at in range(GROUPS * heads)
    ]
    each = width // 32
    bias = []
    for part in range(3):
        cut = slice((part + 2) % 3 * HD, (part + 2) % 3 * HD + HD)
        for pair in range(GROUPS * heads // 2):
            both_heads = jnp.concatenate([own[2 * pair][:, cut], own[2 * pair + 1][:, cut]], axis=1)
            lanes = slice(part * width + pair * LANES, part * width + (pair + 1) * LANES)
            wqkv_ref[:, lanes] = both_heads[:each]
            bias.append(both_heads[each:])
    pairs = GROUPS * heads // 2
    bias_q = jnp.concatenate(bias[:pairs], axis=1)
    bias_v = jnp.concatenate(bias[2 * pairs :], axis=1)
    bias = jnp.where(tab < 2, bias_q, bias_v)

    row = lax.broadcasted_iota(jnp.int32, (width, LANES), 0)
    lane = lax.broadcasted_iota(jnp.int32, (width, LANES), 1)

    def take(block, first, count):
        chosen = jnp.where((row == first + lane) & (lane < count), 1.0, 0.0)
        return jnp.dot(
            block, chosen, preferred_element_type=f32, precision=lax.Precision.HIGHEST
        )

    index = 8 * tab + blk
    little_ref[0:8] = take(total[:8], each * index, each)
    at_row = lax.broadcasted_iota(jnp.int32, total.shape, 0) == 6 + tab
    wide = jnp.sum(jnp.where(at_row, total, 0.0), axis=0, keepdims=True)
    little_ref[6:7] = take(jnp.broadcast_to(wide, (8, width)), 4 * each * blk, 4 * each)[:1]
    little_ref[7:8] = take(bias, 2 * each * lax.rem(index, 16), 2 * each)[:1]

    return_rows(xsend, tgrad_ref, xsend_sem, xrecv_sem, "wait")
    for step in range(1, 4):
        context_copy(group_at(step)).wait_send()

    @pl.loop(0, heads)
    def _(head):
        @pl.loop(1, 4)
        def _(step):
            for copy in gradient_copies(head, lax.rem(group + step, 4), False):
                copy.wait_send()

    for step in range(1, 8):
        for head in range(heads):
            slab_blk(head, step).wait_send()
    for at in range(3):
        small_pair(at).wait_send()
    for step in range(1, 4):
        small_tab(step).wait_send()
        for head in range(heads):
            slab_tab(head, step).wait_send()
            sums_tab(head, step).wait_send()

    stage_copy(0, UNITS - 1).wait_send()

    @pl.loop(0, UNITS)
    def _(unit):
        both(lambda order: stage_copy(1, unit, order).wait_send())
        both(lambda order: stage_copy(2, unit, order).wait_send())
        stage_copy(3, unit).wait_send()
        stage_copy(4, unit).wait_send()


def attend_back(dctx, qkv, ot, lse, full_t, by_head, pre, small, sums, parts, heads):
    width, total = full_t.shape
    blocks = 8
    rows = total // blocks
    each, ff = width // 32, 4 * width
    any_space = pl.BlockSpec(memory_space=pl.ANY)
    vmem = pl.BlockSpec(memory_space=pltpu.VMEM)
    bf16, f32 = jnp.bfloat16, jnp.float32
    dma = pltpu.SemaphoreType.DMA
    unit = parts.shape[-2:]
    shape = jax.ShapeDtypeStruct
    return pl.pallas_call(
        functools.partial(attend_back_kernel, heads),
        name="attend_back",
        out_shape=(
            shape((2, rows, width), bf16),
            shape((each, 3 * width), f32),
            shape((each, width), f32),
            shape((each, ff), f32),
            shape((4 * each, width), f32),
            shape((8, LANES), f32),
        ),
        in_specs=[any_space] * 9 + [vmem],
        out_specs=(any_space,) + (vmem,) * 5,
        scratch_shapes=[
            pltpu.VMEM((GROUPS, rows, 2 * heads * HD), bf16),
            pltpu.VMEM((heads, total, HD), bf16),
            pltpu.VMEM((heads, 4, 8, 2 * rows), f32),
            pltpu.VMEM((3 * heads, total, LANES), bf16),
            pltpu.VMEM(ot.shape, f32),
            pltpu.VMEM(lse.shape, f32),
            pltpu.VMEM((width, total), bf16),
            pltpu.VMEM(by_head.shape, bf16),
            pltpu.VMEM((2 * rows, width), f32),
            pltpu.VMEM((heads, LANES, total), bf16),
            pltpu.VMEM((total, HD), bf16),
            pltpu.VMEM((total, HD), f32),
            pltpu.VMEM((total, HD), f32),
            pltpu.VMEM((heads, total, 3 * HD), bf16),
            pltpu.VMEM((heads, 4, rows, 2 * HD), bf16),
            pltpu.VMEM((heads, 4, 2 * rows, 2 * HD), bf16),
            pltpu.VMEM((GROUPS * heads, rows, 2 * HD), bf16),
            pltpu.VMEM((GROUPS * heads, 2 * rows, 2 * HD), bf16),
            pltpu.VMEM((2 * rows, width), bf16),
            pltpu.VMEM((2 * rows, width), f32),
            pltpu.VMEM((2, rows, width), bf16),
            pltpu.VMEM((2, 2, 2, 2, *unit), bf16),
            pltpu.VMEM((UNITS, 2, 2, 2, 2, *unit), bf16),
            pltpu.VMEM((UNITS, 2, 2, 2, *unit), bf16),
            pltpu.VMEM((UNITS, 2, 2, *unit), bf16),
            pltpu.VMEM((UNITS, 2, *unit), bf16),
            pltpu.VMEM((UNITS, *unit), bf16),
            pltpu.VMEM((heads, 4, 6, 2 * each, 2 * HD), bf16),
            pltpu.VMEM((heads, 4, 6, 2 * each, 2 * HD), bf16),
            pltpu.VMEM((heads, 8, 3 * HD), f32),
            pltpu.VMEM((heads, 4, 8, 3 * HD), f32),
            pltpu.VMEM((heads, 8, each + 8, 3 * HD), bf16),
            pltpu.VMEM((heads, 8, each + 8, 3 * HD), bf16),
            pltpu.VMEM((4, 16, width), f32),
            pltpu.VMEM((4, 16, width), f32),
            pltpu.VMEM((3, 16, width), f32),
            dma((GROUPS,)),
            dma((GROUPS,)),
            dma((2, heads, 4)),
            dma((2, GROUPS * heads)),
            dma((2,)),
            dma((2,)),
            dma((STAGES, UNITS)),
            dma((STAGES, UNITS)),
            dma((2 * heads + 1, 4)),
            dma((2 * heads + 1, 4)),
            dma((heads + 1, 8)),
            dma((heads + 1, 8)),
            dma((8,)),
            dma((1,)),
        ],
        compiler_params=pltpu.CompilerParams(
            collective_id=2, has_side_effects=True, vmem_limit_bytes=62 << 20
        ),
    )(dctx, qkv, ot, lse, full_t, by_head, pre, sums, parts, small)


def finish_kernel(whole, *refs):
    little_ref, outs = refs[whole], refs[whole + 1 :]
    for src, dst in zip(refs[:whole], outs[:whole]):
        dst[...] = src[...]
    for at, dst in enumerate(outs[whole:]):
        dst[...] = little_ref[at, : dst.shape[0]]


def finish(arrays, little, counts):
    vmem = pl.BlockSpec(memory_space=pltpu.VMEM)
    shapes = [jax.ShapeDtypeStruct(a.shape, a.dtype) for a in arrays]
    shapes += [jax.ShapeDtypeStruct((count,), jnp.float32) for count in counts]
    return pl.pallas_call(
        functools.partial(finish_kernel, len(arrays)),
        name="finish",
        out_shape=tuple(shapes),
        in_specs=[vmem] * (len(arrays) + 1),
        out_specs=(vmem,) * len(shapes),
    )(*arrays, little)


def halves(grad):
    cut = grad.shape[2] // 2
    return jnp.concatenate([grad[:, :, :cut], grad[:, :, cut:]], axis=1)


def norm_parts(inputs):
    centred = inputs - jnp.mean(inputs, axis=-1, keepdims=True)
    inverse = lax.rsqrt(jnp.mean(centred * centred, axis=-1, keepdims=True) + EPSILON)
    return centred * inverse, inverse


def norm_back(grad, normed, inverse, gain):
    e = grad * gain
    return inverse * (
        e
        - jnp.mean(e, axis=-1, keepdims=True)
        - normed * jnp.mean(e * normed, axis=-1, keepdims=True)
    )


def column_sum(block):
    return jnp.sum(block.astype(jnp.float32), axis=0, keepdims=True)


def ffn_kernel(
    tok_ref,
    ctx_ref,
    cot_ref,
    par_ref,
    outw_ref,
    upw_hbm,
    downw_hbm,
    layer_ref,
    dctx_ref,
    pre_ref,
    small_ref,
    sums_ref,
    parts_ref,
    upw,
    downw,
    hid,
    hlow,
    hlow_t,
    norm1,
    slopes,
    active_t,
    pre2,
    gbranch,
    ghid,
    out,
    dparts,
    uparts,
    sum0,
    load_sem,
    keep_sem,
    osend_sem,
    orecv_sem,
    ssend_sem,
    srecv_sem,
):
    f32, bf16 = jnp.float32, jnp.bfloat16
    groups, rows, cols = ctx_ref.shape
    cols = cols // 2
    sides = 2
    width = tok_ref.shape[1]
    chunks = active_t.shape[0]
    each = width // 32
    tab, blk, chip, core = place()
    loads = (
        pltpu.make_async_copy(upw_hbm, upw, load_sem.at[0]),
        pltpu.make_async_copy(downw_hbm, downw, load_sem.at[1]),
    )
    for copy in loads:
        copy.start()

    greet_all(tab, blk)

    def par(at):
        return par_ref[at : at + 1]

    inverse1 = []
    contexts = [unfold(ctx_ref[group]) for group in range(groups)]
    for table in range(sides):
        cut = pl.ds(table * rows, rows)
        pre1 = tok_ref[cut].astype(f32) + par(0)
        for group in range(groups):
            pre1 += jnp.dot(
                contexts[group][table * rows : (table + 1) * rows],
                outw_ref[group * cols : (group + 1) * cols],
                preferred_element_type=f32,
            )
        normed, inverse = norm_parts(pre1)
        inverse1.append(inverse)
        hidden = normed * par(1) + par(2)
        low = hidden.astype(bf16)
        norm1[cut] = normed
        hid[cut] = hidden
        hlow[cut] = low
        hlow_t[:, cut] = low.T

    pre2[...] = hid[...] + par(3)
    for copy in loads:
        copy.wait()

    def forward(at):
        cut = pl.ds(pl.multiple_of(at * width, width), width)
        upper = jnp.dot(
            hlow[...], upw[:, cut], preferred_element_type=f32
        ) + par_ref[pl.ds(24 + at, 1)]
        cdf = 0.5 + 0.5 * lax.erf(upper * math.sqrt(0.5))
        act = (upper * cdf).astype(bf16)
        slopes[at] = cdf + upper * jnp.exp(-0.5 * upper * upper) * (1 / math.sqrt(2 * math.pi))
        active_t[at] = act.T
        pre2[...] += jnp.dot(act, downw[cut], preferred_element_type=f32)

    @pl.loop(0, chunks // 2)
    def _(pair):
        forward(2 * pair)
        forward(2 * pair + 1)

    normed, inverse = norm_parts(pre2[...])
    out[...] = (normed * par(4) + par(5)).astype(bf16).reshape(out.shape)
    return_rows(out, layer_ref, osend_sem, orecv_sem, "start")
    grad = cot_ref[...].astype(f32)
    small_ref[4:5] = column_sum(grad * normed)
    small_ref[5:6] = column_sum(grad)
    gpre2 = norm_back(grad, normed, inverse, par(4))
    ghid[...] = gpre2
    low = gpre2.astype(bf16)
    gbranch[...] = low
    small_ref[3:4] = column_sum(low)

    def core_copy(unit, src):
        return send_to(
            src.at[:, :, :, :, 1 - core],
            sum0.at[unit],
            ssend_sem.at[unit],
            srecv_sem.at[unit],
            (tab, 2 * chip + 1 - core),
        )

    def add_core(unit, parts):
        landed(sum0.at[unit], srecv_sem.at[unit])
        for a in range(2):
            for b in range(2):
                sum0[unit, a, b] = sum0[unit, a, b] + parts[a, b, :, :, core]

    def down_grad(at):
        wdown = jnp.dot(active_t[at], gbranch[...], preferred_element_type=f32)
        wdown = wdown.reshape(8, 4, each, width)
        for part in range(4):
            dparts[part, at // 2, lax.rem(at, 2)] = (
                halves(wdown[:, part]).astype(bf16).reshape(dparts.shape[3:])
            )

    @pl.loop(0, chunks // 2)
    def _(pair):
        down_grad(2 * pair)
        down_grad(2 * pair + 1)

    for unit in range(4):
        core_copy(unit, dparts.at[unit]).start()

    def backward(at):
        cut = pl.ds(pl.multiple_of(at * width, width), width)

        gact = times_t(gbranch[...], downw[cut])
        gup = (gact * slopes[at]).astype(bf16)
        small_ref[pl.ds(6 + at, 1)] = column_sum(gup)
        ghid[...] += times_t(gup, upw[:, cut])
        wup = jnp.dot(hlow_t[...], gup, preferred_element_type=f32)
        uparts[at] = halves(wup.reshape(32, each, width)).astype(bf16).reshape(uparts.shape[1:])
        core_copy(4 + at, uparts.at[at]).start()

    @pl.loop(0, chunks // 2)
    def _(pair):
        @pl.when(pair == 1)
        def _():
            for unit in range(4):
                add_core(unit, dparts.at[unit])

        backward(2 * pair)
        backward(2 * pair + 1)

    small = [0.0, 0.0, 0.0]
    lows = []
    for table in range(sides):
        cut = pl.ds(table * rows, rows)
        grad, normed = ghid[cut], norm1[cut]
        small[1] += column_sum(grad * normed)
        small[2] += column_sum(grad)
        gpre1 = norm_back(grad, normed, inverse1[table], par(1))
        pre_ref[cut] = gpre1
        low = gpre1.astype(bf16)
        small[0] += column_sum(low)
        lows.append(low)
    low = jnp.concatenate(lows, axis=0)
    for at in range(3):
        small_ref[at : at + 1] = small[at]
    small_ref[10:] = jnp.zeros((6, width), f32)
    wouts = []
    for group in range(groups):
        dctx_ref[group] = fold(
            times_t(low, outw_ref[group * cols : (group + 1) * cols]).astype(bf16)
        )
        wout = jnp.dot(unfold(ctx_ref[group]).T, low, preferred_element_type=f32)
        wouts.append(halves(wout.reshape(8, each, width)).astype(bf16))
    for unit in range(4):
        core_copy(unit, dparts.at[unit]).wait_send()
    dparts[0] = jnp.concatenate(wouts, axis=0).reshape(dparts.shape[1:])
    keep = [pltpu.make_async_copy(dparts.at[0], parts_ref, keep_sem.at[0])]

    @pl.loop(0, 4)
    def _(at):
        add_core(4 + at, uparts.at[at])
        core_copy(4 + at, uparts.at[at]).wait_send()

    keep.append(pltpu.make_async_copy(sum0, sums_ref, keep_sem.at[1]))
    for copy in keep:
        copy.start()
    return_rows(out, layer_ref, osend_sem, orecv_sem, "wait")
    for copy in keep:
        copy.wait()


def ffn(tokens, ctx, cotangent, params, out_weight, up_weight, down_weight):
    total, width = tokens.shape
    chunks = up_weight.shape[1] // width
    unit = (2 * (width // 32), width // 2)
    any_space = pl.BlockSpec(memory_space=pl.ANY)
    vmem = pl.BlockSpec(memory_space=pltpu.VMEM)
    bf16, f32 = jnp.bfloat16, jnp.float32
    flops = 18 * total * width * chunks * width + 6 * total * width * width
    return pl.pallas_call(
        ffn_kernel,
        name="ffn",
        out_shape=(
            jax.ShapeDtypeStruct((2, total // 2, width), bf16),
            jax.ShapeDtypeStruct(ctx.shape, bf16),
            jax.ShapeDtypeStruct((total, width), f32),
            jax.ShapeDtypeStruct((16, width), f32),
            jax.ShapeDtypeStruct((8, 2, 2, 2, 2, *unit), bf16),
            jax.ShapeDtypeStruct((2, 2, 2, 2, 2, *unit), bf16),
        ),
        in_specs=[vmem, vmem, vmem, vmem, vmem, any_space, any_space],
        out_specs=(any_space, vmem, vmem, vmem, any_space, any_space),
        scratch_shapes=[
            pltpu.VMEM(up_weight.shape, bf16),
            pltpu.VMEM(down_weight.shape, bf16),
            pltpu.VMEM((total, width), f32),
            pltpu.VMEM((total, width), bf16),
            pltpu.VMEM((width, total), bf16),
            pltpu.VMEM((total, width), f32),
            pltpu.VMEM((chunks, total, width), f32),
            pltpu.VMEM((chunks, width, total), bf16),
            pltpu.VMEM((total, width), f32),
            pltpu.VMEM((total, width), bf16),
            pltpu.VMEM((total, width), f32),
            pltpu.VMEM((2, total // 2, width), bf16),
            pltpu.VMEM((4, 2, 2, 2, 2, 2, *unit), bf16),
            pltpu.VMEM((4, 2, 2, 2, 2, 2, *unit), bf16),
            pltpu.VMEM((8, 2, 2, 2, 2, *unit), bf16),
            pltpu.SemaphoreType.DMA((2,)),
            pltpu.SemaphoreType.DMA((2,)),
            pltpu.SemaphoreType.DMA((2,)),
            pltpu.SemaphoreType.DMA((2,)),
            pltpu.SemaphoreType.DMA((8,)),
            pltpu.SemaphoreType.DMA((8,)),
        ],
        compiler_params=pltpu.CompilerParams(
            collective_id=3, has_side_effects=True, vmem_limit_bytes=63 << 20
        ),
        cost_estimate=pl.CostEstimate(
            flops=flops, bytes_accessed=40 << 20, transcendentals=total * width * chunks
        ),
    )(tokens, ctx, cotangent, params, out_weight, up_weight, down_weight)


def shards_direct(
    tokens,
    lengths,
    qkv_weight,
    qkv_bias,
    out_weight,
    out_bias,
    attn_gain,
    attn_shift,
    up_weight,
    up_bias,
    down_weight,
    down_bias,
    ffn_gain,
    ffn_shift,
    cotangent,
):
    tables, rows, width = tokens.shape
    f32 = jnp.float32
    heads = width // HD // GROUPS
    row = lax.broadcasted_iota(jnp.int32, (32, width), 0)
    params = jnp.zeros((32, width), jnp.bfloat16)
    spans = [
        (at, at + 1, vector)
        for at, vector in enumerate(
            (out_bias, attn_gain, attn_shift, down_bias, ffn_gain, ffn_shift)
        )
    ]
    spans += [(8, 16, qkv_bias[:width]), (16, 24, qkv_bias[width:])]
    spans += [
        (24 + at, 25 + at, up_bias[at * width : (at + 1) * width])
        for at in range(up_bias.shape[0] // width)
    ]
    for first, last, vector in spans:
        params = jnp.where((row >= first) & (row < last), vector[None], params)

    params = params.astype(f32)
    ctx, my_tokens, my_cotangent, full_t, qkv, ot, lse, by_head = attend(
        tokens, lengths, params, qkv_weight, cotangent, heads
    )
    layer_out, dctx, pre, small, sums, parts = ffn(
        my_tokens.reshape(tables * rows, width),
        ctx,
        my_cotangent.reshape(tables * rows, width),
        params,
        out_weight,
        up_weight,
        down_weight,
    )
    *whole, little = attend_back(
        dctx, qkv, ot, lse, full_t, by_head, pre, small, sums, parts, heads
    )
    each = width // 32
    whole.insert(1, layer_out)
    (
        token_grad,
        layer_out,
        wgrad_qkv,
        wgrad_out,
        wgrad_up,
        wgrad_down,
        bgrad_out,
        ggrad_attn,
        sgrad_attn,
        bgrad_down,
        ggrad_ffn,
        sgrad_ffn,
        bgrad_up,
        bgrad_qkv,
    ) = finish(whole, little, [each] * 6 + [4 * each, 2 * each])
    return (
        layer_out,
        token_grad,
        wgrad_qkv,
        bgrad_qkv,
        wgrad_out,
        bgrad_out,
        ggrad_attn,
        sgrad_attn,
        wgrad_up,
        bgrad_up,
        wgrad_down,
        bgrad_down,
        ggrad_ffn,
        sgrad_ffn,
    )


def solution(mesh):
    in_specs = (
        P("tab", "blk", None),
        P("tab"),
        P(),
        P(),
        P(),
        P(),
        P(),
        P(),
        P(),
        P(),
        P(),
        P(),
        P(),
        P(),
        P("tab", "blk", None),
    )
    out_specs = (
        P("tab", "blk", None),
        P("tab", "blk", None),
        P(("tab", "blk"), None),
        P(("tab", "blk")),
        P(("tab", "blk"), None),
        P(("tab", "blk")),
        P(("tab", "blk")),
        P(("tab", "blk")),
        P(("tab", "blk"), None),
        P(("tab", "blk")),
        P(("tab", "blk"), None),
        P(("tab", "blk")),
        P(("tab", "blk")),
        P(("tab", "blk")),
    )
    tab_count, blk_count = mesh.shape["tab"], mesh.shape["blk"]

    def pick(*operands):
        table_count = operands[0].shape[0] // tab_count
        head_count = operands[0].shape[2] // HD
        direct = table_count == 2 and blk_count == 8 and tab_count == 4 and head_count % 4 == 0
        body = shards_direct if direct else shards_ring
        return jax.shard_map(
            body, mesh=mesh, in_specs=in_specs, out_specs=out_specs, check_vma=False
        )(*operands)

    return pick
```

```python
import functools
import math

import jax
import jax.numpy as jnp
from jax import lax
from jax.experimental import pallas as pl
from jax.experimental.pallas import tpu as pltpu
from jax.sharding import PartitionSpec as P

HD = 64


EPSILON = 1e-05
NEGATIVE = -1e30


def from_behind(block, axis, distance):
    devices = range(lax.axis_size(axis))
    route = [((i - distance) % len(devices), i) for i in devices]
    return lax.ppermute(block, axis, route)


def norm_rows(inputs, gains, shifts):
    row_mean = jnp.mean(inputs, axis=-1, keepdims=True)
    centred = inputs - row_mean
    row_var = jnp.mean(centred * centred, axis=-1, keepdims=True)
    return centred * lax.rsqrt(row_var + EPSILON) * gains + shifts


def gelu_exact(inputs):
    return jax.nn.gelu(inputs, approximate=False)


def times_back(left, right):
    return lax.dot_general(
        left, right, (((1,), (1,)), ((), ())), preferred_element_type=jnp.float32
    )


def over_rows(left, right):
    return lax.dot_general(
        left, right, (((0,), (0,)), ((), ())), preferred_element_type=jnp.float32
    )


def shards_ring(
    tokens,
    lengths,
    qkv_weight,
    qkv_bias,
    out_weight,
    out_bias,
    attn_gain,
    attn_shift,
    up_weight,
    up_bias,
    down_weight,
    down_bias,
    ffn_gain,
    ffn_shift,
    cotangent,
):
    table_count, row_count, model_width = tokens.shape
    head_count = model_width // HD
    cycle_size = lax.axis_size("blk")
    cycle_place = lax.axis_index("blk")
    score_scale = HD ** (-0.5)
    flat_tokens = tokens.reshape(table_count * row_count, model_width)
    bias_full = jnp.concatenate(
        [
            qkv_bias[:model_width].astype(jnp.float32),
            jnp.zeros((model_width,), jnp.float32),
            qkv_bias[model_width:].astype(jnp.float32),
        ]
    )
    qkv_low = (
        jnp.dot(flat_tokens, qkv_weight, preferred_element_type=jnp.float32) + bias_full
    ).astype(jnp.bfloat16)
    queries = qkv_low[:, :model_width].reshape(table_count, row_count, head_count, HD)
    key_values = qkv_low[:, model_width:].reshape(table_count, row_count, 2 * model_width)

    def key_mask(first_row, key_count):
        positions = first_row + jnp.arange(key_count, dtype=jnp.int32)
        return (positions[None, :] < lengths[:, None])[:, None, None, :]

    def split_pair(pair_block):
        key_count = pair_block.shape[1]
        keys_part = pair_block[:, :, :model_width].reshape(table_count, key_count, head_count, HD)
        values_part = pair_block[:, :, model_width:].reshape(table_count, key_count, head_count, HD)
        return (keys_part, values_part)

    pair_block = lax.all_gather(key_values, "blk", axis=1, tiled=True)
    running_max = jnp.full((table_count, row_count, head_count), NEGATIVE, jnp.float32)
    keys_part, values_part = split_pair(pair_block)
    is_valid = key_mask(jnp.int32(0), pair_block.shape[1])
    raw_scores = jnp.einsum(
        "trhd,tkhd->trhk", queries, keys_part, preferred_element_type=jnp.float32
    )
    scores = jnp.where(is_valid, raw_scores * score_scale, NEGATIVE)
    peak_new = jnp.maximum(running_max, jnp.max(scores, axis=-1))
    exponent = jnp.where(is_valid, jnp.exp(scores - peak_new[..., None]), 0.0)
    running_sum = jnp.sum(exponent, axis=-1)
    weighted = jnp.einsum(
        "trhk,tkhd->trhd",
        exponent.astype(jnp.bfloat16),
        values_part,
        preferred_element_type=jnp.float32,
    )
    running_max, running_sum, weighted = (peak_new, running_sum, weighted)
    context = weighted / running_sum[..., None]
    log_total = running_max + jnp.log(running_sum)
    context_low = context.reshape(table_count * row_count, model_width).astype(jnp.bfloat16)
    attended = jnp.dot(
        context_low, out_weight, preferred_element_type=jnp.float32
    ) + out_bias.astype(jnp.float32)
    pre_one = flat_tokens.astype(jnp.float32) + attended
    gain_one = attn_gain.astype(jnp.float32)
    shift_one = attn_shift.astype(jnp.float32)
    hidden = norm_rows(pre_one, gain_one, shift_one)
    hidden_low = hidden.astype(jnp.bfloat16)
    upper = jnp.dot(hidden_low, up_weight, preferred_element_type=jnp.float32) + up_bias.astype(
        jnp.float32
    )
    active = gelu_exact(upper).astype(jnp.bfloat16)
    pre_two = (
        hidden
        + jnp.dot(active, down_weight, preferred_element_type=jnp.float32)
        + down_bias.astype(jnp.float32)
    )
    gain_two = ffn_gain.astype(jnp.float32)
    shift_two = ffn_shift.astype(jnp.float32)
    layer_out = norm_rows(pre_two, gain_two, shift_two).astype(jnp.bfloat16).reshape(tokens.shape)
    grad_out = cotangent.reshape(table_count * row_count, model_width).astype(jnp.float32)
    _, norm_two_back = jax.vjp(norm_rows, pre_two, gain_two, shift_two)
    grad_pre_two, ggrad_ffn, sgrad_ffn = norm_two_back(grad_out)
    grad_branch = grad_pre_two.astype(jnp.bfloat16)
    wgrad_down = over_rows(active, grad_branch)
    bgrad_down = jnp.sum(grad_branch, axis=0, dtype=jnp.float32)
    grad_active = times_back(grad_branch, down_weight)
    _, gelu_back = jax.vjp(gelu_exact, upper)
    grad_upper = gelu_back(grad_active)[0].astype(jnp.bfloat16)
    wgrad_up = over_rows(hidden_low, grad_upper)
    bgrad_up = jnp.sum(grad_upper, axis=0, dtype=jnp.float32)
    grad_hidden = grad_pre_two + times_back(grad_upper, up_weight)
    _, norm_one_back = jax.vjp(norm_rows, pre_one, gain_one, shift_one)
    grad_pre_one, ggrad_attn, sgrad_attn = norm_one_back(grad_hidden)
    grad_attended = grad_pre_one.astype(jnp.bfloat16)
    wgrad_out = over_rows(context_low, grad_attended)
    bgrad_out = jnp.sum(grad_attended, axis=0, dtype=jnp.float32)
    grad_context = times_back(grad_attended, out_weight).astype(jnp.bfloat16)
    grad_heads = grad_context.reshape(table_count, row_count, head_count, HD)
    row_delta = jnp.sum(grad_heads.astype(jnp.float32) * context, axis=-1)

    def cycle_turn_step(cycle_turn, cycle_state):
        pair_now, pair_grads, grad_queries = cycle_state
        owner_index = (cycle_place - cycle_turn) % cycle_size
        keys_part, values_part = split_pair(pair_now)
        is_valid = key_mask(owner_index * row_count, row_count)
        raw_scores = jnp.einsum(
            "trhd,tkhd->trhk", queries, keys_part, preferred_element_type=jnp.float32
        )
        scores = jnp.where(is_valid, raw_scores * score_scale, NEGATIVE)
        probs = jnp.where(is_valid, jnp.exp(scores - log_total[..., None]), 0.0)
        grad_probs = jnp.einsum(
            "trhd,tkhd->trhk", grad_heads, values_part, preferred_element_type=jnp.float32
        )
        grad_raw = (probs * (grad_probs - row_delta[..., None]) * score_scale).astype(jnp.bfloat16)
        grad_queries = grad_queries + jnp.einsum(
            "trhk,tkhd->trhd", grad_raw, keys_part, preferred_element_type=jnp.float32
        )
        grad_keys = jnp.einsum(
            "trhk,trhd->tkhd", grad_raw, queries, preferred_element_type=jnp.float32
        )
        grad_values = jnp.einsum(
            "trhk,trhd->tkhd",
            probs.astype(jnp.bfloat16),
            grad_heads,
            preferred_element_type=jnp.float32,
        )
        pair_grads = pair_grads + jnp.concatenate(
            [
                grad_keys.reshape(table_count, row_count, model_width),
                grad_values.reshape(table_count, row_count, model_width),
            ],
            axis=-1,
        )
        pair_next = from_behind(pair_now, "blk", 1)
        grads_next = from_behind(pair_grads.astype(jnp.bfloat16), "blk", 1).astype(pair_grads.dtype)
        return (pair_next, grads_next, grad_queries)

    cycle_start = (
        key_values,
        jnp.zeros((table_count, row_count, 2 * model_width), jnp.float32),
        jnp.zeros((table_count, row_count, head_count, HD), jnp.float32),
    )
    _, pair_home, grad_queries = lax.fori_loop(0, cycle_size, cycle_turn_step, cycle_start)
    grad_qkv = jnp.concatenate(
        [
            grad_queries.reshape(table_count * row_count, model_width),
            pair_home.reshape(table_count * row_count, 2 * model_width),
        ],
        axis=-1,
    ).astype(jnp.bfloat16)
    wgrad_qkv = over_rows(flat_tokens, grad_qkv)
    column_sums = jnp.sum(grad_qkv, axis=0, dtype=jnp.float32)
    bgrad_qkv = jnp.concatenate([column_sums[:model_width], column_sums[2 * model_width :]])
    token_grad = (
        (grad_pre_one + times_back(grad_qkv, qkv_weight)).astype(jnp.bfloat16).reshape(tokens.shape)
    )
    (
        wgrad_qkv,
        bgrad_qkv,
        wgrad_out,
        bgrad_out,
        ggrad_attn,
        sgrad_attn,
        wgrad_up,
        bgrad_up,
        wgrad_down,
        bgrad_down,
        ggrad_ffn,
        sgrad_ffn,
    ) = (
        lax.psum_scatter(
            wgrad_qkv.astype(jnp.bfloat16), "tab", scatter_dimension=0, tiled=True
        ).astype(jnp.float32),
        lax.psum_scatter(
            bgrad_qkv.astype(jnp.bfloat16), "tab", scatter_dimension=0, tiled=True
        ).astype(jnp.float32),
        lax.psum_scatter(
            wgrad_out.astype(jnp.bfloat16), "tab", scatter_dimension=0, tiled=True
        ).astype(jnp.float32),
        lax.psum_scatter(
            bgrad_out.astype(jnp.bfloat16), "tab", scatter_dimension=0, tiled=True
        ).astype(jnp.float32),
        lax.psum_scatter(
            ggrad_attn.astype(jnp.bfloat16), "tab", scatter_dimension=0, tiled=True
        ).astype(jnp.float32),
        lax.psum_scatter(
            sgrad_attn.astype(jnp.bfloat16), "tab", scatter_dimension=0, tiled=True
        ).astype(jnp.float32),
        lax.psum_scatter(
            wgrad_up.astype(jnp.bfloat16), "tab", scatter_dimension=0, tiled=True
        ).astype(jnp.float32),
        lax.psum_scatter(
            bgrad_up.astype(jnp.bfloat16), "tab", scatter_dimension=0, tiled=True
        ).astype(jnp.float32),
        lax.psum_scatter(
            wgrad_down.astype(jnp.bfloat16), "tab", scatter_dimension=0, tiled=True
        ).astype(jnp.float32),
        lax.psum_scatter(
            bgrad_down.astype(jnp.bfloat16), "tab", scatter_dimension=0, tiled=True
        ).astype(jnp.float32),
        lax.psum_scatter(
            ggrad_ffn.astype(jnp.bfloat16), "tab", scatter_dimension=0, tiled=True
        ).astype(jnp.float32),
        lax.psum_scatter(
            sgrad_ffn.astype(jnp.bfloat16), "tab", scatter_dimension=0, tiled=True
        ).astype(jnp.float32),
    )
    (
        wgrad_qkv,
        bgrad_qkv,
        wgrad_out,
        bgrad_out,
        ggrad_attn,
        sgrad_attn,
        wgrad_up,
        bgrad_up,
        wgrad_down,
        bgrad_down,
        ggrad_ffn,
        sgrad_ffn,
    ) = (
        lax.psum_scatter(
            wgrad_qkv.astype(jnp.bfloat16), "blk", scatter_dimension=0, tiled=True
        ).astype(jnp.float32),
        lax.psum_scatter(
            bgrad_qkv.astype(jnp.bfloat16), "blk", scatter_dimension=0, tiled=True
        ).astype(jnp.float32),
        lax.psum_scatter(
            wgrad_out.astype(jnp.bfloat16), "blk", scatter_dimension=0, tiled=True
        ).astype(jnp.float32),
        lax.psum_scatter(
            bgrad_out.astype(jnp.bfloat16), "blk", scatter_dimension=0, tiled=True
        ).astype(jnp.float32),
        lax.psum_scatter(
            ggrad_attn.astype(jnp.bfloat16), "blk", scatter_dimension=0, tiled=True
        ).astype(jnp.float32),
        lax.psum_scatter(
            sgrad_attn.astype(jnp.bfloat16), "blk", scatter_dimension=0, tiled=True
        ).astype(jnp.float32),
        lax.psum_scatter(
            wgrad_up.astype(jnp.bfloat16), "blk", scatter_dimension=0, tiled=True
        ).astype(jnp.float32),
        lax.psum_scatter(
            bgrad_up.astype(jnp.bfloat16), "blk", scatter_dimension=0, tiled=True
        ).astype(jnp.float32),
        lax.psum_scatter(
            wgrad_down.astype(jnp.bfloat16), "blk", scatter_dimension=0, tiled=True
        ).astype(jnp.float32),
        lax.psum_scatter(
            bgrad_down.astype(jnp.bfloat16), "blk", scatter_dimension=0, tiled=True
        ).astype(jnp.float32),
        lax.psum_scatter(
            ggrad_ffn.astype(jnp.bfloat16), "blk", scatter_dimension=0, tiled=True
        ).astype(jnp.float32),
        lax.psum_scatter(
            sgrad_ffn.astype(jnp.bfloat16), "blk", scatter_dimension=0, tiled=True
        ).astype(jnp.float32),
    )
    return (
        layer_out,
        token_grad,
        wgrad_qkv,
        bgrad_qkv,
        wgrad_out,
        bgrad_out,
        ggrad_attn,
        sgrad_attn,
        wgrad_up,
        bgrad_up,
        wgrad_down,
        bgrad_down,
        ggrad_ffn,
        sgrad_ffn,
    )


GROUPS = 4
LANES = 128
LOG2E = math.log2(math.e)
MESH = pl.DeviceIdType.MESH


def times_t(left, right):
    return lax.dot_general(
        left, right, (((1,), (1,)), ((), ())), preferred_element_type=jnp.float32
    )


def place():
    tab, blk = lax.axis_index("tab"), lax.axis_index("blk")
    return tab, blk, blk // 2, blk % 2


def meet(tab, blk):
    barrier = pltpu.get_barrier_semaphore()

    @pl.loop(1, 8)
    def _(step):
        pl.semaphore_signal(
            barrier, inc=1, device_id=(tab, lax.rem(blk + step, 8)), device_id_type=MESH
        )

    pl.semaphore_wait(barrier, 7)


def greet_all(tab, blk):
    barrier = pltpu.get_barrier_semaphore()
    for step in range(1, 8):
        pl.semaphore_signal(
            barrier, inc=1, device_id=(tab, lax.rem(blk + step, 8)), device_id_type=MESH
        )
    for step in range(1, 4):
        pl.semaphore_signal(
            barrier, inc=1, device_id=(lax.rem(tab + step, 4), blk), device_id_type=MESH
        )
    pl.semaphore_wait(barrier, 10)


def send_to(src, dst, send_sem, recv_sem, device):
    return pltpu.make_async_remote_copy(
        src_ref=src,
        dst_ref=dst,
        send_sem=send_sem,
        recv_sem=recv_sem,
        device_id=device,
        device_id_type=MESH,
    )


def landed(ref, sem):
    pltpu.make_async_copy(ref, ref, sem).wait()


def return_rows(src, dst, send_sem, recv_sem, act):
    tab, _, chip, core = place()
    half, group = chip // 2, 2 * lax.rem(chip, 2) + core
    for side in range(2):
        is_own = jnp.logical_and(chip == group, core == side)
        own = pltpu.make_async_copy(src.at[side], dst.at[half], recv_sem.at[half])
        away = send_to(
            src.at[side],
            dst.at[half],
            send_sem.at[side],
            recv_sem.at[half],
            (tab, 2 * group + side),
        )
        if act == "start":
            pl.when(is_own)(own.start)
            pl.when(jnp.logical_not(is_own))(away.start)
        else:
            pl.when(jnp.logical_not(is_own))(away.wait_send)
            landed(dst.at[side], recv_sem.at[side])


def by_core(core, act):
    pl.when(core == 0)(functools.partial(act, 0))
    pl.when(core == 1)(functools.partial(act, 1))


def fold(block):
    cut = block.shape[0] // 2
    return jnp.concatenate([block[:cut], block[cut:]], axis=1)


def unfold(block):
    cut = block.shape[1] // 2
    return jnp.concatenate([block[:, :cut], block[:, cut:]], axis=0)


def own_window(group, first, rows_ref, out):
    start = pl.multiple_of(first + LANES * ((3 * group) // 2), LANES)
    window = rows_ref[:, pl.ds(start, 2 * LANES)].astype(jnp.float32)
    window = pltpu.roll(window, lax.rem(2 * LANES - HD * lax.rem(group, 2), 2 * LANES), 1)
    left = window[:, :LANES]
    low = lax.broadcasted_iota(jnp.int32, left.shape, 1) < HD
    for head, lanes in enumerate((left, pltpu.roll(left, HD, 1), window[:, LANES:])):
        out(head, jnp.where(low, lanes, 0.0))


def attend_kernel(
    heads,
    tok_ref,
    len_ref,
    par_ref,
    w_hbm,
    cot_hbm,
    ctx_ref,
    mytok_ref,
    mycot_ref,
    fullt_ref,
    qkv_ref,
    ot_ref,
    lse_ref,
    wr_ref,
    tokv,
    toktv,
    wfull,
    wrv,
    wown,
    bown,
    qkvv,
    vtv,
    otv,
    lsev,
    acc,
    peaks,
    csend,
    send_sem,
    recv,
    csend_sem,
    crecv_sem,
    osend_sem,
    orecv_sem,
    local_sem,
):
    tab, blk, chip, core = place()
    half = chip // 2
    group = 2 * lax.rem(chip, 2) + core
    rows = tok_ref.shape[1]
    width = tok_ref.shape[2]
    is_near = jnp.logical_or(chip == 1, chip == 2)
    mate = chip + 1 - 2 * lax.rem(chip, 2)
    other_near = 2 - half
    other_far = 3 - 3 * half
    own_far = 3 * half
    scale = LOG2E / math.sqrt(HD)

    def remote(src, dst, send_sem, recv_sem, to_chip, to_core):
        return pltpu.make_async_remote_copy(
            src_ref=src,
            dst_ref=dst,
            send_sem=send_sem,
            recv_sem=recv_sem,
            device_id=(tab, 2 * to_chip + to_core),
            device_id_type=MESH,
        )

    here, there = tok_ref.at[half], tok_ref.at[1 - half]
    to_mate = remote(here, tokv.at[blk], send_sem.at[0], recv.at[blk], mate, core)
    to_other = remote(there, tokv.at[blk], send_sem.at[1], recv.at[blk], other_near, core)
    to_side = remote(here, tokv.at[blk], send_sem.at[2], recv.at[blk], chip, 1 - core)

    def to_far(slot, src_chip):
        which = 2 * src_chip + core
        ref = tokv.at[which]
        return remote(ref, ref, send_sem.at[2 + slot], recv.at[which], own_far, core)

    def to_core(slot, src_chip):
        which = 2 * src_chip + core
        ref = tokv.at[which]
        return remote(ref, ref, send_sem.at[5 + slot], recv.at[which], chip, 1 - core)

    def arrived(which):
        pltpu.make_async_copy(tokv.at[which], tokv.at[which], recv.at[which]).wait()

    load = pltpu.make_async_copy(w_hbm, wfull, local_sem.at[5])
    load.start()
    meet(tab, blk)
    pl.when(is_near)(to_other.start)
    to_mate.start()
    to_side.start()
    tokv[blk] = tok_ref[half]

    lane1 = lax.broadcasted_iota(jnp.int32, (8, LANES), 1)
    for at in (0, 2):

        def keep_bias(head, lanes, at=at):
            row = jnp.where(lane1 == HD, 1.0, lanes)
            bown[:, pl.ds((at * heads + head) * LANES, LANES)] = row

        own_window(group, 0, par_ref.at[pl.ds(8 * (1 + at // 2), 8)], keep_bias)
    for head in range(heads):
        bown[:, pl.ds((heads + head) * LANES, LANES)] = jnp.zeros((8, LANES), jnp.float32)
    load.wait()
    for at in range(3):

        def keep_weight(head, lanes, at=at):
            wown[:, pl.ds((at * heads + head) * LANES, LANES)] = lanes.astype(jnp.bfloat16)

        own_window(group, at * width, wfull, keep_weight)

    length = len_ref[half]
    lane = lax.broadcasted_iota(jnp.int32, (rows, LANES), 1)
    row = lax.broadcasted_iota(jnp.int32, (rows, LANES), 0)

    def project(which):
        first = pl.multiple_of(which * rows, rows)
        tok = tokv[which]
        y = jnp.dot(tok, wown[...], preferred_element_type=jnp.float32) + bown[:1]
        pad = jnp.where((lane == HD) & (row + first >= length), NEGATIVE, 0.0)
        for head in range(heads):
            q, k, v = (
                y[:, (part * heads + head) * LANES :][:, :LANES] for part in range(3)
            )
            qkvv[head, pl.ds(first, rows)] = q.astype(jnp.bfloat16)
            qkvv[heads + head, pl.ds(first, rows)] = (k + pad).astype(jnp.bfloat16)
            qkvv[2 * heads + head, pl.ds(first, rows)] = v.astype(jnp.bfloat16)
            vtv[head, :, pl.ds(first, rows)] = v.T.astype(jnp.bfloat16)
        toktv[:, pl.ds(first, rows)] = tok.T

    def take_keys(tile, head, first_key, count, fresh):
        queries = pl.ds(pl.multiple_of(tile * 2 * rows, 2 * rows), 2 * rows)
        keys = pl.ds(pl.multiple_of(first_key, count), count)
        st = times_t(qkvv[heads + head, keys], qkvv[head, queries])
        peak = jnp.max(st, axis=0, keepdims=True)
        if not fresh:
            before = peaks[tile, pl.ds(head, 1)]
            peak = jnp.maximum(peak, before)
        pt = jnp.exp2((st - peak) * scale).astype(jnp.bfloat16)
        ot = jnp.dot(vtv[head, :, keys], pt, preferred_element_type=jnp.float32)
        if not fresh:
            ot += acc[tile, head] * jnp.exp2((before - peak) * scale)
        acc[tile, head] = ot
        peaks[tile, pl.ds(head, 1)] = peak

    def meet_keys_of_own_half():
        @pl.loop(0, 2 * heads)
        def _(at):
            tile = jnp.where(at < heads, chip, mate)
            take_keys(tile, lax.rem(at, heads), half * 4 * rows, 4 * rows, True)

    def meet_keys_of_near():
        @pl.loop(0, heads)
        def _(head):
            take_keys(other_near, head, half * 4 * rows, 4 * rows, True)

        @pl.loop(0, 3 * heads)
        def _(at):
            tile = jnp.where(at < heads, chip, jnp.where(at < 2 * heads, mate, other_near))
            take_keys(tile, lax.rem(at, heads), other_near * 2 * rows, 2 * rows, False)

    project(blk)

    def half_lanes(part, at):
        first = part * width + LANES * (at // 2)
        return wfull[:, first : first + LANES][:, HD * (at % 2) :][:, :HD]

    for head in range(heads):
        for part in range(3):
            for pair in range(GROUPS // 2):
                at = 2 * pair * heads + head
                wrv[head, :, pl.ds((2 * part + pair) * LANES, LANES)] = jnp.concatenate(
                    [half_lanes(part, at), half_lanes(part, at + heads)], axis=1
                )
    arrived(2 * mate + core)
    to_core(0, mate).start()

    @pl.when(jnp.logical_not(is_near))
    def _():
        to_mate.wait_send()
        to_other.start()

    project(2 * mate + core)
    arrived(2 * chip + 1 - core)
    project(2 * chip + 1 - core)
    arrived(2 * mate + 1 - core)
    project(2 * mate + 1 - core)

    def pass_on(slot, src_chip):
        arrived(2 * src_chip + core)
        pl.when(is_near)(to_far(slot, src_chip).start)
        to_core(slot, src_chip).start()

    def project_chip(src_chip):
        project(2 * src_chip + core)
        arrived(2 * src_chip + 1 - core)
        project(2 * src_chip + 1 - core)

    def owner_of(table):
        return 2 * table + chip // 2, lax.rem(chip, 2)

    def cotangent_copy(table, own):
        src, dst = cot_hbm.at[table], mycot_ref.at[core]
        if own:
            return pltpu.make_async_copy(src, dst, orecv_sem.at[core])
        return remote(src, dst, osend_sem.at[table], orecv_sem.at[core], *owner_of(table))

    def is_owner(table):
        to_chip, to_core = owner_of(table)
        return jnp.logical_and(to_chip == chip, to_core == core)

    pl.when(is_near)(functools.partial(pass_on, 1, other_near))
    meet_keys_of_own_half()
    pl.when(jnp.logical_not(is_near))(functools.partial(pass_on, 1, other_near))
    pl.when(is_near)(functools.partial(pass_on, 2, other_far))
    cotangent_copy(1 - half, False).start()
    project_chip(other_near)
    meet_keys_of_near()
    pl.when(jnp.logical_not(is_near))(functools.partial(pass_on, 2, other_far))
    project_chip(other_far)

    keep = (
        pltpu.make_async_copy(toktv, fullt_ref, local_sem.at[0]),
        pltpu.make_async_copy(qkvv, qkv_ref, local_sem.at[1]),
        pltpu.make_async_copy(wrv, wr_ref, local_sem.at[6]),
    )
    for copy in keep:
        copy.start()

    pl.when(is_owner(half))(cotangent_copy(half, True).start)
    pl.when(jnp.logical_not(is_owner(half)))(cotangent_copy(half, False).start)
    my_tokens = [
        pltpu.make_async_copy(
            tokv.at[2 * group + side], mytok_ref.at[side], local_sem.at[7 + side]
        )
        for side in range(2)
    ]
    for copy in my_tokens:
        copy.start()

    def context_copy(which):
        return remote(
            csend.at[which],
            ctx_ref.at[group],
            csend_sem.at[which],
            crecv_sem.at[group],
            2 * half + which // 2,
            lax.rem(which, 2),
        )

    own_context = pltpu.make_async_copy(
        csend.at[group], ctx_ref.at[group], local_sem.at[2]
    )

    @pl.loop(0, 4)
    def _(step):
        at = jnp.where(is_near, step, 3 - step)
        which = jnp.where(
            at < 2, jnp.where(at == 0, chip, mate), jnp.where(at == 2, other_near, other_far)
        )

        @pl.when(at == 3)
        def _():
            @pl.loop(0, heads)
            def _(head):
                take_keys(which, head, 0, 8 * rows, True)

        @pl.when(at < 3)
        def _():
            @pl.loop(0, heads)
            def _(head):
                take_keys(which, head, other_far * 2 * rows, 2 * rows, False)

        for head in range(heads):
            ot = acc[which, head]
            total = ot[HD : HD + 1]
            otv[which, head * HD : (head + 1) * HD] = ot[:HD] / total
            peak = peaks[which, head : head + 1]
            lsev[which, head : head + 1] = peak * scale + jnp.log(total) * LOG2E
        csend[which] = fold(otv[which].T.astype(jnp.bfloat16))

        pl.when(which == group)(own_context.start)
        pl.when(which != group)(context_copy(which).start)

    more = (
        pltpu.make_async_copy(otv, ot_ref, local_sem.at[3]),
        pltpu.make_async_copy(lsev, lse_ref, local_sem.at[4]),
    )
    for copy in more:
        copy.start()
    pl.when(is_near)(to_mate.wait_send)
    to_other.wait_send()
    to_side.wait_send()
    to_core(0, mate).wait_send()
    for slot, src_chip in ((1, other_near), (2, other_far)):
        pl.when(is_near)(to_far(slot, src_chip).wait_send)
        to_core(slot, src_chip).wait_send()

    for step in range(1, 4):
        which = lax.rem(group + step, 4)
        context_copy(which).wait_send()
        pltpu.make_async_copy(ctx_ref.at[which], ctx_ref.at[which], crecv_sem.at[which]).wait()
    own_context.wait()
    pl.when(jnp.logical_not(is_owner(half)))(cotangent_copy(half, False).wait_send)
    cotangent_copy(1 - half, False).wait_send()
    for side in range(2):
        pltpu.make_async_copy(mycot_ref.at[side], mycot_ref.at[side], orecv_sem.at[side]).wait()
    for copy in [*keep, *more, *my_tokens]:
        copy.wait()


def attend(tokens, lengths, params, qkv_weight, cotangent, heads):
    _, rows, width = tokens.shape
    blocks = 8
    total = blocks * rows
    any_space = pl.BlockSpec(memory_space=pl.ANY)
    vmem = pl.BlockSpec(memory_space=pltpu.VMEM)
    bf16, f32 = jnp.bfloat16, jnp.float32
    dma = pltpu.SemaphoreType.DMA
    return pl.pallas_call(
        functools.partial(attend_kernel, heads),
        name="attend",
        out_shape=(
            jax.ShapeDtypeStruct((GROUPS, rows, 2 * heads * HD), bf16),
            jax.ShapeDtypeStruct((2, rows, width), bf16),
            jax.ShapeDtypeStruct((2, rows, width), bf16),
            jax.ShapeDtypeStruct((width, total), bf16),
            jax.ShapeDtypeStruct((3 * heads, total, LANES), bf16),
            jax.ShapeDtypeStruct((4, heads * HD, 2 * rows), f32),
            jax.ShapeDtypeStruct((4, 8, 2 * rows), f32),
            jax.ShapeDtypeStruct((heads, width, width), bf16),
        ),
        in_specs=[vmem, pl.BlockSpec(memory_space=pltpu.SMEM), vmem, any_space, any_space],
        out_specs=(any_space,) * 8,
        scratch_shapes=[
            pltpu.VMEM((blocks, rows, width), bf16),
            pltpu.VMEM((width, total), bf16),
            pltpu.VMEM(qkv_weight.shape, bf16),
            pltpu.VMEM((heads, width, width), bf16),
            pltpu.VMEM((width, 3 * heads * LANES), bf16),
            pltpu.VMEM((8, 3 * heads * LANES), f32),
            pltpu.VMEM((3 * heads, total, LANES), bf16),
            pltpu.VMEM((heads, LANES, total), bf16),
            pltpu.VMEM((4, heads * HD, 2 * rows), f32),
            pltpu.VMEM((4, 8, 2 * rows), f32),
            pltpu.VMEM((4, heads, LANES, 2 * rows), f32),
            pltpu.VMEM((4, 8, 2 * rows), f32),
            pltpu.VMEM((GROUPS, rows, 2 * heads * HD), bf16),
            dma((8,)),
            dma((blocks,)),
            dma((GROUPS,)),
            dma((GROUPS,)),
            dma((2,)),
            dma((2,)),
            dma((9,)),
        ],
        compiler_params=pltpu.CompilerParams(
            collective_id=1, has_side_effects=True, vmem_limit_bytes=60 << 20
        ),
    )(tokens, lengths, params, qkv_weight, cotangent)


UNITS = 9
TURNS = 4
STAGES = 5
PHASE = ((1, 3), (2, 5), (3, 8), (4, 11))


def attend_back_kernel(
    heads,
    dctx_ref,
    qkv_ref,
    ot_ref,
    lse_ref,
    fullt_ref,
    w_ref,
    pre_ref,
    sums_ref,
    parts_ref,
    small_ref,
    tgrad_ref,
    wqkv_ref,
    wout_ref,
    wup_ref,
    wdown_ref,
    little_ref,
    dov,
    doh,
    deltas,
    qkvv,
    otv,
    lsev,
    toktv,
    wv,
    prev,
    ktv,
    dqv,
    dkv,
    dvv,
    dqkv,
    qsend,
    kvsend,
    arrive_q,
    arrive_kv,
    joined,
    xacc,
    xsend,
    mine,
    sum0,
    sum1,
    sum2,
    sum3,
    sum4,
    slab,
    slab_in,
    sums,
    sums_in,
    line,
    line_in,
    small_in,
    small_sum,
    small_pairs,
    dsend_sem,
    drecv_sem,
    gsend_sem,
    grecv_sem,
    xsend_sem,
    xrecv_sem,
    ssend_sem,
    srecv_sem,
    tsend_sem,
    trecv_sem,
    lsend_sem,
    lrecv_sem,
    local_sem,
    mine_sem,
):
    f32, bf16 = jnp.float32, jnp.bfloat16
    tab, blk, chip, core = place()
    y, x, zh, zl = tab // 2, lax.rem(tab, 2), chip // 2, lax.rem(chip, 2)
    half = zh
    group = 2 * zl + core
    blocks, rows = 8, dov.shape[1]
    width = toktv.shape[0]
    tile = 2 * rows
    piece = 256
    scale = LOG2E / math.sqrt(HD)
    shrink = HD**-0.5

    remote = send_to

    loads = [
        pltpu.make_async_copy(src, dst, local_sem.at[at])
        for at, (src, dst) in enumerate(
            (
                (qkv_ref, qkvv),
                (ot_ref, otv),
                (lse_ref, lsev),
                (dctx_ref.at[group], dov.at[group]),
                (fullt_ref, toktv),
                (w_ref, wv),
                (pre_ref, prev),
                (sums_ref, sum0.at[: UNITS - 1]),
            )
        )
    ]
    for copy in [*loads[:4], loads[7]]:
        copy.start()

    greet_all(tab, blk)

    def group_at(step):
        to_chip = jnp.where(step < 2, zl, 1 - zl)
        return 2 * to_chip + jnp.where(lax.rem(step, 2) == 0, core, 1 - core)

    def context_copy(which):
        return remote(
            dctx_ref.at[which],
            dov.at[group],
            dsend_sem.at[which],
            drecv_sem.at[group],
            (tab, 4 * half + which),
        )

    for step in range(1, 4):
        context_copy(group_at(step)).start()

    def stage_copy(stage, unit, order=None, held=None):
        held = sum0 if held is None else held
        send, done = ssend_sem.at[stage, unit], srecv_sem.at[stage, unit]
        if stage == 0:
            src = parts_ref.at[:, :, :, :, 1 - core]
            return remote(src, sum0.at[unit], send, done, (tab, 2 * chip + 1 - core))
        if stage == 1 and order == 0:
            return remote(
                held.at[unit, :, 1 - x], sum1.at[unit], send, done, (2 * y + 1 - x, blk)
            )
        if stage == 1:
            return remote(
                held.at[unit, 1 - y], sum1.at[unit], send, done, (2 * (1 - y) + x, blk)
            )
        if stage == 2 and order == 0:
            return remote(
                sum1.at[unit, 1 - y], sum2.at[unit], send, done, (2 * (1 - y) + x, blk)
            )
        if stage == 2:
            return remote(
                sum1.at[unit, 1 - x], sum2.at[unit], send, done, (2 * y + 1 - x, blk)
            )
        if stage == 3:
            src, there = sum2.at[unit, :, 1 - zl], 2 * zh + 1 - zl
            return remote(src, sum3.at[unit], send, done, (tab, 2 * there + core))
        src, there = sum3.at[unit, 1 - zh], 2 * (1 - zh) + zl
        return remote(src, sum4.at[unit], send, done, (tab, 2 * there + core))

    both = functools.partial(by_core, core)
    mine_copy = pltpu.make_async_copy(
        parts_ref.at[:, :, :, :, core], mine, mine_sem.at[0]
    )

    def finish(unit):
        done = sum4[unit].astype(f32) + sum3[unit, zh].astype(f32)
        top, low = done[: done.shape[0] // 2], done[done.shape[0] // 2 :]
        each, cut = top.shape

        @pl.when(unit < 4)
        def _():
            at = pl.ds(pl.multiple_of(unit * each, each), each)
            wdown_ref[at, :cut] = top
            wdown_ref[at, cut:] = low

        @pl.when(jnp.logical_and(unit >= 4, unit < 8))
        def _():
            at = pl.multiple_of((unit - 4) * 2 * cut, 2 * cut)
            wup_ref[:, pl.ds(at, cut)] = top
            wup_ref[:, pl.ds(pl.multiple_of(at + cut, cut), cut)] = low

        @pl.when(unit == 8)
        def _():
            wout_ref[:, :cut] = top
            wout_ref[:, cut:] = low

    def advance(stage, unit):
        if stage == 0:
            landed(sum0.at[unit], srecv_sem.at[0, unit])
            mine_copy.wait()
            for a in range(2):
                for b in range(2):
                    sum0[unit, a, b] = sum0[unit, a, b] + mine[a, b]

            both(lambda order: stage_copy(1, unit, order).start())
        elif stage == 1:
            landed(sum1.at[unit], srecv_sem.at[1, unit])

            def act(order):
                own = sum0[unit, :, x] if order == 0 else sum0[unit, y]
                sum1[unit] = sum1[unit] + own
                stage_copy(2, unit, order).start()

            both(act)
        elif stage == 2:
            landed(sum2.at[unit], srecv_sem.at[2, unit])

            def act(order):
                sum2[unit] = sum2[unit] + sum1[unit, y if order == 0 else x]

            both(act)
            stage_copy(3, unit).start()
        elif stage == 3:
            landed(sum3.at[unit], srecv_sem.at[3, unit])
            sum3[unit] = sum3[unit] + sum2[unit, :, zl]
            stage_copy(4, unit).start()
        else:
            landed(sum4.at[unit], srecv_sem.at[4, unit])
            finish(unit)

    def tick(now):
        @pl.when(now < UNITS - 1)
        def _():
            both(lambda order: stage_copy(1, now, order, sums_ref).start())

        pl.when(now == UNITS - 1)(functools.partial(advance, 0, UNITS - 1))
        for stage, lag in PHASE:
            unit = now - lag
            due = (unit >= 0) & (unit < UNITS)
            pl.when(due)(functools.partial(advance, stage, unit))

    stage_copy(0, UNITS - 1).start()
    mine_copy.start()

    def tab_copy(src, dst, sem_at, step):
        there = lax.rem(tab + step, 4)
        return remote(
            src(there), dst(tab), tsend_sem.at[sem_at, there], trecv_sem.at[sem_at, tab], (there, blk)
        )

    def line_copy(src, dst, sem_at, step):
        there = lax.rem(blk + step, 8)
        return remote(
            src(there), dst(blk), lsend_sem.at[sem_at, there], lrecv_sem.at[sem_at, blk], (tab, there)
        )

    def small_tab(step):
        return tab_copy(lambda t: small_ref, lambda t: small_in.at[t], heads, step)

    def small_pair(at):
        there = (2 * chip + 1 - core, 2 * (2 * zh + 1 - zl) + core, 2 * (2 * (1 - zh) + zl) + core)
        return remote(
            small_sum.at[at],
            small_pairs.at[at],
            lsend_sem.at[heads, at],
            lrecv_sem.at[heads, at],
            (tab, there[at]),
        )

    def slab_tab(head, step):
        return tab_copy(
            lambda t: slab.at[head, t], lambda t: slab_in.at[head, t], head, step
        )

    def slab_blk(head, step):
        return line_copy(
            lambda b: line.at[head, b], lambda b: line_in.at[head, b], head, step
        )

    for step in range(1, 4):
        small_tab(step).start()

    def pass_small(at):
        if at == 0:
            total = small_ref[...]
            for step in range(1, 4):
                there = lax.rem(tab + step, 4)
                landed(small_in.at[there], trecv_sem.at[heads, there])
                total += small_in[there]
        else:
            landed(small_pairs.at[at - 1], lrecv_sem.at[heads, at - 1])
            total = small_sum[at - 1] + small_pairs[at - 1]
        small_sum[at] = total
        if at < 3:
            small_pair(at).start()

    def sums_tab(head, step):
        return tab_copy(
            lambda t: sums.at[head], lambda t: sums_in.at[head, t], heads + 1 + head, step
        )

    def make_slab(head):
        flat = dqkv[head]
        sums[head] = jnp.broadcast_to(
            jnp.sum(flat.astype(f32), axis=0, keepdims=True), (8, 3 * HD)
        )
        grad = jnp.dot(toktv[...], flat, preferred_element_type=f32)
        each = width // 32
        slab[head, :, :4] = grad[:, : 2 * HD].reshape(4, 4, 2 * each, 2 * HD).astype(bf16)
        q = grad[:, 2 * HD :].reshape(16, 2, each, HD)
        q = jnp.concatenate([q[:, 0], q[:, 1]], axis=2)
        slab[head, :, 4:] = q.reshape(4, 2, 2 * each, 2 * HD).astype(bf16)
        for step in range(1, 4):
            slab_tab(head, step).start()
            sums_tab(head, step).start()

    def pass_slab(head):
        total = slab[head, tab].astype(f32)
        sums_total = sums[head]
        for step in range(1, 4):
            there = lax.rem(tab + step, 4)
            landed(slab_in.at[head, there], trecv_sem.at[head, there])
            landed(sums_in.at[head, there], trecv_sem.at[heads + 1 + head, there])
            total += slab_in[head, there].astype(f32)
            sums_total += sums_in[head, there]
        each = width // 32
        for b in range(8):
            kv = total[b // 2, b % 2 * each :][:each]
            q = total[4 + b // 4, b // 2 % 2 * each :][:each, b % 2 * HD :][:, :HD]
            rows_b = jnp.concatenate([jnp.concatenate([kv, q], axis=1), sums_total], axis=0)
            line[head, b] = fold(rows_b).astype(bf16)
        line_in[head, blk] = line[head, blk]
        for step in range(1, 8):
            slab_blk(head, step).start()

    for copy in loads[:4]:
        copy.wait()
    for head in range(heads):
        ktv[head] = qkvv[heads + head].T

    def gradient_copies(head, which, own):
        slot = group * heads + head
        pairs = (
            (qsend.at[head, which], arrive_q.at[slot]),
            (kvsend.at[head, which], arrive_kv.at[slot]),
        )
        for kind, (src, dst) in enumerate(pairs):
            if own:
                yield pltpu.make_async_copy(src, dst, grecv_sem.at[kind, slot])
            else:
                yield remote(
                    src,
                    dst,
                    gsend_sem.at[kind, head, which],
                    grecv_sem.at[kind, slot],
                    (tab, 4 * half + which),
                )

    def send_gradient(kind, head, which):
        @pl.when(which == group)
        def _():
            list(gradient_copies(head, which, True))[kind].start()

        @pl.when(which != group)
        def _():
            list(gradient_copies(head, which, False))[kind].start()

    def absorb(head):
        for at in range(GROUPS):
            slot = at * heads + head
            landed(arrive_q.at[slot], grecv_sem.at[0, slot])
            landed(arrive_kv.at[slot], grecv_sem.at[1, slot])
        for pair in range(GROUPS // 2):
            left, right = 2 * pair * heads + head, (2 * pair + 1) * heads + head
            lanes = slice(pair * LANES, (pair + 1) * LANES)
            for side in range(2):
                cut = slice(side * HD, (side + 1) * HD)
                joined[side * rows : (side + 1) * rows, lanes] = jnp.concatenate(
                    [arrive_q[left][:, cut], arrive_q[right][:, cut]], axis=1
                )
                lanes_kv = slice((2 * side + 2 + pair) * LANES, (2 * side + 3 + pair) * LANES)
                joined[:, lanes_kv] = jnp.concatenate(
                    [arrive_kv[left][:, cut], arrive_kv[right][:, cut]], axis=1
                )

    @pl.loop(0, heads * TURNS)
    def _(turn):
        head, step = turn // TURNS, lax.rem(turn, TURNS)
        which = group_at(step)
        first = pl.multiple_of(which * tile, tile)

        @pl.when(head == 0)
        def _():
            @pl.when(step > 0)
            def _():
                landed(dov.at[which], drecv_sem.at[which])

            dos = unfold(dov[which])
            for at in range(heads):
                do = dos[:, at * HD : (at + 1) * HD]
                doh[at, pl.ds(first, tile)] = do
                ot = otv[which, at * HD : (at + 1) * HD]
                deltas[at, which, :1] = jnp.sum(ot * do.astype(f32).T, axis=0, keepdims=True)

        @pl.when(step == 0)
        def _():
            dkv[...] = jnp.zeros_like(dkv)
            dvv[...] = jnp.zeros_like(dvv)

        @pl.when(turn == 1)
        def _():
            for copy in loads[4:7]:
                copy.start()

        pl.when(turn == PHASE[0][1])(loads[7].wait)
        tick(turn)

        q_full = qkvv[head, pl.ds(first, tile)]
        q = q_full[:, :HD]
        do = doh[head, pl.ds(first, tile)]
        delta = deltas[head, which, :1]
        lse = lsev[which, pl.ds(head, 1)]
        dqt = jnp.zeros((LANES, tile), f32)
        for at in range(blocks * rows // piece):
            cut = pl.ds(at * piece, piece)
            st = times_t(qkvv[heads + head, cut], q_full)
            pt = jnp.exp2(st * scale - lse)
            dpt = times_t(qkvv[2 * heads + head, cut][:, :HD], do)
            dst = (pt * (dpt - delta)).astype(bf16)
            dvv[cut] += jnp.dot(pt.astype(bf16), do, preferred_element_type=f32)
            dkv[cut] += jnp.dot(dst, q, preferred_element_type=f32)
            dqt += jnp.dot(ktv[head, :, cut], dst, preferred_element_type=f32)
        dq = (dqt[:HD].T * shrink).astype(bf16)
        dqv[pl.ds(first, tile)] = dq
        qsend[head, which] = jnp.concatenate([dq[:rows], dq[rows:]], axis=1)
        send_gradient(0, head, which)

        @pl.when(step == TURNS - 1)
        def _():
            @pl.loop(0, 4)
            def _(at):
                there = lax.rem(group + 1 + at, 4)
                cut = pl.ds(pl.multiple_of(there * tile, tile), tile)
                pair = jnp.concatenate([dkv[cut] * shrink, dvv[cut]], axis=1).astype(bf16)
                kvsend[head, there] = pair
                send_gradient(1, head, there)
                dqkv[head, cut] = jnp.concatenate([pair, dqv[cut]], axis=1)

        @pl.when(turn == TURNS)
        def _():
            loads[4].wait()
            pass_small(0)

        for at in range(1, 4):
            pl.when(turn == TURNS + at)(functools.partial(pass_small, at))


    loads[5].wait()
    for head in range(heads - 1):
        absorb(head)
        product = times_t(joined[...], wv[head])
        xacc[...] = product if head == 0 else xacc[...] + product
    tick(heads * TURNS)
    absorb(heads - 1)
    loads[6].wait()
    for side in range(2):
        at = pl.ds(side * rows, rows)
        total = prev[at] + xacc[at] + times_t(joined[at], wv[heads - 1])
        xsend[side] = total.astype(bf16)
    return_rows(xsend, tgrad_ref, xsend_sem, xrecv_sem, "start")

    for head in range(heads):
        make_slab(head)
        tick(heads * TURNS + 1 + head)
    for head in range(heads):
        pass_slab(head)
    for now in range(heads * TURNS + 1 + heads, PHASE[-1][1] + UNITS):
        tick(now)

    def slabs_in(head, at):
        return [unfold(line_in[head, half_at * GROUPS + at].astype(f32)) for half_at in range(2)]

    for head in range(heads):
        for step in range(1, 8):
            there = lax.rem(blk + step, 8)
            landed(line_in.at[head, there], lrecv_sem.at[head, there])
    total = small_sum[3]
    own = [
        functools.reduce(jnp.add, slabs_in(at % heads, at // heads))
        for at in range(GROUPS * heads)
    ]
    each = width // 32
    bias = []
    for part in range(3):
        cut = slice((part + 2) % 3 * HD, (part + 2) % 3 * HD + HD)
        for pair in range(GROUPS * heads // 2):
            both_heads = jnp.concatenate([own[2 * pair][:, cut], own[2 * pair + 1][:, cut]], axis=1)
            lanes = slice(part * width + pair * LANES, part * width + (pair + 1) * LANES)
            wqkv_ref[:, lanes] = both_heads[:each]
            bias.append(both_heads[each:])
    pairs = GROUPS * heads // 2
    bias_q = jnp.concatenate(bias[:pairs], axis=1)
    bias_v = jnp.concatenate(bias[2 * pairs :], axis=1)
    bias = jnp.where(tab < 2, bias_q, bias_v)

    row = lax.broadcasted_iota(jnp.int32, (width, LANES), 0)
    lane = lax.broadcasted_iota(jnp.int32, (width, LANES), 1)

    def take(block, first, count):
        chosen = jnp.where((row == first + lane) & (lane < count), 1.0, 0.0)
        return jnp.dot(
            block, chosen, preferred_element_type=f32, precision=lax.Precision.HIGHEST
        )

    index = 8 * tab + blk
    little_ref[0:8] = take(total[:8], each * index, each)
    at_row = lax.broadcasted_iota(jnp.int32, total.shape, 0) == 6 + tab
    wide = jnp.sum(jnp.where(at_row, total, 0.0), axis=0, keepdims=True)
    little_ref[6:7] = take(jnp.broadcast_to(wide, (8, width)), 4 * each * blk, 4 * each)[:1]
    little_ref[7:8] = take(bias, 2 * each * lax.rem(index, 16), 2 * each)[:1]

    return_rows(xsend, tgrad_ref, xsend_sem, xrecv_sem, "wait")
    for step in range(1, 4):
        context_copy(group_at(step)).wait_send()

    @pl.loop(0, heads)
    def _(head):
        @pl.loop(1, 4)
        def _(step):
            for copy in gradient_copies(head, lax.rem(group + step, 4), False):
                copy.wait_send()

    for step in range(1, 8):
        for head in range(heads):
            slab_blk(head, step).wait_send()
    for at in range(3):
        small_pair(at).wait_send()
    for step in range(1, 4):
        small_tab(step).wait_send()
        for head in range(heads):
            slab_tab(head, step).wait_send()
            sums_tab(head, step).wait_send()

    stage_copy(0, UNITS - 1).wait_send()

    @pl.loop(0, UNITS)
    def _(unit):
        both(lambda order: stage_copy(1, unit, order).wait_send())
        both(lambda order: stage_copy(2, unit, order).wait_send())
        stage_copy(3, unit).wait_send()
        stage_copy(4, unit).wait_send()


def attend_back(dctx, qkv, ot, lse, full_t, by_head, pre, small, sums, parts, heads):
    width, total = full_t.shape
    blocks = 8
    rows = total // blocks
    each, ff = width // 32, 4 * width
    any_space = pl.BlockSpec(memory_space=pl.ANY)
    vmem = pl.BlockSpec(memory_space=pltpu.VMEM)
    bf16, f32 = jnp.bfloat16, jnp.float32
    dma = pltpu.SemaphoreType.DMA
    unit = parts.shape[-2:]
    shape = jax.ShapeDtypeStruct
    return pl.pallas_call(
        functools.partial(attend_back_kernel, heads),
        name="attend_back",
        out_shape=(
            shape((2, rows, width), bf16),
            shape((each, 3 * width), f32),
            shape((each, width), f32),
            shape((each, ff), f32),
            shape((4 * each, width), f32),
            shape((8, LANES), f32),
        ),
        in_specs=[any_space] * 9 + [vmem],
        out_specs=(any_space,) + (vmem,) * 5,
        scratch_shapes=[
            pltpu.VMEM((GROUPS, rows, 2 * heads * HD), bf16),
            pltpu.VMEM((heads, total, HD), bf16),
            pltpu.VMEM((heads, 4, 8, 2 * rows), f32),
            pltpu.VMEM((3 * heads, total, LANES), bf16),
            pltpu.VMEM(ot.shape, f32),
            pltpu.VMEM(lse.shape, f32),
            pltpu.VMEM((width, total), bf16),
            pltpu.VMEM(by_head.shape, bf16),
            pltpu.VMEM((2 * rows, width), f32),
            pltpu.VMEM((heads, LANES, total), bf16),
            pltpu.VMEM((total, HD), bf16),
            pltpu.VMEM((total, HD), f32),
            pltpu.VMEM((total, HD), f32),
            pltpu.VMEM((heads, total, 3 * HD), bf16),
            pltpu.VMEM((heads, 4, rows, 2 * HD), bf16),
            pltpu.VMEM((heads, 4, 2 * rows, 2 * HD), bf16),
            pltpu.VMEM((GROUPS * heads, rows, 2 * HD), bf16),
            pltpu.VMEM((GROUPS * heads, 2 * rows, 2 * HD), bf16),
            pltpu.VMEM((2 * rows, width), bf16),
            pltpu.VMEM((2 * rows, width), f32),
            pltpu.VMEM((2, rows, width), bf16),
            pltpu.VMEM((2, 2, 2, 2, *unit), bf16),
            pltpu.VMEM((UNITS, 2, 2, 2, 2, *unit), bf16),
            pltpu.VMEM((UNITS, 2, 2, 2, *unit), bf16),
            pltpu.VMEM((UNITS, 2, 2, *unit), bf16),
            pltpu.VMEM((UNITS, 2, *unit), bf16),
            pltpu.VMEM((UNITS, *unit), bf16),
            pltpu.VMEM((heads, 4, 6, 2 * each, 2 * HD), bf16),
            pltpu.VMEM((heads, 4, 6, 2 * each, 2 * HD), bf16),
            pltpu.VMEM((heads, 8, 3 * HD), f32),
            pltpu.VMEM((heads, 4, 8, 3 * HD), f32),
            pltpu.VMEM((heads, 8, (each + 8) // 2, 6 * HD), bf16),
            pltpu.VMEM((heads, 8, (each + 8) // 2, 6 * HD), bf16),
            pltpu.VMEM((4, 16, width), f32),
            pltpu.VMEM((4, 16, width), f32),
            pltpu.VMEM((3, 16, width), f32),
            dma((GROUPS,)),
            dma((GROUPS,)),
            dma((2, heads, 4)),
            dma((2, GROUPS * heads)),
            dma((2,)),
            dma((2,)),
            dma((STAGES, UNITS)),
            dma((STAGES, UNITS)),
            dma((2 * heads + 1, 4)),
            dma((2 * heads + 1, 4)),
            dma((heads + 1, 8)),
            dma((heads + 1, 8)),
            dma((8,)),
            dma((1,)),
        ],
        compiler_params=pltpu.CompilerParams(
            collective_id=2, has_side_effects=True, vmem_limit_bytes=62 << 20
        ),
    )(dctx, qkv, ot, lse, full_t, by_head, pre, sums, parts, small)


def finish_kernel(whole, *refs):
    little_ref, outs = refs[whole], refs[whole + 1 :]
    for src, dst in zip(refs[:whole], outs[:whole]):
        dst[...] = src[...]
    for at, dst in enumerate(outs[whole:]):
        dst[...] = little_ref[at, : dst.shape[0]]


def finish(arrays, little, counts):
    vmem = pl.BlockSpec(memory_space=pltpu.VMEM)
    shapes = [jax.ShapeDtypeStruct(a.shape, a.dtype) for a in arrays]
    shapes += [jax.ShapeDtypeStruct((count,), jnp.float32) for count in counts]
    return pl.pallas_call(
        functools.partial(finish_kernel, len(arrays)),
        name="finish",
        out_shape=tuple(shapes),
        in_specs=[vmem] * (len(arrays) + 1),
        out_specs=(vmem,) * len(shapes),
    )(*arrays, little)


def halves(grad):
    cut = grad.shape[2] // 2
    return jnp.concatenate([grad[:, :, :cut], grad[:, :, cut:]], axis=1)


def norm_parts(inputs):
    centred = inputs - jnp.mean(inputs, axis=-1, keepdims=True)
    inverse = lax.rsqrt(jnp.mean(centred * centred, axis=-1, keepdims=True) + EPSILON)
    return centred * inverse, inverse


def norm_back(grad, normed, inverse, gain):
    e = grad * gain
    return inverse * (
        e
        - jnp.mean(e, axis=-1, keepdims=True)
        - normed * jnp.mean(e * normed, axis=-1, keepdims=True)
    )


def column_sum(block):
    return jnp.sum(block.astype(jnp.float32), axis=0, keepdims=True)


def ffn_kernel(
    tok_ref,
    ctx_ref,
    cot_ref,
    par_ref,
    outw_ref,
    upw_hbm,
    downw_hbm,
    layer_ref,
    dctx_ref,
    pre_ref,
    small_ref,
    sums_ref,
    parts_ref,
    upw,
    downw,
    hid,
    hlow,
    hlow_t,
    norm1,
    slopes,
    active_t,
    pre2,
    gbranch,
    ghid,
    out,
    dparts,
    uparts,
    sum0,
    load_sem,
    keep_sem,
    osend_sem,
    orecv_sem,
    ssend_sem,
    srecv_sem,
):
    f32, bf16 = jnp.float32, jnp.bfloat16
    groups, rows, cols = ctx_ref.shape
    cols = cols // 2
    sides = 2
    width = tok_ref.shape[1]
    chunks = active_t.shape[0]
    each = width // 32
    tab, blk, chip, core = place()
    loads = (
        pltpu.make_async_copy(upw_hbm, upw, load_sem.at[0]),
        pltpu.make_async_copy(downw_hbm, downw, load_sem.at[1]),
    )
    for copy in loads:
        copy.start()

    greet_all(tab, blk)

    def par(at):
        return par_ref[at : at + 1]

    inverse1 = []
    contexts = [unfold(ctx_ref[group]) for group in range(groups)]
    for table in range(sides):
        cut = pl.ds(table * rows, rows)
        pre1 = tok_ref[cut].astype(f32) + par(0)
        for group in range(groups):
            pre1 += jnp.dot(
                contexts[group][table * rows : (table + 1) * rows],
                outw_ref[group * cols : (group + 1) * cols],
                preferred_element_type=f32,
            )
        normed, inverse = norm_parts(pre1)
        inverse1.append(inverse)
        hidden = normed * par(1) + par(2)
        low = hidden.astype(bf16)
        norm1[cut] = normed
        hid[cut] = hidden
        hlow[cut] = low
        hlow_t[:, cut] = low.T

    pre2[...] = hid[...] + par(3)
    for copy in loads:
        copy.wait()

    def forward(at):
        cut = pl.ds(pl.multiple_of(at * width, width), width)
        upper = jnp.dot(
            hlow[...], upw[:, cut], preferred_element_type=f32
        ) + par_ref[pl.ds(24 + at, 1)]
        cdf = 0.5 + 0.5 * lax.erf(upper * math.sqrt(0.5))
        act = (upper * cdf).astype(bf16)
        slopes[at] = cdf + upper * jnp.exp(-0.5 * upper * upper) * (1 / math.sqrt(2 * math.pi))
        active_t[at] = act.T
        pre2[...] += jnp.dot(act, downw[cut], preferred_element_type=f32)

    @pl.loop(0, chunks // 2)
    def _(pair):
        forward(2 * pair)
        forward(2 * pair + 1)

    normed, inverse = norm_parts(pre2[...])
    out[...] = (normed * par(4) + par(5)).astype(bf16).reshape(out.shape)
    return_rows(out, layer_ref, osend_sem, orecv_sem, "start")
    grad = cot_ref[...].astype(f32)
    small_ref[4:5] = column_sum(grad * normed)
    small_ref[5:6] = column_sum(grad)
    gpre2 = norm_back(grad, normed, inverse, par(4))
    ghid[...] = gpre2
    low = gpre2.astype(bf16)
    gbranch[...] = low
    small_ref[3:4] = column_sum(low)

    def core_copy(unit, src):
        return send_to(
            src.at[:, :, :, :, 1 - core],
            sum0.at[unit],
            ssend_sem.at[unit],
            srecv_sem.at[unit],
            (tab, 2 * chip + 1 - core),
        )

    def add_core(unit, parts):
        landed(sum0.at[unit], srecv_sem.at[unit])
        for a in range(2):
            for b in range(2):
                sum0[unit, a, b] = sum0[unit, a, b] + parts[a, b, :, :, core]

    @pl.loop(0, chunks)
    def _(at):
        wdown = jnp.dot(active_t[at], gbranch[...], preferred_element_type=f32)
        wdown = wdown.reshape(8, 4, each, width)
        for part in range(4):
            dparts[part, at // 2, lax.rem(at, 2)] = (
                halves(wdown[:, part]).astype(bf16).reshape(dparts.shape[3:])
            )

    for unit in range(4):
        core_copy(unit, dparts.at[unit]).start()

    @pl.loop(0, chunks)
    def _(at):
        cut = pl.ds(pl.multiple_of(at * width, width), width)

        @pl.when(jnp.logical_or(at == 1, at == 2))
        def _():
            for unit in (2 * at - 2, 2 * at - 1):
                add_core(unit, dparts.at[unit])

        gact = times_t(gbranch[...], downw[cut])
        gup = (gact * slopes[at]).astype(bf16)
        small_ref[pl.ds(6 + at, 1)] = column_sum(gup)
        ghid[...] += times_t(gup, upw[:, cut])
        wup = jnp.dot(hlow_t[...], gup, preferred_element_type=f32)
        uparts[at] = halves(wup.reshape(32, each, width)).astype(bf16).reshape(uparts.shape[1:])
        core_copy(4 + at, uparts.at[at]).start()

    small = [0.0, 0.0, 0.0]
    lows = []
    for table in range(sides):
        cut = pl.ds(table * rows, rows)
        grad, normed = ghid[cut], norm1[cut]
        small[1] += column_sum(grad * normed)
        small[2] += column_sum(grad)
        gpre1 = norm_back(grad, normed, inverse1[table], par(1))
        pre_ref[cut] = gpre1
        low = gpre1.astype(bf16)
        small[0] += column_sum(low)
        lows.append(low)
    low = jnp.concatenate(lows, axis=0)
    for at in range(3):
        small_ref[at : at + 1] = small[at]
    small_ref[10:] = jnp.zeros((6, width), f32)
    wouts = []
    for group in range(groups):
        dctx_ref[group] = fold(
            times_t(low, outw_ref[group * cols : (group + 1) * cols]).astype(bf16)
        )
        wout = jnp.dot(unfold(ctx_ref[group]).T, low, preferred_element_type=f32)
        wouts.append(halves(wout.reshape(8, each, width)).astype(bf16))
    for unit in range(4):
        core_copy(unit, dparts.at[unit]).wait_send()
    dparts[0] = jnp.concatenate(wouts, axis=0).reshape(dparts.shape[1:])
    keep = [pltpu.make_async_copy(dparts.at[0], parts_ref, keep_sem.at[0])]

    @pl.loop(0, 4)
    def _(at):
        add_core(4 + at, uparts.at[at])
        core_copy(4 + at, uparts.at[at]).wait_send()

    keep.append(pltpu.make_async_copy(sum0, sums_ref, keep_sem.at[1]))
    for copy in keep:
        copy.start()
    return_rows(out, layer_ref, osend_sem, orecv_sem, "wait")
    for copy in keep:
        copy.wait()


def ffn(tokens, ctx, cotangent, params, out_weight, up_weight, down_weight):
    total, width = tokens.shape
    chunks = up_weight.shape[1] // width
    unit = (2 * (width // 32), width // 2)
    any_space = pl.BlockSpec(memory_space=pl.ANY)
    vmem = pl.BlockSpec(memory_space=pltpu.VMEM)
    bf16, f32 = jnp.bfloat16, jnp.float32
    flops = 18 * total * width * chunks * width + 6 * total * width * width
    return pl.pallas_call(
        ffn_kernel,
        name="ffn",
        out_shape=(
            jax.ShapeDtypeStruct((2, total // 2, width), bf16),
            jax.ShapeDtypeStruct(ctx.shape, bf16),
            jax.ShapeDtypeStruct((total, width), f32),
            jax.ShapeDtypeStruct((16, width), f32),
            jax.ShapeDtypeStruct((8, 2, 2, 2, 2, *unit), bf16),
            jax.ShapeDtypeStruct((2, 2, 2, 2, 2, *unit), bf16),
        ),
        in_specs=[vmem, vmem, vmem, vmem, vmem, any_space, any_space],
        out_specs=(any_space, vmem, vmem, vmem, any_space, any_space),
        scratch_shapes=[
            pltpu.VMEM(up_weight.shape, bf16),
            pltpu.VMEM(down_weight.shape, bf16),
            pltpu.VMEM((total, width), f32),
            pltpu.VMEM((total, width), bf16),
            pltpu.VMEM((width, total), bf16),
            pltpu.VMEM((total, width), f32),
            pltpu.VMEM((chunks, total, width), f32),
            pltpu.VMEM((chunks, width, total), bf16),
            pltpu.VMEM((total, width), f32),
            pltpu.VMEM((total, width), bf16),
            pltpu.VMEM((total, width), f32),
            pltpu.VMEM((2, total // 2, width), bf16),
            pltpu.VMEM((4, 2, 2, 2, 2, 2, *unit), bf16),
            pltpu.VMEM((4, 2, 2, 2, 2, 2, *unit), bf16),
            pltpu.VMEM((8, 2, 2, 2, 2, *unit), bf16),
            pltpu.SemaphoreType.DMA((2,)),
            pltpu.SemaphoreType.DMA((2,)),
            pltpu.SemaphoreType.DMA((2,)),
            pltpu.SemaphoreType.DMA((2,)),
            pltpu.SemaphoreType.DMA((8,)),
            pltpu.SemaphoreType.DMA((8,)),
        ],
        compiler_params=pltpu.CompilerParams(
            collective_id=3, has_side_effects=True, vmem_limit_bytes=63 << 20
        ),
        cost_estimate=pl.CostEstimate(
            flops=flops, bytes_accessed=40 << 20, transcendentals=total * width * chunks
        ),
    )(tokens, ctx, cotangent, params, out_weight, up_weight, down_weight)


def shards_direct(
    tokens,
    lengths,
    qkv_weight,
    qkv_bias,
    out_weight,
    out_bias,
    attn_gain,
    attn_shift,
    up_weight,
    up_bias,
    down_weight,
    down_bias,
    ffn_gain,
    ffn_shift,
    cotangent,
):
    tables, rows, width = tokens.shape
    f32 = jnp.float32
    heads = width // HD // GROUPS
    row = lax.broadcasted_iota(jnp.int32, (32, width), 0)
    params = jnp.zeros((32, width), jnp.bfloat16)
    spans = [
        (at, at + 1, vector)
        for at, vector in enumerate(
            (out_bias, attn_gain, attn_shift, down_bias, ffn_gain, ffn_shift)
        )
    ]
    spans += [(8, 16, qkv_bias[:width]), (16, 24, qkv_bias[width:])]
    spans += [
        (24 + at, 25 + at, up_bias[at * width : (at + 1) * width])
        for at in range(up_bias.shape[0] // width)
    ]
    for first, last, vector in spans:
        params = jnp.where((row >= first) & (row < last), vector[None], params)

    params = params.astype(f32)
    ctx, my_tokens, my_cotangent, full_t, qkv, ot, lse, by_head = attend(
        tokens, lengths, params, qkv_weight, cotangent, heads
    )
    layer_out, dctx, pre, small, sums, parts = ffn(
        my_tokens.reshape(tables * rows, width),
        ctx,
        my_cotangent.reshape(tables * rows, width),
        params,
        out_weight,
        up_weight,
        down_weight,
    )
    *whole, little = attend_back(
        dctx, qkv, ot, lse, full_t, by_head, pre, small, sums, parts, heads
    )
    each = width // 32
    whole.insert(1, layer_out)
    (
        token_grad,
        layer_out,
        wgrad_qkv,
        wgrad_out,
        wgrad_up,
        wgrad_down,
        bgrad_out,
        ggrad_attn,
        sgrad_attn,
        bgrad_down,
        ggrad_ffn,
        sgrad_ffn,
        bgrad_up,
        bgrad_qkv,
    ) = finish(whole, little, [each] * 6 + [4 * each, 2 * each])
    return (
        layer_out,
        token_grad,
        wgrad_qkv,
        bgrad_qkv,
        wgrad_out,
        bgrad_out,
        ggrad_attn,
        sgrad_attn,
        wgrad_up,
        bgrad_up,
        wgrad_down,
        bgrad_down,
        ggrad_ffn,
        sgrad_ffn,
    )


def solution(mesh):
    in_specs = (
        P("tab", "blk", None),
        P("tab"),
        P(),
        P(),
        P(),
        P(),
        P(),
        P(),
        P(),
        P(),
        P(),
        P(),
        P(),
        P(),
        P("tab", "blk", None),
    )
    out_specs = (
        P("tab", "blk", None),
        P("tab", "blk", None),
        P(("tab", "blk"), None),
        P(("tab", "blk")),
        P(("tab", "blk"), None),
        P(("tab", "blk")),
        P(("tab", "blk")),
        P(("tab", "blk")),
        P(("tab", "blk"), None),
        P(("tab", "blk")),
        P(("tab", "blk"), None),
        P(("tab", "blk")),
        P(("tab", "blk")),
        P(("tab", "blk")),
    )
    tab_count, blk_count = mesh.shape["tab"], mesh.shape["blk"]

    def pick(*operands):
        table_count = operands[0].shape[0] // tab_count
        head_count = operands[0].shape[2] // HD
        direct = table_count == 2 and blk_count == 8 and tab_count == 4 and head_count % 4 == 0
        body = shards_direct if direct else shards_ring
        return jax.shard_map(
            body, mesh=mesh, in_specs=in_specs, out_specs=out_specs, check_vma=False
        )(*operands)

    return pick
```

```python
import functools
import math

import jax
import jax.numpy as jnp
from jax import lax
from jax.experimental import pallas as pl
from jax.experimental.pallas import tpu as pltpu
from jax.sharding import PartitionSpec as P

HD = 64


EPSILON = 1e-05
NEGATIVE = -1e30


def from_behind(block, axis, distance):
    devices = range(lax.axis_size(axis))
    route = [((i - distance) % len(devices), i) for i in devices]
    return lax.ppermute(block, axis, route)


def norm_rows(inputs, gains, shifts):
    row_mean = jnp.mean(inputs, axis=-1, keepdims=True)
    centred = inputs - row_mean
    row_var = jnp.mean(centred * centred, axis=-1, keepdims=True)
    return centred * lax.rsqrt(row_var + EPSILON) * gains + shifts


def gelu_exact(inputs):
    return jax.nn.gelu(inputs, approximate=False)


def times_back(left, right):
    return lax.dot_general(
        left, right, (((1,), (1,)), ((), ())), preferred_element_type=jnp.float32
    )


def over_rows(left, right):
    return lax.dot_general(
        left, right, (((0,), (0,)), ((), ())), preferred_element_type=jnp.float32
    )


def shards_ring(
    tokens,
    lengths,
    qkv_weight,
    qkv_bias,
    out_weight,
    out_bias,
    attn_gain,
    attn_shift,
    up_weight,
    up_bias,
    down_weight,
    down_bias,
    ffn_gain,
    ffn_shift,
    cotangent,
):
    table_count, row_count, model_width = tokens.shape
    head_count = model_width // HD
    cycle_size = lax.axis_size("blk")
    cycle_place = lax.axis_index("blk")
    score_scale = HD ** (-0.5)
    flat_tokens = tokens.reshape(table_count * row_count, model_width)
    bias_full = jnp.concatenate(
        [
            qkv_bias[:model_width].astype(jnp.float32),
            jnp.zeros((model_width,), jnp.float32),
            qkv_bias[model_width:].astype(jnp.float32),
        ]
    )
    qkv_low = (
        jnp.dot(flat_tokens, qkv_weight, preferred_element_type=jnp.float32) + bias_full
    ).astype(jnp.bfloat16)
    queries = qkv_low[:, :model_width].reshape(table_count, row_count, head_count, HD)
    key_values = qkv_low[:, model_width:].reshape(table_count, row_count, 2 * model_width)

    def key_mask(first_row, key_count):
        positions = first_row + jnp.arange(key_count, dtype=jnp.int32)
        return (positions[None, :] < lengths[:, None])[:, None, None, :]

    def split_pair(pair_block):
        key_count = pair_block.shape[1]
        keys_part = pair_block[:, :, :model_width].reshape(table_count, key_count, head_count, HD)
        values_part = pair_block[:, :, model_width:].reshape(table_count, key_count, head_count, HD)
        return (keys_part, values_part)

    pair_block = lax.all_gather(key_values, "blk", axis=1, tiled=True)
    running_max = jnp.full((table_count, row_count, head_count), NEGATIVE, jnp.float32)
    keys_part, values_part = split_pair(pair_block)
    is_valid = key_mask(jnp.int32(0), pair_block.shape[1])
    raw_scores = jnp.einsum(
        "trhd,tkhd->trhk", queries, keys_part, preferred_element_type=jnp.float32
    )
    scores = jnp.where(is_valid, raw_scores * score_scale, NEGATIVE)
    peak_new = jnp.maximum(running_max, jnp.max(scores, axis=-1))
    exponent = jnp.where(is_valid, jnp.exp(scores - peak_new[..., None]), 0.0)
    running_sum = jnp.sum(exponent, axis=-1)
    weighted = jnp.einsum(
        "trhk,tkhd->trhd",
        exponent.astype(jnp.bfloat16),
        values_part,
        preferred_element_type=jnp.float32,
    )
    running_max, running_sum, weighted = (peak_new, running_sum, weighted)
    context = weighted / running_sum[..., None]
    log_total = running_max + jnp.log(running_sum)
    context_low = context.reshape(table_count * row_count, model_width).astype(jnp.bfloat16)
    attended = jnp.dot(
        context_low, out_weight, preferred_element_type=jnp.float32
    ) + out_bias.astype(jnp.float32)
    pre_one = flat_tokens.astype(jnp.float32) + attended
    gain_one = attn_gain.astype(jnp.float32)
    shift_one = attn_shift.astype(jnp.float32)
    hidden = norm_rows(pre_one, gain_one, shift_one)
    hidden_low = hidden.astype(jnp.bfloat16)
    upper = jnp.dot(hidden_low, up_weight, preferred_element_type=jnp.float32) + up_bias.astype(
        jnp.float32
    )
    active = gelu_exact(upper).astype(jnp.bfloat16)
    pre_two = (
        hidden
        + jnp.dot(active, down_weight, preferred_element_type=jnp.float32)
        + down_bias.astype(jnp.float32)
    )
    gain_two = ffn_gain.astype(jnp.float32)
    shift_two = ffn_shift.astype(jnp.float32)
    layer_out = norm_rows(pre_two, gain_two, shift_two).astype(jnp.bfloat16).reshape(tokens.shape)
    grad_out = cotangent.reshape(table_count * row_count, model_width).astype(jnp.float32)
    _, norm_two_back = jax.vjp(norm_rows, pre_two, gain_two, shift_two)
    grad_pre_two, ggrad_ffn, sgrad_ffn = norm_two_back(grad_out)
    grad_branch = grad_pre_two.astype(jnp.bfloat16)
    wgrad_down = over_rows(active, grad_branch)
    bgrad_down = jnp.sum(grad_branch, axis=0, dtype=jnp.float32)
    grad_active = times_back(grad_branch, down_weight)
    _, gelu_back = jax.vjp(gelu_exact, upper)
    grad_upper = gelu_back(grad_active)[0].astype(jnp.bfloat16)
    wgrad_up = over_rows(hidden_low, grad_upper)
    bgrad_up = jnp.sum(grad_upper, axis=0, dtype=jnp.float32)
    grad_hidden = grad_pre_two + times_back(grad_upper, up_weight)
    _, norm_one_back = jax.vjp(norm_rows, pre_one, gain_one, shift_one)
    grad_pre_one, ggrad_attn, sgrad_attn = norm_one_back(grad_hidden)
    grad_attended = grad_pre_one.astype(jnp.bfloat16)
    wgrad_out = over_rows(context_low, grad_attended)
    bgrad_out = jnp.sum(grad_attended, axis=0, dtype=jnp.float32)
    grad_context = times_back(grad_attended, out_weight).astype(jnp.bfloat16)
    grad_heads = grad_context.reshape(table_count, row_count, head_count, HD)
    row_delta = jnp.sum(grad_heads.astype(jnp.float32) * context, axis=-1)

    def cycle_turn_step(cycle_turn, cycle_state):
        pair_now, pair_grads, grad_queries = cycle_state
        owner_index = (cycle_place - cycle_turn) % cycle_size
        keys_part, values_part = split_pair(pair_now)
        is_valid = key_mask(owner_index * row_count, row_count)
        raw_scores = jnp.einsum(
            "trhd,tkhd->trhk", queries, keys_part, preferred_element_type=jnp.float32
        )
        scores = jnp.where(is_valid, raw_scores * score_scale, NEGATIVE)
        probs = jnp.where(is_valid, jnp.exp(scores - log_total[..., None]), 0.0)
        grad_probs = jnp.einsum(
            "trhd,tkhd->trhk", grad_heads, values_part, preferred_element_type=jnp.float32
        )
        grad_raw = (probs * (grad_probs - row_delta[..., None]) * score_scale).astype(jnp.bfloat16)
        grad_queries = grad_queries + jnp.einsum(
            "trhk,tkhd->trhd", grad_raw, keys_part, preferred_element_type=jnp.float32
        )
        grad_keys = jnp.einsum(
            "trhk,trhd->tkhd", grad_raw, queries, preferred_element_type=jnp.float32
        )
        grad_values = jnp.einsum(
            "trhk,trhd->tkhd",
            probs.astype(jnp.bfloat16),
            grad_heads,
            preferred_element_type=jnp.float32,
        )
        pair_grads = pair_grads + jnp.concatenate(
            [
                grad_keys.reshape(table_count, row_count, model_width),
                grad_values.reshape(table_count, row_count, model_width),
            ],
            axis=-1,
        )
        pair_next = from_behind(pair_now, "blk", 1)
        grads_next = from_behind(pair_grads.astype(jnp.bfloat16), "blk", 1).astype(pair_grads.dtype)
        return (pair_next, grads_next, grad_queries)

    cycle_start = (
        key_values,
        jnp.zeros((table_count, row_count, 2 * model_width), jnp.float32),
        jnp.zeros((table_count, row_count, head_count, HD), jnp.float32),
    )
    _, pair_home, grad_queries = lax.fori_loop(0, cycle_size, cycle_turn_step, cycle_start)
    grad_qkv = jnp.concatenate(
        [
            grad_queries.reshape(table_count * row_count, model_width),
            pair_home.reshape(table_count * row_count, 2 * model_width),
        ],
        axis=-1,
    ).astype(jnp.bfloat16)
    wgrad_qkv = over_rows(flat_tokens, grad_qkv)
    column_sums = jnp.sum(grad_qkv, axis=0, dtype=jnp.float32)
    bgrad_qkv = jnp.concatenate([column_sums[:model_width], column_sums[2 * model_width :]])
    token_grad = (
        (grad_pre_one + times_back(grad_qkv, qkv_weight)).astype(jnp.bfloat16).reshape(tokens.shape)
    )
    (
        wgrad_qkv,
        bgrad_qkv,
        wgrad_out,
        bgrad_out,
        ggrad_attn,
        sgrad_attn,
        wgrad_up,
        bgrad_up,
        wgrad_down,
        bgrad_down,
        ggrad_ffn,
        sgrad_ffn,
    ) = (
        lax.psum_scatter(
            wgrad_qkv.astype(jnp.bfloat16), "tab", scatter_dimension=0, tiled=True
        ).astype(jnp.float32),
        lax.psum_scatter(
            bgrad_qkv.astype(jnp.bfloat16), "tab", scatter_dimension=0, tiled=True
        ).astype(jnp.float32),
        lax.psum_scatter(
            wgrad_out.astype(jnp.bfloat16), "tab", scatter_dimension=0, tiled=True
        ).astype(jnp.float32),
        lax.psum_scatter(
            bgrad_out.astype(jnp.bfloat16), "tab", scatter_dimension=0, tiled=True
        ).astype(jnp.float32),
        lax.psum_scatter(
            ggrad_attn.astype(jnp.bfloat16), "tab", scatter_dimension=0, tiled=True
        ).astype(jnp.float32),
        lax.psum_scatter(
            sgrad_attn.astype(jnp.bfloat16), "tab", scatter_dimension=0, tiled=True
        ).astype(jnp.float32),
        lax.psum_scatter(
            wgrad_up.astype(jnp.bfloat16), "tab", scatter_dimension=0, tiled=True
        ).astype(jnp.float32),
        lax.psum_scatter(
            bgrad_up.astype(jnp.bfloat16), "tab", scatter_dimension=0, tiled=True
        ).astype(jnp.float32),
        lax.psum_scatter(
            wgrad_down.astype(jnp.bfloat16), "tab", scatter_dimension=0, tiled=True
        ).astype(jnp.float32),
        lax.psum_scatter(
            bgrad_down.astype(jnp.bfloat16), "tab", scatter_dimension=0, tiled=True
        ).astype(jnp.float32),
        lax.psum_scatter(
            ggrad_ffn.astype(jnp.bfloat16), "tab", scatter_dimension=0, tiled=True
        ).astype(jnp.float32),
        lax.psum_scatter(
            sgrad_ffn.astype(jnp.bfloat16), "tab", scatter_dimension=0, tiled=True
        ).astype(jnp.float32),
    )
    (
        wgrad_qkv,
        bgrad_qkv,
        wgrad_out,
        bgrad_out,
        ggrad_attn,
        sgrad_attn,
        wgrad_up,
        bgrad_up,
        wgrad_down,
        bgrad_down,
        ggrad_ffn,
        sgrad_ffn,
    ) = (
        lax.psum_scatter(
            wgrad_qkv.astype(jnp.bfloat16), "blk", scatter_dimension=0, tiled=True
        ).astype(jnp.float32),
        lax.psum_scatter(
            bgrad_qkv.astype(jnp.bfloat16), "blk", scatter_dimension=0, tiled=True
        ).astype(jnp.float32),
        lax.psum_scatter(
            wgrad_out.astype(jnp.bfloat16), "blk", scatter_dimension=0, tiled=True
        ).astype(jnp.float32),
        lax.psum_scatter(
            bgrad_out.astype(jnp.bfloat16), "blk", scatter_dimension=0, tiled=True
        ).astype(jnp.float32),
        lax.psum_scatter(
            ggrad_attn.astype(jnp.bfloat16), "blk", scatter_dimension=0, tiled=True
        ).astype(jnp.float32),
        lax.psum_scatter(
            sgrad_attn.astype(jnp.bfloat16), "blk", scatter_dimension=0, tiled=True
        ).astype(jnp.float32),
        lax.psum_scatter(
            wgrad_up.astype(jnp.bfloat16), "blk", scatter_dimension=0, tiled=True
        ).astype(jnp.float32),
        lax.psum_scatter(
            bgrad_up.astype(jnp.bfloat16), "blk", scatter_dimension=0, tiled=True
        ).astype(jnp.float32),
        lax.psum_scatter(
            wgrad_down.astype(jnp.bfloat16), "blk", scatter_dimension=0, tiled=True
        ).astype(jnp.float32),
        lax.psum_scatter(
            bgrad_down.astype(jnp.bfloat16), "blk", scatter_dimension=0, tiled=True
        ).astype(jnp.float32),
        lax.psum_scatter(
            ggrad_ffn.astype(jnp.bfloat16), "blk", scatter_dimension=0, tiled=True
        ).astype(jnp.float32),
        lax.psum_scatter(
            sgrad_ffn.astype(jnp.bfloat16), "blk", scatter_dimension=0, tiled=True
        ).astype(jnp.float32),
    )
    return (
        layer_out,
        token_grad,
        wgrad_qkv,
        bgrad_qkv,
        wgrad_out,
        bgrad_out,
        ggrad_attn,
        sgrad_attn,
        wgrad_up,
        bgrad_up,
        wgrad_down,
        bgrad_down,
        ggrad_ffn,
        sgrad_ffn,
    )


GROUPS = 4
LANES = 128
LOG2E = math.log2(math.e)
MESH = pl.DeviceIdType.MESH


def times_t(left, right):
    return lax.dot_general(
        left, right, (((1,), (1,)), ((), ())), preferred_element_type=jnp.float32
    )


def place():
    tab, blk = lax.axis_index("tab"), lax.axis_index("blk")
    return tab, blk, blk // 2, blk % 2


def meet(tab, blk):
    barrier = pltpu.get_barrier_semaphore()

    @pl.loop(1, 8)
    def _(step):
        pl.semaphore_signal(
            barrier, inc=1, device_id=(tab, lax.rem(blk + step, 8)), device_id_type=MESH
        )

    pl.semaphore_wait(barrier, 7)


def greet_all(tab, blk):
    barrier = pltpu.get_barrier_semaphore()
    for step in range(1, 8):
        pl.semaphore_signal(
            barrier, inc=1, device_id=(tab, lax.rem(blk + step, 8)), device_id_type=MESH
        )
    for step in range(1, 4):
        pl.semaphore_signal(
            barrier, inc=1, device_id=(lax.rem(tab + step, 4), blk), device_id_type=MESH
        )
    pl.semaphore_wait(barrier, 10)


def send_to(src, dst, send_sem, recv_sem, device):
    return pltpu.make_async_remote_copy(
        src_ref=src,
        dst_ref=dst,
        send_sem=send_sem,
        recv_sem=recv_sem,
        device_id=device,
        device_id_type=MESH,
    )


def landed(ref, sem):
    pltpu.make_async_copy(ref, ref, sem).wait()


def return_rows(src, dst, send_sem, recv_sem, act):
    tab, _, chip, core = place()
    half, group = chip // 2, 2 * lax.rem(chip, 2) + core
    for side in range(2):
        is_own = jnp.logical_and(chip == group, core == side)
        own = pltpu.make_async_copy(src.at[side], dst.at[half], recv_sem.at[half])
        away = send_to(
            src.at[side],
            dst.at[half],
            send_sem.at[side],
            recv_sem.at[half],
            (tab, 2 * group + side),
        )
        if act == "start":
            pl.when(is_own)(own.start)
            pl.when(jnp.logical_not(is_own))(away.start)
        else:
            pl.when(jnp.logical_not(is_own))(away.wait_send)
            landed(dst.at[side], recv_sem.at[side])


def by_core(core, act):
    pl.when(core == 0)(functools.partial(act, 0))
    pl.when(core == 1)(functools.partial(act, 1))


def fold(block):
    cut = block.shape[0] // 2
    return jnp.concatenate([block[:cut], block[cut:]], axis=1)


def unfold(block):
    cut = block.shape[1] // 2
    return jnp.concatenate([block[:, :cut], block[:, cut:]], axis=0)


def own_window(group, first, rows_ref, out):
    start = pl.multiple_of(first + LANES * ((3 * group) // 2), LANES)
    window = rows_ref[:, pl.ds(start, 2 * LANES)].astype(jnp.float32)
    window = pltpu.roll(window, lax.rem(2 * LANES - HD * lax.rem(group, 2), 2 * LANES), 1)
    left = window[:, :LANES]
    low = lax.broadcasted_iota(jnp.int32, left.shape, 1) < HD
    for head, lanes in enumerate((left, pltpu.roll(left, HD, 1), window[:, LANES:])):
        out(head, jnp.where(low, lanes, 0.0))


def attend_kernel(
    heads,
    tok_ref,
    len_ref,
    par_ref,
    w_hbm,
    cot_hbm,
    ctx_ref,
    mytok_ref,
    mycot_ref,
    fullt_ref,
    qkv_ref,
    ot_ref,
    lse_ref,
    wr_ref,
    kt_ref,
    tokv,
    toktv,
    wfull,
    wrv,
    wown,
    bown,
    qkvv,
    vtv,
    ktv,
    otv,
    lsev,
    acc,
    peaks,
    cotv,
    csend,
    send_sem,
    recv,
    csend_sem,
    crecv_sem,
    osend_sem,
    orecv_sem,
    local_sem,
):
    tab, blk, chip, core = place()
    half = chip // 2
    group = 2 * lax.rem(chip, 2) + core
    rows = tok_ref.shape[1]
    width = tok_ref.shape[2]
    is_near = jnp.logical_or(chip == 1, chip == 2)
    mate = chip + 1 - 2 * lax.rem(chip, 2)
    other_near = 2 - half
    other_far = 3 - 3 * half
    own_far = 3 * half
    scale = LOG2E / math.sqrt(HD)

    def remote(src, dst, send_sem, recv_sem, to_chip, to_core):
        return pltpu.make_async_remote_copy(
            src_ref=src,
            dst_ref=dst,
            send_sem=send_sem,
            recv_sem=recv_sem,
            device_id=(tab, 2 * to_chip + to_core),
            device_id_type=MESH,
        )

    here, there = tok_ref.at[half], tok_ref.at[1 - half]
    to_mate = remote(here, tokv.at[blk], send_sem.at[0], recv.at[blk], mate, core)
    to_other = remote(there, tokv.at[blk], send_sem.at[1], recv.at[blk], other_near, core)
    to_side = remote(here, tokv.at[blk], send_sem.at[2], recv.at[blk], chip, 1 - core)

    def to_far(slot, src_chip):
        which = 2 * src_chip + core
        ref = tokv.at[which]
        return remote(ref, ref, send_sem.at[2 + slot], recv.at[which], own_far, core)

    def to_core(slot, src_chip):
        which = 2 * src_chip + core
        ref = tokv.at[which]
        return remote(ref, ref, send_sem.at[5 + slot], recv.at[which], chip, 1 - core)

    def arrived(which):
        pltpu.make_async_copy(tokv.at[which], tokv.at[which], recv.at[which]).wait()

    load = pltpu.make_async_copy(w_hbm, wfull, local_sem.at[5])
    load.start()
    meet(tab, blk)
    pl.when(is_near)(to_other.start)
    to_mate.start()
    to_side.start()
    own_tokens = pltpu.make_async_copy(tok_ref.at[half], tokv.at[blk], local_sem.at[11])
    own_tokens.start()

    lane1 = lax.broadcasted_iota(jnp.int32, (8, LANES), 1)
    for at in (0, 2):

        def keep_bias(head, lanes, at=at):
            row = jnp.where(lane1 == HD, 1.0, lanes)
            bown[:, pl.ds((at * heads + head) * LANES, LANES)] = row

        own_window(group, 0, par_ref.at[pl.ds(8 * (1 + at // 2), 8)], keep_bias)
    for head in range(heads):
        bown[:, pl.ds((heads + head) * LANES, LANES)] = jnp.zeros((8, LANES), jnp.float32)
    load.wait()
    for at in range(3):

        def keep_weight(head, lanes, at=at):
            wown[:, pl.ds((at * heads + head) * LANES, LANES)] = lanes.astype(jnp.bfloat16)

        own_window(group, at * width, wfull, keep_weight)

    length = len_ref[half]
    lane = lax.broadcasted_iota(jnp.int32, (rows, LANES), 1)
    row = lax.broadcasted_iota(jnp.int32, (rows, LANES), 0)

    def project(which):
        first = pl.multiple_of(which * rows, rows)
        tok = tokv[which]
        y = jnp.dot(tok, wown[...], preferred_element_type=jnp.float32) + bown[:1]
        pad = jnp.where((lane == HD) & (row + first >= length), NEGATIVE, 0.0)
        for head in range(heads):
            q, k, v = (
                y[:, (part * heads + head) * LANES :][:, :LANES] for part in range(3)
            )
            qkvv[head, pl.ds(first, rows)] = q.astype(jnp.bfloat16)
            qkvv[heads + head, pl.ds(first, rows)] = (k + pad).astype(jnp.bfloat16)
            qkvv[2 * heads + head, pl.ds(first, rows)] = v.astype(jnp.bfloat16)
            vtv[head, :, pl.ds(first, rows)] = v.T.astype(jnp.bfloat16)
            ktv[head, :, pl.ds(first, rows)] = k.T.astype(jnp.bfloat16)
        toktv[:, pl.ds(first, rows)] = tok.T

    def take_keys(tile, head, first_key, count, fresh):
        queries = pl.ds(pl.multiple_of(tile * 2 * rows, 2 * rows), 2 * rows)
        keys = pl.ds(pl.multiple_of(first_key, count), count)
        st = times_t(qkvv[heads + head, keys], qkvv[head, queries])
        peak = jnp.max(st, axis=0, keepdims=True)
        if not fresh:
            before = peaks[tile, pl.ds(head, 1)]
            peak = jnp.maximum(peak, before)
        pt = jnp.exp2((st - peak) * scale).astype(jnp.bfloat16)
        ot = jnp.dot(vtv[head, :, keys], pt, preferred_element_type=jnp.float32)
        if not fresh:
            ot += acc[tile, head] * jnp.exp2((before - peak) * scale)
        acc[tile, head] = ot
        peaks[tile, pl.ds(head, 1)] = peak

    def meet_keys_of_own_half():
        @pl.loop(0, 2 * heads)
        def _(at):
            tile = jnp.where(at < heads, chip, mate)
            take_keys(tile, lax.rem(at, heads), half * 4 * rows, 4 * rows, True)

    def meet_keys_of_near():
        @pl.loop(0, heads)
        def _(head):
            take_keys(other_near, head, half * 4 * rows, 4 * rows, True)

        @pl.loop(0, 3 * heads)
        def _(at):
            tile = jnp.where(at < heads, chip, jnp.where(at < 2 * heads, mate, other_near))
            take_keys(tile, lax.rem(at, heads), other_near * 2 * rows, 2 * rows, False)

    def owner_of(table):
        return 2 * table + chip // 2, lax.rem(chip, 2)

    def cotangent_copy(table, own):
        src, dst = cot_hbm.at[table], mycot_ref.at[core]
        if own:
            return pltpu.make_async_copy(cotv, dst, orecv_sem.at[core])
        return remote(src, dst, osend_sem.at[table], orecv_sem.at[core], *owner_of(table))

    def is_owner(table):
        to_chip, to_core = owner_of(table)
        return jnp.logical_and(to_chip == chip, to_core == core)

    own_tokens.wait()
    own_cotangent = pltpu.make_async_copy(cot_hbm.at[half], cotv, local_sem.at[10])
    pl.when(is_owner(half))(own_cotangent.start)
    project(blk)

    @pl.when(is_owner(half))
    def _():
        own_cotangent.wait()
        cotangent_copy(half, True).start()

    def half_lanes(part, at):
        first = part * width + LANES * (at // 2)
        return wfull[:, first : first + LANES][:, HD * (at % 2) :][:, :HD]

    for head in range(heads):
        for part in range(3):
            for pair in range(GROUPS // 2):
                at = 2 * pair * heads + head
                wrv[head, :, pl.ds((2 * part + pair) * LANES, LANES)] = jnp.concatenate(
                    [half_lanes(part, at), half_lanes(part, at + heads)], axis=1
                )
    arrived(2 * mate + core)
    to_core(0, mate).start()

    @pl.when(jnp.logical_not(is_near))
    def _():
        to_mate.wait_send()
        to_other.start()

    project(2 * mate + core)
    arrived(2 * chip + 1 - core)
    project(2 * chip + 1 - core)
    arrived(2 * mate + 1 - core)
    project(2 * mate + 1 - core)

    def pass_on(slot, src_chip):
        arrived(2 * src_chip + core)
        pl.when(is_near)(to_far(slot, src_chip).start)
        to_core(slot, src_chip).start()

    def project_chip(src_chip):
        project(2 * src_chip + core)
        arrived(2 * src_chip + 1 - core)
        project(2 * src_chip + 1 - core)

    pl.when(is_near)(functools.partial(pass_on, 1, other_near))
    meet_keys_of_own_half()
    pl.when(jnp.logical_not(is_near))(functools.partial(pass_on, 1, other_near))
    pl.when(is_near)(functools.partial(pass_on, 2, other_far))
    cotangent_copy(1 - half, False).start()
    project_chip(other_near)
    meet_keys_of_near()
    pl.when(jnp.logical_not(is_near))(functools.partial(pass_on, 2, other_far))
    project_chip(other_far)

    keep = (
        pltpu.make_async_copy(toktv, fullt_ref, local_sem.at[0]),
        pltpu.make_async_copy(qkvv, qkv_ref, local_sem.at[1]),
        pltpu.make_async_copy(wrv, wr_ref, local_sem.at[6]),
        pltpu.make_async_copy(ktv, kt_ref, local_sem.at[9]),
    )
    for copy in keep:
        copy.start()

    pl.when(jnp.logical_not(is_owner(half)))(cotangent_copy(half, False).start)
    my_tokens = [
        pltpu.make_async_copy(
            tokv.at[2 * group + side], mytok_ref.at[side], local_sem.at[7 + side]
        )
        for side in range(2)
    ]
    for copy in my_tokens:
        copy.start()

    def context_copy(which):
        return remote(
            csend.at[which],
            ctx_ref.at[group],
            csend_sem.at[which],
            crecv_sem.at[group],
            2 * half + which // 2,
            lax.rem(which, 2),
        )

    own_context = pltpu.make_async_copy(
        csend.at[group], ctx_ref.at[group], local_sem.at[2]
    )

    @pl.loop(0, 4)
    def _(step):
        at = jnp.where(is_near, step, 3 - step)
        which = jnp.where(
            at < 2, jnp.where(at == 0, chip, mate), jnp.where(at == 2, other_near, other_far)
        )

        @pl.when(at == 3)
        def _():
            @pl.loop(0, heads)
            def _(head):
                take_keys(which, head, 0, 8 * rows, True)

        @pl.when(at < 3)
        def _():
            @pl.loop(0, heads)
            def _(head):
                take_keys(which, head, other_far * 2 * rows, 2 * rows, False)

        for head in range(heads):
            ot = acc[which, head]
            total = ot[HD : HD + 1]
            otv[which, head * HD : (head + 1) * HD] = ot[:HD] / total
            peak = peaks[which, head : head + 1]
            lsev[which, head : head + 1] = peak * scale + jnp.log(total) * LOG2E
        csend[which] = fold(otv[which].T.astype(jnp.bfloat16))

        pl.when(which == group)(own_context.start)
        pl.when(which != group)(context_copy(which).start)

    more = (
        pltpu.make_async_copy(otv, ot_ref, local_sem.at[3]),
        pltpu.make_async_copy(lsev, lse_ref, local_sem.at[4]),
    )
    for copy in more:
        copy.start()
    pl.when(is_near)(to_mate.wait_send)
    to_other.wait_send()
    to_side.wait_send()
    to_core(0, mate).wait_send()
    for slot, src_chip in ((1, other_near), (2, other_far)):
        pl.when(is_near)(to_far(slot, src_chip).wait_send)
        to_core(slot, src_chip).wait_send()

    for step in range(1, 4):
        which = lax.rem(group + step, 4)
        context_copy(which).wait_send()
        pltpu.make_async_copy(ctx_ref.at[which], ctx_ref.at[which], crecv_sem.at[which]).wait()
    own_context.wait()
    pl.when(jnp.logical_not(is_owner(half)))(cotangent_copy(half, False).wait_send)
    cotangent_copy(1 - half, False).wait_send()
    for side in range(2):
        pltpu.make_async_copy(mycot_ref.at[side], mycot_ref.at[side], orecv_sem.at[side]).wait()
    for copy in [*keep, *more, *my_tokens]:
        copy.wait()


def attend(tokens, lengths, params, qkv_weight, cotangent, heads):
    _, rows, width = tokens.shape
    blocks = 8
    total = blocks * rows
    any_space = pl.BlockSpec(memory_space=pl.ANY)
    vmem = pl.BlockSpec(memory_space=pltpu.VMEM)
    bf16, f32 = jnp.bfloat16, jnp.float32
    dma = pltpu.SemaphoreType.DMA
    return pl.pallas_call(
        functools.partial(attend_kernel, heads),
        name="attend",
        out_shape=(
            jax.ShapeDtypeStruct((GROUPS, rows, 2 * heads * HD), bf16),
            jax.ShapeDtypeStruct((2, rows, width), bf16),
            jax.ShapeDtypeStruct((2, rows, width), bf16),
            jax.ShapeDtypeStruct((width, total), bf16),
            jax.ShapeDtypeStruct((3 * heads, total, LANES), bf16),
            jax.ShapeDtypeStruct((4, heads * HD, 2 * rows), f32),
            jax.ShapeDtypeStruct((4, 8, 2 * rows), f32),
            jax.ShapeDtypeStruct((heads, width, width), bf16),
            jax.ShapeDtypeStruct((heads, LANES, total), bf16),
        ),
        in_specs=[
            any_space,
            pl.BlockSpec(memory_space=pltpu.SMEM),
            vmem,
            any_space,
            any_space,
        ],
        out_specs=(any_space,) * 9,
        scratch_shapes=[
            pltpu.VMEM((blocks, rows, width), bf16),
            pltpu.VMEM((width, total), bf16),
            pltpu.VMEM(qkv_weight.shape, bf16),
            pltpu.VMEM((heads, width, width), bf16),
            pltpu.VMEM((width, 3 * heads * LANES), bf16),
            pltpu.VMEM((8, 3 * heads * LANES), f32),
            pltpu.VMEM((3 * heads, total, LANES), bf16),
            pltpu.VMEM((heads, LANES, total), bf16),
            pltpu.VMEM((heads, LANES, total), bf16),
            pltpu.VMEM((4, heads * HD, 2 * rows), f32),
            pltpu.VMEM((4, 8, 2 * rows), f32),
            pltpu.VMEM((4, heads, LANES, 2 * rows), f32),
            pltpu.VMEM((4, 8, 2 * rows), f32),
            pltpu.VMEM((rows, width), bf16),
            pltpu.VMEM((GROUPS, rows, 2 * heads * HD), bf16),
            dma((8,)),
            dma((blocks,)),
            dma((GROUPS,)),
            dma((GROUPS,)),
            dma((2,)),
            dma((2,)),
            dma((12,)),
        ],
        compiler_params=pltpu.CompilerParams(
            collective_id=1, has_side_effects=True, vmem_limit_bytes=60 << 20
        ),
    )(tokens, lengths, params, qkv_weight, cotangent)


UNITS = 9
TURNS = 4
STAGES = 5
PHASE = ((1, 3), (2, 5), (3, 8), (4, 11))


def attend_back_kernel(
    heads,
    dctx_ref,
    qkv_ref,
    ot_ref,
    lse_ref,
    kt_ref,
    fullt_ref,
    w_ref,
    pre_ref,
    sums_ref,
    parts_ref,
    small_ref,
    tgrad_ref,
    wqkv_ref,
    wout_ref,
    wup_ref,
    wdown_ref,
    little_ref,
    dov,
    doh,
    deltas,
    qkvv,
    otv,
    lsev,
    toktv,
    wv,
    prev,
    ktv,
    dqv,
    dkv,
    dvv,
    dqkv,
    qsend,
    kvsend,
    arrive_q,
    arrive_kv,
    joined,
    xacc,
    xsend,
    mine,
    sum0,
    sum1,
    sum2,
    sum3,
    sum4,
    slab,
    slab_in,
    sums,
    sums_in,
    line,
    line_in,
    small_in,
    small_sum,
    small_pairs,
    dsend_sem,
    drecv_sem,
    gsend_sem,
    grecv_sem,
    xsend_sem,
    xrecv_sem,
    ssend_sem,
    srecv_sem,
    tsend_sem,
    trecv_sem,
    lsend_sem,
    lrecv_sem,
    local_sem,
    mine_sem,
):
    f32, bf16 = jnp.float32, jnp.bfloat16
    tab, blk, chip, core = place()
    y, x, zh, zl = tab // 2, lax.rem(tab, 2), chip // 2, lax.rem(chip, 2)
    half = zh
    group = 2 * zl + core
    blocks, rows = 8, dov.shape[1]
    width = toktv.shape[0]
    tile = 2 * rows
    piece = 256
    scale = LOG2E / math.sqrt(HD)
    shrink = HD**-0.5

    remote = send_to

    loads = [
        pltpu.make_async_copy(src, dst, local_sem.at[at])
        for at, (src, dst) in enumerate(
            (
                (qkv_ref, qkvv),
                (ot_ref, otv),
                (lse_ref, lsev),
                (dctx_ref.at[group], dov.at[group]),
                (fullt_ref, toktv),
                (w_ref, wv),
                (pre_ref, prev),
                (sums_ref, sum0.at[: UNITS - 1]),
                (kt_ref, ktv),
            )
        )
    ]
    for copy in [*loads[:4], loads[8], loads[7]]:
        copy.start()

    greet_all(tab, blk)

    def group_at(step):
        to_chip = jnp.where(step < 2, zl, 1 - zl)
        return 2 * to_chip + jnp.where(lax.rem(step, 2) == 0, core, 1 - core)

    def context_copy(which):
        return remote(
            dctx_ref.at[which],
            dov.at[group],
            dsend_sem.at[which],
            drecv_sem.at[group],
            (tab, 4 * half + which),
        )

    for step in range(1, 4):
        context_copy(group_at(step)).start()

    def stage_copy(stage, unit, order=None, held=None):
        held = sum0 if held is None else held
        send, done = ssend_sem.at[stage, unit], srecv_sem.at[stage, unit]
        if stage == 0:
            src = parts_ref.at[:, :, :, :, 1 - core]
            return remote(src, sum0.at[unit], send, done, (tab, 2 * chip + 1 - core))
        if stage == 1 and order == 0:
            return remote(
                held.at[unit, :, 1 - x], sum1.at[unit], send, done, (2 * y + 1 - x, blk)
            )
        if stage == 1:
            return remote(
                held.at[unit, 1 - y], sum1.at[unit], send, done, (2 * (1 - y) + x, blk)
            )
        if stage == 2 and order == 0:
            return remote(
                sum1.at[unit, 1 - y], sum2.at[unit], send, done, (2 * (1 - y) + x, blk)
            )
        if stage == 2:
            return remote(
                sum1.at[unit, 1 - x], sum2.at[unit], send, done, (2 * y + 1 - x, blk)
            )
        if stage == 3:
            src, there = sum2.at[unit, :, 1 - zl], 2 * zh + 1 - zl
            return remote(src, sum3.at[unit], send, done, (tab, 2 * there + core))
        src, there = sum3.at[unit, 1 - zh], 2 * (1 - zh) + zl
        return remote(src, sum4.at[unit], send, done, (tab, 2 * there + core))

    both = functools.partial(by_core, core)
    mine_copy = pltpu.make_async_copy(
        parts_ref.at[:, :, :, :, core], mine, mine_sem.at[0]
    )

    def finish(unit):
        done = sum4[unit].astype(f32) + sum3[unit, zh].astype(f32)
        top, low = done[: done.shape[0] // 2], done[done.shape[0] // 2 :]
        each, cut = top.shape

        @pl.when(unit < 4)
        def _():
            at = pl.ds(pl.multiple_of(unit * each, each), each)
            wdown_ref[at, :cut] = top
            wdown_ref[at, cut:] = low

        @pl.when(jnp.logical_and(unit >= 4, unit < 8))
        def _():
            at = pl.multiple_of((unit - 4) * 2 * cut, 2 * cut)
            wup_ref[:, pl.ds(at, cut)] = top
            wup_ref[:, pl.ds(pl.multiple_of(at + cut, cut), cut)] = low

        @pl.when(unit == 8)
        def _():
            wout_ref[:, :cut] = top
            wout_ref[:, cut:] = low

    def advance(stage, unit):
        if stage == 0:
            landed(sum0.at[unit], srecv_sem.at[0, unit])
            mine_copy.wait()
            for a in range(2):
                for b in range(2):
                    sum0[unit, a, b] = sum0[unit, a, b] + mine[a, b]

            both(lambda order: stage_copy(1, unit, order).start())
        elif stage == 1:
            landed(sum1.at[unit], srecv_sem.at[1, unit])

            def act(order):
                own = sum0[unit, :, x] if order == 0 else sum0[unit, y]
                sum1[unit] = sum1[unit] + own
                stage_copy(2, unit, order).start()

            both(act)
        elif stage == 2:
            landed(sum2.at[unit], srecv_sem.at[2, unit])

            def act(order):
                sum2[unit] = sum2[unit] + sum1[unit, y if order == 0 else x]

            both(act)
            stage_copy(3, unit).start()
        elif stage == 3:
            landed(sum3.at[unit], srecv_sem.at[3, unit])
            sum3[unit] = sum3[unit] + sum2[unit, :, zl]
            stage_copy(4, unit).start()
        else:
            landed(sum4.at[unit], srecv_sem.at[4, unit])
            finish(unit)

    def tick(now):
        @pl.when(now < UNITS - 1)
        def _():
            both(lambda order: stage_copy(1, now, order, sums_ref).start())

        pl.when(now == UNITS - 1)(functools.partial(advance, 0, UNITS - 1))
        for stage, lag in PHASE:
            unit = now - lag
            due = (unit >= 0) & (unit < UNITS)
            pl.when(due)(functools.partial(advance, stage, unit))

    stage_copy(0, UNITS - 1).start()
    mine_copy.start()

    def tab_copy(src, dst, sem_at, step):
        there = lax.rem(tab + step, 4)
        return remote(
            src(there), dst(tab), tsend_sem.at[sem_at, there], trecv_sem.at[sem_at, tab], (there, blk)
        )

    def line_copy(src, dst, sem_at, step):
        there = lax.rem(blk + step, 8)
        return remote(
            src(there), dst(blk), lsend_sem.at[sem_at, there], lrecv_sem.at[sem_at, blk], (tab, there)
        )

    def small_tab(step):
        return tab_copy(lambda t: small_ref, lambda t: small_in.at[t], heads, step)

    def small_pair(at):
        there = (2 * chip + 1 - core, 2 * (2 * zh + 1 - zl) + core, 2 * (2 * (1 - zh) + zl) + core)
        return remote(
            small_sum.at[at],
            small_pairs.at[at],
            lsend_sem.at[heads, at],
            lrecv_sem.at[heads, at],
            (tab, there[at]),
        )

    def slab_tab(head, step):
        return tab_copy(
            lambda t: slab.at[head, t], lambda t: slab_in.at[head, t], head, step
        )

    def slab_blk(head, step):
        return line_copy(
            lambda b: line.at[head, b], lambda b: line_in.at[head, b], head, step
        )

    for step in range(1, 4):
        small_tab(step).start()

    def pass_small(at):
        if at == 0:
            total = small_ref[...]
            for step in range(1, 4):
                there = lax.rem(tab + step, 4)
                landed(small_in.at[there], trecv_sem.at[heads, there])
                total += small_in[there]
        else:
            landed(small_pairs.at[at - 1], lrecv_sem.at[heads, at - 1])
            total = small_sum[at - 1] + small_pairs[at - 1]
        small_sum[at] = total
        if at < 3:
            small_pair(at).start()

    def sums_tab(head, step):
        return tab_copy(
            lambda t: sums.at[head], lambda t: sums_in.at[head, t], heads + 1 + head, step
        )

    def make_slab(head):
        flat = dqkv[head]
        sums[head] = jnp.broadcast_to(
            jnp.sum(flat.astype(f32), axis=0, keepdims=True), (8, 3 * HD)
        )
        grad = jnp.dot(toktv[...], flat, preferred_element_type=f32)
        each = width // 32
        slab[head, :, :4] = grad[:, : 2 * HD].reshape(4, 4, 2 * each, 2 * HD).astype(bf16)
        q = grad[:, 2 * HD :].reshape(16, 2, each, HD)
        q = jnp.concatenate([q[:, 0], q[:, 1]], axis=2)
        slab[head, :, 4:] = q.reshape(4, 2, 2 * each, 2 * HD).astype(bf16)
        for step in range(1, 4):
            slab_tab(head, step).start()
            sums_tab(head, step).start()

    def pass_slab(head):
        total = slab[head, tab].astype(f32)
        sums_total = sums[head]
        for step in range(1, 4):
            there = lax.rem(tab + step, 4)
            landed(slab_in.at[head, there], trecv_sem.at[head, there])
            landed(sums_in.at[head, there], trecv_sem.at[heads + 1 + head, there])
            total += slab_in[head, there].astype(f32)
            sums_total += sums_in[head, there]
        each = width // 32
        for b in range(8):
            kv = total[b // 2, b % 2 * each :][:each]
            q = total[4 + b // 4, b // 2 % 2 * each :][:each, b % 2 * HD :][:, :HD]
            rows_b = jnp.concatenate([jnp.concatenate([kv, q], axis=1), sums_total], axis=0)
            line[head, b] = fold(rows_b).astype(bf16)
        line_in[head, blk] = line[head, blk]
        for step in range(1, 8):
            slab_blk(head, step).start()

    for copy in [*loads[:4], loads[8]]:
        copy.wait()

    def gradient_copies(head, which, own):
        slot = group * heads + head
        pairs = (
            (qsend.at[head, which], arrive_q.at[slot]),
            (kvsend.at[head, which], arrive_kv.at[slot]),
        )
        for kind, (src, dst) in enumerate(pairs):
            if own:
                yield pltpu.make_async_copy(src, dst, grecv_sem.at[kind, slot])
            else:
                yield remote(
                    src,
                    dst,
                    gsend_sem.at[kind, head, which],
                    grecv_sem.at[kind, slot],
                    (tab, 4 * half + which),
                )

    def send_gradient(kind, head, which):
        @pl.when(which == group)
        def _():
            list(gradient_copies(head, which, True))[kind].start()

        @pl.when(which != group)
        def _():
            list(gradient_copies(head, which, False))[kind].start()

    def absorb(head):
        for at in range(GROUPS):
            slot = at * heads + head
            landed(arrive_q.at[slot], grecv_sem.at[0, slot])
            landed(arrive_kv.at[slot], grecv_sem.at[1, slot])
        for pair in range(GROUPS // 2):
            left, right = 2 * pair * heads + head, (2 * pair + 1) * heads + head
            lanes = slice(pair * LANES, (pair + 1) * LANES)
            for side in range(2):
                cut = slice(side * HD, (side + 1) * HD)
                joined[side * rows : (side + 1) * rows, lanes] = jnp.concatenate(
                    [arrive_q[left][:, cut], arrive_q[right][:, cut]], axis=1
                )
                lanes_kv = slice((2 * side + 2 + pair) * LANES, (2 * side + 3 + pair) * LANES)
                joined[:, lanes_kv] = jnp.concatenate(
                    [arrive_kv[left][:, cut], arrive_kv[right][:, cut]], axis=1
                )

    @pl.loop(0, heads * TURNS)
    def _(turn):
        head, step = turn // TURNS, lax.rem(turn, TURNS)
        which = group_at(step)
        first = pl.multiple_of(which * tile, tile)

        @pl.when(head == 0)
        def _():
            @pl.when(step > 0)
            def _():
                landed(dov.at[which], drecv_sem.at[which])

            dos = unfold(dov[which])
            dos_t = dos.T.astype(f32)
            for at in range(heads):
                do = dos[:, at * HD : (at + 1) * HD]
                doh[at, pl.ds(first, tile)] = do
                rows_at = slice(at * HD, (at + 1) * HD)
                ot = otv[which, rows_at]
                deltas[at, which, :1] = jnp.sum(ot * dos_t[rows_at], axis=0, keepdims=True)

        @pl.when(step == 0)
        def _():
            dkv[...] = jnp.zeros_like(dkv)
            dvv[...] = jnp.zeros_like(dvv)

        @pl.when(turn == 1)
        def _():
            for copy in loads[4:7]:
                copy.start()

        pl.when(turn == PHASE[0][1])(loads[7].wait)
        tick(turn)

        q_full = qkvv[head, pl.ds(first, tile)]
        q = q_full[:, :HD]
        do = doh[head, pl.ds(first, tile)]
        delta = deltas[head, which, :1]
        lse = lsev[which, pl.ds(head, 1)]
        dqt = jnp.zeros((LANES, tile), f32)
        for at in range(blocks * rows // piece):
            cut = pl.ds(at * piece, piece)
            st = times_t(qkvv[heads + head, cut], q_full)
            pt = jnp.exp2(st * scale - lse)
            dpt = times_t(qkvv[2 * heads + head, cut][:, :HD], do)
            dst = (pt * (dpt - delta)).astype(bf16)
            dvv[cut] += jnp.dot(pt.astype(bf16), do, preferred_element_type=f32)
            dkv[cut] += jnp.dot(dst, q, preferred_element_type=f32)
            dqt += jnp.dot(ktv[head, :, cut], dst, preferred_element_type=f32)
        dq = (dqt[:HD].T * shrink).astype(bf16)
        dqv[pl.ds(first, tile)] = dq
        qsend[head, which] = jnp.concatenate([dq[:rows], dq[rows:]], axis=1)
        send_gradient(0, head, which)

        @pl.when(step == TURNS - 1)
        def _():
            @pl.loop(0, 4)
            def _(at):
                there = lax.rem(group + 1 + at, 4)
                cut = pl.ds(pl.multiple_of(there * tile, tile), tile)
                pair = jnp.concatenate([dkv[cut] * shrink, dvv[cut]], axis=1).astype(bf16)
                kvsend[head, there] = pair
                send_gradient(1, head, there)
                dqkv[head, cut] = jnp.concatenate([pair, dqv[cut]], axis=1)

        @pl.when(turn == TURNS)
        def _():
            loads[4].wait()
            pass_small(0)

        for at in range(1, 4):
            pl.when(turn == TURNS + at)(functools.partial(pass_small, at))


    loads[5].wait()
    for head in range(heads - 1):
        absorb(head)
        product = times_t(joined[...], wv[head])
        xacc[...] = product if head == 0 else xacc[...] + product
    tick(heads * TURNS)
    absorb(heads - 1)
    loads[6].wait()
    for side in range(2):
        at = pl.ds(side * rows, rows)
        total = prev[at] + xacc[at] + times_t(joined[at], wv[heads - 1])
        xsend[side] = total.astype(bf16)
    return_rows(xsend, tgrad_ref, xsend_sem, xrecv_sem, "start")

    for head in range(heads):
        make_slab(head)
        tick(heads * TURNS + 1 + head)
    for head in range(heads):
        pass_slab(head)
    for now in range(heads * TURNS + 1 + heads, PHASE[-1][1] + UNITS):
        tick(now)

    def slabs_in(head, at):
        return [unfold(line_in[head, half_at * GROUPS + at].astype(f32)) for half_at in range(2)]

    for head in range(heads):
        for step in range(1, 8):
            there = lax.rem(blk + step, 8)
            landed(line_in.at[head, there], lrecv_sem.at[head, there])
    total = small_sum[3]
    own = [
        functools.reduce(jnp.add, slabs_in(at % heads, at // heads))
        for at in range(GROUPS * heads)
    ]
    each = width // 32
    bias = []
    for part in range(3):
        cut = slice((part + 2) % 3 * HD, (part + 2) % 3 * HD + HD)
        for pair in range(GROUPS * heads // 2):
            both_heads = jnp.concatenate([own[2 * pair][:, cut], own[2 * pair + 1][:, cut]], axis=1)
            lanes = slice(part * width + pair * LANES, part * width + (pair + 1) * LANES)
            wqkv_ref[:, lanes] = both_heads[:each]
            bias.append(both_heads[each:])
    pairs = GROUPS * heads // 2
    bias_q = jnp.concatenate(bias[:pairs], axis=1)
    bias_v = jnp.concatenate(bias[2 * pairs :], axis=1)
    bias = jnp.where(tab < 2, bias_q, bias_v)

    row = lax.broadcasted_iota(jnp.int32, (width, LANES), 0)
    lane = lax.broadcasted_iota(jnp.int32, (width, LANES), 1)

    def take(block, first, count):
        chosen = jnp.where((row == first + lane) & (lane < count), 1.0, 0.0)
        return jnp.dot(
            block, chosen, preferred_element_type=f32, precision=lax.Precision.HIGHEST
        )

    index = 8 * tab + blk
    little_ref[0:8] = take(total[:8], each * index, each)
    at_row = lax.broadcasted_iota(jnp.int32, total.shape, 0) == 6 + tab
    wide = jnp.sum(jnp.where(at_row, total, 0.0), axis=0, keepdims=True)
    little_ref[6:7] = take(jnp.broadcast_to(wide, (8, width)), 4 * each * blk, 4 * each)[:1]
    little_ref[7:8] = take(bias, 2 * each * lax.rem(index, 16), 2 * each)[:1]

    return_rows(xsend, tgrad_ref, xsend_sem, xrecv_sem, "wait")
    for step in range(1, 4):
        context_copy(group_at(step)).wait_send()

    @pl.loop(0, heads)
    def _(head):
        @pl.loop(1, 4)
        def _(step):
            for copy in gradient_copies(head, lax.rem(group + step, 4), False):
                copy.wait_send()

    for step in range(1, 8):
        for head in range(heads):
            slab_blk(head, step).wait_send()
    for at in range(3):
        small_pair(at).wait_send()
    for step in range(1, 4):
        small_tab(step).wait_send()
        for head in range(heads):
            slab_tab(head, step).wait_send()
            sums_tab(head, step).wait_send()

    stage_copy(0, UNITS - 1).wait_send()

    @pl.loop(0, UNITS)
    def _(unit):
        both(lambda order: stage_copy(1, unit, order).wait_send())
        both(lambda order: stage_copy(2, unit, order).wait_send())
        stage_copy(3, unit).wait_send()
        stage_copy(4, unit).wait_send()


def attend_back(dctx, qkv, ot, lse, kt, full_t, by_head, pre, small, sums, parts, heads):
    width, total = full_t.shape
    blocks = 8
    rows = total // blocks
    each, ff = width // 32, 4 * width
    any_space = pl.BlockSpec(memory_space=pl.ANY)
    vmem = pl.BlockSpec(memory_space=pltpu.VMEM)
    bf16, f32 = jnp.bfloat16, jnp.float32
    dma = pltpu.SemaphoreType.DMA
    unit = parts.shape[-2:]
    shape = jax.ShapeDtypeStruct
    return pl.pallas_call(
        functools.partial(attend_back_kernel, heads),
        name="attend_back",
        out_shape=(
            shape((2, rows, width), bf16),
            shape((each, 3 * width), f32),
            shape((each, width), f32),
            shape((each, ff), f32),
            shape((4 * each, width), f32),
            shape((8, LANES), f32),
        ),
        in_specs=[any_space] * 10 + [vmem],
        out_specs=(any_space,) + (vmem,) * 5,
        scratch_shapes=[
            pltpu.VMEM((GROUPS, rows, 2 * heads * HD), bf16),
            pltpu.VMEM((heads, total, HD), bf16),
            pltpu.VMEM((heads, 4, 8, 2 * rows), f32),
            pltpu.VMEM((3 * heads, total, LANES), bf16),
            pltpu.VMEM(ot.shape, f32),
            pltpu.VMEM(lse.shape, f32),
            pltpu.VMEM((width, total), bf16),
            pltpu.VMEM(by_head.shape, bf16),
            pltpu.VMEM((2 * rows, width), f32),
            pltpu.VMEM((heads, LANES, total), bf16),
            pltpu.VMEM((total, HD), bf16),
            pltpu.VMEM((total, HD), f32),
            pltpu.VMEM((total, HD), f32),
            pltpu.VMEM((heads, total, 3 * HD), bf16),
            pltpu.VMEM((heads, 4, rows, 2 * HD), bf16),
            pltpu.VMEM((heads, 4, 2 * rows, 2 * HD), bf16),
            pltpu.VMEM((GROUPS * heads, rows, 2 * HD), bf16),
            pltpu.VMEM((GROUPS * heads, 2 * rows, 2 * HD), bf16),
            pltpu.VMEM((2 * rows, width), bf16),
            pltpu.VMEM((2 * rows, width), f32),
            pltpu.VMEM((2, rows, width), bf16),
            pltpu.VMEM((2, 2, 2, 2, *unit), bf16),
            pltpu.VMEM((UNITS, 2, 2, 2, 2, *unit), bf16),
            pltpu.VMEM((UNITS, 2, 2, 2, *unit), bf16),
            pltpu.VMEM((UNITS, 2, 2, *unit), bf16),
            pltpu.VMEM((UNITS, 2, *unit), bf16),
            pltpu.VMEM((UNITS, *unit), bf16),
            pltpu.VMEM((heads, 4, 6, 2 * each, 2 * HD), bf16),
            pltpu.VMEM((heads, 4, 6, 2 * each, 2 * HD), bf16),
            pltpu.VMEM((heads, 8, 3 * HD), f32),
            pltpu.VMEM((heads, 4, 8, 3 * HD), f32),
            pltpu.VMEM((heads, 8, (each + 8) // 2, 6 * HD), bf16),
            pltpu.VMEM((heads, 8, (each + 8) // 2, 6 * HD), bf16),
            pltpu.VMEM((4, 16, width), f32),
            pltpu.VMEM((4, 16, width), f32),
            pltpu.VMEM((3, 16, width), f32),
            dma((GROUPS,)),
            dma((GROUPS,)),
            dma((2, heads, 4)),
            dma((2, GROUPS * heads)),
            dma((2,)),
            dma((2,)),
            dma((STAGES, UNITS)),
            dma((STAGES, UNITS)),
            dma((2 * heads + 1, 4)),
            dma((2 * heads + 1, 4)),
            dma((heads + 1, 8)),
            dma((heads + 1, 8)),
            dma((9,)),
            dma((1,)),
        ],
        compiler_params=pltpu.CompilerParams(
            collective_id=2, has_side_effects=True, vmem_limit_bytes=62 << 20
        ),
    )(dctx, qkv, ot, lse, kt, full_t, by_head, pre, sums, parts, small)


def finish_kernel(whole, *refs):
    little_ref, outs = refs[whole], refs[whole + 1 :]
    for src, dst in zip(refs[:whole], outs[:whole]):
        dst[...] = src[...]
    for at, dst in enumerate(outs[whole:]):
        dst[...] = little_ref[at, : dst.shape[0]]


def finish(arrays, little, counts):
    vmem = pl.BlockSpec(memory_space=pltpu.VMEM)
    shapes = [jax.ShapeDtypeStruct(a.shape, a.dtype) for a in arrays]
    shapes += [jax.ShapeDtypeStruct((count,), jnp.float32) for count in counts]
    return pl.pallas_call(
        functools.partial(finish_kernel, len(arrays)),
        name="finish",
        out_shape=tuple(shapes),
        in_specs=[vmem] * (len(arrays) + 1),
        out_specs=(vmem,) * len(shapes),
    )(*arrays, little)


def halves(grad):
    cut = grad.shape[2] // 2
    return jnp.concatenate([grad[:, :, :cut], grad[:, :, cut:]], axis=1)


def norm_parts(inputs):
    centred = inputs - jnp.mean(inputs, axis=-1, keepdims=True)
    inverse = lax.rsqrt(jnp.mean(centred * centred, axis=-1, keepdims=True) + EPSILON)
    return centred * inverse, inverse


def norm_back(grad, normed, inverse, gain):
    e = grad * gain
    return inverse * (
        e
        - jnp.mean(e, axis=-1, keepdims=True)
        - normed * jnp.mean(e * normed, axis=-1, keepdims=True)
    )


def column_sum(block):
    return jnp.sum(block.astype(jnp.float32), axis=0, keepdims=True)


def ffn_kernel(
    tok_hbm,
    ctx_hbm,
    cot_hbm,
    par_ref,
    outw_hbm,
    upw_hbm,
    downw_hbm,
    layer_ref,
    dctx_ref,
    pre_ref,
    small_ref,
    sums_ref,
    parts_ref,
    tok_ref,
    ctx_ref,
    cot_ref,
    outw_ref,
    upw,
    downw,
    hid,
    hlow,
    hlow_t,
    norm1,
    slopes,
    active_t,
    pre2,
    gbranch,
    ghid,
    out,
    dparts,
    uparts,
    sum0,
    load_sem,
    keep_sem,
    osend_sem,
    orecv_sem,
    ssend_sem,
    srecv_sem,
):
    f32, bf16 = jnp.float32, jnp.bfloat16
    groups, rows, cols = ctx_ref.shape
    cols = cols // 2
    sides = 2
    width = tok_ref.shape[1]
    chunks = active_t.shape[0]
    each = width // 32
    tab, blk, chip, core = place()
    loads = (
        pltpu.make_async_copy(upw_hbm, upw, load_sem.at[0]),
        pltpu.make_async_copy(downw_hbm, downw, load_sem.at[1]),
    )
    first = [
        pltpu.make_async_copy(src, dst, load_sem.at[2 + at])
        for at, (src, dst) in enumerate(
            ((tok_hbm, tok_ref), (ctx_hbm, ctx_ref), (outw_hbm, outw_ref), (cot_hbm, cot_ref))
        )
    ]
    for copy in first:
        copy.start()
    for copy in loads:
        copy.start()

    greet_all(tab, blk)
    for copy in first:
        copy.wait()

    def par(at):
        return par_ref[at : at + 1]

    inverse1 = []
    contexts = [unfold(ctx_ref[group]) for group in range(groups)]
    for table in range(sides):
        cut = pl.ds(table * rows, rows)
        pre1 = tok_ref[cut].astype(f32) + par(0)
        for group in range(groups):
            pre1 += jnp.dot(
                contexts[group][table * rows : (table + 1) * rows],
                outw_ref[group * cols : (group + 1) * cols],
                preferred_element_type=f32,
            )
        normed, inverse = norm_parts(pre1)
        inverse1.append(inverse)
        hidden = normed * par(1) + par(2)
        low = hidden.astype(bf16)
        norm1[cut] = normed
        hid[cut] = hidden
        hlow[cut] = low
        hlow_t[:, cut] = low.T

    pre2[...] = hid[...] + par(3)
    for copy in loads:
        copy.wait()

    def forward(at):
        cut = pl.ds(pl.multiple_of(at * width, width), width)
        upper = jnp.dot(
            hlow[...], upw[:, cut], preferred_element_type=f32
        ) + par_ref[pl.ds(24 + at, 1)]
        cdf = 0.5 + 0.5 * lax.erf(upper * math.sqrt(0.5))
        act = (upper * cdf).astype(bf16)
        slopes[at] = cdf + upper * jnp.exp(-0.5 * upper * upper) * (1 / math.sqrt(2 * math.pi))
        active_t[at] = act.T
        pre2[...] += jnp.dot(act, downw[cut], preferred_element_type=f32)

    @pl.loop(0, chunks // 2)
    def _(pair):
        forward(2 * pair)
        forward(2 * pair + 1)

    normed, inverse = norm_parts(pre2[...])
    out[...] = (normed * par(4) + par(5)).astype(bf16).reshape(out.shape)
    return_rows(out, layer_ref, osend_sem, orecv_sem, "start")
    grad = cot_ref[...].astype(f32)
    small_ref[4:5] = column_sum(grad * normed)
    small_ref[5:6] = column_sum(grad)
    gpre2 = norm_back(grad, normed, inverse, par(4))
    ghid[...] = gpre2
    low = gpre2.astype(bf16)
    gbranch[...] = low
    small_ref[3:4] = column_sum(low)

    def core_copy(unit, src):
        return send_to(
            src.at[:, :, :, :, 1 - core],
            sum0.at[unit],
            ssend_sem.at[unit],
            srecv_sem.at[unit],
            (tab, 2 * chip + 1 - core),
        )

    def add_core(unit, parts):
        landed(sum0.at[unit], srecv_sem.at[unit])
        for a in range(2):
            for b in range(2):
                sum0[unit, a, b] = sum0[unit, a, b] + parts[a, b, :, :, core]

    @pl.loop(0, chunks)
    def _(at):
        wdown = jnp.dot(active_t[at], gbranch[...], preferred_element_type=f32)
        wdown = wdown.reshape(8, 4, each, width)
        for part in range(4):
            dparts[part, at // 2, lax.rem(at, 2)] = (
                halves(wdown[:, part]).astype(bf16).reshape(dparts.shape[3:])
            )

    for unit in range(4):
        core_copy(unit, dparts.at[unit]).start()

    @pl.loop(0, chunks)
    def _(at):
        cut = pl.ds(pl.multiple_of(at * width, width), width)

        @pl.when(jnp.logical_or(at == 1, at == 2))
        def _():
            for unit in (2 * at - 2, 2 * at - 1):
                add_core(unit, dparts.at[unit])

        gact = times_t(gbranch[...], downw[cut])
        gup = (gact * slopes[at]).astype(bf16)
        small_ref[pl.ds(6 + at, 1)] = column_sum(gup)
        ghid[...] += times_t(gup, upw[:, cut])
        wup = jnp.dot(hlow_t[...], gup, preferred_element_type=f32)
        uparts[at] = halves(wup.reshape(32, each, width)).astype(bf16).reshape(uparts.shape[1:])
        core_copy(4 + at, uparts.at[at]).start()

    small = [0.0, 0.0, 0.0]
    lows = []
    for table in range(sides):
        cut = pl.ds(table * rows, rows)
        grad, normed = ghid[cut], norm1[cut]
        small[1] += column_sum(grad * normed)
        small[2] += column_sum(grad)
        gpre1 = norm_back(grad, normed, inverse1[table], par(1))
        pre_ref[cut] = gpre1
        low = gpre1.astype(bf16)
        small[0] += column_sum(low)
        lows.append(low)
    low = jnp.concatenate(lows, axis=0)
    for at in range(3):
        small_ref[at : at + 1] = small[at]
    small_ref[10:] = jnp.zeros((6, width), f32)
    wouts = []
    for group in range(groups):
        dctx_ref[group] = fold(
            times_t(low, outw_ref[group * cols : (group + 1) * cols]).astype(bf16)
        )
        wout = jnp.dot(unfold(ctx_ref[group]).T, low, preferred_element_type=f32)
        wouts.append(halves(wout.reshape(8, each, width)).astype(bf16))
    for unit in range(4):
        core_copy(unit, dparts.at[unit]).wait_send()
    dparts[0] = jnp.concatenate(wouts, axis=0).reshape(dparts.shape[1:])
    keep = [pltpu.make_async_copy(dparts.at[0], parts_ref, keep_sem.at[0])]

    @pl.loop(0, 4)
    def _(at):
        add_core(4 + at, uparts.at[at])
        core_copy(4 + at, uparts.at[at]).wait_send()

    keep.append(pltpu.make_async_copy(sum0, sums_ref, keep_sem.at[1]))
    for copy in keep:
        copy.start()
    return_rows(out, layer_ref, osend_sem, orecv_sem, "wait")
    for copy in keep:
        copy.wait()


def ffn(tokens, ctx, cotangent, params, out_weight, up_weight, down_weight):
    total, width = tokens.shape
    chunks = up_weight.shape[1] // width
    unit = (2 * (width // 32), width // 2)
    any_space = pl.BlockSpec(memory_space=pl.ANY)
    vmem = pl.BlockSpec(memory_space=pltpu.VMEM)
    bf16, f32 = jnp.bfloat16, jnp.float32
    flops = 18 * total * width * chunks * width + 6 * total * width * width
    return pl.pallas_call(
        ffn_kernel,
        name="ffn",
        out_shape=(
            jax.ShapeDtypeStruct((2, total // 2, width), bf16),
            jax.ShapeDtypeStruct(ctx.shape, bf16),
            jax.ShapeDtypeStruct((total, width), f32),
            jax.ShapeDtypeStruct((16, width), f32),
            jax.ShapeDtypeStruct((8, 2, 2, 2, 2, *unit), bf16),
            jax.ShapeDtypeStruct((2, 2, 2, 2, 2, *unit), bf16),
        ),
        in_specs=[any_space] * 3 + [vmem] + [any_space] * 3,
        out_specs=(any_space, vmem, vmem, vmem, any_space, any_space),
        scratch_shapes=[
            pltpu.VMEM(tokens.shape, bf16),
            pltpu.VMEM(ctx.shape, bf16),
            pltpu.VMEM(cotangent.shape, bf16),
            pltpu.VMEM(out_weight.shape, bf16),
            pltpu.VMEM(up_weight.shape, bf16),
            pltpu.VMEM(down_weight.shape, bf16),
            pltpu.VMEM((total, width), f32),
            pltpu.VMEM((total, width), bf16),
            pltpu.VMEM((width, total), bf16),
            pltpu.VMEM((total, width), f32),
            pltpu.VMEM((chunks, total, width), f32),
            pltpu.VMEM((chunks, width, total), bf16),
            pltpu.VMEM((total, width), f32),
            pltpu.VMEM((total, width), bf16),
            pltpu.VMEM((total, width), f32),
            pltpu.VMEM((2, total // 2, width), bf16),
            pltpu.VMEM((4, 2, 2, 2, 2, 2, *unit), bf16),
            pltpu.VMEM((4, 2, 2, 2, 2, 2, *unit), bf16),
            pltpu.VMEM((8, 2, 2, 2, 2, *unit), bf16),
            pltpu.SemaphoreType.DMA((6,)),
            pltpu.SemaphoreType.DMA((2,)),
            pltpu.SemaphoreType.DMA((2,)),
            pltpu.SemaphoreType.DMA((2,)),
            pltpu.SemaphoreType.DMA((8,)),
            pltpu.SemaphoreType.DMA((8,)),
        ],
        compiler_params=pltpu.CompilerParams(
            collective_id=3, has_side_effects=True, vmem_limit_bytes=63 << 20
        ),
        cost_estimate=pl.CostEstimate(
            flops=flops, bytes_accessed=40 << 20, transcendentals=total * width * chunks
        ),
    )(tokens, ctx, cotangent, params, out_weight, up_weight, down_weight)


def shards_direct(
    tokens,
    lengths,
    qkv_weight,
    qkv_bias,
    out_weight,
    out_bias,
    attn_gain,
    attn_shift,
    up_weight,
    up_bias,
    down_weight,
    down_bias,
    ffn_gain,
    ffn_shift,
    cotangent,
):
    tables, rows, width = tokens.shape
    f32 = jnp.float32
    heads = width // HD // GROUPS
    row = lax.broadcasted_iota(jnp.int32, (32, width), 0)
    params = jnp.zeros((32, width), jnp.bfloat16)
    spans = [
        (at, at + 1, vector)
        for at, vector in enumerate(
            (out_bias, attn_gain, attn_shift, down_bias, ffn_gain, ffn_shift)
        )
    ]
    spans += [(8, 16, qkv_bias[:width]), (16, 24, qkv_bias[width:])]
    spans += [
        (24 + at, 25 + at, up_bias[at * width : (at + 1) * width])
        for at in range(up_bias.shape[0] // width)
    ]
    for first, last, vector in spans:
        params = jnp.where((row >= first) & (row < last), vector[None], params)

    params = params.astype(f32)
    ctx, my_tokens, my_cotangent, full_t, qkv, ot, lse, by_head, kt = attend(
        tokens, lengths, params, qkv_weight, cotangent, heads
    )
    layer_out, dctx, pre, small, sums, parts = ffn(
        my_tokens.reshape(tables * rows, width),
        ctx,
        my_cotangent.reshape(tables * rows, width),
        params,
        out_weight,
        up_weight,
        down_weight,
    )
    *whole, little = attend_back(
        dctx, qkv, ot, lse, kt, full_t, by_head, pre, small, sums, parts, heads
    )
    each = width // 32
    whole.insert(1, layer_out)
    (
        token_grad,
        layer_out,
        wgrad_qkv,
        wgrad_out,
        wgrad_up,
        wgrad_down,
        bgrad_out,
        ggrad_attn,
        sgrad_attn,
        bgrad_down,
        ggrad_ffn,
        sgrad_ffn,
        bgrad_up,
        bgrad_qkv,
    ) = finish(whole, little, [each] * 6 + [4 * each, 2 * each])
    return (
        layer_out,
        token_grad,
        wgrad_qkv,
        bgrad_qkv,
        wgrad_out,
        bgrad_out,
        ggrad_attn,
        sgrad_attn,
        wgrad_up,
        bgrad_up,
        wgrad_down,
        bgrad_down,
        ggrad_ffn,
        sgrad_ffn,
    )


def solution(mesh):
    in_specs = (
        P("tab", "blk", None),
        P("tab"),
        P(),
        P(),
        P(),
        P(),
        P(),
        P(),
        P(),
        P(),
        P(),
        P(),
        P(),
        P(),
        P("tab", "blk", None),
    )
    out_specs = (
        P("tab", "blk", None),
        P("tab", "blk", None),
        P(("tab", "blk"), None),
        P(("tab", "blk")),
        P(("tab", "blk"), None),
        P(("tab", "blk")),
        P(("tab", "blk")),
        P(("tab", "blk")),
        P(("tab", "blk"), None),
        P(("tab", "blk")),
        P(("tab", "blk"), None),
        P(("tab", "blk")),
        P(("tab", "blk")),
        P(("tab", "blk")),
    )
    tab_count, blk_count = mesh.shape["tab"], mesh.shape["blk"]

    def pick(*operands):
        table_count = operands[0].shape[0] // tab_count
        head_count = operands[0].shape[2] // HD
        direct = table_count == 2 and blk_count == 8 and tab_count == 4 and head_count % 4 == 0
        body = shards_direct if direct else shards_ring
        return jax.shard_map(
            body, mesh=mesh, in_specs=in_specs, out_specs=out_specs, check_vma=False
        )(*operands)

    return pick
```

```python
import functools
import math

import jax
import jax.numpy as jnp
from jax import lax
from jax.experimental import pallas as pl
from jax.experimental.pallas import tpu as pltpu
from jax.sharding import PartitionSpec as P

HD = 64


EPSILON = 1e-05
NEGATIVE = -1e30


def from_behind(block, axis, distance):
    devices = range(lax.axis_size(axis))
    route = [((i - distance) % len(devices), i) for i in devices]
    return lax.ppermute(block, axis, route)


def norm_rows(inputs, gains, shifts):
    row_mean = jnp.mean(inputs, axis=-1, keepdims=True)
    centred = inputs - row_mean
    row_var = jnp.mean(centred * centred, axis=-1, keepdims=True)
    return centred * lax.rsqrt(row_var + EPSILON) * gains + shifts


def gelu_exact(inputs):
    return jax.nn.gelu(inputs, approximate=False)


def times_back(left, right):
    return lax.dot_general(
        left, right, (((1,), (1,)), ((), ())), preferred_element_type=jnp.float32
    )


def over_rows(left, right):
    return lax.dot_general(
        left, right, (((0,), (0,)), ((), ())), preferred_element_type=jnp.float32
    )


def shards_ring(
    tokens,
    lengths,
    qkv_weight,
    qkv_bias,
    out_weight,
    out_bias,
    attn_gain,
    attn_shift,
    up_weight,
    up_bias,
    down_weight,
    down_bias,
    ffn_gain,
    ffn_shift,
    cotangent,
):
    table_count, row_count, model_width = tokens.shape
    head_count = model_width // HD
    cycle_size = lax.axis_size("blk")
    cycle_place = lax.axis_index("blk")
    score_scale = HD ** (-0.5)
    flat_tokens = tokens.reshape(table_count * row_count, model_width)
    bias_full = jnp.concatenate(
        [
            qkv_bias[:model_width].astype(jnp.float32),
            jnp.zeros((model_width,), jnp.float32),
            qkv_bias[model_width:].astype(jnp.float32),
        ]
    )
    qkv_low = (
        jnp.dot(flat_tokens, qkv_weight, preferred_element_type=jnp.float32) + bias_full
    ).astype(jnp.bfloat16)
    queries = qkv_low[:, :model_width].reshape(table_count, row_count, head_count, HD)
    key_values = qkv_low[:, model_width:].reshape(table_count, row_count, 2 * model_width)

    def key_mask(first_row, key_count):
        positions = first_row + jnp.arange(key_count, dtype=jnp.int32)
        return (positions[None, :] < lengths[:, None])[:, None, None, :]

    def split_pair(pair_block):
        key_count = pair_block.shape[1]
        keys_part = pair_block[:, :, :model_width].reshape(table_count, key_count, head_count, HD)
        values_part = pair_block[:, :, model_width:].reshape(table_count, key_count, head_count, HD)
        return (keys_part, values_part)

    pair_block = lax.all_gather(key_values, "blk", axis=1, tiled=True)
    running_max = jnp.full((table_count, row_count, head_count), NEGATIVE, jnp.float32)
    keys_part, values_part = split_pair(pair_block)
    is_valid = key_mask(jnp.int32(0), pair_block.shape[1])
    raw_scores = jnp.einsum(
        "trhd,tkhd->trhk", queries, keys_part, preferred_element_type=jnp.float32
    )
    scores = jnp.where(is_valid, raw_scores * score_scale, NEGATIVE)
    peak_new = jnp.maximum(running_max, jnp.max(scores, axis=-1))
    exponent = jnp.where(is_valid, jnp.exp(scores - peak_new[..., None]), 0.0)
    running_sum = jnp.sum(exponent, axis=-1)
    weighted = jnp.einsum(
        "trhk,tkhd->trhd",
        exponent.astype(jnp.bfloat16),
        values_part,
        preferred_element_type=jnp.float32,
    )
    running_max, running_sum, weighted = (peak_new, running_sum, weighted)
    context = weighted / running_sum[..., None]
    log_total = running_max + jnp.log(running_sum)
    context_low = context.reshape(table_count * row_count, model_width).astype(jnp.bfloat16)
    attended = jnp.dot(
        context_low, out_weight, preferred_element_type=jnp.float32
    ) + out_bias.astype(jnp.float32)
    pre_one = flat_tokens.astype(jnp.float32) + attended
    gain_one = attn_gain.astype(jnp.float32)
    shift_one = attn_shift.astype(jnp.float32)
    hidden = norm_rows(pre_one, gain_one, shift_one)
    hidden_low = hidden.astype(jnp.bfloat16)
    upper = jnp.dot(hidden_low, up_weight, preferred_element_type=jnp.float32) + up_bias.astype(
        jnp.float32
    )
    active = gelu_exact(upper).astype(jnp.bfloat16)
    pre_two = (
        hidden
        + jnp.dot(active, down_weight, preferred_element_type=jnp.float32)
        + down_bias.astype(jnp.float32)
    )
    gain_two = ffn_gain.astype(jnp.float32)
    shift_two = ffn_shift.astype(jnp.float32)
    layer_out = norm_rows(pre_two, gain_two, shift_two).astype(jnp.bfloat16).reshape(tokens.shape)
    grad_out = cotangent.reshape(table_count * row_count, model_width).astype(jnp.float32)
    _, norm_two_back = jax.vjp(norm_rows, pre_two, gain_two, shift_two)
    grad_pre_two, ggrad_ffn, sgrad_ffn = norm_two_back(grad_out)
    grad_branch = grad_pre_two.astype(jnp.bfloat16)
    wgrad_down = over_rows(active, grad_branch)
    bgrad_down = jnp.sum(grad_branch, axis=0, dtype=jnp.float32)
    grad_active = times_back(grad_branch, down_weight)
    _, gelu_back = jax.vjp(gelu_exact, upper)
    grad_upper = gelu_back(grad_active)[0].astype(jnp.bfloat16)
    wgrad_up = over_rows(hidden_low, grad_upper)
    bgrad_up = jnp.sum(grad_upper, axis=0, dtype=jnp.float32)
    grad_hidden = grad_pre_two + times_back(grad_upper, up_weight)
    _, norm_one_back = jax.vjp(norm_rows, pre_one, gain_one, shift_one)
    grad_pre_one, ggrad_attn, sgrad_attn = norm_one_back(grad_hidden)
    grad_attended = grad_pre_one.astype(jnp.bfloat16)
    wgrad_out = over_rows(context_low, grad_attended)
    bgrad_out = jnp.sum(grad_attended, axis=0, dtype=jnp.float32)
    grad_context = times_back(grad_attended, out_weight).astype(jnp.bfloat16)
    grad_heads = grad_context.reshape(table_count, row_count, head_count, HD)
    row_delta = jnp.sum(grad_heads.astype(jnp.float32) * context, axis=-1)

    def cycle_turn_step(cycle_turn, cycle_state):
        pair_now, pair_grads, grad_queries = cycle_state
        owner_index = (cycle_place - cycle_turn) % cycle_size
        keys_part, values_part = split_pair(pair_now)
        is_valid = key_mask(owner_index * row_count, row_count)
        raw_scores = jnp.einsum(
            "trhd,tkhd->trhk", queries, keys_part, preferred_element_type=jnp.float32
        )
        scores = jnp.where(is_valid, raw_scores * score_scale, NEGATIVE)
        probs = jnp.where(is_valid, jnp.exp(scores - log_total[..., None]), 0.0)
        grad_probs = jnp.einsum(
            "trhd,tkhd->trhk", grad_heads, values_part, preferred_element_type=jnp.float32
        )
        grad_raw = (probs * (grad_probs - row_delta[..., None]) * score_scale).astype(jnp.bfloat16)
        grad_queries = grad_queries + jnp.einsum(
            "trhk,tkhd->trhd", grad_raw, keys_part, preferred_element_type=jnp.float32
        )
        grad_keys = jnp.einsum(
            "trhk,trhd->tkhd", grad_raw, queries, preferred_element_type=jnp.float32
        )
        grad_values = jnp.einsum(
            "trhk,trhd->tkhd",
            probs.astype(jnp.bfloat16),
            grad_heads,
            preferred_element_type=jnp.float32,
        )
        pair_grads = pair_grads + jnp.concatenate(
            [
                grad_keys.reshape(table_count, row_count, model_width),
                grad_values.reshape(table_count, row_count, model_width),
            ],
            axis=-1,
        )
        pair_next = from_behind(pair_now, "blk", 1)
        grads_next = from_behind(pair_grads.astype(jnp.bfloat16), "blk", 1).astype(pair_grads.dtype)
        return (pair_next, grads_next, grad_queries)

    cycle_start = (
        key_values,
        jnp.zeros((table_count, row_count, 2 * model_width), jnp.float32),
        jnp.zeros((table_count, row_count, head_count, HD), jnp.float32),
    )
    _, pair_home, grad_queries = lax.fori_loop(0, cycle_size, cycle_turn_step, cycle_start)
    grad_qkv = jnp.concatenate(
        [
            grad_queries.reshape(table_count * row_count, model_width),
            pair_home.reshape(table_count * row_count, 2 * model_width),
        ],
        axis=-1,
    ).astype(jnp.bfloat16)
    wgrad_qkv = over_rows(flat_tokens, grad_qkv)
    column_sums = jnp.sum(grad_qkv, axis=0, dtype=jnp.float32)
    bgrad_qkv = jnp.concatenate([column_sums[:model_width], column_sums[2 * model_width :]])
    token_grad = (
        (grad_pre_one + times_back(grad_qkv, qkv_weight)).astype(jnp.bfloat16).reshape(tokens.shape)
    )
    (
        wgrad_qkv,
        bgrad_qkv,
        wgrad_out,
        bgrad_out,
        ggrad_attn,
        sgrad_attn,
        wgrad_up,
        bgrad_up,
        wgrad_down,
        bgrad_down,
        ggrad_ffn,
        sgrad_ffn,
    ) = (
        lax.psum_scatter(
            wgrad_qkv.astype(jnp.bfloat16), "tab", scatter_dimension=0, tiled=True
        ).astype(jnp.float32),
        lax.psum_scatter(
            bgrad_qkv.astype(jnp.bfloat16), "tab", scatter_dimension=0, tiled=True
        ).astype(jnp.float32),
        lax.psum_scatter(
            wgrad_out.astype(jnp.bfloat16), "tab", scatter_dimension=0, tiled=True
        ).astype(jnp.float32),
        lax.psum_scatter(
            bgrad_out.astype(jnp.bfloat16), "tab", scatter_dimension=0, tiled=True
        ).astype(jnp.float32),
        lax.psum_scatter(
            ggrad_attn.astype(jnp.bfloat16), "tab", scatter_dimension=0, tiled=True
        ).astype(jnp.float32),
        lax.psum_scatter(
            sgrad_attn.astype(jnp.bfloat16), "tab", scatter_dimension=0, tiled=True
        ).astype(jnp.float32),
        lax.psum_scatter(
            wgrad_up.astype(jnp.bfloat16), "tab", scatter_dimension=0, tiled=True
        ).astype(jnp.float32),
        lax.psum_scatter(
            bgrad_up.astype(jnp.bfloat16), "tab", scatter_dimension=0, tiled=True
        ).astype(jnp.float32),
        lax.psum_scatter(
            wgrad_down.astype(jnp.bfloat16), "tab", scatter_dimension=0, tiled=True
        ).astype(jnp.float32),
        lax.psum_scatter(
            bgrad_down.astype(jnp.bfloat16), "tab", scatter_dimension=0, tiled=True
        ).astype(jnp.float32),
        lax.psum_scatter(
            ggrad_ffn.astype(jnp.bfloat16), "tab", scatter_dimension=0, tiled=True
        ).astype(jnp.float32),
        lax.psum_scatter(
            sgrad_ffn.astype(jnp.bfloat16), "tab", scatter_dimension=0, tiled=True
        ).astype(jnp.float32),
    )
    (
        wgrad_qkv,
        bgrad_qkv,
        wgrad_out,
        bgrad_out,
        ggrad_attn,
        sgrad_attn,
        wgrad_up,
        bgrad_up,
        wgrad_down,
        bgrad_down,
        ggrad_ffn,
        sgrad_ffn,
    ) = (
        lax.psum_scatter(
            wgrad_qkv.astype(jnp.bfloat16), "blk", scatter_dimension=0, tiled=True
        ).astype(jnp.float32),
        lax.psum_scatter(
            bgrad_qkv.astype(jnp.bfloat16), "blk", scatter_dimension=0, tiled=True
        ).astype(jnp.float32),
        lax.psum_scatter(
            wgrad_out.astype(jnp.bfloat16), "blk", scatter_dimension=0, tiled=True
        ).astype(jnp.float32),
        lax.psum_scatter(
            bgrad_out.astype(jnp.bfloat16), "blk", scatter_dimension=0, tiled=True
        ).astype(jnp.float32),
        lax.psum_scatter(
            ggrad_attn.astype(jnp.bfloat16), "blk", scatter_dimension=0, tiled=True
        ).astype(jnp.float32),
        lax.psum_scatter(
            sgrad_attn.astype(jnp.bfloat16), "blk", scatter_dimension=0, tiled=True
        ).astype(jnp.float32),
        lax.psum_scatter(
            wgrad_up.astype(jnp.bfloat16), "blk", scatter_dimension=0, tiled=True
        ).astype(jnp.float32),
        lax.psum_scatter(
            bgrad_up.astype(jnp.bfloat16), "blk", scatter_dimension=0, tiled=True
        ).astype(jnp.float32),
        lax.psum_scatter(
            wgrad_down.astype(jnp.bfloat16), "blk", scatter_dimension=0, tiled=True
        ).astype(jnp.float32),
        lax.psum_scatter(
            bgrad_down.astype(jnp.bfloat16), "blk", scatter_dimension=0, tiled=True
        ).astype(jnp.float32),
        lax.psum_scatter(
            ggrad_ffn.astype(jnp.bfloat16), "blk", scatter_dimension=0, tiled=True
        ).astype(jnp.float32),
        lax.psum_scatter(
            sgrad_ffn.astype(jnp.bfloat16), "blk", scatter_dimension=0, tiled=True
        ).astype(jnp.float32),
    )
    return (
        layer_out,
        token_grad,
        wgrad_qkv,
        bgrad_qkv,
        wgrad_out,
        bgrad_out,
        ggrad_attn,
        sgrad_attn,
        wgrad_up,
        bgrad_up,
        wgrad_down,
        bgrad_down,
        ggrad_ffn,
        sgrad_ffn,
    )


GROUPS = 4
LANES = 128
LOG2E = math.log2(math.e)
MESH = pl.DeviceIdType.MESH


def times_t(left, right):
    return lax.dot_general(
        left, right, (((1,), (1,)), ((), ())), preferred_element_type=jnp.float32
    )


def place():
    tab, blk = lax.axis_index("tab"), lax.axis_index("blk")
    return tab, blk, blk // 2, blk % 2


def meet(tab, blk):
    barrier = pltpu.get_barrier_semaphore()

    @pl.loop(1, 8)
    def _(step):
        pl.semaphore_signal(
            barrier, inc=1, device_id=(tab, lax.rem(blk + step, 8)), device_id_type=MESH
        )

    pl.semaphore_wait(barrier, 7)


def greet_all(tab, blk):
    barrier = pltpu.get_barrier_semaphore()
    for step in range(1, 8):
        pl.semaphore_signal(
            barrier, inc=1, device_id=(tab, lax.rem(blk + step, 8)), device_id_type=MESH
        )
    for step in range(1, 4):
        pl.semaphore_signal(
            barrier, inc=1, device_id=(lax.rem(tab + step, 4), blk), device_id_type=MESH
        )
    pl.semaphore_wait(barrier, 10)


def send_to(src, dst, send_sem, recv_sem, device):
    return pltpu.make_async_remote_copy(
        src_ref=src,
        dst_ref=dst,
        send_sem=send_sem,
        recv_sem=recv_sem,
        device_id=device,
        device_id_type=MESH,
    )


def landed(ref, sem):
    pltpu.make_async_copy(ref, ref, sem).wait()


def return_rows(src, dst, send_sem, recv_sem, act):
    tab, _, chip, core = place()
    half, group = chip // 2, 2 * lax.rem(chip, 2) + core
    for side in range(2):
        is_own = jnp.logical_and(chip == group, core == side)
        own = pltpu.make_async_copy(src.at[side], dst.at[half], recv_sem.at[half])
        away = send_to(
            src.at[side],
            dst.at[half],
            send_sem.at[side],
            recv_sem.at[half],
            (tab, 2 * group + side),
        )
        if act == "start":
            pl.when(is_own)(own.start)
            pl.when(jnp.logical_not(is_own))(away.start)
        else:
            pl.when(jnp.logical_not(is_own))(away.wait_send)
            landed(dst.at[side], recv_sem.at[side])


def by_core(core, act):
    pl.when(core == 0)(functools.partial(act, 0))
    pl.when(core == 1)(functools.partial(act, 1))


def fold(block):
    cut = block.shape[0] // 2
    return jnp.concatenate([block[:cut], block[cut:]], axis=1)


def unfold(block):
    cut = block.shape[1] // 2
    return jnp.concatenate([block[:, :cut], block[:, cut:]], axis=0)


def own_window(group, first, rows_ref, out):
    start = pl.multiple_of(first + LANES * ((3 * group) // 2), LANES)
    window = rows_ref[:, pl.ds(start, 2 * LANES)].astype(jnp.float32)
    window = pltpu.roll(window, lax.rem(2 * LANES - HD * lax.rem(group, 2), 2 * LANES), 1)
    left = window[:, :LANES]
    low = lax.broadcasted_iota(jnp.int32, left.shape, 1) < HD
    for head, lanes in enumerate((left, pltpu.roll(left, HD, 1), window[:, LANES:])):
        out(head, jnp.where(low, lanes, 0.0))


def attend_kernel(
    heads,
    tok_ref,
    len_ref,
    par_ref,
    w_hbm,
    cot_hbm,
    ctx_ref,
    mytok_ref,
    mycot_ref,
    fullt_ref,
    qkv_ref,
    ot_ref,
    lse_ref,
    wr_ref,
    kt_ref,
    tokv,
    toktv,
    wfull,
    wrv,
    wown,
    bown,
    qkvv,
    vtv,
    ktv,
    otv,
    lsev,
    acc,
    peaks,
    cotv,
    csend,
    send_sem,
    recv,
    csend_sem,
    crecv_sem,
    osend_sem,
    orecv_sem,
    local_sem,
):
    tab, blk, chip, core = place()
    half = chip // 2
    group = 2 * lax.rem(chip, 2) + core
    rows = tok_ref.shape[1]
    width = tok_ref.shape[2]
    is_near = jnp.logical_or(chip == 1, chip == 2)
    mate = chip + 1 - 2 * lax.rem(chip, 2)
    other_near = 2 - half
    other_far = 3 - 3 * half
    own_far = 3 * half
    scale = LOG2E / math.sqrt(HD)

    def remote(src, dst, send_sem, recv_sem, to_chip, to_core):
        return pltpu.make_async_remote_copy(
            src_ref=src,
            dst_ref=dst,
            send_sem=send_sem,
            recv_sem=recv_sem,
            device_id=(tab, 2 * to_chip + to_core),
            device_id_type=MESH,
        )

    here, there = tok_ref.at[half], tok_ref.at[1 - half]
    to_mate = remote(here, tokv.at[blk], send_sem.at[0], recv.at[blk], mate, core)
    to_other = remote(there, tokv.at[blk], send_sem.at[1], recv.at[blk], other_near, core)
    to_side = remote(here, tokv.at[blk], send_sem.at[2], recv.at[blk], chip, 1 - core)

    def to_far(slot, src_chip):
        which = 2 * src_chip + core
        ref = tokv.at[which]
        return remote(ref, ref, send_sem.at[2 + slot], recv.at[which], own_far, core)

    def to_core(slot, src_chip):
        which = 2 * src_chip + core
        ref = tokv.at[which]
        return remote(ref, ref, send_sem.at[5 + slot], recv.at[which], chip, 1 - core)

    def arrived(which):
        pltpu.make_async_copy(tokv.at[which], tokv.at[which], recv.at[which]).wait()

    load = pltpu.make_async_copy(w_hbm, wfull, local_sem.at[5])
    load.start()
    meet(tab, blk)
    pl.when(is_near)(to_other.start)
    to_mate.start()
    to_side.start()
    own_tokens = pltpu.make_async_copy(tok_ref.at[half], tokv.at[blk], local_sem.at[11])
    own_tokens.start()

    lane1 = lax.broadcasted_iota(jnp.int32, (8, LANES), 1)
    for at in (0, 2):

        def keep_bias(head, lanes, at=at):
            row = jnp.where(lane1 == HD, 1.0, lanes)
            bown[:, pl.ds((at * heads + head) * LANES, LANES)] = row

        own_window(group, 0, par_ref.at[pl.ds(8 * (1 + at // 2), 8)], keep_bias)
    for head in range(heads):
        bown[:, pl.ds((heads + head) * LANES, LANES)] = jnp.zeros((8, LANES), jnp.float32)
    load.wait()
    for at in range(3):

        def keep_weight(head, lanes, at=at):
            wown[:, pl.ds((at * heads + head) * LANES, LANES)] = lanes.astype(jnp.bfloat16)

        own_window(group, at * width, wfull, keep_weight)

    length = len_ref[half]
    lane = lax.broadcasted_iota(jnp.int32, (rows, LANES), 1)
    row = lax.broadcasted_iota(jnp.int32, (rows, LANES), 0)

    def project(which):
        first = pl.multiple_of(which * rows, rows)
        tok = tokv[which]
        y = jnp.dot(tok, wown[...], preferred_element_type=jnp.float32) + bown[:1]
        pad = jnp.where((lane == HD) & (row + first >= length), NEGATIVE, 0.0)
        for head in range(heads):
            q, k, v = (
                y[:, (part * heads + head) * LANES :][:, :LANES] for part in range(3)
            )
            qkvv[head, pl.ds(first, rows)] = q.astype(jnp.bfloat16)
            qkvv[heads + head, pl.ds(first, rows)] = (k + pad).astype(jnp.bfloat16)
            qkvv[2 * heads + head, pl.ds(first, rows)] = v.astype(jnp.bfloat16)
            vtv[head, :, pl.ds(first, rows)] = v.T.astype(jnp.bfloat16)
            ktv[head, :, pl.ds(first, rows)] = k.T.astype(jnp.bfloat16)
        toktv[:, pl.ds(first, rows)] = tok.T

    def take_keys(tile, head, first_key, count, fresh):
        queries = pl.ds(pl.multiple_of(tile * 2 * rows, 2 * rows), 2 * rows)
        keys = pl.ds(pl.multiple_of(first_key, count), count)
        st = times_t(qkvv[heads + head, keys], qkvv[head, queries])
        peak = jnp.max(st, axis=0, keepdims=True)
        if not fresh:
            before = peaks[tile, pl.ds(head, 1)]
            peak = jnp.maximum(peak, before)
        pt = jnp.exp2((st - peak) * scale).astype(jnp.bfloat16)
        ot = jnp.dot(vtv[head, :, keys], pt, preferred_element_type=jnp.float32)
        if not fresh:
            ot += acc[tile, head] * jnp.exp2((before - peak) * scale)
        acc[tile, head] = ot
        peaks[tile, pl.ds(head, 1)] = peak

    def meet_keys_of_own_half():
        @pl.loop(0, 2 * heads)
        def _(at):
            tile = jnp.where(at < heads, chip, mate)
            take_keys(tile, lax.rem(at, heads), half * 4 * rows, 4 * rows, True)

    def meet_keys_of_near():
        @pl.loop(0, heads)
        def _(head):
            take_keys(other_near, head, half * 4 * rows, 4 * rows, True)

        @pl.loop(0, 3 * heads)
        def _(at):
            tile = jnp.where(at < heads, chip, jnp.where(at < 2 * heads, mate, other_near))
            take_keys(tile, lax.rem(at, heads), other_near * 2 * rows, 2 * rows, False)

    def owner_of(table):
        return 2 * table + chip // 2, lax.rem(chip, 2)

    def cotangent_copy(table, own):
        src, dst = cot_hbm.at[table], mycot_ref.at[core]
        if own:
            return pltpu.make_async_copy(cotv, dst, orecv_sem.at[core])
        return remote(src, dst, osend_sem.at[table], orecv_sem.at[core], *owner_of(table))

    def is_owner(table):
        to_chip, to_core = owner_of(table)
        return jnp.logical_and(to_chip == chip, to_core == core)

    own_tokens.wait()
    own_cotangent = pltpu.make_async_copy(cot_hbm.at[half], cotv, local_sem.at[10])
    pl.when(is_owner(half))(own_cotangent.start)
    project(blk)

    @pl.when(is_owner(half))
    def _():
        own_cotangent.wait()
        cotangent_copy(half, True).start()

    def half_lanes(part, at):
        first = part * width + LANES * (at // 2)
        return wfull[:, first : first + LANES][:, HD * (at % 2) :][:, :HD]

    for head in range(heads):
        for part in range(3):
            for pair in range(GROUPS // 2):
                at = 2 * pair * heads + head
                wrv[head, :, pl.ds((2 * part + pair) * LANES, LANES)] = jnp.concatenate(
                    [half_lanes(part, at), half_lanes(part, at + heads)], axis=1
                )
    arrived(2 * mate + core)
    to_core(0, mate).start()

    @pl.when(jnp.logical_not(is_near))
    def _():
        to_mate.wait_send()
        to_other.start()

    project(2 * mate + core)
    arrived(2 * chip + 1 - core)
    project(2 * chip + 1 - core)
    arrived(2 * mate + 1 - core)
    project(2 * mate + 1 - core)

    def pass_on(slot, src_chip):
        arrived(2 * src_chip + core)
        pl.when(is_near)(to_far(slot, src_chip).start)
        to_core(slot, src_chip).start()

    def project_chip(src_chip):
        project(2 * src_chip + core)
        arrived(2 * src_chip + 1 - core)
        project(2 * src_chip + 1 - core)

    pl.when(is_near)(functools.partial(pass_on, 1, other_near))
    meet_keys_of_own_half()
    pl.when(jnp.logical_not(is_near))(functools.partial(pass_on, 1, other_near))
    pl.when(is_near)(functools.partial(pass_on, 2, other_far))
    cotangent_copy(1 - half, False).start()
    project_chip(other_near)
    meet_keys_of_near()
    pl.when(jnp.logical_not(is_near))(functools.partial(pass_on, 2, other_far))
    project_chip(other_far)

    keep = (
        pltpu.make_async_copy(toktv, fullt_ref, local_sem.at[0]),
        pltpu.make_async_copy(qkvv, qkv_ref, local_sem.at[1]),
        pltpu.make_async_copy(wrv, wr_ref, local_sem.at[6]),
        pltpu.make_async_copy(ktv, kt_ref, local_sem.at[9]),
    )
    for copy in keep:
        copy.start()

    pl.when(jnp.logical_not(is_owner(half)))(cotangent_copy(half, False).start)
    my_tokens = [
        pltpu.make_async_copy(
            tokv.at[2 * group + side], mytok_ref.at[side], local_sem.at[7 + side]
        )
        for side in range(2)
    ]
    for copy in my_tokens:
        copy.start()

    def context_copy(which):
        return remote(
            csend.at[which],
            ctx_ref.at[group],
            csend_sem.at[which],
            crecv_sem.at[group],
            2 * half + which // 2,
            lax.rem(which, 2),
        )

    own_context = pltpu.make_async_copy(
        csend.at[group], ctx_ref.at[group], local_sem.at[2]
    )

    @pl.loop(0, 4)
    def _(step):
        at = jnp.where(is_near, step, 3 - step)
        which = jnp.where(
            at < 2, jnp.where(at == 0, chip, mate), jnp.where(at == 2, other_near, other_far)
        )

        @pl.when(at == 3)
        def _():
            @pl.loop(0, heads)
            def _(head):
                take_keys(which, head, 0, 8 * rows, True)

        @pl.when(at < 3)
        def _():
            @pl.loop(0, heads)
            def _(head):
                take_keys(which, head, other_far * 2 * rows, 2 * rows, False)

        for head in range(heads):
            ot = acc[which, head]
            total = ot[HD : HD + 1]
            otv[which, head * HD : (head + 1) * HD] = ot[:HD] / total
            peak = peaks[which, head : head + 1]
            lsev[which, head : head + 1] = peak * scale + jnp.log(total) * LOG2E
        csend[which] = fold(otv[which].T.astype(jnp.bfloat16))

        pl.when(which == group)(own_context.start)
        pl.when(which != group)(context_copy(which).start)

    more = (
        pltpu.make_async_copy(otv, ot_ref, local_sem.at[3]),
        pltpu.make_async_copy(lsev, lse_ref, local_sem.at[4]),
    )
    for copy in more:
        copy.start()
    pl.when(is_near)(to_mate.wait_send)
    to_other.wait_send()
    to_side.wait_send()
    to_core(0, mate).wait_send()
    for slot, src_chip in ((1, other_near), (2, other_far)):
        pl.when(is_near)(to_far(slot, src_chip).wait_send)
        to_core(slot, src_chip).wait_send()

    for step in range(1, 4):
        which = lax.rem(group + step, 4)
        context_copy(which).wait_send()
        pltpu.make_async_copy(ctx_ref.at[which], ctx_ref.at[which], crecv_sem.at[which]).wait()
    own_context.wait()
    pl.when(jnp.logical_not(is_owner(half)))(cotangent_copy(half, False).wait_send)
    cotangent_copy(1 - half, False).wait_send()
    for side in range(2):
        pltpu.make_async_copy(mycot_ref.at[side], mycot_ref.at[side], orecv_sem.at[side]).wait()
    for copy in [*keep, *more, *my_tokens]:
        copy.wait()


def attend(tokens, lengths, params, qkv_weight, cotangent, heads):
    _, rows, width = tokens.shape
    blocks = 8
    total = blocks * rows
    any_space = pl.BlockSpec(memory_space=pl.ANY)
    vmem = pl.BlockSpec(memory_space=pltpu.VMEM)
    bf16, f32 = jnp.bfloat16, jnp.float32
    dma = pltpu.SemaphoreType.DMA
    return pl.pallas_call(
        functools.partial(attend_kernel, heads),
        name="attend",
        out_shape=(
            jax.ShapeDtypeStruct((GROUPS, rows, 2 * heads * HD), bf16),
            jax.ShapeDtypeStruct((2, rows, width), bf16),
            jax.ShapeDtypeStruct((2, rows, width), bf16),
            jax.ShapeDtypeStruct((width, total), bf16),
            jax.ShapeDtypeStruct((3 * heads, total, LANES), bf16),
            jax.ShapeDtypeStruct((4, heads * HD, 2 * rows), f32),
            jax.ShapeDtypeStruct((4, 8, 2 * rows), f32),
            jax.ShapeDtypeStruct((heads, width, width), bf16),
            jax.ShapeDtypeStruct((heads, LANES, total), bf16),
        ),
        in_specs=[
            any_space,
            pl.BlockSpec(memory_space=pltpu.SMEM),
            vmem,
            any_space,
            any_space,
        ],
        out_specs=(any_space,) * 9,
        scratch_shapes=[
            pltpu.VMEM((blocks, rows, width), bf16),
            pltpu.VMEM((width, total), bf16),
            pltpu.VMEM(qkv_weight.shape, bf16),
            pltpu.VMEM((heads, width, width), bf16),
            pltpu.VMEM((width, 3 * heads * LANES), bf16),
            pltpu.VMEM((8, 3 * heads * LANES), f32),
            pltpu.VMEM((3 * heads, total, LANES), bf16),
            pltpu.VMEM((heads, LANES, total), bf16),
            pltpu.VMEM((heads, LANES, total), bf16),
            pltpu.VMEM((4, heads * HD, 2 * rows), f32),
            pltpu.VMEM((4, 8, 2 * rows), f32),
            pltpu.VMEM((4, heads, LANES, 2 * rows), f32),
            pltpu.VMEM((4, 8, 2 * rows), f32),
            pltpu.VMEM((rows, width), bf16),
            pltpu.VMEM((GROUPS, rows, 2 * heads * HD), bf16),
            dma((8,)),
            dma((blocks,)),
            dma((GROUPS,)),
            dma((GROUPS,)),
            dma((2,)),
            dma((2,)),
            dma((12,)),
        ],
        compiler_params=pltpu.CompilerParams(
            collective_id=1, has_side_effects=True, vmem_limit_bytes=60 << 20
        ),
    )(tokens, lengths, params, qkv_weight, cotangent)


UNITS = 9
TURNS = 4
STAGES = 5
PHASE = ((1, 3), (2, 5), (3, 8), (4, 11))


def attend_back_kernel(
    heads,
    dctx_ref,
    qkv_ref,
    ot_ref,
    lse_ref,
    kt_ref,
    fullt_ref,
    w_ref,
    pre_ref,
    sums_ref,
    parts_ref,
    small_ref,
    tgrad_ref,
    wqkv_ref,
    wout_ref,
    wup_ref,
    wdown_ref,
    little_ref,
    dov,
    doh,
    deltas,
    qkvv,
    otv,
    lsev,
    toktv,
    wv,
    prev,
    ktv,
    dqv,
    dkv,
    dvv,
    dqkv,
    qsend,
    kvsend,
    arrive_q,
    arrive_kv,
    joined,
    xacc,
    xsend,
    mine,
    sum0,
    sum1,
    sum2,
    sum3,
    sum4,
    slab,
    slab_in,
    sums,
    sums_in,
    line,
    line_in,
    small_in,
    small_sum,
    small_pairs,
    dsend_sem,
    drecv_sem,
    gsend_sem,
    grecv_sem,
    xsend_sem,
    xrecv_sem,
    ssend_sem,
    srecv_sem,
    tsend_sem,
    trecv_sem,
    lsend_sem,
    lrecv_sem,
    local_sem,
    mine_sem,
):
    f32, bf16 = jnp.float32, jnp.bfloat16
    tab, blk, chip, core = place()
    y, x, zh, zl = tab // 2, lax.rem(tab, 2), chip // 2, lax.rem(chip, 2)
    half = zh
    group = 2 * zl + core
    blocks, rows = 8, dov.shape[1]
    width = toktv.shape[0]
    tile = 2 * rows
    piece = 256
    scale = LOG2E / math.sqrt(HD)
    shrink = HD**-0.5

    remote = send_to

    loads = [
        pltpu.make_async_copy(src, dst, local_sem.at[at])
        for at, (src, dst) in enumerate(
            (
                (qkv_ref, qkvv),
                (ot_ref, otv),
                (lse_ref, lsev),
                (dctx_ref.at[group], dov.at[group]),
                (fullt_ref, toktv),
                (w_ref, wv),
                (pre_ref, prev),
                (sums_ref, sum0.at[: UNITS - 1]),
                (kt_ref, ktv),
            )
        )
    ]
    for copy in [*loads[:4], loads[8], loads[7]]:
        copy.start()

    greet_all(tab, blk)

    def group_at(step):
        to_chip = jnp.where(step < 2, zl, 1 - zl)
        return 2 * to_chip + jnp.where(lax.rem(step, 2) == 0, core, 1 - core)

    def context_copy(which):
        return remote(
            dctx_ref.at[which],
            dov.at[group],
            dsend_sem.at[which],
            drecv_sem.at[group],
            (tab, 4 * half + which),
        )

    for step in range(1, 4):
        context_copy(group_at(step)).start()

    def stage_copy(stage, unit, order=None, held=None):
        held = sum0 if held is None else held
        send, done = ssend_sem.at[stage, unit], srecv_sem.at[stage, unit]
        if stage == 0:
            src = parts_ref.at[:, :, :, :, 1 - core]
            return remote(src, sum0.at[unit], send, done, (tab, 2 * chip + 1 - core))
        if stage == 1 and order == 0:
            return remote(
                held.at[unit, :, 1 - x], sum1.at[unit], send, done, (2 * y + 1 - x, blk)
            )
        if stage == 1:
            return remote(
                held.at[unit, 1 - y], sum1.at[unit], send, done, (2 * (1 - y) + x, blk)
            )
        if stage == 2 and order == 0:
            return remote(
                sum1.at[unit, 1 - y], sum2.at[unit], send, done, (2 * (1 - y) + x, blk)
            )
        if stage == 2:
            return remote(
                sum1.at[unit, 1 - x], sum2.at[unit], send, done, (2 * y + 1 - x, blk)
            )
        if stage == 3:
            src, there = sum2.at[unit, :, 1 - zl], 2 * zh + 1 - zl
            return remote(src, sum3.at[unit], send, done, (tab, 2 * there + core))
        src, there = sum3.at[unit, 1 - zh], 2 * (1 - zh) + zl
        return remote(src, sum4.at[unit], send, done, (tab, 2 * there + core))

    both = functools.partial(by_core, core)
    mine_copy = pltpu.make_async_copy(
        parts_ref.at[:, :, :, :, core], mine, mine_sem.at[0]
    )

    def finish(unit):
        done = sum4[unit].astype(f32) + sum3[unit, zh].astype(f32)
        top, low = done[: done.shape[0] // 2], done[done.shape[0] // 2 :]
        each, cut = top.shape

        @pl.when(unit < 4)
        def _():
            at = pl.ds(pl.multiple_of(unit * each, each), each)
            wdown_ref[at, :cut] = top
            wdown_ref[at, cut:] = low

        @pl.when(jnp.logical_and(unit >= 4, unit < 8))
        def _():
            at = pl.multiple_of((unit - 4) * 2 * cut, 2 * cut)
            wup_ref[:, pl.ds(at, cut)] = top
            wup_ref[:, pl.ds(pl.multiple_of(at + cut, cut), cut)] = low

        @pl.when(unit == 8)
        def _():
            wout_ref[:, :cut] = top
            wout_ref[:, cut:] = low

    def advance(stage, unit):
        if stage == 0:
            landed(sum0.at[unit], srecv_sem.at[0, unit])
            mine_copy.wait()
            for a in range(2):
                for b in range(2):
                    sum0[unit, a, b] = sum0[unit, a, b] + mine[a, b]

            both(lambda order: stage_copy(1, unit, order).start())
        elif stage == 1:
            landed(sum1.at[unit], srecv_sem.at[1, unit])

            def act(order):
                own = sum0[unit, :, x] if order == 0 else sum0[unit, y]
                sum1[unit] = sum1[unit] + own
                stage_copy(2, unit, order).start()

            both(act)
        elif stage == 2:
            landed(sum2.at[unit], srecv_sem.at[2, unit])

            def act(order):
                sum2[unit] = sum2[unit] + sum1[unit, y if order == 0 else x]

            both(act)
            stage_copy(3, unit).start()
        elif stage == 3:
            landed(sum3.at[unit], srecv_sem.at[3, unit])
            sum3[unit] = sum3[unit] + sum2[unit, :, zl]
            stage_copy(4, unit).start()
        else:
            landed(sum4.at[unit], srecv_sem.at[4, unit])
            finish(unit)

    def tick(now):
        @pl.when(now < UNITS - 1)
        def _():
            both(lambda order: stage_copy(1, now, order, sums_ref).start())

        pl.when(now == UNITS - 1)(functools.partial(advance, 0, UNITS - 1))
        for stage, lag in PHASE:
            unit = now - lag
            due = (unit >= 0) & (unit < UNITS)
            pl.when(due)(functools.partial(advance, stage, unit))

    stage_copy(0, UNITS - 1).start()
    mine_copy.start()

    def tab_copy(src, dst, sem_at, step):
        there = lax.rem(tab + step, 4)
        return remote(
            src(there), dst(tab), tsend_sem.at[sem_at, there], trecv_sem.at[sem_at, tab], (there, blk)
        )

    def line_copy(src, dst, sem_at, step):
        there = lax.rem(blk + step, 8)
        return remote(
            src(there), dst(blk), lsend_sem.at[sem_at, there], lrecv_sem.at[sem_at, blk], (tab, there)
        )

    def small_tab(step):
        return tab_copy(lambda t: small_ref, lambda t: small_in.at[t], heads, step)

    def small_pair(at):
        there = (2 * chip + 1 - core, 2 * (2 * zh + 1 - zl) + core, 2 * (2 * (1 - zh) + zl) + core)
        return remote(
            small_sum.at[at],
            small_pairs.at[at],
            lsend_sem.at[heads, at],
            lrecv_sem.at[heads, at],
            (tab, there[at]),
        )

    def slab_tab(head, step):
        return tab_copy(
            lambda t: slab.at[head, t], lambda t: slab_in.at[head, t], head, step
        )

    def slab_blk(head, step):
        return line_copy(
            lambda b: line.at[head, b], lambda b: line_in.at[head, b], head, step
        )

    for step in range(1, 4):
        small_tab(step).start()

    def pass_small(at):
        if at == 0:
            total = small_ref[...]
            for step in range(1, 4):
                there = lax.rem(tab + step, 4)
                landed(small_in.at[there], trecv_sem.at[heads, there])
                total += small_in[there]
        else:
            landed(small_pairs.at[at - 1], lrecv_sem.at[heads, at - 1])
            total = small_sum[at - 1] + small_pairs[at - 1]
        small_sum[at] = total
        if at < 3:
            small_pair(at).start()

    def sums_tab(head, step):
        return tab_copy(
            lambda t: sums.at[head], lambda t: sums_in.at[head, t], heads + 1 + head, step
        )

    def make_slab(head):
        flat = dqkv[head]
        sums[head] = jnp.broadcast_to(
            jnp.sum(flat.astype(f32), axis=0, keepdims=True), (8, 3 * HD)
        )
        grad = jnp.dot(toktv[...], flat, preferred_element_type=f32)
        each = width // 32
        slab[head, :, :4] = grad[:, : 2 * HD].reshape(4, 4, 2 * each, 2 * HD).astype(bf16)
        q = grad[:, 2 * HD :].reshape(16, 2, each, HD)
        q = jnp.concatenate([q[:, 0], q[:, 1]], axis=2)
        slab[head, :, 4:] = q.reshape(4, 2, 2 * each, 2 * HD).astype(bf16)
        for step in range(1, 4):
            slab_tab(head, step).start()
            sums_tab(head, step).start()

    def pass_slab(head):
        total = slab[head, tab].astype(f32)
        sums_total = sums[head]
        for step in range(1, 4):
            there = lax.rem(tab + step, 4)
            landed(slab_in.at[head, there], trecv_sem.at[head, there])
            landed(sums_in.at[head, there], trecv_sem.at[heads + 1 + head, there])
            total += slab_in[head, there].astype(f32)
            sums_total += sums_in[head, there]
        each = width // 32
        for b in range(8):
            kv = total[b // 2, b % 2 * each :][:each]
            q = total[4 + b // 4, b // 2 % 2 * each :][:each, b % 2 * HD :][:, :HD]
            rows_b = jnp.concatenate([jnp.concatenate([kv, q], axis=1), sums_total], axis=0)
            line[head, b] = fold(rows_b).astype(bf16)
        line_in[head, blk] = line[head, blk]
        for step in range(1, 8):
            slab_blk(head, step).start()

    for copy in [*loads[:4], loads[8]]:
        copy.wait()

    def gradient_copies(head, which, own):
        slot = group * heads + head
        pairs = (
            (qsend.at[head, which], arrive_q.at[slot]),
            (kvsend.at[head, which], arrive_kv.at[slot]),
        )
        for kind, (src, dst) in enumerate(pairs):
            if own:
                yield pltpu.make_async_copy(src, dst, grecv_sem.at[kind, slot])
            else:
                yield remote(
                    src,
                    dst,
                    gsend_sem.at[kind, head, which],
                    grecv_sem.at[kind, slot],
                    (tab, 4 * half + which),
                )

    def send_gradient(kind, head, which):
        @pl.when(which == group)
        def _():
            list(gradient_copies(head, which, True))[kind].start()

        @pl.when(which != group)
        def _():
            list(gradient_copies(head, which, False))[kind].start()

    def absorb(head):
        for at in range(GROUPS):
            slot = at * heads + head
            landed(arrive_q.at[slot], grecv_sem.at[0, slot])
            landed(arrive_kv.at[slot], grecv_sem.at[1, slot])
        for pair in range(GROUPS // 2):
            left, right = 2 * pair * heads + head, (2 * pair + 1) * heads + head
            lanes = slice(pair * LANES, (pair + 1) * LANES)
            for side in range(2):
                cut = slice(side * HD, (side + 1) * HD)
                joined[side * rows : (side + 1) * rows, lanes] = jnp.concatenate(
                    [arrive_q[left][:, cut], arrive_q[right][:, cut]], axis=1
                )
                lanes_kv = slice((2 * side + 2 + pair) * LANES, (2 * side + 3 + pair) * LANES)
                joined[:, lanes_kv] = jnp.concatenate(
                    [arrive_kv[left][:, cut], arrive_kv[right][:, cut]], axis=1
                )

    @pl.loop(0, heads * TURNS)
    def _(turn):
        head, step = turn // TURNS, lax.rem(turn, TURNS)
        which = group_at(step)
        first = pl.multiple_of(which * tile, tile)

        @pl.when(head == 0)
        def _():
            @pl.when(step > 0)
            def _():
                landed(dov.at[which], drecv_sem.at[which])

            dos = unfold(dov[which])
            dos_t = dos.T.astype(f32)
            for at in range(heads):
                do = dos[:, at * HD : (at + 1) * HD]
                doh[at, pl.ds(first, tile)] = do
                rows_at = slice(at * HD, (at + 1) * HD)
                ot = otv[which, rows_at]
                deltas[at, which, :1] = jnp.sum(ot * dos_t[rows_at], axis=0, keepdims=True)

        @pl.when(step == 0)
        def _():
            dkv[...] = jnp.zeros_like(dkv)
            dvv[...] = jnp.zeros_like(dvv)

        @pl.when(turn == 1)
        def _():
            for copy in loads[4:7]:
                copy.start()

        pl.when(turn == PHASE[0][1])(loads[7].wait)
        tick(turn)

        q_full = qkvv[head, pl.ds(first, tile)]
        q = q_full[:, :HD]
        do = doh[head, pl.ds(first, tile)]
        delta = deltas[head, which, :1]
        lse = lsev[which, pl.ds(head, 1)]
        dqt = jnp.zeros((LANES, tile), f32)
        for at in range(blocks * rows // piece):
            cut = pl.ds(at * piece, piece)
            st = times_t(qkvv[heads + head, cut], q_full)
            pt = jnp.exp2(st * scale - lse)
            dpt = times_t(qkvv[2 * heads + head, cut][:, :HD], do)
            dst = (pt * (dpt - delta)).astype(bf16)
            dvv[cut] += jnp.dot(pt.astype(bf16), do, preferred_element_type=f32)
            dkv[cut] += jnp.dot(dst, q, preferred_element_type=f32)
            dqt += jnp.dot(ktv[head, :, cut], dst, preferred_element_type=f32)
        dq = (dqt[:HD].T * shrink).astype(bf16)
        dqv[pl.ds(first, tile)] = dq
        qsend[head, which] = jnp.concatenate([dq[:rows], dq[rows:]], axis=1)
        send_gradient(0, head, which)

        @pl.when(step == TURNS - 1)
        def _():
            @pl.loop(0, 4)
            def _(at):
                there = lax.rem(group + 1 + at, 4)
                cut = pl.ds(pl.multiple_of(there * tile, tile), tile)
                pair = jnp.concatenate([dkv[cut] * shrink, dvv[cut]], axis=1).astype(bf16)
                kvsend[head, there] = pair
                send_gradient(1, head, there)
                dqkv[head, cut] = jnp.concatenate([pair, dqv[cut]], axis=1)

        @pl.when(turn == TURNS)
        def _():
            loads[4].wait()
            pass_small(0)

        for at in range(1, 4):
            pl.when(turn == TURNS + at)(functools.partial(pass_small, at))


    loads[5].wait()
    for head in range(heads - 1):
        absorb(head)
        product = times_t(joined[...], wv[head])
        xacc[...] = product if head == 0 else xacc[...] + product
    tick(heads * TURNS)
    absorb(heads - 1)
    loads[6].wait()
    for side in range(2):
        at = pl.ds(side * rows, rows)
        total = prev[at] + xacc[at] + times_t(joined[at], wv[heads - 1])
        xsend[side] = total.astype(bf16)
    return_rows(xsend, tgrad_ref, xsend_sem, xrecv_sem, "start")

    for head in range(heads):
        make_slab(head)
        tick(heads * TURNS + 1 + head)
    for head in range(heads):
        pass_slab(head)
    for now in range(heads * TURNS + 1 + heads, PHASE[-1][1] + UNITS):
        tick(now)

    def slabs_in(head, at):
        return [unfold(line_in[head, half_at * GROUPS + at].astype(f32)) for half_at in range(2)]

    for head in range(heads):
        for step in range(1, 8):
            there = lax.rem(blk + step, 8)
            landed(line_in.at[head, there], lrecv_sem.at[head, there])
    total = small_sum[3]
    own = [
        functools.reduce(jnp.add, slabs_in(at % heads, at // heads))
        for at in range(GROUPS * heads)
    ]
    each = width // 32
    bias = []
    for part in range(3):
        cut = slice((part + 2) % 3 * HD, (part + 2) % 3 * HD + HD)
        for pair in range(GROUPS * heads // 2):
            both_heads = jnp.concatenate([own[2 * pair][:, cut], own[2 * pair + 1][:, cut]], axis=1)
            lanes = slice(part * width + pair * LANES, part * width + (pair + 1) * LANES)
            wqkv_ref[:, lanes] = both_heads[:each]
            bias.append(both_heads[each:])
    pairs = GROUPS * heads // 2
    bias_q = jnp.concatenate(bias[:pairs], axis=1)
    bias_v = jnp.concatenate(bias[2 * pairs :], axis=1)
    bias = jnp.where(tab < 2, bias_q, bias_v)

    row = lax.broadcasted_iota(jnp.int32, (width, LANES), 0)
    lane = lax.broadcasted_iota(jnp.int32, (width, LANES), 1)

    def take(block, first, count):
        chosen = jnp.where((row == first + lane) & (lane < count), 1.0, 0.0)
        return jnp.dot(
            block, chosen, preferred_element_type=f32, precision=lax.Precision.HIGHEST
        )

    index = 8 * tab + blk
    little_ref[0:8] = take(total[:8], each * index, each)
    at_row = lax.broadcasted_iota(jnp.int32, total.shape, 0) == 6 + tab
    wide = jnp.sum(jnp.where(at_row, total, 0.0), axis=0, keepdims=True)
    little_ref[6:7] = take(jnp.broadcast_to(wide, (8, width)), 4 * each * blk, 4 * each)[:1]
    little_ref[7:8] = take(bias, 2 * each * lax.rem(index, 16), 2 * each)[:1]

    return_rows(xsend, tgrad_ref, xsend_sem, xrecv_sem, "wait")
    for step in range(1, 4):
        context_copy(group_at(step)).wait_send()

    @pl.loop(0, heads)
    def _(head):
        @pl.loop(1, 4)
        def _(step):
            for copy in gradient_copies(head, lax.rem(group + step, 4), False):
                copy.wait_send()

    for step in range(1, 8):
        for head in range(heads):
            slab_blk(head, step).wait_send()
    for at in range(3):
        small_pair(at).wait_send()
    for step in range(1, 4):
        small_tab(step).wait_send()
        for head in range(heads):
            slab_tab(head, step).wait_send()
            sums_tab(head, step).wait_send()

    stage_copy(0, UNITS - 1).wait_send()

    @pl.loop(0, UNITS)
    def _(unit):
        both(lambda order: stage_copy(1, unit, order).wait_send())
        both(lambda order: stage_copy(2, unit, order).wait_send())
        stage_copy(3, unit).wait_send()
        stage_copy(4, unit).wait_send()


def attend_back(dctx, qkv, ot, lse, kt, full_t, by_head, pre, small, sums, parts, heads):
    width, total = full_t.shape
    blocks = 8
    rows = total // blocks
    each, ff = width // 32, 4 * width
    any_space = pl.BlockSpec(memory_space=pl.ANY)
    vmem = pl.BlockSpec(memory_space=pltpu.VMEM)
    bf16, f32 = jnp.bfloat16, jnp.float32
    dma = pltpu.SemaphoreType.DMA
    unit = parts.shape[-2:]
    shape = jax.ShapeDtypeStruct
    return pl.pallas_call(
        functools.partial(attend_back_kernel, heads),
        name="attend_back",
        out_shape=(
            shape((2, rows, width), bf16),
            shape((each, 3 * width), f32),
            shape((each, width), f32),
            shape((each, ff), f32),
            shape((4 * each, width), f32),
            shape((8, LANES), f32),
        ),
        in_specs=[any_space] * 10 + [vmem],
        out_specs=(any_space,) + (vmem,) * 5,
        scratch_shapes=[
            pltpu.VMEM((GROUPS, rows, 2 * heads * HD), bf16),
            pltpu.VMEM((heads, total, HD), bf16),
            pltpu.VMEM((heads, 4, 8, 2 * rows), f32),
            pltpu.VMEM((3 * heads, total, LANES), bf16),
            pltpu.VMEM(ot.shape, f32),
            pltpu.VMEM(lse.shape, f32),
            pltpu.VMEM((width, total), bf16),
            pltpu.VMEM(by_head.shape, bf16),
            pltpu.VMEM((2 * rows, width), f32),
            pltpu.VMEM((heads, LANES, total), bf16),
            pltpu.VMEM((total, HD), bf16),
            pltpu.VMEM((total, HD), f32),
            pltpu.VMEM((total, HD), f32),
            pltpu.VMEM((heads, total, 3 * HD), bf16),
            pltpu.VMEM((heads, 4, rows, 2 * HD), bf16),
            pltpu.VMEM((heads, 4, 2 * rows, 2 * HD), bf16),
            pltpu.VMEM((GROUPS * heads, rows, 2 * HD), bf16),
            pltpu.VMEM((GROUPS * heads, 2 * rows, 2 * HD), bf16),
            pltpu.VMEM((2 * rows, width), bf16),
            pltpu.VMEM((2 * rows, width), f32),
            pltpu.VMEM((2, rows, width), bf16),
            pltpu.VMEM((2, 2, 2, 2, *unit), bf16),
            pltpu.VMEM((UNITS, 2, 2, 2, 2, *unit), bf16),
            pltpu.VMEM((UNITS, 2, 2, 2, *unit), bf16),
            pltpu.VMEM((UNITS, 2, 2, *unit), bf16),
            pltpu.VMEM((UNITS, 2, *unit), bf16),
            pltpu.VMEM((UNITS, *unit), bf16),
            pltpu.VMEM((heads, 4, 6, 2 * each, 2 * HD), bf16),
            pltpu.VMEM((heads, 4, 6, 2 * each, 2 * HD), bf16),
            pltpu.VMEM((heads, 8, 3 * HD), f32),
            pltpu.VMEM((heads, 4, 8, 3 * HD), f32),
            pltpu.VMEM((heads, 8, (each + 8) // 2, 6 * HD), bf16),
            pltpu.VMEM((heads, 8, (each + 8) // 2, 6 * HD), bf16),
            pltpu.VMEM((4, 16, width), f32),
            pltpu.VMEM((4, 16, width), f32),
            pltpu.VMEM((3, 16, width), f32),
            dma((GROUPS,)),
            dma((GROUPS,)),
            dma((2, heads, 4)),
            dma((2, GROUPS * heads)),
            dma((2,)),
            dma((2,)),
            dma((STAGES, UNITS)),
            dma((STAGES, UNITS)),
            dma((2 * heads + 1, 4)),
            dma((2 * heads + 1, 4)),
            dma((heads + 1, 8)),
            dma((heads + 1, 8)),
            dma((9,)),
            dma((1,)),
        ],
        compiler_params=pltpu.CompilerParams(
            collective_id=2, has_side_effects=True, vmem_limit_bytes=62 << 20
        ),
    )(dctx, qkv, ot, lse, kt, full_t, by_head, pre, sums, parts, small)


def finish_kernel(whole, *refs):
    little_ref, outs = refs[whole], refs[whole + 1 :]
    for src, dst in zip(refs[:whole], outs[:whole]):
        dst[...] = src[...]
    for at, dst in enumerate(outs[whole:]):
        dst[...] = little_ref[at, : dst.shape[0]]


def finish(arrays, little, counts):
    vmem = pl.BlockSpec(memory_space=pltpu.VMEM)
    shapes = [jax.ShapeDtypeStruct(a.shape, a.dtype) for a in arrays]
    shapes += [jax.ShapeDtypeStruct((count,), jnp.float32) for count in counts]
    return pl.pallas_call(
        functools.partial(finish_kernel, len(arrays)),
        name="finish",
        out_shape=tuple(shapes),
        in_specs=[vmem] * (len(arrays) + 1),
        out_specs=(vmem,) * len(shapes),
    )(*arrays, little)


def halves(grad):
    cut = grad.shape[2] // 2
    return jnp.concatenate([grad[:, :, :cut], grad[:, :, cut:]], axis=1)


def norm_parts(inputs):
    centred = inputs - jnp.mean(inputs, axis=-1, keepdims=True)
    inverse = lax.rsqrt(jnp.mean(centred * centred, axis=-1, keepdims=True) + EPSILON)
    return centred * inverse, inverse


def norm_back(grad, normed, inverse, gain):
    e = grad * gain
    return inverse * (
        e
        - jnp.mean(e, axis=-1, keepdims=True)
        - normed * jnp.mean(e * normed, axis=-1, keepdims=True)
    )


def column_sum(block):
    return jnp.sum(block.astype(jnp.float32), axis=0, keepdims=True)


def ffn_kernel(
    tok_hbm,
    ctx_hbm,
    cot_hbm,
    par_ref,
    outw_hbm,
    upw_hbm,
    downw_hbm,
    layer_ref,
    dctx_ref,
    pre_ref,
    small_ref,
    sums_ref,
    parts_ref,
    tok_ref,
    ctx_ref,
    cot_ref,
    outw_ref,
    upw,
    downw,
    hid,
    hlow,
    hlow_t,
    norm1,
    slopes,
    active_t,
    pre2,
    gbranch,
    ghid,
    out,
    dparts,
    uparts,
    sum0,
    load_sem,
    keep_sem,
    osend_sem,
    orecv_sem,
    ssend_sem,
    srecv_sem,
):
    f32, bf16 = jnp.float32, jnp.bfloat16
    groups, rows, cols = ctx_ref.shape
    cols = cols // 2
    sides = 2
    width = tok_ref.shape[1]
    chunks = active_t.shape[0]
    each = width // 32
    tab, blk, chip, core = place()
    loads = (
        pltpu.make_async_copy(upw_hbm, upw, load_sem.at[0]),
        pltpu.make_async_copy(downw_hbm, downw, load_sem.at[1]),
    )
    first = [
        pltpu.make_async_copy(src, dst, load_sem.at[2 + at])
        for at, (src, dst) in enumerate(
            ((tok_hbm, tok_ref), (ctx_hbm, ctx_ref), (outw_hbm, outw_ref), (cot_hbm, cot_ref))
        )
    ]
    for copy in first:
        copy.start()
    for copy in loads:
        copy.start()

    greet_all(tab, blk)
    for copy in first:
        copy.wait()

    def par(at):
        return par_ref[at : at + 1]

    inverse1 = []
    contexts = [unfold(ctx_ref[group]) for group in range(groups)]
    for table in range(sides):
        cut = pl.ds(table * rows, rows)
        pre1 = tok_ref[cut].astype(f32) + par(0)
        for group in range(groups):
            pre1 += jnp.dot(
                contexts[group][table * rows : (table + 1) * rows],
                outw_ref[group * cols : (group + 1) * cols],
                preferred_element_type=f32,
            )
        normed, inverse = norm_parts(pre1)
        inverse1.append(inverse)
        hidden = normed * par(1) + par(2)
        low = hidden.astype(bf16)
        norm1[cut] = normed
        hid[cut] = hidden
        hlow[cut] = low
        hlow_t[:, cut] = low.T

    pre2[...] = hid[...] + par(3)
    for copy in loads:
        copy.wait()

    def forward(at):
        cut = pl.ds(pl.multiple_of(at * width, width), width)
        upper = jnp.dot(
            hlow[...], upw[:, cut], preferred_element_type=f32
        ) + par_ref[pl.ds(24 + at, 1)]
        cdf = 0.5 + 0.5 * lax.erf(upper * math.sqrt(0.5))
        act = (upper * cdf).astype(bf16)
        slopes[at] = cdf + upper * jnp.exp(-0.5 * upper * upper) * (1 / math.sqrt(2 * math.pi))
        active_t[at] = act.T
        pre2[...] += jnp.dot(act, downw[cut], preferred_element_type=f32)

    @pl.loop(0, chunks // 2)
    def _(pair):
        forward(2 * pair)
        forward(2 * pair + 1)

    normed, inverse = norm_parts(pre2[...])
    out[...] = (normed * par(4) + par(5)).astype(bf16).reshape(out.shape)
    return_rows(out, layer_ref, osend_sem, orecv_sem, "start")
    grad = cot_ref[...].astype(f32)
    small_ref[4:5] = column_sum(grad * normed)
    small_ref[5:6] = column_sum(grad)
    gpre2 = norm_back(grad, normed, inverse, par(4))
    ghid[...] = gpre2
    low = gpre2.astype(bf16)
    gbranch[...] = low
    small_ref[3:4] = column_sum(low)

    def core_copy(unit, src):
        return send_to(
            src.at[:, :, :, :, 1 - core],
            sum0.at[unit],
            ssend_sem.at[unit],
            srecv_sem.at[unit],
            (tab, 2 * chip + 1 - core),
        )

    def add_core(unit, parts):
        landed(sum0.at[unit], srecv_sem.at[unit])
        for a in range(2):
            for b in range(2):
                sum0[unit, a, b] = sum0[unit, a, b] + parts[a, b, :, :, core]

    @pl.loop(0, chunks)
    def _(at):
        wdown = jnp.dot(active_t[at], gbranch[...], preferred_element_type=f32)
        wdown = wdown.reshape(8, 4, each, width)
        for part in range(4):
            dparts[part, at // 2, lax.rem(at, 2)] = (
                halves(wdown[:, part]).astype(bf16).reshape(dparts.shape[3:])
            )

    for unit in range(4):
        core_copy(unit, dparts.at[unit]).start()

    @pl.loop(0, chunks)
    def _(at):
        cut = pl.ds(pl.multiple_of(at * width, width), width)

        @pl.when(jnp.logical_or(at == 1, at == 2))
        def _():
            for unit in (2 * at - 2, 2 * at - 1):
                add_core(unit, dparts.at[unit])

        gact = times_t(gbranch[...], downw[cut])
        gup = (gact * slopes[at]).astype(bf16)
        small_ref[pl.ds(6 + at, 1)] = column_sum(gup)
        ghid[...] += times_t(gup, upw[:, cut])
        wup = jnp.dot(hlow_t[...], gup, preferred_element_type=f32)
        uparts[at] = halves(wup.reshape(32, each, width)).astype(bf16).reshape(uparts.shape[1:])
        core_copy(4 + at, uparts.at[at]).start()

    down_sums = pltpu.make_async_copy(sum0.at[:4], sums_ref.at[:4], keep_sem.at[2])
    down_sums.start()

    small = [0.0, 0.0, 0.0]
    lows = []
    for table in range(sides):
        cut = pl.ds(table * rows, rows)
        grad, normed = ghid[cut], norm1[cut]
        small[1] += column_sum(grad * normed)
        small[2] += column_sum(grad)
        gpre1 = norm_back(grad, normed, inverse1[table], par(1))
        pre_ref[cut] = gpre1
        low = gpre1.astype(bf16)
        small[0] += column_sum(low)
        lows.append(low)
    low = jnp.concatenate(lows, axis=0)
    for at in range(3):
        small_ref[at : at + 1] = small[at]
    small_ref[10:] = jnp.zeros((6, width), f32)
    wouts = []
    for group in range(groups):
        dctx_ref[group] = fold(
            times_t(low, outw_ref[group * cols : (group + 1) * cols]).astype(bf16)
        )
        wout = jnp.dot(unfold(ctx_ref[group]).T, low, preferred_element_type=f32)
        wouts.append(halves(wout.reshape(8, each, width)).astype(bf16))
    for unit in range(4):
        core_copy(unit, dparts.at[unit]).wait_send()
    dparts[0] = jnp.concatenate(wouts, axis=0).reshape(dparts.shape[1:])
    keep = [pltpu.make_async_copy(dparts.at[0], parts_ref, keep_sem.at[0])]
    keep[0].start()

    @pl.loop(0, 4)
    def _(at):
        add_core(4 + at, uparts.at[at])
        core_copy(4 + at, uparts.at[at]).wait_send()

    keep.append(pltpu.make_async_copy(sum0.at[4:], sums_ref.at[4:], keep_sem.at[1]))
    keep[1].start()
    keep.append(down_sums)
    return_rows(out, layer_ref, osend_sem, orecv_sem, "wait")
    for copy in keep:
        copy.wait()


def ffn(tokens, ctx, cotangent, params, out_weight, up_weight, down_weight):
    total, width = tokens.shape
    chunks = up_weight.shape[1] // width
    unit = (2 * (width // 32), width // 2)
    any_space = pl.BlockSpec(memory_space=pl.ANY)
    vmem = pl.BlockSpec(memory_space=pltpu.VMEM)
    bf16, f32 = jnp.bfloat16, jnp.float32
    flops = 18 * total * width * chunks * width + 6 * total * width * width
    return pl.pallas_call(
        ffn_kernel,
        name="ffn",
        out_shape=(
            jax.ShapeDtypeStruct((2, total // 2, width), bf16),
            jax.ShapeDtypeStruct(ctx.shape, bf16),
            jax.ShapeDtypeStruct((total, width), f32),
            jax.ShapeDtypeStruct((16, width), f32),
            jax.ShapeDtypeStruct((8, 2, 2, 2, 2, *unit), bf16),
            jax.ShapeDtypeStruct((2, 2, 2, 2, 2, *unit), bf16),
        ),
        in_specs=[any_space] * 3 + [vmem] + [any_space] * 3,
        out_specs=(any_space, vmem, vmem, vmem, any_space, any_space),
        scratch_shapes=[
            pltpu.VMEM(tokens.shape, bf16),
            pltpu.VMEM(ctx.shape, bf16),
            pltpu.VMEM(cotangent.shape, bf16),
            pltpu.VMEM(out_weight.shape, bf16),
            pltpu.VMEM(up_weight.shape, bf16),
            pltpu.VMEM(down_weight.shape, bf16),
            pltpu.VMEM((total, width), f32),
            pltpu.VMEM((total, width), bf16),
            pltpu.VMEM((width, total), bf16),
            pltpu.VMEM((total, width), f32),
            pltpu.VMEM((chunks, total, width), f32),
            pltpu.VMEM((chunks, width, total), bf16),
            pltpu.VMEM((total, width), f32),
            pltpu.VMEM((total, width), bf16),
            pltpu.VMEM((total, width), f32),
            pltpu.VMEM((2, total // 2, width), bf16),
            pltpu.VMEM((4, 2, 2, 2, 2, 2, *unit), bf16),
            pltpu.VMEM((4, 2, 2, 2, 2, 2, *unit), bf16),
            pltpu.VMEM((8, 2, 2, 2, 2, *unit), bf16),
            pltpu.SemaphoreType.DMA((6,)),
            pltpu.SemaphoreType.DMA((3,)),
            pltpu.SemaphoreType.DMA((2,)),
            pltpu.SemaphoreType.DMA((2,)),
            pltpu.SemaphoreType.DMA((8,)),
            pltpu.SemaphoreType.DMA((8,)),
        ],
        compiler_params=pltpu.CompilerParams(
            collective_id=3, has_side_effects=True, vmem_limit_bytes=63 << 20
        ),
        cost_estimate=pl.CostEstimate(
            flops=flops, bytes_accessed=40 << 20, transcendentals=total * width * chunks
        ),
    )(tokens, ctx, cotangent, params, out_weight, up_weight, down_weight)


def shards_direct(
    tokens,
    lengths,
    qkv_weight,
    qkv_bias,
    out_weight,
    out_bias,
    attn_gain,
    attn_shift,
    up_weight,
    up_bias,
    down_weight,
    down_bias,
    ffn_gain,
    ffn_shift,
    cotangent,
):
    tables, rows, width = tokens.shape
    f32 = jnp.float32
    heads = width // HD // GROUPS
    row = lax.broadcasted_iota(jnp.int32, (32, width), 0)
    params = jnp.zeros((32, width), jnp.bfloat16)
    spans = [
        (at, at + 1, vector)
        for at, vector in enumerate(
            (out_bias, attn_gain, attn_shift, down_bias, ffn_gain, ffn_shift)
        )
    ]
    spans += [(8, 16, qkv_bias[:width]), (16, 24, qkv_bias[width:])]
    spans += [
        (24 + at, 25 + at, up_bias[at * width : (at + 1) * width])
        for at in range(up_bias.shape[0] // width)
    ]
    for first, last, vector in spans:
        params = jnp.where((row >= first) & (row < last), vector[None], params)

    params = params.astype(f32)
    ctx, my_tokens, my_cotangent, full_t, qkv, ot, lse, by_head, kt = attend(
        tokens, lengths, params, qkv_weight, cotangent, heads
    )
    layer_out, dctx, pre, small, sums, parts = ffn(
        my_tokens.reshape(tables * rows, width),
        ctx,
        my_cotangent.reshape(tables * rows, width),
        params,
        out_weight,
        up_weight,
        down_weight,
    )
    *whole, little = attend_back(
        dctx, qkv, ot, lse, kt, full_t, by_head, pre, small, sums, parts, heads
    )
    each = width // 32
    whole.insert(1, layer_out)
    (
        token_grad,
        layer_out,
        wgrad_qkv,
        wgrad_out,
        wgrad_up,
        wgrad_down,
        bgrad_out,
        ggrad_attn,
        sgrad_attn,
        bgrad_down,
        ggrad_ffn,
        sgrad_ffn,
        bgrad_up,
        bgrad_qkv,
    ) = finish(whole, little, [each] * 6 + [4 * each, 2 * each])
    return (
        layer_out,
        token_grad,
        wgrad_qkv,
        bgrad_qkv,
        wgrad_out,
        bgrad_out,
        ggrad_attn,
        sgrad_attn,
        wgrad_up,
        bgrad_up,
        wgrad_down,
        bgrad_down,
        ggrad_ffn,
        sgrad_ffn,
    )


def solution(mesh):
    in_specs = (
        P("tab", "blk", None),
        P("tab"),
        P(),
        P(),
        P(),
        P(),
        P(),
        P(),
        P(),
        P(),
        P(),
        P(),
        P(),
        P(),
        P("tab", "blk", None),
    )
    out_specs = (
        P("tab", "blk", None),
        P("tab", "blk", None),
        P(("tab", "blk"), None),
        P(("tab", "blk")),
        P(("tab", "blk"), None),
        P(("tab", "blk")),
        P(("tab", "blk")),
        P(("tab", "blk")),
        P(("tab", "blk"), None),
        P(("tab", "blk")),
        P(("tab", "blk"), None),
        P(("tab", "blk")),
        P(("tab", "blk")),
        P(("tab", "blk")),
    )
    tab_count, blk_count = mesh.shape["tab"], mesh.shape["blk"]

    def pick(*operands):
        table_count = operands[0].shape[0] // tab_count
        head_count = operands[0].shape[2] // HD
        direct = table_count == 2 and blk_count == 8 and tab_count == 4 and head_count % 4 == 0
        body = shards_direct if direct else shards_ring
        return jax.shard_map(
            body, mesh=mesh, in_specs=in_specs, out_specs=out_specs, check_vma=False
        )(*operands)

    return pick
```
